32 devices in a mesh: replica: 8 (over z, y), shard: 4 (over x, core).
Axes of the slice: x: 2, y: 2, z: 4, core: 2. Of those that a mesh axis runs over, the one named last changes fastest.
Arguments:
- block_input: bfloat16 [16, 256, 2048], P('replica', 'shard'), may hold values from -6 to 6
- segment_ids: int32 [16, 256], P('replica'), may hold values from 0 to 3, never falling along the last dimension, each value on 1 to 192 neighbouring positions
- norm_gain: bfloat16 [2048], P('shard'), may hold values from 0.5 to 1.5
- w_in: bfloat16 [2048, 8192], P(None, 'shard'), may hold values from -0.125 to 0.125
- conv_weight: bfloat16 [4, 4096], P(None, 'shard'), may hold values from -3 to 3
- conv_bias: bfloat16 [4096], P('shard'), may hold values from -1.5 to 1.5
- x_proj: bfloat16 [160, 4096], P(None, 'shard'), may hold values from -1 to 1
- dt_proj: bfloat16 [128, 4096], P(None, 'shard'), may hold values from -0.5 to 0.5
- dt_bias: bfloat16 [4096], P('shard'), may hold values from -4 to 1
- d_skip: bfloat16 [4096], P('shard'), may hold values from 0.5 to 1.5
- out_proj: bfloat16 [4096, 2048], P(None, 'shard'), may hold values from -0.1875 to 0.1875
- out_grad: bfloat16 [16, 256, 2048], P('replica', 'shard'), may hold values from -6 to 6
Outputs:
- block_output: bfloat16 [16, 256, 2048], P('replica', 'shard')
- input_grad: bfloat16 [16, 256, 2048], P('replica', 'shard')
- grad_norm_gain: float32 [2048], P('shard')
- grad_w_in: float32 [2048, 8192], P('replica', 'shard')
- grad_conv_weight: float32 [4, 4096], P(None, 'shard')
- grad_conv_bias: float32 [4096], P('shard')
- grad_x_proj: float32 [160, 4096], P(None, 'shard')
- grad_dt_proj: float32 [128, 4096], P(None, 'shard')
- grad_dt_bias: float32 [4096], P('shard')
- grad_d_skip: float32 [4096], P('shard')
- grad_out_proj: float32 [4096, 2048], P('replica', 'shard')
The draws below stay inside these ranges and needn't reach their ends.
Inputs may be any that keep to these rules, and one draw needn't show every extreme that they name: `segment_ids`: within each sequence the ids never fall; each of the 4 documents holds 1 to 192 tokens and one holds exactly 192.
All inputs are finite; a program needn't handle non-finite values.
Results may differ from the reference program's by a relative error of at most 0.012.
The reference program's roundings to bfloat16 on the way count: a program that leaves them out, or rounds other values in their place, can miss the bound.
Values may be sent and summed in bfloat16 or wider, within the bound.
A program may use at most 240 MiB of HBM per device.

```python
import math
import jax
import jax.numpy as jnp
import numpy as np
from jax import lax

D = 2048
E = 4096
N = 16
R = 128
KW = 4
DOCS = 4
LEN = 256
SEQS = 16
DOC_MOST = 192


def draw_x_proj(key, part):
    key_base, key_scale = jax.random.split(jax.random.fold_in(key, 11))
    row_count = R + 2 * N
    base_vals = jnp.clip(jax.random.normal(key_base, (row_count, E), jnp.float32), -4.0, 4.0)
    row_factor = jnp.exp(jax.random.uniform(key_scale, (row_count, 1), jnp.float32, jnp.log(0.05), jnp.log(2.0)))
    row_index = jnp.arange(row_count)[:, None]
    is_key = (row_index >= R) & (row_index < R + N)
    scaled = jnp.where(is_key, row_factor, 1.0)
    return (base_vals * scaled * E ** (-0.5)).astype(jnp.bfloat16)


def levels(own_key, dims, cuts, least, top_value):
    level, own = 1.0, jax.random.fold_in(own_key, 6)
    for axis_at, parts in cuts:
        heights = jnp.exp(jax.random.uniform(jax.random.fold_in(own, axis_at), (parts,), jnp.float32, least / len(cuts), top_value / len(cuts)))
        level = level * jnp.repeat(heights, dims[axis_at] // parts).reshape([-1 if axis == axis_at else 1 for axis in range(len(dims))])
    return level


def split_up(number_of, total, limit, skew):
    portions = [(1 << 20) // math.isqrt(grade ** skew) + 1 for grade in range(2, number_of + 1)]
    rest, given = total - limit - (number_of - 1), [1] * (number_of - 1)
    while rest > 0:
        free = [i for i in range(number_of - 1) if given[i] < limit]
        pool, remaining = sum([portions[i] for i in free]), rest
        for i in free:
            extra = min(limit - given[i], max(1, remaining * portions[i] // pool), rest)
            given[i] = given[i] + extra
            rest = rest - extra
    return np.array([limit] + given)


def uneven(stream_key, count, total, most, lean):
    if count == 2:
        one = jax.random.randint(stream_key, (), max(1, total - most), min(most, total - 1) + 1)
        return jnp.stack([one, total - one])
    sizes = jnp.asarray(split_up(count, total, most, lean), jnp.int32)
    twos = (count - 1) // 2
    giver, sink = sizes[1:1 + 2 * twos:2], sizes[2:2 + 2 * twos:2]
    margin = jnp.minimum(giver - 1, most - sink)
    shifted = jax.random.randint(jax.random.fold_in(stream_key, 1), (twos,), 0, 1 << 20) % (margin + 1)
    sizes = sizes.at[1:1 + 2 * twos:2].set(giver - shifted).at[2:2 + 2 * twos:2].set(sink + shifted)
    return sizes[jax.random.permutation(jax.random.fold_in(stream_key, 2), count)]


def normal_values(rng, shape, deviation, limit, shards=(), held_as=jnp.bfloat16):
    values = jax.random.normal(rng, shape, jnp.float32) * deviation
    if len(shards) > 0:
        values = levels(rng, shape, shards, -0.22, 0.18) * values
    return jnp.clip(values, min=-limit, max=limit).astype(held_as)


def setup_inputs(seed: int = 0) -> dict:
    arg_keys = jax.random.split(jax.random.key(seed), 13)
    return {
        "block_input": normal_values(arg_keys[0], (SEQS, LEN, D), 1.0, 6.0, ((0, 8), (1, 4))),
        "segment_ids": jax.vmap(lambda own: jnp.searchsorted(jnp.cumsum(uneven(own, DOCS, LEN, DOC_MOST, 1)), jnp.arange(LEN), side="right"))(jax.random.split(arg_keys[1], SEQS)).reshape((SEQS, LEN)).astype(jnp.int32),
        "norm_gain": jnp.clip(1.0 + 0.1 * jax.random.normal(arg_keys[2], (D,), jnp.float32), 0.5, 1.5).astype(jnp.bfloat16),
        "w_in": normal_values(arg_keys[3], (D, 2 * E), D ** -0.5, 0.125, ((1, 4),)),
        "conv_weight": normal_values(arg_keys[4], (KW, E), KW ** -0.5, 3.0, ((1, 4),)),
        "conv_bias": normal_values(arg_keys[5], (E,), 0.3, 1.5, ((0, 4),)),
        "x_proj": draw_x_proj(jax.random.fold_in(arg_keys[12], 71), 0),
        "dt_proj": normal_values(arg_keys[7], (R, E), R ** -0.5, 0.5, ((1, 4),)),
        "dt_bias": jnp.clip(-4.0 + 5.0 * jax.random.uniform(arg_keys[8], (E,), jnp.float32) ** levels(arg_keys[8], (E,), ((0, 4),), -0.2, 0.2), -4.0, 1.0).astype(jnp.bfloat16),
        "d_skip": jnp.clip(0.5 + 1.0 * jax.random.uniform(arg_keys[9], (E,), jnp.float32) ** levels(arg_keys[9], (E,), ((0, 4),), -0.2, 0.2), 0.5, 1.5).astype(jnp.bfloat16),
        "out_proj": normal_values(arg_keys[10], (E, D), (E // 4) ** -0.5, 0.1875, ((1, 4),)),
        "out_grad": normal_values(arg_keys[11], (SEQS, LEN, D), 1.0, 6.0, ((0, 8), (1, 4))),
    }


@jax.custom_vjp
def low(v):
    return lax.optimization_barrier(v.astype(jnp.bfloat16)).astype(jnp.float32)

@jax.custom_vjp
def low_back(v):
    return v

def low_keep(v):
    return (low(v), None)

def low_pass(kept, grad):
    return (grad,)

def back_keep(v):
    return (v, None)

def back_low(kept, grad):
    return (low(grad),)
low.defvjp(low_keep, low_pass)
low_back.defvjp(back_keep, back_low)
EPS = 1e-05

def precise(first_op, second_op):
    return jnp.einsum('gtk,kn->gtn', first_op, second_op, precision=lax.Precision.HIGHEST)

def make_masks(seg_rows):
    length = seg_rows.shape[-1]
    tap_masks = []
    for offset in range(1, KW):
        earlier = jnp.pad(seg_rows, ((0, 0), (offset, 0)), constant_values=-1)[:, :length]
        tap_masks.append((earlier == seg_rows).astype(jnp.float32))
    return tap_masks

def ref_block(carried, pieces):
    rate_blk, conv_blk, key_blk, query_blk, keep_blk = pieces
    outputs = []
    for t in range(rate_blk.shape[1]):
        decay_now = (1.0 - rate_blk[:, t, :, None] * (key_blk[:, t, None, :] * key_blk[:, t, None, :])) * keep_blk[:, t, None, None]
        carried = decay_now * carried + (rate_blk[:, t] * conv_blk[:, t])[:, :, None] * key_blk[:, t, None, :]
        outputs.append(lax.optimization_barrier(jnp.sum(carried * query_blk[:, t, None, :], axis=2)))
    return (carried, jnp.stack(outputs, axis=1))

def recurrence(step_rate, conv_vals, key_rows, query_rows, keep_mask):
    groups_now, length, width = step_rate.shape
    count_blocks = length // 16

    def blocked(values):
        shaped = values.reshape((groups_now, count_blocks, 16) + values.shape[2:])
        return jnp.moveaxis(shaped, 1, 0)
    pieces = (blocked(step_rate), blocked(conv_vals), blocked(key_rows), blocked(query_rows), blocked(keep_mask))
    start_state = jnp.zeros((groups_now, width, N), jnp.float32)
    outputs = lax.scan(jax.checkpoint(ref_block), start_state, pieces)[1]
    return jnp.moveaxis(outputs, 0, 1).reshape(groups_now, length, width)

def forward(x_vals, norm_gain, w_in, conv_weight, conv_bias, x_proj, dt_proj, dt_bias, d_skip, out_proj, tap_masks):
    length = x_vals.shape[1]
    inv_rms = lax.rsqrt(lax.optimization_barrier(jnp.mean(x_vals * x_vals, axis=-1, keepdims=True)) + EPS)
    normed = low(x_vals * inv_rms * norm_gain)
    mixed = low(low_back(precise(normed, w_in)))
    x_part = mixed[..., :E]
    z_part = mixed[..., E:]
    padded = jnp.pad(x_part, ((0, 0), (KW - 1, 0), (0, 0)))
    conv_pre = conv_bias + conv_weight[KW - 1] * x_part
    for j in range(KW - 1):
        offset = KW - 1 - j
        conv_pre = conv_pre + conv_weight[j] * padded[:, j:j + length] * tap_masks[offset - 1][..., None]
    conv_out = low(jax.nn.silu(conv_pre))
    proj_vals = low_back(jnp.einsum('gtk,rk->gtr', conv_out, x_proj, precision=lax.Precision.HIGHEST))
    dt_in = proj_vals[..., :R]
    key_rows = proj_vals[..., R:R + N]
    query_rows = proj_vals[..., R + N:]
    beta_vals = jax.nn.sigmoid(low_back(precise(low(dt_in), dt_proj)) + dt_bias)
    step_rate = beta_vals / (1.0 + beta_vals * lax.optimization_barrier(jnp.sum(key_rows * key_rows, axis=-1, keepdims=True)))
    recurrent = recurrence(step_rate, conv_out, key_rows, query_rows, tap_masks[0])
    y_total = recurrent + d_skip * conv_out
    gated = low(y_total * jax.nn.silu(z_part))
    return x_vals + precise(gated, out_proj)

def reference(block_input, segment_ids, norm_gain, w_in, conv_weight, conv_bias, x_proj, dt_proj, dt_bias, d_skip, out_proj, out_grad):
    weights = tuple((w.astype(jnp.float32) for w in (norm_gain, w_in, conv_weight, conv_bias, x_proj, dt_proj, dt_bias, d_skip, out_proj)))
    seq_count = block_input.shape[0]
    groups = seq_count // 4
    x_groups = block_input.reshape((groups, 4) + block_input.shape[1:])
    seg_groups = segment_ids.reshape((groups, 4) + segment_ids.shape[1:])
    cot_groups = out_grad.reshape((groups, 4) + out_grad.shape[1:])

    def one_group(totals, inputs):
        x_grp, seg_grp, cot_grp = inputs
        tap_masks = make_masks(seg_grp)

        def apply_group(x_vals, *wts):
            return forward(x_vals, *wts, tap_masks)
        out_vals, pullback = jax.vjp(apply_group, x_grp.astype(jnp.float32), *weights)
        grad_list = pullback(cot_grp.astype(jnp.float32))
        totals = tuple((a + b for a, b in zip(totals, grad_list[1:])))
        return (totals, (out_vals.astype(jnp.bfloat16), grad_list[0].astype(jnp.bfloat16)))
    zero_grads = tuple((jnp.zeros_like(w) for w in weights))
    totals, (out_rows, grad_rows) = lax.scan(one_group, zero_grads, (x_groups, seg_groups, cot_groups))
    block_output = out_rows.reshape(block_input.shape)
    input_grad = grad_rows.reshape(block_input.shape)
    return (block_output, input_grad, totals[0], totals[1], totals[2], totals[3], totals[4], totals[5], totals[6], totals[7], totals[8])
```

```python
import functools

import jax
import jax.numpy as jnp
from jax import lax
from jax.experimental import pallas as pl
from jax.experimental.pallas import tpu as pltpu
from jax.sharding import PartitionSpec as P

KW = 4
EPS = 1e-05
CHUNK = 16
LANES = 128
f32 = jnp.float32
bf16 = jnp.bfloat16


def rows_dot(a, b):
    return jnp.dot(a, b, preferred_element_type=f32)


def inner_dot(a, b):
    return lax.dot_general(a, b, (((0,), (0,)), ((), ())), preferred_element_type=f32)


def outer_dot(a, b):
    return lax.dot_general(a, b, (((1,), (1,)), ((), ())), preferred_element_type=f32)


def silu_slope(values):
    sig_val = jax.nn.sigmoid(values)
    return sig_val + values * sig_val * (1.0 - sig_val)


def recurrence_kernel(
    rate_ref, conv_ref, dy_ref, keyc_ref, queryc_ref, key_ref, keep_ref, qd_ref, kd_ref, k2d_ref,
    y_ref, grate_ref, gconv_ref, gkey_ref, gquery_ref,
    state, rk, u, dys, kept, adj, adj_state, diag1, diag2, diag3,
):
    length, width = rate_ref.shape[1:]
    n = keyc_ref.shape[2]
    groups = width // LANES
    span = CHUNK * n
    chunks = length // CHUNK

    def lane(g):
        return slice(g * LANES, (g + 1) * LANES)

    def prepare(base):
        rows = pl.ds(base, CHUNK)
        rate = rate_ref[0, rows, :]
        keep = keep_ref[0, rows, :]
        conv = conv_ref[0, rows, :].astype(f32)
        for g in range(groups):
            rk[:, lane(g)] = rate[:, lane(g)] * keep
        u[...] = rate * conv
        kept[...] = keep
        return rate, conv, keep

    def column(block, t):
        return jnp.broadcast_to(block[:, t : t + 1], (n, LANES))

    def row(ref, t, g):
        return jnp.broadcast_to(ref[t : t + 1, lane(g)], (n, LANES))

    state[0:n, :] = jnp.zeros((n, width), state.dtype)

    def forward(j, held):
        base = pl.multiple_of(j * CHUNK, CHUNK)
        prepare(base)
        keys = keyc_ref[0, j]
        held = list(held)
        for t in range(CHUNK):
            key = column(keys, t)
            key2 = key * key
            keep = jnp.broadcast_to(kept[t : t + 1, :], (n, LANES))
            at = pl.ds(pl.multiple_of((base + t + 1) * n, n), n)
            for g in range(groups):
                decay = keep - row(rk, t, g) * key2
                held[g] = decay * held[g] + row(u, t, g) * key
                state[at, lane(g)] = held[g].astype(bf16)
        block = state[pl.ds(pl.multiple_of(base * n + n, n), span), :]
        y_ref[0, pl.ds(base, CHUNK), :] = rows_dot(qd_ref[0, pl.ds(base, CHUNK), :], block)
        return tuple(held)

    zero = tuple(jnp.zeros((n, LANES), f32) for _ in range(groups))
    lax.fori_loop(0, chunks, forward, zero)

    mask = (
        lax.broadcasted_iota(jnp.int32, (CHUNK, span), 1) // n
        == lax.broadcasted_iota(jnp.int32, (CHUNK, span), 0)
    )

    def backward(step, held):
        j = chunks - 1 - step
        base = pl.multiple_of(j * CHUNK, CHUNK)
        rows = pl.ds(base, CHUNK)
        rate, conv, keeps = prepare(base)
        dys[...] = dy_ref[0, rows, :]
        keys = keyc_ref[0, j]
        queries = queryc_ref[0, j]
        held = list(held)
        for t in reversed(range(CHUNK)):
            key = column(keys, t)
            key2 = key * key
            query = column(queries, t)
            keep = jnp.broadcast_to(kept[t : t + 1, :], (n, LANES))
            at = pl.ds(pl.multiple_of((base + t) * n, n), n)
            for g in range(groups):
                grad = held[g] + row(dys, t, g) * query
                decay = keep - row(rk, t, g) * key2
                held[g] = decay * grad
                adj[t * n : (t + 1) * n, lane(g)] = grad.astype(bf16)
                before = state[at, lane(g)].astype(f32)
                adj_state[t * n : (t + 1) * n, lane(g)] = (grad * before).astype(bf16)
        block = state[pl.ds(pl.multiple_of(base * n + n, n), span), :]
        w1 = rows_dot(kd_ref[0, rows, :], adj[...])
        w2 = rows_dot(k2d_ref[0, rows, :], adj_state[...])
        a1 = outer_dot(u[...].astype(bf16), adj[...])
        a2 = outer_dot(rk[...].astype(bf16), adj_state[...])
        a3 = outer_dot(dys[...].astype(bf16), block)
        diag1[rows, :] = jnp.where(mask, a1, 0.0)
        diag2[rows, :] = jnp.where(mask, a2, 0.0)
        diag3[rows, :] = jnp.where(mask, a3, 0.0)
        keep_all = jnp.concatenate([keeps] * groups, axis=1)
        grate = conv * w1 - keep_all * w2
        grate_ref[0, rows, :] = grate
        gconv_ref[0, rows, :] = rate * w1
        return tuple(held)

    lax.fori_loop(0, chunks, backward, zero)

    pick = (
        lax.broadcasted_iota(jnp.int32, (span, n), 0) % n
        == lax.broadcasted_iota(jnp.int32, (span, n), 1)
    ).astype(bf16)

    def picked(ref):
        value = ref[...]
        high = value.astype(bf16)
        low = (value - high.astype(f32)).astype(bf16)
        return rows_dot(high, pick) + rows_dot(low, pick)

    rate = rate_ref[0]
    self_term = jnp.sum(grate_ref[0] * rate * rate, axis=1, keepdims=True)
    gkey_ref[0] = picked(diag1) - 2.0 * key_ref[0] * (picked(diag2) + self_term)
    gquery_ref[0] = picked(diag3)


def recurrence(rate, conv, dy, keys, queries, keep):
    seqs, length, width = rate.shape
    n = keys.shape[2]
    span = CHUNK * n
    chunks = length // CHUNK

    def chunked(values):
        return values.reshape(seqs, chunks, CHUNK, n).transpose(0, 1, 3, 2)

    spot = (jnp.arange(length)[:, None] % CHUNK == jnp.arange(span)[None, :] // n)

    def diagonal(values):
        return jnp.where(spot, jnp.tile(values, (1, 1, CHUNK)), 0.0).astype(bf16)

    keep_lanes = jnp.broadcast_to(keep[:, :, None], (seqs, length, LANES))

    def spec(*shape):
        return pl.BlockSpec((1,) + shape, lambda s: (s,) + (0,) * len(shape))

    wide = spec(length, width)
    small = spec(length, n)
    square = spec(length, span)
    chunk_spec = spec(chunks, n, CHUNK)
    return pl.pallas_call(
        recurrence_kernel,
        grid=(seqs,),
        in_specs=[wide, wide, wide, chunk_spec, chunk_spec, small, spec(length, LANES), square, square, square],
        out_specs=[wide, wide, wide, small, small],
        out_shape=[jax.ShapeDtypeStruct((seqs, length, width), f32)] * 3
        + [jax.ShapeDtypeStruct((seqs, length, n), f32)] * 2,
        scratch_shapes=[
            pltpu.VMEM(((length + 1) * n, width), bf16),
            pltpu.VMEM((CHUNK, width), f32),
            pltpu.VMEM((CHUNK, width), f32),
            pltpu.VMEM((CHUNK, width), f32),
            pltpu.VMEM((CHUNK, LANES), f32),
            pltpu.VMEM((span, width), bf16),
            pltpu.VMEM((span, width), bf16),
            pltpu.VMEM((length, span), f32),
            pltpu.VMEM((length, span), f32),
            pltpu.VMEM((length, span), f32),
        ],
        compiler_params=pltpu.CompilerParams(vmem_limit_bytes=56 << 20),
        name="recurrence",
    )(rate, conv, dy, chunked(keys), chunked(queries), keys, keep_lanes, diagonal(queries), diagonal(keys), diagonal(keys * keys))


def to_channels(cols):
    half = cols.shape[1] // 2
    me = lax.axis_index("shard")
    first, second = cols[:, :half], cols[:, half:]
    low = me < 2
    one = lax.ppermute(jnp.where(low, first, second), "shard", [(0, 0), (1, 2), (2, 1), (3, 3)])
    two = lax.ppermute(jnp.where(low, second, first), "shard", [(0, 1), (1, 3), (2, 0), (3, 2)])
    even = me % 2 == 0
    return jnp.where(even, one, two), jnp.where(even, two, one)


def to_columns(x_part, z_part):
    me = lax.axis_index("shard")
    even = me % 2 == 0
    one = lax.ppermute(jnp.where(even, x_part, z_part), "shard", [(0, 0), (2, 1), (1, 2), (3, 3)])
    two = lax.ppermute(jnp.where(even, z_part, x_part), "shard", [(1, 0), (3, 1), (0, 2), (2, 3)])
    low = me < 2
    return jnp.concatenate([jnp.where(low, one, two), jnp.where(low, two, one)], axis=1)


def body(
    block_input, segment_ids, norm_gain, w_in, conv_weight, conv_bias, x_proj, dt_proj, dt_bias,
    d_skip, out_proj, out_grad,
):
    seqs, local, model = block_input.shape
    length = segment_ids.shape[1]
    tokens = seqs * length
    width = d_skip.shape[0]
    rank = dt_proj.shape[0]
    n = (x_proj.shape[0] - rank) // 2
    me = lax.axis_index("shard")

    x_all = lax.all_gather(block_input, "shard", axis=1, tiled=True).reshape(tokens, model)
    cot = lax.all_to_all(out_grad, "shard", split_axis=2, concat_axis=1, tiled=True).reshape(tokens, -1)
    gain = lax.all_gather(norm_gain, "shard", axis=0, tiled=True).astype(f32)

    def normalise(rows):
        vals = rows.astype(f32)
        inv = lax.rsqrt(jnp.mean(vals * vals, axis=-1, keepdims=True) + EPS)
        return vals, inv

    x_vals, inv_rms = normalise(x_all)
    normed = (x_vals * inv_rms * gain).astype(bf16)
    mixed = rows_dot(normed, w_in).astype(bf16)
    x_part, z_part = to_channels(mixed)
    grad_gated = lax.psum_scatter(outer_dot(cot, out_proj).astype(bf16), "shard", scatter_dimension=1, tiled=True).astype(f32)

    def split(values):
        return values.reshape(seqs, length, -1)

    seg_padded = jnp.pad(segment_ids, ((0, 0), (KW - 1, 0)), constant_values=-1)
    taps = [
        (seg_padded[:, KW - 1 - d : KW - 1 - d + length] == segment_ids).astype(f32) for d in range(KW)
    ]
    conv_w = conv_weight.astype(f32)
    xs = split(x_part).astype(f32)
    x_padded = jnp.pad(xs, ((0, 0), (KW - 1, 0), (0, 0)))
    conv_pre = conv_bias.astype(f32) + conv_w[KW - 1] * xs
    for j in range(KW - 1):
        d = KW - 1 - j
        conv_pre = conv_pre + conv_w[j] * x_padded[:, j : j + length] * taps[d][:, :, None]
    conv_out = jax.nn.silu(conv_pre).astype(bf16)
    conv_vals = conv_out.astype(f32)
    conv_flat = conv_out.reshape(tokens, width)
    proj = lax.psum(outer_dot(conv_flat, x_proj), "shard")
    dt_low = proj[:, :rank].astype(bf16)
    keys = split(proj[:, rank : rank + n])
    queries = split(proj[:, rank + n :])
    beta = split(jax.nn.sigmoid(rows_dot(dt_low, dt_proj) + dt_bias.astype(f32)))
    key_square = jnp.sum(keys * keys, axis=2, keepdims=True)
    denom_inv = 1.0 / (1.0 + beta * key_square)
    rate = beta * denom_inv

    z_vals = split(z_part).astype(f32)
    gate = jax.nn.silu(z_vals)
    grad_gated = split(grad_gated)
    dy = grad_gated * gate
    recurrent, grad_rate, grad_conv_rec, grad_keys, grad_queries = recurrence(
        rate, conv_out, dy, keys, queries, taps[1]
    )
    skip = d_skip.astype(f32)
    y_total = recurrent + skip * conv_vals
    gated = (y_total * gate).astype(bf16).reshape(tokens, width)
    gated_all = lax.all_gather(gated, "shard", axis=1, tiled=True)
    cols = model // 4
    x_cols = lax.dynamic_slice_in_dim(x_all, me * cols, cols, 1).astype(f32)
    out_cols = (x_cols + rows_dot(gated_all, out_proj)).astype(bf16).reshape(seqs, length, cols)
    block_output = lax.all_to_all(out_cols, "shard", split_axis=1, concat_axis=2, tiled=True)
    grad_out_proj = lax.psum_scatter(
        inner_dot(gated_all, cot).astype(bf16), "replica", scatter_dimension=0, tiled=True
    ).astype(f32)

    grad_z = (grad_gated * y_total * silu_slope(z_vals)).astype(bf16)
    grad_d_skip = jnp.sum(dy * conv_vals, axis=(0, 1))
    grad_dt = grad_rate * denom_inv * denom_inv * beta * (1.0 - beta)
    grad_dt_bias = jnp.sum(grad_dt, axis=(0, 1))
    grad_dt_low = grad_dt.astype(bf16).reshape(tokens, width)
    grad_dt_proj = inner_dot(dt_low, grad_dt_low)
    grad_proj = jnp.concatenate(
        [outer_dot(grad_dt_low, dt_proj), grad_keys.reshape(tokens, n), grad_queries.reshape(tokens, n)], axis=1
    )
    grad_proj = lax.psum(grad_proj, "shard").astype(bf16)
    grad_x_proj = inner_dot(grad_proj, conv_flat)
    grad_conv = dy * skip + grad_conv_rec + split(rows_dot(grad_proj, x_proj))
    grad_pre = grad_conv * silu_slope(conv_pre)
    grad_conv_bias = jnp.sum(grad_pre, axis=(0, 1))
    grad_conv_weight = jnp.stack(
        [
            jnp.sum(grad_pre * x_padded[:, j : j + length] * taps[KW - 1 - j][:, :, None], axis=(0, 1))
            for j in range(KW)
        ]
    )
    grad_x = conv_w[KW - 1] * grad_pre
    for j in range(KW - 1):
        d = KW - 1 - j
        ahead = jnp.pad(grad_pre * taps[d][:, :, None], ((0, 0), (0, d), (0, 0)))[:, d:]
        grad_x = grad_x + conv_w[j] * ahead
    grad_mixed = to_columns(grad_x.astype(bf16).reshape(tokens, width), grad_z.reshape(tokens, width))
    grad_w_in = lax.psum_scatter(
        inner_dot(normed, grad_mixed).astype(bf16), "replica", scatter_dimension=0, tiled=True
    ).astype(f32)
    grad_normed = lax.psum_scatter(
        split(outer_dot(grad_mixed, w_in)).astype(bf16), "shard", scatter_dimension=1, tiled=True
    ).astype(f32)
    x_own, inv_own = normalise(block_input)
    grad_gain = jnp.sum(grad_normed * x_own * inv_own, axis=(0, 1))
    scaled = grad_normed * gain
    grad_in = inv_own * (
        scaled - x_own * inv_own * inv_own * jnp.mean(scaled * x_own, axis=-1, keepdims=True)
    )
    input_grad = (out_grad.astype(f32) + grad_in).astype(bf16)

    small = jnp.concatenate(
        [
            grad_x_proj, grad_dt_proj, grad_conv_weight, grad_conv_bias[None], grad_dt_bias[None],
            grad_d_skip[None],
        ]
    )
    small = lax.psum(small.astype(bf16), "replica").astype(f32)
    grad_gain = lax.psum_scatter(lax.psum(grad_gain, "replica"), "shard", scatter_dimension=0, tiled=True)
    top = x_proj.shape[0]
    return (
        block_output, input_grad, grad_gain, grad_w_in,
        small[top + rank : top + rank + KW], small[top + rank + KW], small[:top], small[top : top + rank],
        small[top + rank + KW + 1], small[top + rank + KW + 2], grad_out_proj,
    )


def solution(mesh):
    return jax.shard_map(
        body,
        mesh=mesh,
        in_specs=(
            P("replica", "shard", None), P("replica", None), P("shard"), P(None, "shard"), P(None, "shard"),
            P("shard"), P(None, "shard"), P(None, "shard"), P("shard"), P("shard"), P(None, "shard"),
            P("replica", "shard", None),
        ),
        out_specs=(
            P("replica", "shard", None), P("replica", "shard", None), P("shard"), P("replica", "shard"),
            P(None, "shard"), P("shard"), P(None, "shard"), P(None, "shard"), P("shard"), P("shard"),
            P("replica", "shard"),
        ),
        check_vma=False,
    )
```

```python
import functools

import jax
import jax.numpy as jnp
from jax import lax
from jax.experimental import pallas as pl
from jax.experimental.pallas import tpu as pltpu
from jax.sharding import PartitionSpec as P

KW = 4
EPS = 1e-05
CHUNK = 16
LANES = 128
f32 = jnp.float32
bf16 = jnp.bfloat16


def rows_dot(a, b):
    return jnp.dot(a, b, preferred_element_type=f32)


def inner_dot(a, b):
    return lax.dot_general(a, b, (((0,), (0,)), ((), ())), preferred_element_type=f32)


def outer_dot(a, b):
    return lax.dot_general(a, b, (((1,), (1,)), ((), ())), preferred_element_type=f32)


def silu_slope(values):
    sig_val = jax.nn.sigmoid(values)
    return sig_val + values * sig_val * (1.0 - sig_val)

MESH = pl.DeviceIdType.MESH
BLOCK = 64


def lane(g):
    return slice(g * LANES, (g + 1) * LANES)


def column(block, t):
    return jnp.broadcast_to(block[:, t : t + 1], (block.shape[0], LANES))


def row(ref, t, g, n):
    return jnp.broadcast_to(ref[t : t + 1, lane(g)], (n, LANES))


def prepare(base, rate_ref, conv_ref, keep_ref, rk, u, kept):
    rows = pl.ds(base, CHUNK)
    rate = rate_ref[0, rows, :]
    keep = keep_ref[0, rows, :]
    conv = conv_ref[0, rows, :].astype(f32)
    for g in range(rate.shape[1] // LANES):
        rk[:, lane(g)] = rate[:, lane(g)] * keep
    u[...] = rate * conv
    kept[...] = keep
    return rate, conv, keep


def forward_kernel(rate_ref, conv_ref, keyc_ref, keep_ref, qd_ref, y_ref, state_ref, held_ref, rk, u, kept):
    width = rate_ref.shape[2]
    n = keyc_ref.shape[2]
    groups = width // LANES
    span = CHUNK * n

    @pl.when(pl.program_id(1) == 0)
    def _():
        held_ref[...] = jnp.zeros_like(held_ref)

    def chunk(j, held):
        base = pl.multiple_of(j * CHUNK, CHUNK)
        prepare(base, rate_ref, conv_ref, keep_ref, rk, u, kept)
        keys = keyc_ref[0, j]
        held = list(held)
        for t in range(CHUNK):
            key = column(keys, t)
            key2 = key * key
            keep = jnp.broadcast_to(kept[t : t + 1, :], (n, LANES))
            at = pl.ds(pl.multiple_of((base + t) * n, n), n)
            for g in range(groups):
                decay = keep - row(rk, t, g, n) * key2
                held[g] = decay * held[g] + row(u, t, g, n) * key
                state_ref[0, at, lane(g)] = held[g].astype(bf16)
        block = state_ref[0, pl.ds(pl.multiple_of(base * n, span), span), :]
        y_ref[0, pl.ds(base, CHUNK), :] = rows_dot(qd_ref[0, pl.ds(base, CHUNK), :], block)
        return tuple(held)

    start = tuple(held_ref[:, lane(g)] for g in range(groups))
    end = lax.fori_loop(0, rate_ref.shape[1] // CHUNK, chunk, start)
    for g in range(groups):
        held_ref[:, lane(g)] = end[g]


def backward_kernel(
    rate_ref, conv_ref, dy_ref, keyc_ref, queryc_ref, key_ref, keep_ref, kd_ref, k2d_ref, state_ref, last_ref,
    grate_ref, gconv_ref, gkey_ref, gquery_ref,
    held_ref, rk, u, dys, kept, adj, adj_state, diag1, diag2, diag3,
):
    block_rows, width = rate_ref.shape[1:]
    n = keyc_ref.shape[2]
    groups = width // LANES
    span = CHUNK * n
    chunks = block_rows // CHUNK

    @pl.when(pl.program_id(1) == 0)
    def _():
        held_ref[...] = jnp.zeros_like(held_ref)

    mask = (
        lax.broadcasted_iota(jnp.int32, (CHUNK, span), 1) // n
        == lax.broadcasted_iota(jnp.int32, (CHUNK, span), 0)
    )

    def chunk(step, held):
        j = chunks - 1 - step
        base = pl.multiple_of(j * CHUNK, CHUNK)
        rows = pl.ds(base, CHUNK)
        rate, conv, keeps = prepare(base, rate_ref, conv_ref, keep_ref, rk, u, kept)
        dys[...] = dy_ref[0, rows, :]
        keys = keyc_ref[0, j]
        queries = queryc_ref[0, j]
        held = list(held)
        for t in reversed(range(CHUNK)):
            key = column(keys, t)
            key2 = key * key
            query = column(queries, t)
            keep = jnp.broadcast_to(kept[t : t + 1, :], (n, LANES))
            prior = jnp.maximum(base + t - 1, 0)
            at = pl.ds(pl.multiple_of(prior * n, n), n)
            for g in range(groups):
                grad = held[g] + row(dys, t, g, n) * query
                decay = keep - row(rk, t, g, n) * key2
                held[g] = decay * grad
                adj[t * n : (t + 1) * n, lane(g)] = grad.astype(bf16)
                before = state_ref[0, at, lane(g)].astype(f32)
                if t == 0:
                    before = jnp.where(j == 0, last_ref[0, :, lane(g)].astype(f32), before)
                adj_state[t * n : (t + 1) * n, lane(g)] = (grad * before).astype(bf16)
        block = state_ref[0, pl.ds(pl.multiple_of(base * n, span), span), :]
        w1 = rows_dot(kd_ref[0, rows, :], adj[...])
        w2 = rows_dot(k2d_ref[0, rows, :], adj_state[...])
        a1 = outer_dot(u[...].astype(bf16), adj[...])
        a2 = outer_dot(rk[...].astype(bf16), adj_state[...])
        a3 = outer_dot(dys[...].astype(bf16), block)
        diag1[rows, :] = jnp.where(mask, a1, 0.0)
        diag2[rows, :] = jnp.where(mask, a2, 0.0)
        diag3[rows, :] = jnp.where(mask, a3, 0.0)
        for g in range(groups):
            grate_ref[0, rows, lane(g)] = conv[:, lane(g)] * w1[:, lane(g)] - keeps * w2[:, lane(g)]
        gconv_ref[0, rows, :] = rate * w1
        return tuple(held)

    start = tuple(held_ref[:, lane(g)] for g in range(groups))
    end = lax.fori_loop(0, chunks, chunk, start)
    for g in range(groups):
        held_ref[:, lane(g)] = end[g]

    pick = (
        lax.broadcasted_iota(jnp.int32, (span, n), 0) % n
        == lax.broadcasted_iota(jnp.int32, (span, n), 1)
    ).astype(bf16)

    def picked(ref):
        value = ref[...]
        high = value.astype(bf16)
        low = (value - high.astype(f32)).astype(bf16)
        return rows_dot(high, pick) + rows_dot(low, pick)

    rate = rate_ref[0]
    self_term = jnp.sum(grate_ref[0] * rate * rate, axis=1, keepdims=True)
    gkey_ref[0] = picked(diag1) - 2.0 * key_ref[0] * (picked(diag2) + self_term)
    gquery_ref[0] = picked(diag3)


def chunked(values, seqs):
    n = values.shape[0]
    return values.reshape(n, seqs, -1, CHUNK).transpose(1, 2, 0, 3)


def diagonal(values):
    length, n = values.shape[1:]
    spot = jnp.arange(length)[:, None] % CHUNK == jnp.arange(CHUNK * n)[None, :] // n
    return jnp.where(spot, jnp.tile(values, (1, 1, CHUNK)), 0.0).astype(bf16)


def specs_for(length, reverse):
    blocks = length // BLOCK

    def place(b):
        return blocks - 1 - b if reverse else b

    def spec(*shape):
        return pl.BlockSpec((1,) + shape, lambda s, b: (s, place(b)) + (0,) * (len(shape) - 1))

    return blocks, spec


def recurrence_forward(rate, conv, keyc, keep_lanes, qd):
    seqs, length, width = rate.shape
    n = keyc.shape[2]
    span = CHUNK * n
    blocks, spec = specs_for(length, False)
    wide = spec(BLOCK, width)
    return pl.pallas_call(
        forward_kernel,
        grid=(seqs, blocks),
        in_specs=[wide, wide, spec(BLOCK // CHUNK, n, CHUNK), spec(BLOCK, LANES), spec(BLOCK, span)],
        out_specs=[wide, spec(BLOCK * n, width)],
        out_shape=[
            jax.ShapeDtypeStruct((seqs, length, width), f32),
            jax.ShapeDtypeStruct((seqs, length * n, width), bf16),
        ],
        scratch_shapes=[
            pltpu.VMEM((n, width), f32),
            pltpu.VMEM((CHUNK, width), f32),
            pltpu.VMEM((CHUNK, width), f32),
            pltpu.VMEM((CHUNK, LANES), f32),
        ],
        compiler_params=pltpu.CompilerParams(vmem_limit_bytes=24 << 20),
        cost_estimate=pl.CostEstimate(flops=16_000_000_000, bytes_accessed=24 << 20, transcendentals=0),
        name="recurrence_forward",
    )(rate, conv, keyc, keep_lanes, qd)


def recurrence_backward(rate, conv, dy, keyc, queryc, keys, keep_lanes, kd, k2d, states):
    seqs, length, width = rate.shape
    n = keyc.shape[2]
    span = CHUNK * n
    blocks, spec = specs_for(length, True)
    wide = spec(BLOCK, width)
    small = spec(BLOCK, n)
    square = spec(BLOCK, span)
    chunk_spec = spec(BLOCK // CHUNK, n, CHUNK)
    before = pl.BlockSpec((1, n, width), lambda s, b: (s, jnp.maximum((blocks - 1 - b) * BLOCK - 1, 0), 0))
    return pl.pallas_call(
        backward_kernel,
        grid=(seqs, blocks),
        in_specs=[
            wide, wide, wide, chunk_spec, chunk_spec, small, spec(BLOCK, LANES), square, square,
            spec(BLOCK * n, width), before,
        ],
        out_specs=[wide, wide, small, small],
        out_shape=[jax.ShapeDtypeStruct((seqs, length, width), f32)] * 2
        + [jax.ShapeDtypeStruct((seqs, length, n), f32)] * 2,
        scratch_shapes=[
            pltpu.VMEM((n, width), f32),
            pltpu.VMEM((CHUNK, width), f32),
            pltpu.VMEM((CHUNK, width), f32),
            pltpu.VMEM((CHUNK, width), f32),
            pltpu.VMEM((CHUNK, LANES), f32),
            pltpu.VMEM((span, width), bf16),
            pltpu.VMEM((span, width), bf16),
            pltpu.VMEM((BLOCK, span), f32),
            pltpu.VMEM((BLOCK, span), f32),
            pltpu.VMEM((BLOCK, span), f32),
        ],
        compiler_params=pltpu.CompilerParams(vmem_limit_bytes=28 << 20),
        cost_estimate=pl.CostEstimate(flops=30_000_000_000, bytes_accessed=28 << 20, transcendentals=0),
        name="recurrence_backward",
    )(rate, conv, dy, keyc, queryc, keys, keep_lanes, kd, k2d, states, states)


def peer(hop):
    me = lax.axis_index("shard")
    core = lax.rem(me, 2)
    chip = me // 2
    if hop & 1:
        core = 1 - core
    if hop & 2:
        chip = 1 - chip
    return chip * 2 + core


def meet_group():
    barrier = pltpu.get_barrier_semaphore()
    for hop in (1, 2, 3):
        pl.semaphore_signal(barrier, inc=1, device_id={"shard": peer(hop)}, device_id_type=MESH)
    pl.semaphore_wait(barrier, 3)


def remote(src, dst, sends, recvs, at, hop):
    return pltpu.make_async_remote_copy(
        src_ref=src, dst_ref=dst, send_sem=sends.at[at], recv_sem=recvs.at[at],
        device_id={"shard": peer(hop)}, device_id_type=MESH,
    )


def group_params(collective_id, limit):
    return pltpu.CompilerParams(collective_id=collective_id, has_side_effects=True, vmem_limit_bytes=limit)


VMEM_SPEC = pl.BlockSpec(memory_space=pltpu.VMEM)


def gather_kernel(x_ref, cot_ref, gain_ref, xs_ref, cots_ref, gains_ref, sends, recvs, local):
    me = lax.axis_index("shard")
    rows = x_ref.shape[1]
    cols = cots_ref.shape[2]
    lift = gain_ref.shape[0]
    meet_group()

    def mine(ref, owner):
        return ref.at[:, pl.ds(pl.multiple_of(owner * rows, 16), rows), :]

    def part(owner):
        return cot_ref.at[:, :, pl.ds(pl.multiple_of(owner * cols, 128), cols)]

    def gain_rows(owner):
        return gains_ref.at[pl.ds(pl.multiple_of(owner * lift, 8), lift), :]

    x_core = remote(x_ref, mine(xs_ref, me), sends, recvs, 0, 1)
    x_chip = remote(x_ref, mine(xs_ref, me), sends, recvs, 1, 2)
    x_chip.start()
    x_core.start()
    rest = [remote(part(peer(hop)), mine(cots_ref, me), sends, recvs, 2 + hop, hop) for hop in (1, 2, 3)]
    rest += [remote(gain_ref, gain_rows(me), sends, recvs, 5 + hop, hop) for hop in (1, 2, 3)]
    for copy in rest:
        copy.start()
    own = [
        pltpu.make_async_copy(x_ref, mine(xs_ref, me), local.at[0]),
        pltpu.make_async_copy(part(me), mine(cots_ref, me), local.at[1]),
        pltpu.make_async_copy(gain_ref, gain_rows(me), local.at[2]),
    ]
    for copy in own:
        copy.start()
    x_chip.wait_recv()
    onward = remote(mine(xs_ref, peer(2)), mine(xs_ref, peer(2)), sends, recvs, 2, 1)
    onward.start()
    for copy in own + rest:
        copy.wait()
    x_chip.wait_send()
    x_core.wait()
    onward.wait()


def gather_inputs(x, cot, gain):
    seqs, rows, model = x.shape
    group = lax.axis_size("shard")
    lifted = jnp.broadcast_to(gain.astype(f32)[None], (8, gain.shape[0]))
    xs, cots, gains = pl.pallas_call(
        gather_kernel,
        in_specs=[VMEM_SPEC] * 3,
        out_specs=[VMEM_SPEC] * 3,
        out_shape=[
            jax.ShapeDtypeStruct((seqs, rows * group, model), x.dtype),
            jax.ShapeDtypeStruct((seqs, rows * group, model // group), x.dtype),
            jax.ShapeDtypeStruct((8 * group, gain.shape[0]), f32),
        ],
        scratch_shapes=[
            pltpu.SemaphoreType.DMA((9,)), pltpu.SemaphoreType.DMA((9,)), pltpu.SemaphoreType.DMA((3,)),
        ],
        compiler_params=group_params(1, 16 << 20),
        name="gather_inputs",
    )(x, cot, lifted)
    return xs, cots, gains[::8].reshape(-1)


def split_kernel(mixed_ref, parts_ref, sends, recvs, local):
    me = lax.axis_index("shard")
    width = parts_ref.shape[2]
    slot = me // 2
    meet_group()

    def send(i):
        return pltpu.make_async_remote_copy(
            src_ref=mixed_ref.at[:, pl.ds(i * width, width)],
            dst_ref=parts_ref.at[slot],
            send_sem=sends.at[i],
            recv_sem=recvs.at[slot],
            device_id={"shard": lax.rem(2 * me + i, 4)},
            device_id_type=MESH,
        )

    def keep(i):
        return pltpu.make_async_copy(mixed_ref.at[:, pl.ds(i * width, width)], parts_ref.at[slot], local.at[0])

    for i in range(2):
        away = lax.rem(2 * me + i, 4) != me

        @pl.when(away)
        def _(i=i):
            send(i).start()

        @pl.when(jnp.logical_not(away))
        def _(i=i):
            keep(i).start()

    for i in range(2):
        away = lax.rem(2 * me + i, 4) != me

        @pl.when(away)
        def _(i=i):
            send(i).wait_send()

        @pl.when(jnp.logical_not(away))
        def _(i=i):
            keep(i).wait()

    for at in range(2):

        @pl.when(2 * at + me // 2 != me)
        def _(at=at):
            pltpu.make_async_remote_copy(
                src_ref=parts_ref.at[at], dst_ref=parts_ref.at[at], send_sem=sends.at[at], recv_sem=recvs.at[at],
                device_id={"shard": peer(1)}, device_id_type=MESH,
            ).wait_recv()


def to_channels(mixed):
    tokens, cols = mixed.shape
    return pl.pallas_call(
        split_kernel,
        in_specs=[VMEM_SPEC],
        out_specs=VMEM_SPEC,
        out_shape=jax.ShapeDtypeStruct((2, tokens, cols // 2), mixed.dtype),
        scratch_shapes=[
            pltpu.SemaphoreType.DMA((2,)), pltpu.SemaphoreType.DMA((2,)), pltpu.SemaphoreType.DMA((1,)),
        ],
        compiler_params=group_params(2, 16 << 20),
        name="to_channels",
    )(mixed)


def total_kernel(part_ref, out_ref, near, chip_sum, far, sends, recvs):
    me = lax.axis_index("shard")
    half = part_ref.shape[1] // 2
    mine = pl.ds(pl.multiple_of(lax.rem(me, 2) * half, 128), half)
    other = pl.ds(pl.multiple_of((1 - lax.rem(me, 2)) * half, 128), half)
    meet_group()
    first = remote(part_ref.at[:, other], near, sends, recvs, 0, 1)
    first.start()
    first.wait()
    chip_sum[...] = part_ref[:, mine] + near[...]
    second = remote(chip_sum, far, sends, recvs, 1, 2)
    second.start()
    second.wait()
    out_ref[:, mine] = chip_sum[...] + far[...]
    third = remote(out_ref.at[:, mine], out_ref.at[:, mine], sends, recvs, 2, 1)
    third.start()
    third.wait()


def group_total(part, collective_id):
    rows, cols = part.shape
    half = pltpu.VMEM((rows, cols // 2), f32)
    return pl.pallas_call(
        total_kernel,
        in_specs=[VMEM_SPEC],
        out_specs=VMEM_SPEC,
        out_shape=jax.ShapeDtypeStruct((rows, cols), f32),
        scratch_shapes=[half, half, half, pltpu.SemaphoreType.DMA((3,)), pltpu.SemaphoreType.DMA((3,))],
        compiler_params=group_params(collective_id, 16 << 20),
        name="group_total",
    )(part)


def gain_kernel(part_ref, out_ref, near, mine, far, sends, recvs, far_sends, far_recvs):
    me = lax.axis_index("shard")
    home = lax.axis_index("replica")
    count = far.shape[0]
    barrier = pltpu.get_barrier_semaphore()
    for hop in (1, 2, 3):
        pl.semaphore_signal(barrier, inc=1, device_id={"shard": peer(hop)}, device_id_type=MESH)
    for step in range(1, count):
        pl.semaphore_signal(
            barrier, inc=1, device_id={"replica": lax.rem(home + step, count)}, device_id_type=MESH
        )
    pl.semaphore_wait(barrier, count + 2)
    copies = [remote(part_ref.at[peer(hop)], near.at[hop - 1], sends, recvs, hop - 1, hop) for hop in (1, 2, 3)]
    for copy in copies:
        copy.start()
    for copy in copies:
        copy.wait()
    mine[...] = part_ref[me] + near[0] + near[1] + near[2]
    far[0] = mine[...]
    copies = [
        pltpu.make_async_remote_copy(
            src_ref=mine, dst_ref=far.at[step], send_sem=far_sends.at[step], recv_sem=far_recvs.at[step],
            device_id={"replica": lax.rem(home + step, count)}, device_id_type=MESH,
        )
        for step in range(1, count)
    ]
    for copy in copies:
        copy.start()
    for copy in copies:
        copy.wait()
    out_ref[...] = jnp.sum(far[...], axis=0)


def gain_total(part):
    group, count = lax.axis_size("shard"), lax.axis_size("replica")
    tile = (part.shape[0] // group // 128, 128)
    return pl.pallas_call(
        gain_kernel,
        in_specs=[VMEM_SPEC],
        out_specs=VMEM_SPEC,
        out_shape=jax.ShapeDtypeStruct(tile, f32),
        scratch_shapes=[
            pltpu.VMEM((3,) + tile, f32), pltpu.VMEM(tile, f32), pltpu.VMEM((count,) + tile, f32),
            pltpu.SemaphoreType.DMA((3,)), pltpu.SemaphoreType.DMA((3,)),
            pltpu.SemaphoreType.DMA((count,)), pltpu.SemaphoreType.DMA((count,)),
        ],
        compiler_params=group_params(5, 16 << 20),
        name="gain_total",
    )(part.reshape((group,) + tile)).reshape(-1)


def by_hop(value, hop):
    return lax.ppermute(value, "shard", [(i, i ^ hop) for i in range(4)])


def pair(value):
    return lax.ppermute(value, "replica", [(i, i ^ 1) for i in range(lax.axis_size("replica"))])


def far_sum(blocks):
    count = lax.axis_size("replica")
    height = count // 2
    mine = lax.axis_index("replica") // 2

    def pick(at):
        return lax.dynamic_index_in_dim(blocks, at, 0, False)

    total = pick(mine)
    for step in range(1, height):
        out = pick(lax.rem(mine + step, height)).astype(bf16)
        total = total + lax.ppermute(out, "replica", [(i, (i + 2 * step) % count) for i in range(count)]).astype(f32)
    return total


def far_gather(block):
    count = lax.axis_size("replica")
    height = count // 2
    mine = lax.axis_index("replica") // 2
    full = jnp.zeros((height,) + block.shape, block.dtype)
    full = lax.dynamic_update_index_in_dim(full, block, mine, 0)
    for step in range(1, height):
        got = lax.ppermute(block, "replica", [(i, (i + 2 * step) % count) for i in range(count)])
        full = lax.dynamic_update_index_in_dim(full, got, lax.rem(mine + height - step, height), 0)
    return full


def x_home(x_own):
    one = lax.ppermute(x_own, "shard", [(1, 0), (2, 1)])
    two = lax.ppermute(x_own, "shard", [(3, 1)])
    return one, two


def z_home(z_own):
    one = lax.ppermute(z_own, "shard", [(0, 2), (2, 3)])
    two = lax.ppermute(z_own, "shard", [(1, 2)])
    return one, two


def columns_home(x_own, x_got, z_own, z_got):
    me = lax.axis_index("shard")
    first = jnp.where(me == 0, x_own, jnp.where(me == 1, x_got[0], z_got[0]))
    second = jnp.where(me == 3, z_own, jnp.where(me == 2, z_got[1], jnp.where(me == 1, x_got[1], x_got[0])))
    return jnp.concatenate([first, second], axis=1)


def after(value, *others):
    return lax.optimization_barrier((value,) + others)[0]


def body(
    block_input, segment_ids, norm_gain, w_in, conv_weight, conv_bias, x_proj, dt_proj, dt_bias,
    d_skip, out_proj, out_grad,
):
    seqs, local, model = block_input.shape
    length = segment_ids.shape[1]
    tokens = seqs * length
    width = d_skip.shape[0]
    rank = dt_proj.shape[0]
    n = (x_proj.shape[0] - rank) // 2
    me = lax.axis_index("shard")
    count = lax.axis_size("replica")
    height = count // 2
    side = lax.rem(lax.axis_index("replica"), 2)

    def split(values):
        return values.reshape(seqs, length, -1)

    def halves(values, blocks):
        parts = values.reshape(values.shape[0], blocks, 2, -1)
        keep = lax.dynamic_index_in_dim(parts, side, 2, False)
        give = lax.dynamic_index_in_dim(parts, 1 - side, 2, False)
        return keep.reshape(values.shape[0], -1), give.reshape(values.shape[0], -1)

    def both(keep, got):
        return jnp.concatenate([keep, got], axis=0)

    xs, cots, gain = gather_inputs(block_input, out_grad, norm_gain)
    x_all = xs.reshape(tokens, model)
    cot = cots.reshape(tokens, -1)

    def normalise(rows):
        vals = rows.astype(f32)
        inv = lax.rsqrt(jnp.mean(vals * vals, axis=-1, keepdims=True) + EPS)
        return vals, inv

    x_vals, inv_rms = normalise(x_all)
    scaled_x = x_vals * inv_rms
    normed = (scaled_x * gain).astype(bf16)
    mixed = rows_dot(normed, w_in).astype(bf16)
    parts = to_channels(mixed)
    x_part, z_part = parts[0], parts[1]

    cot_late = after(cot, parts)
    partial = outer_dot(cot_late, out_proj).astype(bf16).reshape(tokens, 2, 2, width)
    core = lax.rem(me, 2)
    chip = me // 2
    near = by_hop(lax.dynamic_index_in_dim(partial, 1 - core, 2, False), 1)
    chip_part = lax.dynamic_index_in_dim(partial, core, 2, False).astype(f32) + near.astype(f32)
    grad_gated = lax.dynamic_index_in_dim(chip_part, chip, 1, False) + by_hop(
        lax.dynamic_index_in_dim(chip_part, 1 - chip, 1, False).astype(bf16), 2
    ).astype(f32)
    grad_gated = split(grad_gated)

    normed_late = after(normed, parts)
    normed_keep, normed_give = halves(normed_late, height)
    normed_pair = both(normed_keep, pair(normed_give))
    cot_pair = both(cot, pair(cot_late))

    seg_padded = jnp.pad(segment_ids, ((0, 0), (KW - 1, 0)), constant_values=-1)
    taps = [
        (seg_padded[:, KW - 1 - d : KW - 1 - d + length] == segment_ids).astype(f32) for d in range(KW)
    ]
    conv_w = conv_weight.astype(f32)
    xv = split(x_part).astype(f32)
    x_padded = jnp.pad(xv, ((0, 0), (KW - 1, 0), (0, 0)))
    conv_pre = conv_bias.astype(f32) + conv_w[KW - 1] * xv
    for j in range(KW - 1):
        d = KW - 1 - j
        conv_pre = conv_pre + conv_w[j] * x_padded[:, j : j + length] * taps[d][:, :, None]
    conv_out = jax.nn.silu(conv_pre).astype(bf16)
    conv_vals = conv_out.astype(f32)
    conv_flat = conv_out.reshape(tokens, width)
    proj = group_total(outer_dot(x_proj, conv_flat), 3)
    dt_low = proj[:rank].astype(bf16)
    key_cols = proj[rank : rank + n]
    query_cols = proj[rank + n :]
    keys = split(key_cols.T)
    queries = split(query_cols.T)
    beta = split(jax.nn.sigmoid(inner_dot(dt_low, dt_proj) + dt_bias.astype(f32)))
    key_square = jnp.sum(keys * keys, axis=2, keepdims=True)
    denom_inv = 1.0 / (1.0 + beta * key_square)
    rate = beta * denom_inv
    keep_lanes = jnp.broadcast_to(taps[1][:, :, None], (seqs, length, LANES))
    keyc = chunked(key_cols, seqs)
    recurrent, states = recurrence_forward(rate, conv_out, keyc, keep_lanes, diagonal(queries))

    z_vals = split(z_part).astype(f32)
    gate = jax.nn.silu(z_vals)
    dy = grad_gated * gate
    skip = d_skip.astype(f32)
    y_total = recurrent + skip * conv_vals
    gated = (y_total * gate).astype(bf16).reshape(tokens, width)
    grad_z = (grad_gated * y_total * silu_slope(z_vals)).astype(bf16).reshape(tokens, width)

    def group_gather(value):
        across = by_hop(value, 2)
        near_two = by_hop(jnp.concatenate([value], axis=1), 1)
        near_far = by_hop(across, 1)
        stacked = jnp.stack([value, near_two, across, near_far])
        order = jnp.stack([jnp.bitwise_xor(me, i) for i in range(4)])
        return [lax.dynamic_index_in_dim(stacked, order[i], 0, False) for i in range(4)]

    gated_keep, gated_give = halves(gated, height // 4 if height >= 4 else 1)
    gated_got = pair(gated_give)
    gated_parts = group_gather(gated)
    gated_all = jnp.concatenate(gated_parts, axis=1)
    got_all = jnp.concatenate(group_gather(gated_got), axis=1)
    keep_all, _ = halves(gated_all, height)
    cols = model // 4
    x_cols = lax.dynamic_slice_in_dim(x_all, me * cols, cols, 1).astype(f32)
    out_cols = (x_cols + rows_dot(gated_all, out_proj)).astype(bf16).reshape(seqs, 4, local, cols)

    def rows_for(hop):
        return lax.dynamic_index_in_dim(out_cols, jnp.bitwise_xor(me, hop), 1, False)

    out_stack = jnp.stack([rows_for(0)] + [by_hop(rows_for(hop), hop) for hop in (1, 2, 3)])
    block_output = jnp.concatenate(
        [lax.dynamic_index_in_dim(out_stack, jnp.bitwise_xor(me, i), 0, False) for i in range(4)], axis=2
    )
    grad_out_proj = far_sum(
        inner_dot(both(keep_all, got_all), cot_pair).reshape(height, -1, cols)
    )
    z_got = z_home(grad_z)
    grad_w_z = far_sum(
        inner_dot(normed_pair, both(grad_z, pair(grad_z))).reshape(height, -1, width)
    ).astype(bf16)

    grad_rate, grad_conv_rec, grad_keys, grad_queries = recurrence_backward(
        rate, conv_out, dy, keyc, chunked(query_cols, seqs), keys, keep_lanes, diagonal(keys),
        diagonal(keys * keys), states,
    )
    grad_d_skip = jnp.sum(dy * conv_vals, axis=(0, 1))
    grad_dt = grad_rate * denom_inv * denom_inv * beta * (1.0 - beta)
    grad_dt_bias = jnp.sum(grad_dt, axis=(0, 1))
    grad_dt_low = grad_dt.astype(bf16).reshape(tokens, width)
    grad_proj = jnp.concatenate(
        [outer_dot(dt_proj, grad_dt_low), grad_keys.reshape(tokens, n).T, grad_queries.reshape(tokens, n).T]
    )
    grad_proj = group_total(grad_proj, 4).astype(bf16)
    grad_dt_proj = rows_dot(dt_low, grad_dt_low)
    grad_x_proj = rows_dot(grad_proj, conv_flat)
    grad_conv = dy * skip + grad_conv_rec + split(inner_dot(grad_proj, x_proj))
    grad_pre = grad_conv * silu_slope(conv_pre)
    grad_conv_bias = jnp.sum(grad_pre, axis=(0, 1))
    grad_conv_weight = jnp.stack(
        [
            jnp.sum(grad_pre * x_padded[:, j : j + length] * taps[KW - 1 - j][:, :, None], axis=(0, 1))
            for j in range(KW)
        ]
    )
    grad_x = conv_w[KW - 1] * grad_pre
    for j in range(KW - 1):
        d = KW - 1 - j
        ahead = jnp.pad(grad_pre * taps[d][:, :, None], ((0, 0), (0, d), (0, 0)))[:, d:]
        grad_x = grad_x + conv_w[j] * ahead
    grad_x = grad_x.astype(bf16).reshape(tokens, width)
    x_rows = inner_dot(normed_pair, both(grad_x, pair(grad_x))).reshape(height, -1, width)

    small = jnp.concatenate(
        [
            grad_x_proj, grad_dt_proj, grad_conv_weight, grad_conv_bias[None], grad_dt_bias[None],
            grad_d_skip[None],
        ]
    )
    unit = 16 * count
    padded = -(-small.shape[0] // unit) * unit
    small = jnp.pad(small, ((0, padded - small.shape[0]), (0, 0))).reshape(height, 2, -1, width)
    small_keep = lax.dynamic_index_in_dim(small, side, 1, False)
    small_got = pair(lax.dynamic_index_in_dim(small, 1 - side, 1, False).astype(bf16))
    small_rows = small_keep + small_got.astype(f32)
    summed = far_sum(jnp.concatenate([x_rows, small_rows], axis=1))
    per = x_rows.shape[1]
    grad_w_x = summed[:per].astype(bf16)
    small_side = far_gather(summed[per:].astype(bf16))
    other_side = pair(small_side)
    small = jnp.stack(
        [jnp.where(side == 0, small_side, other_side), jnp.where(side == 0, other_side, small_side)], axis=1
    ).reshape(padded, width).astype(f32)

    grad_cols = columns_home(grad_x, x_home(grad_x), grad_z, z_got)
    grad_w_in = columns_home(grad_w_x, x_home(grad_w_x), grad_w_z, z_home(grad_w_z)).astype(f32)
    grad_normed = outer_dot(grad_cols, w_in)
    grad_gain = gain_total(jnp.sum(grad_normed * scaled_x, axis=0))
    by_owner = grad_normed.astype(bf16).reshape(seqs, 2, 2, local, model)
    near = by_hop(lax.dynamic_index_in_dim(by_owner, 1 - core, 2, False), 1)
    chip_rows = lax.dynamic_index_in_dim(by_owner, core, 2, False).astype(f32) + near.astype(f32)
    grad_normed = lax.dynamic_index_in_dim(chip_rows, chip, 1, False) + by_hop(
        lax.dynamic_index_in_dim(chip_rows, 1 - chip, 1, False).astype(bf16), 2
    ).astype(f32)
    x_own, inv_own = normalise(block_input)
    scaled = grad_normed * gain
    grad_in = inv_own * (
        scaled - x_own * inv_own * inv_own * jnp.mean(scaled * x_own, axis=-1, keepdims=True)
    )
    input_grad = (out_grad.astype(f32) + grad_in).astype(bf16)

    top = x_proj.shape[0]
    return (
        block_output, input_grad, grad_gain, grad_w_in,
        small[top + rank : top + rank + KW], small[top + rank + KW], small[:top], small[top : top + rank],
        small[top + rank + KW + 1], small[top + rank + KW + 2], grad_out_proj,
    )


def solution(mesh):
    return jax.shard_map(
        body,
        mesh=mesh,
        in_specs=(
            P("replica", "shard", None), P("replica", None), P("shard"), P(None, "shard"), P(None, "shard"),
            P("shard"), P(None, "shard"), P(None, "shard"), P("shard"), P("shard"), P(None, "shard"),
            P("replica", "shard", None),
        ),
        out_specs=(
            P("replica", "shard", None), P("replica", "shard", None), P("shard"), P("replica", "shard"),
            P(None, "shard"), P("shard"), P(None, "shard"), P(None, "shard"), P("shard"), P("shard"),
            P("replica", "shard"),
        ),
        check_vma=False,
    )
```

```python
import functools

import jax
import jax.numpy as jnp
from jax import lax
from jax.experimental import pallas as pl
from jax.experimental.pallas import tpu as pltpu
from jax.sharding import PartitionSpec as P

KW = 4
EPS = 1e-05
CHUNK = 16
LANES = 128
f32 = jnp.float32
bf16 = jnp.bfloat16


def rows_dot(a, b):
    return jnp.dot(a, b, preferred_element_type=f32)


def inner_dot(a, b):
    return lax.dot_general(a, b, (((0,), (0,)), ((), ())), preferred_element_type=f32)


def outer_dot(a, b):
    return lax.dot_general(a, b, (((1,), (1,)), ((), ())), preferred_element_type=f32)


def silu_slope(values):
    sig_val = jax.nn.sigmoid(values)
    return sig_val + values * sig_val * (1.0 - sig_val)

MESH = pl.DeviceIdType.MESH
BLOCK = 128


def lane(g):
    return slice(g * LANES, (g + 1) * LANES)


def column(block, t):
    return jnp.broadcast_to(block[:, t : t + 1], (block.shape[0], LANES))


def row(ref, t, g, n):
    return jnp.broadcast_to(ref[t : t + 1, lane(g)], (n, LANES))


def prepare(base, rate_ref, conv_ref, keep_ref, rk, u, kept):
    rows = pl.ds(base, CHUNK)
    rate = rate_ref[0, rows, :]
    keep = keep_ref[0, rows, :]
    conv = conv_ref[0, rows, :].astype(f32)
    for g in range(rate.shape[1] // LANES):
        rk[:, lane(g)] = rate[:, lane(g)] * keep
    u[...] = rate * conv
    kept[...] = keep
    return rate, conv, keep


def shifted(cols, j):
    size = cols.shape[1]
    return pltpu.roll(cols, lax.rem(size - j * CHUNK, size), 1)


def spread_mask(n):
    shape = (CHUNK, CHUNK * n)
    return lax.broadcasted_iota(jnp.int32, shape, 1) // n == lax.broadcasted_iota(jnp.int32, shape, 0)


def picker(n):
    shape = (n, CHUNK * n)
    return (lax.broadcasted_iota(jnp.int32, shape, 1) % n == lax.broadcasted_iota(jnp.int32, shape, 0)).astype(bf16)


def diagonal(rows, mask, pick):
    return jnp.where(mask, rows_dot(rows.astype(bf16), pick), 0.0).astype(bf16)


def forward_kernel(
    conv_ref, z_ref, proj_ref, keep_ref, dt_proj_ref, dt_bias_ref, skip_ref,
    y_ref, gated_ref, rate_ref, beta_ref, state_ref,
    held_ref, rk, u, kept, query_rows,
):
    width = conv_ref.shape[2]
    rank = dt_proj_ref.shape[0]
    n = (proj_ref.shape[0] - rank) // 2
    groups = width // LANES
    span = CHUNK * n

    @pl.when(pl.program_id(1) == 0)
    def _():
        held_ref[...] = jnp.zeros_like(held_ref)

    dt_low = proj_ref[0:rank, :].astype(bf16)
    keys = proj_ref[rank : rank + n, :]
    query_rows[...] = proj_ref[rank + n :, :].T
    key_square = jnp.sum(keys.T * keys.T, axis=1, keepdims=True)
    beta = jax.nn.sigmoid(inner_dot(dt_low, dt_proj_ref[...]) + dt_bias_ref[...])
    beta_ref[0] = beta
    rate_ref[0] = beta / (1.0 + beta * key_square)
    mask, pick = spread_mask(n), picker(n)

    def chunk(j, held):
        base = pl.multiple_of(j * CHUNK, CHUNK)
        rows = pl.ds(base, CHUNK)
        _, conv, _ = prepare(base, rate_ref, conv_ref, keep_ref, rk, u, kept)
        near_keys = shifted(keys, j)
        held = list(held)
        for t in range(CHUNK):
            key = column(near_keys, t)
            key2 = key * key
            keep = jnp.broadcast_to(kept[t : t + 1, :], (n, LANES))
            at = pl.ds(pl.multiple_of((base + t) * n, n), n)
            for g in range(groups):
                decay = keep - row(rk, t, g, n) * key2
                held[g] = decay * held[g] + row(u, t, g, n) * key
                state_ref[0, at, lane(g)] = held[g].astype(bf16)
        block = state_ref[0, pl.ds(pl.multiple_of(base * n, span), span), :]
        total = rows_dot(diagonal(query_rows[rows, :], mask, pick), block) + skip_ref[...] * conv
        y_ref[0, rows, :] = total
        z = z_ref[0, rows, :].astype(f32)
        gated_ref[0, rows, :] = (total * (z * jax.nn.sigmoid(z))).astype(bf16)
        return tuple(held)

    start = tuple(held_ref[:, lane(g)] for g in range(groups))
    end = lax.fori_loop(0, conv_ref.shape[1] // CHUNK, chunk, start)
    for g in range(groups):
        held_ref[:, lane(g)] = end[g]


def backward_kernel(
    rate_ref, beta_ref, conv_ref, dy_ref, proj_ref, keep_ref, dt_proj_ref, state_ref, last_ref,
    gconv_ref, gdt_ref, gproj_ref, gdt_proj_ref, gdt_bias_ref, gskip_ref,
    held_ref, grate, rk, u, dys, kept, key_rows, adj, adj_state, diag1, diag2, diag3,
):
    block_rows, width = rate_ref.shape[1:]
    rank = dt_proj_ref.shape[0]
    n = (proj_ref.shape[0] - rank) // 2
    groups = width // LANES
    span = CHUNK * n
    chunks = block_rows // CHUNK

    @pl.when(pl.program_id(1) == 0)
    def _():
        held_ref[...] = jnp.zeros_like(held_ref)

    @pl.when((pl.program_id(0) == 0) & (pl.program_id(1) == 0))
    def _():
        gdt_proj_ref[...] = jnp.zeros_like(gdt_proj_ref)
        gdt_bias_ref[...] = jnp.zeros_like(gdt_bias_ref)
        gskip_ref[...] = jnp.zeros_like(gskip_ref)

    keys = proj_ref[rank : rank + n, :]
    queries = proj_ref[rank + n :, :]
    key_rows[...] = keys.T
    mask, pick = spread_mask(n), picker(n)

    def chunk(step, held):
        j = chunks - 1 - step
        base = pl.multiple_of(j * CHUNK, CHUNK)
        rows = pl.ds(base, CHUNK)
        rate, conv, keeps = prepare(base, rate_ref, conv_ref, keep_ref, rk, u, kept)
        dys[...] = dy_ref[0, rows, :]
        near_keys = shifted(keys, j)
        near_queries = shifted(queries, j)
        held = list(held)
        for t in reversed(range(CHUNK)):
            key = column(near_keys, t)
            key2 = key * key
            query = column(near_queries, t)
            keep = jnp.broadcast_to(kept[t : t + 1, :], (n, LANES))
            prior = jnp.maximum(base + t - 1, 0)
            at = pl.ds(pl.multiple_of(prior * n, n), n)
            for g in range(groups):
                grad = held[g] + row(dys, t, g, n) * query
                decay = keep - row(rk, t, g, n) * key2
                held[g] = decay * grad
                adj[t * n : (t + 1) * n, lane(g)] = grad.astype(bf16)
                before = state_ref[0, at, lane(g)].astype(f32)
                if t == 0:
                    before = jnp.where(j == 0, last_ref[0, :, lane(g)].astype(f32), before)
                adj_state[t * n : (t + 1) * n, lane(g)] = (grad * before).astype(bf16)
        block = state_ref[0, pl.ds(pl.multiple_of(base * n, span), span), :]
        key_block = key_rows[rows, :]
        w1 = rows_dot(diagonal(key_block, mask, pick), adj[...])
        w2 = rows_dot(diagonal(key_block * key_block, mask, pick), adj_state[...])
        a1 = outer_dot(u[...].astype(bf16), adj[...])
        a2 = outer_dot(rk[...].astype(bf16), adj_state[...])
        a3 = outer_dot(dys[...].astype(bf16), block)
        diag1[rows, :] = jnp.where(mask, a1, 0.0)
        diag2[rows, :] = jnp.where(mask, a2, 0.0)
        diag3[rows, :] = jnp.where(mask, a3, 0.0)
        for g in range(groups):
            grate[rows, lane(g)] = conv[:, lane(g)] * w1[:, lane(g)] - keeps * w2[:, lane(g)]
        gconv_ref[0, rows, :] = rate * w1
        return tuple(held)

    start = tuple(held_ref[:, lane(g)] for g in range(groups))
    end = lax.fori_loop(0, chunks, chunk, start)
    for g in range(groups):
        held_ref[:, lane(g)] = end[g]

    def picked(left, value):
        high = value.astype(bf16)
        low = (value - high.astype(f32)).astype(bf16)
        return outer_dot(left, high) + outer_dot(left, low)

    rate = rate_ref[0]
    beta = beta_ref[0]
    grad_rate = grate[...]
    self_term = picked(jnp.ones((n, width), bf16), grad_rate * rate * rate)
    key_square = jnp.sum(key_rows[...] * key_rows[...], axis=1, keepdims=True)
    denom_inv = 1.0 / (1.0 + beta * key_square)
    grad_dt = grad_rate * denom_inv * denom_inv * beta * (1.0 - beta)
    low = grad_dt.astype(bf16)
    gdt_ref[0] = low
    gdt_bias_ref[...] += jnp.sum(grad_dt, axis=0, keepdims=True)
    gskip_ref[...] += jnp.sum(dy_ref[0] * conv_ref[0].astype(f32), axis=0, keepdims=True)
    gdt_proj_ref[...] += rows_dot(proj_ref[0:rank, :].astype(bf16), low)
    gproj_ref[0:rank, :] = outer_dot(dt_proj_ref[...], low)
    gproj_ref[rank : rank + n, :] = picked(pick, diag1[...]) - 2.0 * keys * (picked(pick, diag2[...]) + self_term)
    gproj_ref[rank + n :, :] = picked(pick, diag3[...])


def specs_for(length, reverse):
    blocks = length // BLOCK

    def place(b):
        return blocks - 1 - b if reverse else b

    def spec(*shape):
        return pl.BlockSpec((1,) + shape, lambda s, b: (s, place(b)) + (0,) * (len(shape) - 1))

    def across_spec(rows):
        return pl.BlockSpec((rows, BLOCK), lambda s, b: (0, s * blocks + place(b)))

    def whole(*shape):
        return pl.BlockSpec(shape, lambda s, b: (0,) * len(shape))

    return blocks, spec, across_spec, whole


def recurrence_forward(conv, z, proj, keep_lanes, dt_proj, dt_bias, skip):
    seqs, length, width = conv.shape
    rank = dt_proj.shape[0]
    n = (proj.shape[0] - rank) // 2
    blocks, spec, across_spec, whole = specs_for(length, False)
    wide = spec(BLOCK, width)
    full = jax.ShapeDtypeStruct((seqs, length, width), f32)
    return pl.pallas_call(
        forward_kernel,
        grid=(seqs, blocks),
        in_specs=[
            wide, wide, across_spec(proj.shape[0]), spec(BLOCK, LANES), whole(rank, width), whole(1, width),
            whole(1, width),
        ],
        out_specs=[wide, wide, wide, wide, spec(BLOCK * n, width)],
        out_shape=[
            full, jax.ShapeDtypeStruct((seqs, length, width), bf16), full, full,
            jax.ShapeDtypeStruct((seqs, length * n, width), bf16),
        ],
        scratch_shapes=[
            pltpu.VMEM((n, width), f32),
            pltpu.VMEM((CHUNK, width), f32),
            pltpu.VMEM((CHUNK, width), f32),
            pltpu.VMEM((CHUNK, LANES), f32),
            pltpu.VMEM((BLOCK, n), f32),
        ],
        compiler_params=pltpu.CompilerParams(vmem_limit_bytes=24 << 20),
        cost_estimate=pl.CostEstimate(flops=16_000_000_000, bytes_accessed=24 << 20, transcendentals=0),
        name="recurrence_forward",
    )(conv, z, proj, keep_lanes, dt_proj, dt_bias, skip)


def recurrence_backward(rate, beta, conv, dy, proj, keep_lanes, dt_proj, states):
    seqs, length, width = rate.shape
    rank = dt_proj.shape[0]
    n = (proj.shape[0] - rank) // 2
    span = CHUNK * n
    blocks, spec, across_spec, whole = specs_for(length, True)
    wide = spec(BLOCK, width)
    before = pl.BlockSpec((1, n, width), lambda s, b: (s, jnp.maximum((blocks - 1 - b) * BLOCK - 1, 0), 0))
    lined = pltpu.VMEM((BLOCK, span), f32)
    return pl.pallas_call(
        backward_kernel,
        grid=(seqs, blocks),
        in_specs=[
            wide, wide, wide, wide, across_spec(proj.shape[0]), spec(BLOCK, LANES), whole(rank, width),
            spec(BLOCK * n, width), before,
        ],
        out_specs=[wide, wide, across_spec(proj.shape[0]), whole(rank, width), whole(1, width), whole(1, width)],
        out_shape=[
            jax.ShapeDtypeStruct((seqs, length, width), f32),
            jax.ShapeDtypeStruct((seqs, length, width), bf16),
            jax.ShapeDtypeStruct(proj.shape, f32),
            jax.ShapeDtypeStruct((rank, width), f32),
            jax.ShapeDtypeStruct((1, width), f32),
            jax.ShapeDtypeStruct((1, width), f32),
        ],
        scratch_shapes=[
            pltpu.VMEM((n, width), f32),
            pltpu.VMEM((BLOCK, width), f32),
            pltpu.VMEM((CHUNK, width), f32),
            pltpu.VMEM((CHUNK, width), f32),
            pltpu.VMEM((CHUNK, width), f32),
            pltpu.VMEM((CHUNK, LANES), f32),
            pltpu.VMEM((BLOCK, n), f32),
            pltpu.VMEM((span, width), bf16),
            pltpu.VMEM((span, width), bf16),
            lined, lined, lined,
        ],
        compiler_params=pltpu.CompilerParams(vmem_limit_bytes=28 << 20),
        cost_estimate=pl.CostEstimate(flops=30_000_000_000, bytes_accessed=28 << 20, transcendentals=0),
        name="recurrence_backward",
    )(rate, beta, conv, dy, proj, keep_lanes, dt_proj, states, states)


def peer(hop):
    me = lax.axis_index("shard")
    core = lax.rem(me, 2)
    chip = me // 2
    if hop & 1:
        core = 1 - core
    if hop & 2:
        chip = 1 - chip
    return chip * 2 + core


def meet_group():
    barrier = pltpu.get_barrier_semaphore()
    for hop in (1, 2, 3):
        pl.semaphore_signal(barrier, inc=1, device_id={"shard": peer(hop)}, device_id_type=MESH)
    pl.semaphore_wait(barrier, 3)


def remote(src, dst, sends, recvs, at, hop):
    return pltpu.make_async_remote_copy(
        src_ref=src, dst_ref=dst, send_sem=sends.at[at], recv_sem=recvs.at[at],
        device_id={"shard": peer(hop)}, device_id_type=MESH,
    )


def group_params(collective_id, limit):
    return pltpu.CompilerParams(collective_id=collective_id, has_side_effects=True, vmem_limit_bytes=limit)


VMEM_SPEC = pl.BlockSpec(memory_space=pltpu.VMEM)


ANY_SPEC = pl.BlockSpec(memory_space=pl.ANY)


def part_copy(src, dst, send, recv, shard):
    return pltpu.make_async_remote_copy(
        src_ref=src, dst_ref=dst, send_sem=send, recv_sem=recv, device_id={"shard": shard}, device_id_type=MESH
    )


def front_kernel(
    x_ref, cot_ref, gain_ref, w_hbm, o_hbm,
    xs_ref, all_cots_ref, gains_ref, normed_ref, pair_ref, parts_ref, own_ref, send_ref,
    w_ref, o_ref, lhs, mixed, pairs, near, sends, recvs, local, part_sends, part_recvs, part_local,
    pair_sends, pair_recvs, pair_local,
):
    me = lax.axis_index("shard")
    chip = me // 2
    slot = me // 2
    seqs, rows, model = x_ref.shape
    cots_ref = all_cots_ref.at[0]
    cols = all_cots_ref.shape[3]
    side = lax.rem(lax.axis_index("replica"), 2)
    height = lax.axis_size("replica") // 2
    block = model // 2 // height
    aligned = block % LANES == 0
    width = parts_ref.shape[3]
    lift = gain_ref.shape[0]
    span = 2 * rows
    tile = 256
    loads = [
        pltpu.make_async_copy(w_hbm, w_ref, local.at[3]),
        pltpu.make_async_copy(o_hbm, o_ref, local.at[4]),
    ]
    for copy in loads:
        copy.start()
    other = meet_group_and_pair()

    def mine(ref, owner):
        return ref.at[:, pl.ds(pl.multiple_of(owner * rows, 16), rows), :]

    def part(owner):
        return cot_ref.at[:, :, pl.ds(pl.multiple_of(owner * cols, 128), cols)]

    def gain_rows(owner):
        return gains_ref.at[pl.ds(pl.multiple_of(owner * lift, 8), lift), :]

    gain_sends = [remote(gain_ref, gain_rows(me), sends, recvs, 5 + hop, hop) for hop in (1, 2, 3)]
    x_core = remote(x_ref, mine(xs_ref, me), sends, recvs, 0, 1)
    x_chip = remote(x_ref, mine(xs_ref, me), sends, recvs, 1, 2)
    cot_sends = [remote(part(peer(hop)), mine(cots_ref, me), sends, recvs, 2 + hop, hop) for hop in (1, 2, 3)]
    for copy in gain_sends + [x_core, x_chip] + cot_sends:
        copy.start()
    own = [
        pltpu.make_async_copy(x_ref, mine(xs_ref, me), local.at[0]),
        pltpu.make_async_copy(part(me), mine(cots_ref, me), local.at[1]),
        pltpu.make_async_copy(gain_ref, gain_rows(me), local.at[2]),
    ]
    for copy in own:
        copy.start()
    for copy in own:
        copy.wait()
    for copy in gain_sends:
        copy.wait()
    x_core.wait()
    gain = jnp.concatenate([gains_ref[lift * d : lift * d + 1, :] for d in range(4)], axis=1)
    loads[0].wait()

    def piece(half, i):
        where = jnp.bitwise_xor(chip, half)
        return parts_ref.at[slot, :, pl.ds(pl.multiple_of(where * span, 16), span), :]

    def away(i):
        return lax.rem(2 * me + i, 4) != me

    def send(half, i):
        return part_copy(
            mixed.at[half, i], piece(half, i), part_sends.at[2 * half + i], part_recvs.at[2 * slot + half],
            lax.rem(2 * me + i, 4),
        )

    def keep(half, i):
        return pltpu.make_async_copy(mixed.at[half, i], piece(half, i), part_local.at[half])

    def either(i, yes, no):
        pl.when(away(i))(yes)
        pl.when(jnp.logical_not(away(i)))(no)

    def run_half(half):
        where = jnp.bitwise_xor(chip, half) * span

        for seq in range(seqs):

            def norm(r, carry, seq=seq):
                at = pl.ds(pl.multiple_of(where + r * 16, 16), 16)
                vals = xs_ref[seq, at, :].astype(f32)
                inv = lax.rsqrt(jnp.mean(vals * vals, axis=1, keepdims=True) + EPS)
                out = (vals * inv * gain).astype(bf16)
                normed_ref[seq, at, :] = out
                lhs[pl.ds(pl.multiple_of(seq * span + r * 16, 16), 16), :] = out
                return carry

            lax.fori_loop(0, span // 16, norm, 0)
        for copy in normed_copies(half):
            copy.start()
        for i in range(2):

            def product(t, carry, i=i):
                value = rows_dot(lhs[...], w_ref[:, pl.ds(pl.multiple_of(i * width + t * tile, tile), tile)])
                for seq in range(seqs):
                    mixed[half, i, seq, :, pl.ds(pl.multiple_of(t * tile, tile), tile)] = value[
                        seq * span : (seq + 1) * span
                    ].astype(bf16)
                return carry

            lax.fori_loop(0, width // tile, product, 0)
            either(i, lambda i=i: send(half, i).start(), lambda i=i: keep(half, i).start())

    def normed_copies(half):
        where = pl.ds(pl.multiple_of(jnp.bitwise_xor(chip, half) * span, 16), span)
        copies = []
        for b in range(height if aligned else 0):
            def cut(which, b=b):
                return normed_ref.at[:, where, pl.ds(pl.multiple_of((2 * b + which) * block, LANES), block)]

            goal = (slice(None), where, slice(b * block, (b + 1) * block))
            at = half * height + b
            copies.append(pltpu.make_async_copy(cut(side), pair_ref.at[(0,) + goal], pair_local.at[at]))
            copies.append(across(cut(1 - side), pair_ref.at[(1,) + goal], pair_sends, pair_recvs, at, other))
        return copies

    run_half(0)
    x_chip.wait_recv()
    onward = remote(mine(xs_ref, peer(2)), mine(xs_ref, peer(2)), sends, recvs, 2, 1)
    onward.start()
    onward.wait()
    run_half(1)

    for copy in cot_sends:
        copy.wait()
    cot_pair = across(all_cots_ref.at[0], all_cots_ref.at[1], sends, recvs, 11, other)
    cot_pair.start()
    loads[1].wait()

    def partial(block, t):
        return outer_dot(
            cots_ref[...].reshape(seqs * 4 * rows, cols),
            o_ref[pl.ds(pl.multiple_of(block * width + t * tile, tile), tile), :],
        )

    def lanes(t):
        return pl.ds(pl.multiple_of(t * tile, tile), tile)

    near_sends = []
    for at, hop in enumerate((3, 1)):

        def fill(t, carry, at=at, hop=hop):
            pairs[at, :, lanes(t)] = partial(peer(hop), t).astype(bf16)
            return carry

        lax.fori_loop(0, width // tile, fill, 0)
        copy = remote(pairs.at[at], near.at[at], sends, recvs, 9 + at, 1)
        copy.start()
        near_sends.append(copy)
    near_sends[0].wait()

    def to_send(t, carry):
        send_ref[:, lanes(t)] = (partial(peer(2), t) + near[0, :, lanes(t)].astype(f32)).astype(bf16)
        return carry

    lax.fori_loop(0, width // tile, to_send, 0)
    near_sends[1].wait()

    def to_own(t, carry):
        own_ref[:, lanes(t)] = partial(me, t) + near[1, :, lanes(t)].astype(f32)
        return carry

    lax.fori_loop(0, width // tile, to_own, 0)

    x_chip.wait_send()
    cot_pair.wait()
    for copy in normed_copies(0) + normed_copies(1):
        copy.wait()
    for half in range(2):
        for i in range(2):
            either(i, lambda half=half, i=i: send(half, i).wait_send(), lambda half=half, i=i: keep(half, i).wait())
        for at in range(2):

            @pl.when(2 * at + me // 2 != me)
            def _(at=at, half=half):
                part_copy(
                    mixed.at[0, 0], mixed.at[0, 0], part_sends.at[0], part_recvs.at[2 * at + half], peer(1)
                ).wait_recv()


def front(x, cot, gain, w_in, out_proj):
    seqs, rows, model = x.shape
    group = lax.axis_size("shard")
    length = rows * group
    cols = model // group
    width = w_in.shape[1] // 2
    tokens = seqs * length
    lifted = jnp.broadcast_to(gain.astype(f32)[None], (8, gain.shape[0]))
    far_sems = pltpu.SemaphoreType.DMA((lax.axis_size("replica"),))
    return pl.pallas_call(
        front_kernel,
        in_specs=[VMEM_SPEC] * 3 + [ANY_SPEC] * 2,
        out_specs=[VMEM_SPEC] * 8,
        out_shape=[
            jax.ShapeDtypeStruct((seqs, length, model), bf16),
            jax.ShapeDtypeStruct((2, seqs, length, cols), bf16),
            jax.ShapeDtypeStruct((8 * group, gain.shape[0]), f32),
            jax.ShapeDtypeStruct((seqs, length, model), bf16),
            jax.ShapeDtypeStruct((2, seqs, length, model // 2), bf16),
            jax.ShapeDtypeStruct((2, seqs, length, width), bf16),
            jax.ShapeDtypeStruct((tokens, width), f32),
            jax.ShapeDtypeStruct((tokens, width), bf16),
        ],
        scratch_shapes=[
            pltpu.VMEM(w_in.shape, bf16),
            pltpu.VMEM(out_proj.shape, bf16),
            pltpu.VMEM((tokens // 2, model), bf16),
            pltpu.VMEM((2, 2, seqs, 2 * rows, width), bf16),
            pltpu.VMEM((2, tokens, width), bf16),
            pltpu.VMEM((2, tokens, width), bf16),
            pltpu.SemaphoreType.DMA((12,)), pltpu.SemaphoreType.DMA((12,)), pltpu.SemaphoreType.DMA((5,)),
            pltpu.SemaphoreType.DMA((4,)), pltpu.SemaphoreType.DMA((4,)), pltpu.SemaphoreType.DMA((2,)),
            far_sems, far_sems, far_sems,
        ],
        compiler_params=group_params(1, 48 << 20),
        name="front",
    )(x, cot, lifted, w_in, out_proj)


def pair_signal(barrier):
    home = lax.axis_index("replica")
    other = home + 1 - 2 * lax.rem(home, 2)
    pl.semaphore_signal(barrier, inc=1, device_id={"replica": other}, device_id_type=MESH)
    return other


def across(src, dst, sends, recvs, at, other):
    return pltpu.make_async_remote_copy(
        src_ref=src, dst_ref=dst, send_sem=sends.at[at], recv_sem=recvs.at[at],
        device_id={"replica": other}, device_id_type=MESH,
    )


def meet_group_and_pair():
    barrier = pltpu.get_barrier_semaphore()
    for hop in (1, 2, 3):
        pl.semaphore_signal(barrier, inc=1, device_id={"shard": peer(hop)}, device_id_type=MESH)
    other = pair_signal(barrier)
    pl.semaphore_wait(barrier, 4)
    return other


def middle_kernel(
    keep_ref, give_ref, gz_ref, x_hbm, o_hbm,
    both_ref, gz_got_ref, out_ref,
    o_ref, gives, xcol, acc, outs, sends, recvs, local, o_local,
):
    me = lax.axis_index("shard")
    side = lax.rem(lax.axis_index("replica"), 2)
    tokens, half = keep_ref.shape
    keeps_ref, gots_ref = both_ref.at[0], both_ref.at[1]
    seqs, rows, _ = out_ref.shape
    cols = acc.shape[1]
    piece = o_hbm.shape[0] // lax.axis_size("replica")
    per = half // piece
    loads = []
    for d in range(4):
        for q in range(2):
            for j in range(per):
                at = d * 2 * half + (2 * j) * piece + (side if q == 0 else 1 - side) * piece
                loads.append(
                    pltpu.make_async_copy(
                        o_hbm.at[pl.ds(pl.multiple_of(at, piece), piece), :],
                        o_ref.at[q, pl.ds(d * half + j * piece, piece), :],
                        o_local.at[len(loads)],
                    )
                )
    for copy in loads:
        copy.start()
    fetch = pltpu.make_async_copy(
        x_hbm.at[:, pl.ds(pl.multiple_of(me * cols, 128), cols)], xcol, local.at[0]
    )
    fetch.start()
    other = meet_group_and_pair()

    def spot(ref, owner):
        return ref.at[:, pl.ds(pl.multiple_of(owner * half, 128), half)]

    give_pair = across(give_ref, spot(gots_ref, me), sends, recvs, 0, other)
    gz_pair = across(gz_ref, gz_got_ref, sends, recvs, 1, other)
    k_chip = remote(keep_ref, spot(keeps_ref, me), sends, recvs, 2, 2)
    v_chip = remote(give_ref, spot(gives, me), sends, recvs, 3, 2)
    k_core = remote(keep_ref, spot(keeps_ref, me), sends, recvs, 4, 1)
    v_core = remote(give_ref, spot(gives, me), sends, recvs, 5, 1)
    k_own = pltpu.make_async_copy(keep_ref, spot(keeps_ref, me), local.at[1])
    v_own = pltpu.make_async_copy(give_ref, spot(gives, me), local.at[2])
    for copy in (k_core, v_core, k_chip, give_pair, v_chip, gz_pair, k_own, v_own):
        copy.start()

    def gated_rows(q, owner):
        where = pl.ds(pl.multiple_of(owner * half, 128), half)
        left = keeps_ref if q == 0 else gives
        return rows_dot(left[:, where], o_ref[q, where, :])

    k_own.wait()
    v_own.wait()
    for copy in loads:
        copy.wait()
    fetch.wait()
    acc[...] = xcol[...].astype(f32) + gated_rows(0, me)
    acc[...] += gated_rows(1, me)
    k_core.wait()
    acc[...] += gated_rows(0, peer(1))
    v_core.wait()
    acc[...] += gated_rows(1, peer(1))
    k_chip.wait_recv()
    k_on = remote(spot(keeps_ref, peer(2)), spot(keeps_ref, peer(2)), sends, recvs, 6, 1)
    k_on.start()
    give_pair.wait_recv()
    g_chip = remote(spot(gots_ref, me), spot(gots_ref, me), sends, recvs, 7, 2)
    g_core = remote(spot(gots_ref, me), spot(gots_ref, me), sends, recvs, 8, 1)
    g_core.start()
    acc[...] += gated_rows(0, peer(2))
    k_on.wait()
    acc[...] += gated_rows(0, peer(3))
    v_chip.wait_recv()
    v_on = remote(spot(gives, peer(2)), spot(gives, peer(2)), sends, recvs, 9, 1)
    v_on.start()
    acc[...] += gated_rows(1, peer(2))
    v_on.wait()
    outs[...] = (acc[...] + gated_rows(1, peer(3))).astype(bf16).reshape(outs.shape)

    def out_rows(owner):
        return outs.at[:, pl.ds(pl.multiple_of(owner * rows, 16), rows), :]

    home = out_ref.at[:, :, pl.ds(pl.multiple_of(me * cols, 128), cols)]
    out_own = pltpu.make_async_copy(out_rows(me), home, local.at[3])
    out_own.start()
    out_sends = [remote(out_rows(peer(hop)), home, sends, recvs, 9 + hop, hop) for hop in (2, 3, 1)]
    for copy in out_sends:
        copy.start()
    g_chip.start()
    g_chip.wait_recv()
    g_on = remote(spot(gots_ref, peer(2)), spot(gots_ref, peer(2)), sends, recvs, 13, 1)
    g_on.start()
    for copy in out_sends + [g_on, g_core, gz_pair]:
        copy.wait()
    for copy in (g_chip, give_pair, k_chip, v_chip):
        copy.wait_send()
    out_own.wait()


def middle(keep, give, grad_z, x_all, out_proj, seqs):
    tokens, half = keep.shape
    group = lax.axis_size("shard")
    model = x_all.shape[1]
    cols = model // group
    return pl.pallas_call(
        middle_kernel,
        in_specs=[VMEM_SPEC] * 3 + [ANY_SPEC] * 2,
        out_specs=[VMEM_SPEC] * 3,
        out_shape=[
            jax.ShapeDtypeStruct((2, tokens, half * group), bf16),
            jax.ShapeDtypeStruct(grad_z.shape, bf16),
            jax.ShapeDtypeStruct((seqs, tokens // seqs // group, model), bf16),
        ],
        scratch_shapes=[
            pltpu.VMEM((2, half * group, cols), bf16),
            pltpu.VMEM((tokens, half * group), bf16),
            pltpu.VMEM((tokens, cols), bf16),
            pltpu.VMEM((tokens, cols), f32),
            pltpu.VMEM((seqs, tokens // seqs, cols), bf16),
            pltpu.SemaphoreType.DMA((14,)), pltpu.SemaphoreType.DMA((14,)), pltpu.SemaphoreType.DMA((4,)),
            pltpu.SemaphoreType.DMA((8 * max(1, half * group // 4 // (out_proj.shape[0] // lax.axis_size("replica"))),)),
        ],
        compiler_params=group_params(6, 20 << 20),
        name="middle",
    )(keep, give, grad_z, x_all, out_proj)


def home_kernel(gx_ref, gz_ref, small_ref, got_ref, cols_ref, small_got_ref, sends, recvs, local):
    me = lax.axis_index("shard")
    width = gx_ref.shape[1]
    other = meet_group_and_pair()
    pair_copy = across(gx_ref, got_ref, sends, recvs, 0, other)
    pair_copy.start()
    small_copy = across(small_ref, small_got_ref, sends, recvs, 3, other)
    small_copy.start()

    def goal(slot):
        return (4 * slot + me) // 2

    spot = cols_ref.at[:, pl.ds(pl.multiple_of(lax.rem(me, 2) * width, 128), width)]

    def send(slot, ref):
        return part_copy(ref, spot, sends.at[1 + slot], recvs.at[1 + lax.rem(me, 2)], goal(slot))

    def keep(ref):
        return pltpu.make_async_copy(ref, spot, local.at[0])

    refs = (gx_ref, gz_ref)
    for slot in (0, 1):
        pl.when(goal(slot) != me)(lambda slot=slot: send(slot, refs[slot]).start())
        pl.when(goal(slot) == me)(lambda slot=slot: keep(refs[slot]).start())
    for slot in (0, 1):
        pl.when(goal(slot) != me)(lambda slot=slot: send(slot, refs[slot]).wait_send())
        pl.when(goal(slot) == me)(lambda slot=slot: keep(refs[slot]).wait())
    for at in range(2):

        @pl.when(lax.rem(2 * me + at, 4) != me)
        def _(at=at):
            part_copy(gx_ref, gx_ref, sends.at[0], recvs.at[1 + at], peer(1)).wait_recv()

    pair_copy.wait()
    small_copy.wait()


def to_home(gx, gz, small):
    tokens, width = gx.shape
    return pl.pallas_call(
        home_kernel,
        in_specs=[VMEM_SPEC] * 3,
        out_specs=[VMEM_SPEC] * 3,
        out_shape=[
            jax.ShapeDtypeStruct(gx.shape, bf16),
            jax.ShapeDtypeStruct((tokens, 2 * width), bf16),
            jax.ShapeDtypeStruct(small.shape, bf16),
        ],
        scratch_shapes=[
            pltpu.SemaphoreType.DMA((4,)), pltpu.SemaphoreType.DMA((4,)), pltpu.SemaphoreType.DMA((1,)),
        ],
        compiler_params=group_params(7, 16 << 20),
        name="to_home",
    )(gx, gz, small)


def finish_kernel(
    xb_ref, sb_ref, wz_ref, cols_ref, w_hbm, x_ref, cot_ref, gain_ref,
    gw_ref, small_ref, dx_ref, ggain_ref,
    w_ref, x_in, s_in, lhs, pairs, near, g_own, g_send, g_far, h_send, h_cols, s_own, gains, gain_near, gain_sum,
    gain_pair, gain_two, gain_in,
    sends, recvs, far_sends, far_recvs, local,
):
    me = lax.axis_index("shard")
    home = lax.axis_index("replica")
    count = lax.axis_size("replica")
    height = count // 2
    mine = home // 2
    side = lax.rem(home, 2)
    seqs, rows, model = x_ref.shape
    tokens = cols_ref.shape[0]
    length = tokens // seqs
    deep, width = wz_ref.shape
    half = deep // 2
    tile = 256
    span = seqs * rows
    load = pltpu.make_async_copy(w_hbm, w_ref, local.at[0])
    load.start()
    barrier = pltpu.get_barrier_semaphore()
    for hop in (1, 2, 3):
        pl.semaphore_signal(barrier, inc=1, device_id={"shard": peer(hop)}, device_id_type=MESH)
    other = pair_signal(barrier)

    def far(step):
        return lax.rem(home + 2 * step, count)

    for step in range(1, height):
        pl.semaphore_signal(barrier, inc=1, device_id={"replica": far(step)}, device_id_type=MESH)
    pl.semaphore_wait(barrier, 3 + height)

    def far_copy(src, dst, kind, step):
        at = kind * height + step
        return across(src, dst, far_sends, far_recvs, at, far(step))

    def block(step):
        return lax.rem(mine + step, height)

    order = range(1, height)
    s_sends = [far_copy(sb_ref.at[block(step)], s_in.at[step - 1], 0, step) for step in order]

    def x_sends(part):
        cut = slice(part * half, (part + 1) * half)
        return [
            far_copy(xb_ref.at[block(step), cut], x_in.at[step - 1, cut], 1 + part, step) for step in order
        ]

    for copy in s_sends + x_sends(0):
        copy.start()

    spot = pl.ds(pl.multiple_of(lax.rem(me, 2) * width, LANES), width)

    def goal(slot):
        return (4 * slot + me) // 2

    def home_pieces(at):
        if at == 2:
            return 1, wz_ref, h_cols.at[:, spot]
        cut = slice(at * half, (at + 1) * half)
        return 0, h_send.at[cut], h_cols.at[cut, spot]

    def home_send(at):
        slot, src, dst = home_pieces(at)
        return part_copy(src, dst, sends.at[at], recvs.at[at * 2 + lax.rem(me, 2)], goal(slot))

    def home_keep(at):
        _, src, dst = home_pieces(at)
        return pltpu.make_async_copy(src, dst, local.at[1 + at])

    def home_start(at):
        slot = home_pieces(at)[0]
        pl.when(goal(slot) != me)(lambda: home_send(at).start())
        pl.when(goal(slot) == me)(lambda: home_keep(at).start())

    home_start(2)

    def stage(owners):
        for i, owner in enumerate(owners):
            for seq in range(seqs):
                at = pl.ds(pl.multiple_of(seq * length + owner * rows, 16), rows)
                lhs[i * span + seq * rows : i * span + (seq + 1) * rows, :] = cols_ref[at, :]

    def lanes(t):
        return pl.ds(pl.multiple_of(t * tile, tile), tile)

    def product(t):
        return outer_dot(lhs[...], w_ref[lanes(t), :])

    stage((peer(3), peer(1)))
    load.wait()

    def first(t, carry):
        value = product(t)
        pairs[0, :, lanes(t)] = value[:span].astype(bf16)
        pairs[1, :, lanes(t)] = value[span:].astype(bf16)
        return carry

    lax.fori_loop(0, model // tile, first, 0)
    near_send = remote(pairs, near, sends, recvs, 6, 1)
    near_send.start()

    for copy in s_sends:
        copy.wait_recv()
    total = sb_ref[mine].astype(f32)
    for step in order:
        total = total + s_in[step - 1].astype(f32)
    s_own[...] = total.astype(bf16)
    small_ref[side, mine] = s_own[...]
    spread = [far_copy(s_own, small_ref.at[side, mine], 3, step) for step in order]
    for copy in spread + x_sends(1):
        copy.start()

    stage((peer(2), me))
    near_send.wait()

    def second(t, carry):
        value = product(t)
        g_send[:, lanes(t)] = (value[:span] + near[0, :, lanes(t)].astype(f32)).astype(bf16)
        g_own[:, lanes(t)] = value[span:] + near[1, :, lanes(t)].astype(f32)
        return carry

    lax.fori_loop(0, model // tile, second, 0)
    chip_send = remote(g_send, g_far, sends, recvs, 7, 2)
    chip_send.start()
    chip_send.wait()

    gains[...] = jnp.zeros_like(gains)
    for seq in range(seqs):

        def last(r, carry, seq=seq):
            at = pl.ds(pl.multiple_of(r * 16, 16), 16)
            flat = pl.ds(pl.multiple_of(seq * rows + r * 16, 16), 16)
            grad = g_own[flat, :] + g_far[flat, :].astype(f32)
            vals = x_ref[seq, at, :].astype(f32)
            inv = lax.rsqrt(jnp.mean(vals * vals, axis=1, keepdims=True) + EPS)
            scaled = grad * gain_ref[...]
            mean = jnp.mean(scaled * vals, axis=1, keepdims=True)
            out = inv * (scaled - vals * (inv * inv * mean))
            dx_ref[seq, at, :] = (cot_ref[seq, at, :].astype(f32) + out).astype(bf16)
            terms = grad * (vals * inv)
            gains[...] += terms[:8] + terms[8:]
            return carry

        lax.fori_loop(0, rows // 16, last, 0)
    gains[...] = jnp.broadcast_to(jnp.sum(gains[...], axis=0, keepdims=True), gains.shape)
    wide = model // 4

    def gain_part(owner):
        return gains.at[:, pl.ds(pl.multiple_of(owner * wide, LANES), wide)]

    gain_sends = [remote(gain_part(peer(hop)), gain_near.at[hop - 1], sends, recvs, 7 + hop, hop) for hop in (1, 2, 3)]
    for copy in gain_sends:
        copy.start()

    def home_sum(part):
        for copy in x_sends(part):
            copy.wait_recv()
        cut = slice(part * half, (part + 1) * half)
        total = xb_ref[mine, cut].astype(f32)
        for step in order:
            total = total + x_in[step - 1, cut].astype(f32)
        h_send[cut] = total.astype(bf16)
        home_start(part)

    for copy in gain_sends:
        copy.wait()
    gain_sum[...] = gains[:, pl.ds(pl.multiple_of(me * wide, LANES), wide)] + gain_near[0] + gain_near[1] + gain_near[2]
    gain_copy = across(gain_sum, gain_pair, sends, recvs, 11, other)
    gain_copy.start()
    home_sum(0)
    gain_copy.wait()
    gain_two[...] = gain_sum[...] + gain_pair[...]
    gain_far = [far_copy(gain_two, gain_in.at[step - 1], 4, step) for step in order]
    for copy in gain_far:
        copy.start()
    for copy in spread:
        copy.wait_recv()
    small_pair = across(small_ref.at[side], small_ref.at[side], sends, recvs, 12, other)
    small_pair.start()
    home_sum(1)
    for copy in gain_far:
        copy.wait()
    total = gain_two[...]
    for step in order:
        total = total + gain_in[step - 1]
    ggain_ref[...] = total

    for at in (2, 0, 1):
        slot = home_pieces(at)[0]
        pl.when(goal(slot) != me)(lambda at=at: home_send(at).wait_send())
        pl.when(goal(slot) == me)(lambda at=at: home_keep(at).wait())

        for place in range(2):
            source = lax.rem(2 * me + place, 4)
            wanted = (me // 2 == slot) & (source != me)

            @pl.when(wanted)
            def _(at=at, place=place):
                _, src, _ = home_pieces(at)
                part_copy(src, src, sends.at[at], recvs.at[at * 2 + place], peer(1)).wait_recv()

    for r in range(0, deep, 32):
        gw_ref[r : r + 32, :] = h_cols[r : r + 32, :].astype(f32)
    small_pair.wait()
    for copy in s_sends + spread + x_sends(0) + x_sends(1):
        copy.wait_send()


def finish(x_blocks, small_blocks, wz, cols, w_in, x, cot, gain):
    height, deep, width = x_blocks.shape
    seqs, rows, model = x.shape
    span = seqs * rows
    lines = small_blocks.shape[1]
    wide = model // 4
    gain_tile = pltpu.VMEM((8, wide), f32)
    other = max(height - 1, 1)
    return pl.pallas_call(
        finish_kernel,
        in_specs=[VMEM_SPEC] * 4 + [ANY_SPEC] + [VMEM_SPEC] * 3,
        out_specs=[VMEM_SPEC] * 4,
        out_shape=[
            jax.ShapeDtypeStruct((deep, 2 * width), f32),
            jax.ShapeDtypeStruct((2, height, lines, width), bf16),
            jax.ShapeDtypeStruct(x.shape, bf16),
            jax.ShapeDtypeStruct((8, wide), f32),
        ],
        scratch_shapes=[
            pltpu.VMEM(w_in.shape, bf16),
            pltpu.VMEM((other, deep, width), bf16),
            pltpu.VMEM((other, lines, width), bf16),
            pltpu.VMEM((2 * span, cols.shape[1]), bf16),
            pltpu.VMEM((2, span, model), bf16),
            pltpu.VMEM((2, span, model), bf16),
            pltpu.VMEM((span, model), f32),
            pltpu.VMEM((span, model), bf16),
            pltpu.VMEM((span, model), bf16),
            pltpu.VMEM((deep, width), bf16),
            pltpu.VMEM((deep, 2 * width), bf16),
            pltpu.VMEM((lines, width), bf16),
            pltpu.VMEM((8, model), f32),
            pltpu.VMEM((3, 8, wide), f32),
            gain_tile, gain_tile, gain_tile,
            pltpu.VMEM((other, 8, wide), f32),
            pltpu.SemaphoreType.DMA((13,)), pltpu.SemaphoreType.DMA((13,)),
            pltpu.SemaphoreType.DMA((5 * height,)), pltpu.SemaphoreType.DMA((5 * height,)),
            pltpu.SemaphoreType.DMA((4,)),
        ],
        compiler_params=group_params(8, 48 << 20),
        name="finish",
    )(x_blocks, small_blocks, wz, cols, w_in, x, cot, gain)


def total_kernel(part_ref, out_ref, near, chip_sum, far, sends, recvs):
    me = lax.axis_index("shard")
    half = part_ref.shape[1] // 2
    mine = pl.ds(pl.multiple_of(lax.rem(me, 2) * half, 128), half)
    other = pl.ds(pl.multiple_of((1 - lax.rem(me, 2)) * half, 128), half)
    meet_group()
    first = remote(part_ref.at[:, other], near, sends, recvs, 0, 1)
    first.start()
    first.wait()
    chip_sum[...] = part_ref[:, mine] + near[...]
    second = remote(chip_sum, far, sends, recvs, 1, 2)
    second.start()
    second.wait()
    out_ref[:, mine] = chip_sum[...] + far[...]
    third = remote(out_ref.at[:, mine], out_ref.at[:, mine], sends, recvs, 2, 1)
    third.start()
    third.wait()


def group_total(part, collective_id):
    rows, cols = part.shape
    half = pltpu.VMEM((rows, cols // 2), f32)
    return pl.pallas_call(
        total_kernel,
        in_specs=[VMEM_SPEC],
        out_specs=VMEM_SPEC,
        out_shape=jax.ShapeDtypeStruct((rows, cols), f32),
        scratch_shapes=[half, half, half, pltpu.SemaphoreType.DMA((3,)), pltpu.SemaphoreType.DMA((3,))],
        compiler_params=group_params(collective_id, 16 << 20),
        name="group_total",
    )(part)


def by_hop(value, hop):
    return lax.ppermute(value, "shard", [(i, i ^ hop) for i in range(4)])


def pair(value):
    return lax.ppermute(value, "replica", [(i, i ^ 1) for i in range(lax.axis_size("replica"))])


def far_send(blocks):
    count = lax.axis_size("replica")
    height = count // 2
    mine = lax.axis_index("replica") // 2

    def pick(at):
        return lax.dynamic_index_in_dim(blocks, at, 0, False)

    sent = []
    for step in range(1, height):
        out = pick(lax.rem(mine + step, height)).astype(bf16)
        sent.append(lax.ppermute(out, "replica", [(i, (i + 2 * step) % count) for i in range(count)]))
    return pick(mine), tuple(sent)


def far_total(own, sent):
    total = own
    for value in sent:
        total = total + value.astype(f32)
    return total


def after(value, *others):
    return lax.optimization_barrier((value,) + others)[0]


def body(
    block_input, segment_ids, norm_gain, w_in, conv_weight, conv_bias, x_proj, dt_proj, dt_bias,
    d_skip, out_proj, out_grad,
):
    seqs, local, model = block_input.shape
    length = segment_ids.shape[1]
    tokens = seqs * length
    width = d_skip.shape[0]
    rank = dt_proj.shape[0]
    n = (x_proj.shape[0] - rank) // 2
    me = lax.axis_index("shard")
    count = lax.axis_size("replica")
    height = count // 2
    side = lax.rem(lax.axis_index("replica"), 2)

    def split(values):
        return values.reshape(seqs, length, -1)

    def halves(values, blocks):
        piece = values.shape[1] // blocks // 2
        cuts = [values[:, b * piece : (b + 1) * piece] for b in range(2 * blocks)]
        even = jnp.concatenate(cuts[0::2], axis=1)
        odd = jnp.concatenate(cuts[1::2], axis=1)
        return jnp.where(side == 0, even, odd), jnp.where(side == 0, odd, even)

    def both(keep, got):
        return jnp.concatenate([keep, got], axis=0)

    xs, cots, gains, normed, normed_pair, parts, gated_own, gated_send = front(
        block_input, out_grad, norm_gain, w_in, out_proj
    )
    gain = gains[::8].reshape(1, -1)
    x_all = xs.reshape(tokens, model)
    cot_pair = cots.reshape(2 * tokens, -1)
    if model // count % LANES == 0:
        normed_pair = normed_pair.reshape(2 * tokens, -1)
    else:
        normed_keep, normed_give = halves(normed.reshape(tokens, model), height)
        normed_pair = jnp.concatenate([normed_keep, pair(normed_give)], axis=0)
    x_part, z_part = parts[0], parts[1]

    seg_padded = jnp.pad(segment_ids, ((0, 0), (KW - 1, 0)), constant_values=-1)
    taps = [
        (seg_padded[:, KW - 1 - d : KW - 1 - d + length] == segment_ids).astype(f32) for d in range(KW)
    ]
    conv_w = conv_weight.astype(f32)
    xv = x_part.astype(f32)
    x_padded = jnp.pad(xv, ((0, 0), (KW - 1, 0), (0, 0)))
    conv_pre = conv_bias.astype(f32) + conv_w[KW - 1] * xv
    for j in range(KW - 1):
        d = KW - 1 - j
        conv_pre = conv_pre + conv_w[j] * x_padded[:, j : j + length] * taps[d][:, :, None]
    conv_out = jax.nn.silu(conv_pre).astype(bf16)
    conv_flat = conv_out.reshape(tokens, width)
    proj = group_total(outer_dot(x_proj, conv_flat), 3)
    gated_far = by_hop(after(gated_send, proj), 2)
    keep_lanes = jnp.broadcast_to(taps[1][:, :, None], (seqs, length, LANES))
    skip = d_skip.astype(f32)
    y_total, gated, rate, beta, states = recurrence_forward(
        conv_out, z_part, proj, keep_lanes, dt_proj, dt_bias.astype(f32)[None], skip[None]
    )
    y_total, gated, gated_far = lax.optimization_barrier((y_total, gated, gated_far))
    grad_gated = split(gated_own + gated_far.astype(f32))
    z_vals = z_part.astype(f32)
    dy = grad_gated * jax.nn.silu(z_vals)
    grad_z = (grad_gated * y_total * silu_slope(z_vals)).astype(bf16).reshape(tokens, width)

    gated_keep, gated_give = halves(gated.reshape(tokens, width), height // 4)
    cols = model // 4
    gated_both, grad_z_got, block_output = middle(gated_keep, gated_give, grad_z, x_all, out_proj, seqs)
    out_blocks = inner_dot(gated_both.reshape(2 * tokens, -1), cot_pair).astype(bf16).reshape(height, -1, cols)
    z_blocks = inner_dot(normed_pair, both(grad_z, grad_z_got)).astype(bf16).reshape(height, -1, width)
    out_own, out_sent = far_send(out_blocks)
    z_own, z_sent = far_send(z_blocks)
    rate, out_own, z_own = lax.optimization_barrier((rate, out_own, z_own))

    grad_conv_rec, grad_dt_low, grad_proj, grad_dt_proj, grad_dt_bias, grad_d_skip = recurrence_backward(
        rate, beta, conv_out, dy, proj, keep_lanes, dt_proj, states
    )
    grad_proj, out_sent = lax.optimization_barrier((grad_proj, out_sent))
    grad_proj = group_total(grad_proj, 4).astype(bf16)
    grad_x_proj = rows_dot(grad_proj, conv_flat)
    grad_conv = dy * skip + grad_conv_rec + split(inner_dot(grad_proj, x_proj))
    grad_pre = grad_conv * silu_slope(conv_pre)
    grad_conv_bias = jnp.sum(grad_pre, axis=(0, 1))
    grad_conv_weight = jnp.stack(
        [
            jnp.sum(grad_pre * x_padded[:, j : j + length] * taps[KW - 1 - j][:, :, None], axis=(0, 1))
            for j in range(KW)
        ]
    )
    grad_x = conv_w[KW - 1] * grad_pre
    for j in range(KW - 1):
        d = KW - 1 - j
        ahead = jnp.pad(grad_pre * taps[d][:, :, None], ((0, 0), (0, d), (0, 0)))[:, d:]
        grad_x = grad_x + conv_w[j] * ahead
    grad_x = grad_x.astype(bf16).reshape(tokens, width)

    small = jnp.concatenate(
        [grad_x_proj, grad_dt_proj, grad_conv_weight, grad_conv_bias[None], grad_dt_bias, grad_d_skip]
    )
    unit = 16 * count
    padded = -(-small.shape[0] // unit) * unit
    small = jnp.pad(small, ((0, padded - small.shape[0]), (0, 0))).reshape(height, 2, -1, width)
    small_keep = jnp.where(side == 0, small[:, 0], small[:, 1])
    small_give = jnp.where(side == 0, small[:, 1], small[:, 0]).astype(bf16).reshape(-1, width)
    grad_x_got, grad_cols, small_got = to_home(grad_x, grad_z, small_give)
    small_blocks = (small_keep + small_got.reshape(small_keep.shape).astype(f32)).astype(bf16)
    x_blocks = inner_dot(normed_pair, both(grad_x, grad_x_got)).astype(bf16).reshape(height, -1, width)
    x_blocks, z_sent = lax.optimization_barrier((x_blocks, z_sent))
    grad_w_z = far_total(z_own.astype(f32), z_sent).astype(bf16)
    grad_out_proj = far_total(out_own.astype(f32), out_sent)
    grad_w_in, small, input_grad, grad_gain = finish(
        x_blocks, small_blocks, grad_w_z, grad_cols, w_in, block_input, out_grad, gain
    )
    small = small.transpose(1, 0, 2, 3).reshape(padded, width).astype(f32)

    top = x_proj.shape[0]
    return (
        block_output, input_grad, grad_gain[0], grad_w_in,
        small[top + rank : top + rank + KW], small[top + rank + KW], small[:top], small[top : top + rank],
        small[top + rank + KW + 1], small[top + rank + KW + 2], grad_out_proj,
    )


def solution(mesh):
    return jax.shard_map(
        body,
        mesh=mesh,
        in_specs=(
            P("replica", "shard", None), P("replica", None), P("shard"), P(None, "shard"), P(None, "shard"),
            P("shard"), P(None, "shard"), P(None, "shard"), P("shard"), P("shard"), P(None, "shard"),
            P("replica", "shard", None),
        ),
        out_specs=(
            P("replica", "shard", None), P("replica", "shard", None), P("shard"), P("replica", "shard"),
            P(None, "shard"), P("shard"), P(None, "shard"), P(None, "shard"), P("shard"), P("shard"),
            P("replica", "shard"),
        ),
        check_vma=False,
    )
```

```python
import functools

import jax
import jax.numpy as jnp
from jax import lax
from jax.experimental import pallas as pl
from jax.experimental.pallas import tpu as pltpu
from jax.sharding import PartitionSpec as P

KW = 4
EPS = 1e-05
CHUNK = 16
LANES = 128
f32 = jnp.float32
bf16 = jnp.bfloat16


def rows_dot(a, b):
    return jnp.dot(a, b, preferred_element_type=f32)


def inner_dot(a, b):
    return lax.dot_general(a, b, (((0,), (0,)), ((), ())), preferred_element_type=f32)


def outer_dot(a, b):
    return lax.dot_general(a, b, (((1,), (1,)), ((), ())), preferred_element_type=f32)


def silu_slope(values):
    sig_val = jax.nn.sigmoid(values)
    return sig_val + values * sig_val * (1.0 - sig_val)

MESH = pl.DeviceIdType.MESH
BLOCK = 128
PIECES = 1


def lane(g):
    return slice(g * LANES, (g + 1) * LANES)


def column(block, t):
    return jnp.broadcast_to(block[:, t : t + 1], (block.shape[0], LANES))


def row(ref, t, g, n):
    return jnp.broadcast_to(ref[t : t + 1, lane(g)], (n, LANES))


def prepare(base, rate_ref, conv_ref, keep_ref, rk, u, kept):
    rows = pl.ds(base, CHUNK)
    rate = rate_ref[0, rows, :]
    keep = keep_ref[0, rows, :]
    conv = conv_ref[0, rows, :].astype(f32)
    for g in range(rate.shape[1] // LANES):
        rk[:, lane(g)] = rate[:, lane(g)] * keep
    u[...] = rate * conv
    kept[...] = keep
    return rate, conv, keep


def shifted(cols, j):
    size = cols.shape[1]
    return pltpu.roll(cols, lax.rem(size - j * CHUNK, size), 1)


def spread_mask(n, size=CHUNK):
    shape = (size, size * n)
    return lax.broadcasted_iota(jnp.int32, shape, 1) // n == lax.broadcasted_iota(jnp.int32, shape, 0)


def picker(n, size=CHUNK):
    shape = (n, size * n)
    return (lax.broadcasted_iota(jnp.int32, shape, 1) % n == lax.broadcasted_iota(jnp.int32, shape, 0)).astype(bf16)


def diagonal(rows, mask, pick):
    return jnp.where(mask, rows_dot(rows.astype(bf16), pick), 0.0).astype(bf16)


def forward_kernel(
    conv_ref, z_ref, proj_ref, keep_ref, dt_proj_ref, dt_bias_ref, skip_ref,
    y_ref, gated_ref, rate_ref, beta_ref, state_ref,
    held_ref, rk, u, kept, query_rows,
):
    width = conv_ref.shape[2]
    rank = dt_proj_ref.shape[0]
    n = (proj_ref.shape[0] - rank) // 2
    groups = width // LANES
    span = CHUNK * n

    @pl.when(pl.program_id(1) == 0)
    def _():
        held_ref[...] = jnp.zeros_like(held_ref)

    dt_low = proj_ref[0:rank, :].astype(bf16)
    keys = proj_ref[rank : rank + n, :]
    query_rows[...] = proj_ref[rank + n :, :].T
    key_square = jnp.sum(keys.T * keys.T, axis=1, keepdims=True)
    beta = jax.nn.sigmoid(inner_dot(dt_low, dt_proj_ref[...]) + dt_bias_ref[...])
    beta_ref[0] = beta
    rate_ref[0] = beta / (1.0 + beta * key_square)
    mask, pick = spread_mask(n), picker(n)

    def chunk(j, held):
        base = pl.multiple_of(j * CHUNK, CHUNK)
        rows = pl.ds(base, CHUNK)
        _, conv, _ = prepare(base, rate_ref, conv_ref, keep_ref, rk, u, kept)
        near_keys = shifted(keys, j)
        held = list(held)
        for t in range(CHUNK):
            key = column(near_keys, t)
            key2 = key * key
            keep = jnp.broadcast_to(kept[t : t + 1, :], (n, LANES))
            at = pl.ds(pl.multiple_of((base + t) * n, n), n)
            for g in range(groups):
                decay = keep - row(rk, t, g, n) * key2
                held[g] = decay * held[g] + row(u, t, g, n) * key
                state_ref[0, at, lane(g)] = held[g].astype(bf16)
        block = state_ref[0, pl.ds(pl.multiple_of(base * n, span), span), :]
        total = rows_dot(diagonal(query_rows[rows, :], mask, pick), block) + skip_ref[...] * conv
        y_ref[0, rows, :] = total
        z = z_ref[0, rows, :].astype(f32)
        gated_ref[0, rows, :] = (total * (z * jax.nn.sigmoid(z))).astype(bf16)
        return tuple(held)

    start = tuple(held_ref[:, lane(g)] for g in range(groups))
    end = lax.fori_loop(0, conv_ref.shape[1] // CHUNK, chunk, start)
    for g in range(groups):
        held_ref[:, lane(g)] = end[g]


def backward_kernel(
    rate_ref, beta_ref, conv_ref, dy_ref, proj_ref, keep_ref, dt_proj_ref, state_ref, last_ref,
    gconv_ref, gdt_ref, gproj_ref, gdt_proj_ref, gdt_bias_ref, gskip_ref,
    held_ref, grate, rk, u, dys, kept, key_rows, adj, adj_state, sums,
):
    block_rows, width = rate_ref.shape[1:]
    rank = dt_proj_ref.shape[0]
    n = (proj_ref.shape[0] - rank) // 2
    groups = width // LANES
    chunks = block_rows // CHUNK

    @pl.when(pl.program_id(1) == 0)
    def _():
        held_ref[...] = jnp.zeros_like(held_ref)

    @pl.when((pl.program_id(0) == 0) & (pl.program_id(1) == 0))
    def _():
        gdt_proj_ref[...] = jnp.zeros_like(gdt_proj_ref)
        gdt_bias_ref[...] = jnp.zeros_like(gdt_bias_ref)
        gskip_ref[...] = jnp.zeros_like(gskip_ref)

    keys = proj_ref[rank : rank + n, :]
    queries = proj_ref[rank + n :, :]
    key_rows[...] = keys.T
    mask, pick = spread_mask(n, CHUNK // PIECES), picker(n, CHUNK // PIECES)

    spot = lax.broadcasted_iota(jnp.int32, (n, LANES), 1)
    sums[...] = jnp.zeros_like(sums)

    def chunk(step, held):
        j = chunks - 1 - step
        base = pl.multiple_of(j * CHUNK, CHUNK)
        rows = pl.ds(base, CHUNK)
        rate, conv, keeps = prepare(base, rate_ref, conv_ref, keep_ref, rk, u, kept)
        dys[...] = dy_ref[0, rows, :]
        near_keys = shifted(keys, j)
        near_queries = shifted(queries, j)
        held = list(held)
        after = [state_ref[0, pl.ds(pl.multiple_of((base + CHUNK - 1) * n, n), n), lane(g)] for g in range(groups)]
        found = [jnp.zeros((n, LANES), f32) for _ in range(3)]
        def settle(p):
            size = CHUNK // PIECES
            part = slice(p * size, (p + 1) * size)
            some = pl.ds(base + p * size, size)
            key_block = key_rows[some, :]
            w1 = rows_dot(diagonal(key_block, mask, pick), adj[p][...].astype(bf16))
            w2 = rows_dot(diagonal(key_block * key_block, mask, pick), adj_state[p][...].astype(bf16))
            for g in range(groups):
                grate[some, lane(g)] = conv[part, lane(g)] * w1[:, lane(g)] - keeps[part] * w2[:, lane(g)]
            gconv_ref[0, some, :] = rate[part] * w1

        for t in reversed(range(CHUNK)):
            piece, place = t // (CHUNK // PIECES), t % (CHUNK // PIECES)
            own = slice(place * n, (place + 1) * n)
            key = column(near_keys, t)
            key2 = key * key
            query = column(near_queries, t)
            keep = jnp.broadcast_to(kept[t : t + 1, :], (n, LANES))
            prior = jnp.maximum(base + t - 1, 0)
            at = pl.ds(pl.multiple_of(prior * n, n), n)
            parts = [None] * 3
            for g in range(groups):
                slope = row(dys, t, g, n)
                pace = row(rk, t, g, n)
                grad = held[g] + slope * query
                decay = keep - pace * key2
                held[g] = decay * grad
                before = state_ref[0, at, lane(g)]
                if t == 0:
                    before = jnp.where(j == 0, last_ref[0, :, lane(g)], before)
                cross = grad * before.astype(f32)
                adj[piece][own, lane(g)] = grad
                adj_state[piece][own, lane(g)] = cross
                terms = (grad * row(u, t, g, n), cross * pace, after[g].astype(f32) * slope)
                parts = [v if p is None else p + v for p, v in zip(parts, terms)]
                after[g] = before
            if place == 0:
                settle(piece)
            here = spot == base + t
            found = [jnp.where(here, jnp.sum(p, axis=1, keepdims=True), f) for p, f in zip(parts, found)]
        for i in range(3):
            sums[i] += found[i]
        return tuple(held)

    start = tuple(held_ref[:, lane(g)] for g in range(groups))
    end = lax.fori_loop(0, chunks, chunk, start)
    for g in range(groups):
        held_ref[:, lane(g)] = end[g]

    def picked(left, value):
        high = value.astype(bf16)
        low = (value - high.astype(f32)).astype(bf16)
        return outer_dot(left, high) + outer_dot(left, low)

    rate = rate_ref[0]
    beta = beta_ref[0]
    grad_rate = grate[...]
    self_term = picked(jnp.ones((n, width), bf16), grad_rate * rate * rate)
    key_square = jnp.sum(key_rows[...] * key_rows[...], axis=1, keepdims=True)
    denom_inv = 1.0 / (1.0 + beta * key_square)
    grad_dt = grad_rate * denom_inv * denom_inv * beta * (1.0 - beta)
    low = grad_dt.astype(bf16)
    gdt_ref[0] = low
    gdt_bias_ref[...] += jnp.sum(grad_dt, axis=0, keepdims=True)
    gskip_ref[...] += jnp.sum(dy_ref[0] * conv_ref[0].astype(f32), axis=0, keepdims=True)
    gdt_proj_ref[...] += rows_dot(proj_ref[0:rank, :].astype(bf16), low)
    gproj_ref[0:rank, :] = outer_dot(dt_proj_ref[...], low)
    gproj_ref[rank : rank + n, :] = sums[0] - 2.0 * keys * (sums[1] + self_term)
    gproj_ref[rank + n :, :] = sums[2]


def specs_for(length, reverse):
    blocks = length // BLOCK

    def place(b):
        return blocks - 1 - b if reverse else b

    def spec(*shape):
        return pl.BlockSpec((1,) + shape, lambda s, b: (s, place(b)) + (0,) * (len(shape) - 1))

    def across_spec(rows):
        return pl.BlockSpec((rows, BLOCK), lambda s, b: (0, s * blocks + place(b)))

    def whole(*shape):
        return pl.BlockSpec(shape, lambda s, b: (0,) * len(shape))

    return blocks, spec, across_spec, whole


def recurrence_forward(conv, z, proj, keep_lanes, dt_proj, dt_bias, skip):
    seqs, length, width = conv.shape
    rank = dt_proj.shape[0]
    n = (proj.shape[0] - rank) // 2
    blocks, spec, across_spec, whole = specs_for(length, False)
    wide = spec(BLOCK, width)
    full = jax.ShapeDtypeStruct((seqs, length, width), f32)
    return pl.pallas_call(
        forward_kernel,
        grid=(seqs, blocks),
        in_specs=[
            wide, wide, across_spec(proj.shape[0]), spec(BLOCK, LANES), whole(rank, width), whole(1, width),
            whole(1, width),
        ],
        out_specs=[wide, wide, wide, wide, spec(BLOCK * n, width)],
        out_shape=[
            full, jax.ShapeDtypeStruct((seqs, length, width), bf16), full, full,
            jax.ShapeDtypeStruct((seqs, length * n, width), bf16),
        ],
        scratch_shapes=[
            pltpu.VMEM((n, width), f32),
            pltpu.VMEM((CHUNK, width), f32),
            pltpu.VMEM((CHUNK, width), f32),
            pltpu.VMEM((CHUNK, LANES), f32),
            pltpu.VMEM((BLOCK, n), f32),
        ],
        compiler_params=pltpu.CompilerParams(vmem_limit_bytes=24 << 20),
        cost_estimate=pl.CostEstimate(flops=16_000_000_000, bytes_accessed=24 << 20, transcendentals=0),
        name="recurrence_forward",
    )(conv, z, proj, keep_lanes, dt_proj, dt_bias, skip)


def recurrence_backward(rate, beta, conv, dy, proj, keep_lanes, dt_proj, states):
    seqs, length, width = rate.shape
    rank = dt_proj.shape[0]
    n = (proj.shape[0] - rank) // 2
    span = CHUNK * n
    blocks, spec, across_spec, whole = specs_for(length, True)
    wide = spec(BLOCK, width)
    before = pl.BlockSpec((1, n, width), lambda s, b: (s, jnp.maximum((blocks - 1 - b) * BLOCK - 1, 0), 0))
    return pl.pallas_call(
        backward_kernel,
        grid=(seqs, blocks),
        in_specs=[
            wide, wide, wide, wide, across_spec(proj.shape[0]), spec(BLOCK, LANES), whole(rank, width),
            spec(BLOCK * n, width), before,
        ],
        out_specs=[wide, wide, across_spec(proj.shape[0]), whole(rank, width), whole(1, width), whole(1, width)],
        out_shape=[
            jax.ShapeDtypeStruct((seqs, length, width), f32),
            jax.ShapeDtypeStruct((seqs, length, width), bf16),
            jax.ShapeDtypeStruct(proj.shape, f32),
            jax.ShapeDtypeStruct((rank, width), f32),
            jax.ShapeDtypeStruct((1, width), f32),
            jax.ShapeDtypeStruct((1, width), f32),
        ],
        scratch_shapes=[
            pltpu.VMEM((n, width), f32),
            pltpu.VMEM((BLOCK, width), f32),
            pltpu.VMEM((CHUNK, width), f32),
            pltpu.VMEM((CHUNK, width), f32),
            pltpu.VMEM((CHUNK, width), f32),
            pltpu.VMEM((CHUNK, LANES), f32),
            pltpu.VMEM((BLOCK, n), f32),
            [pltpu.VMEM((span // PIECES, width), f32)] * PIECES,
            [pltpu.VMEM((span // PIECES, width), f32)] * PIECES,
            pltpu.VMEM((3, n, BLOCK), f32),
        ],
        compiler_params=pltpu.CompilerParams(vmem_limit_bytes=28 << 20),
        cost_estimate=pl.CostEstimate(flops=30_000_000_000, bytes_accessed=28 << 20, transcendentals=0),
        name="recurrence_backward",
    )(rate, beta, conv, dy, proj, keep_lanes, dt_proj, states, states)


def peer(hop):
    me = lax.axis_index("shard")
    core = lax.rem(me, 2)
    chip = me // 2
    if hop & 1:
        core = 1 - core
    if hop & 2:
        chip = 1 - chip
    return chip * 2 + core


def meet_group():
    barrier = pltpu.get_barrier_semaphore()
    for hop in (1, 2, 3):
        pl.semaphore_signal(barrier, inc=1, device_id={"shard": peer(hop)}, device_id_type=MESH)
    pl.semaphore_wait(barrier, 3)


def remote(src, dst, sends, recvs, at, hop):
    return pltpu.make_async_remote_copy(
        src_ref=src, dst_ref=dst, send_sem=sends.at[at], recv_sem=recvs.at[at],
        device_id={"shard": peer(hop)}, device_id_type=MESH,
    )


def group_params(collective_id, limit):
    return pltpu.CompilerParams(collective_id=collective_id, has_side_effects=True, vmem_limit_bytes=limit)


VMEM_SPEC = pl.BlockSpec(memory_space=pltpu.VMEM)


ANY_SPEC = pl.BlockSpec(memory_space=pl.ANY)


def part_copy(src, dst, send, recv, shard):
    return pltpu.make_async_remote_copy(
        src_ref=src, dst_ref=dst, send_sem=send, recv_sem=recv, device_id={"shard": shard}, device_id_type=MESH
    )


def front_kernel(
    x_ref, cot_ref, gain_ref, w_hbm, o_hbm,
    xs_ref, cots_ref, gains_ref, normed_ref, pair_ref, parts_ref, own_ref, send_ref,
    w_ref, o_ref, lhs, mixed, pairs, near, sends, recvs, local, part_sends, part_recvs, part_local,
    pair_sends, pair_recvs, pair_local,
):
    me = lax.axis_index("shard")
    chip = me // 2
    slot = me // 2
    seqs, rows, model = x_ref.shape
    cols = cots_ref.shape[2]
    side = lax.rem(lax.axis_index("replica"), 2)
    height = lax.axis_size("replica") // 2
    block = model // 2 // height
    aligned = block % LANES == 0
    width = parts_ref.shape[3]
    lift = gain_ref.shape[0]
    span = 2 * rows
    tile = 256
    loads = [
        pltpu.make_async_copy(w_hbm, w_ref, local.at[3]),
        pltpu.make_async_copy(o_hbm, o_ref, local.at[4]),
    ]
    for copy in loads:
        copy.start()
    other = meet_group_and_pair()

    def mine(ref, owner):
        return ref.at[:, pl.ds(pl.multiple_of(owner * rows, 16), rows), :]

    def part(owner):
        return cot_ref.at[:, :, pl.ds(pl.multiple_of(owner * cols, 128), cols)]

    def gain_rows(owner):
        return gains_ref.at[pl.ds(pl.multiple_of(owner * lift, 8), lift), :]

    gain_sends = [remote(gain_ref, gain_rows(me), sends, recvs, 5 + hop, hop) for hop in (1, 2, 3)]
    x_core = remote(x_ref, mine(xs_ref, me), sends, recvs, 0, 1)
    x_chip = remote(x_ref, mine(xs_ref, me), sends, recvs, 1, 2)
    cot_sends = [remote(part(peer(hop)), mine(cots_ref, me), sends, recvs, 2 + hop, hop) for hop in (1, 2, 3)]
    for copy in gain_sends + [x_core, x_chip] + cot_sends:
        copy.start()
    own = [
        pltpu.make_async_copy(x_ref, mine(xs_ref, me), local.at[0]),
        pltpu.make_async_copy(part(me), mine(cots_ref, me), local.at[1]),
        pltpu.make_async_copy(gain_ref, gain_rows(me), local.at[2]),
    ]
    for copy in own:
        copy.start()
    for copy in own:
        copy.wait()
    for copy in gain_sends:
        copy.wait()
    x_core.wait()
    gain = jnp.concatenate([gains_ref[lift * d : lift * d + 1, :] for d in range(4)], axis=1)
    loads[0].wait()

    def piece(half, i):
        where = jnp.bitwise_xor(chip, half)
        return parts_ref.at[slot, :, pl.ds(pl.multiple_of(where * span, 16), span), :]

    def away(i):
        return lax.rem(2 * me + i, 4) != me

    def send(half, i):
        return part_copy(
            mixed.at[half, i], piece(half, i), part_sends.at[2 * half + i], part_recvs.at[2 * slot + half],
            lax.rem(2 * me + i, 4),
        )

    def keep(half, i):
        return pltpu.make_async_copy(mixed.at[half, i], piece(half, i), part_local.at[half])

    def either(i, yes, no):
        pl.when(away(i))(yes)
        pl.when(jnp.logical_not(away(i)))(no)

    def run_half(half):
        where = jnp.bitwise_xor(chip, half) * span

        for seq in range(seqs):

            def norm(r, carry, seq=seq):
                at = pl.ds(pl.multiple_of(where + r * 16, 16), 16)
                vals = xs_ref[seq, at, :].astype(f32)
                inv = lax.rsqrt(jnp.mean(vals * vals, axis=1, keepdims=True) + EPS)
                out = (vals * inv * gain).astype(bf16)
                normed_ref[seq, at, :] = out
                lhs[pl.ds(pl.multiple_of(seq * span + r * 16, 16), 16), :] = out
                return carry

            lax.fori_loop(0, span // 16, norm, 0)
        for copy in normed_copies(half):
            copy.start()
        for i in range(2):

            def product(t, carry, i=i):
                value = rows_dot(lhs[...], w_ref[:, pl.ds(pl.multiple_of(i * width + t * tile, tile), tile)])
                for seq in range(seqs):
                    mixed[half, i, seq, :, pl.ds(pl.multiple_of(t * tile, tile), tile)] = value[
                        seq * span : (seq + 1) * span
                    ].astype(bf16)
                return carry

            lax.fori_loop(0, width // tile, product, 0)
            either(i, lambda i=i: send(half, i).start(), lambda i=i: keep(half, i).start())

    def normed_copies(half):
        where = pl.ds(pl.multiple_of(jnp.bitwise_xor(chip, half) * span, 16), span)
        copies = []
        for b in range(height if aligned else 0):
            def cut(which, b=b):
                return normed_ref.at[:, where, pl.ds(pl.multiple_of((2 * b + which) * block, LANES), block)]

            goal = (slice(None), where, slice(b * block, (b + 1) * block))
            at = half * height + b
            copies.append(pltpu.make_async_copy(cut(side), pair_ref.at[(0,) + goal], pair_local.at[at]))
            copies.append(across(cut(1 - side), pair_ref.at[(1,) + goal], pair_sends, pair_recvs, at, other))
        return copies

    run_half(0)
    x_chip.wait_recv()
    onward = remote(mine(xs_ref, peer(2)), mine(xs_ref, peer(2)), sends, recvs, 2, 1)
    onward.start()
    onward.wait()
    run_half(1)

    for copy in cot_sends:
        copy.wait()
    loads[1].wait()

    def partial(block, t):
        return outer_dot(
            cots_ref[...].reshape(seqs * 4 * rows, cols),
            o_ref[pl.ds(pl.multiple_of(block * width + t * tile, tile), tile), :],
        )

    def lanes(t):
        return pl.ds(pl.multiple_of(t * tile, tile), tile)

    near_sends = []
    for at, hop in enumerate((3, 1)):

        def fill(t, carry, at=at, hop=hop):
            pairs[at, :, lanes(t)] = partial(peer(hop), t).astype(bf16)
            return carry

        lax.fori_loop(0, width // tile, fill, 0)
        copy = remote(pairs.at[at], near.at[at], sends, recvs, 9 + at, 1)
        copy.start()
        near_sends.append(copy)
    near_sends[0].wait()

    def to_send(t, carry):
        send_ref[:, lanes(t)] = (partial(peer(2), t) + near[0, :, lanes(t)].astype(f32)).astype(bf16)
        return carry

    lax.fori_loop(0, width // tile, to_send, 0)
    near_sends[1].wait()

    def to_own(t, carry):
        own_ref[:, lanes(t)] = partial(me, t) + near[1, :, lanes(t)].astype(f32)
        return carry

    lax.fori_loop(0, width // tile, to_own, 0)

    x_chip.wait_send()
    for copy in normed_copies(0) + normed_copies(1):
        copy.wait()
    for half in range(2):
        for i in range(2):
            either(i, lambda half=half, i=i: send(half, i).wait_send(), lambda half=half, i=i: keep(half, i).wait())
        for at in range(2):

            @pl.when(2 * at + me // 2 != me)
            def _(at=at, half=half):
                part_copy(
                    mixed.at[0, 0], mixed.at[0, 0], part_sends.at[0], part_recvs.at[2 * at + half], peer(1)
                ).wait_recv()


def front(x, cot, gain, w_in, out_proj):
    seqs, rows, model = x.shape
    group = lax.axis_size("shard")
    length = rows * group
    cols = model // group
    width = w_in.shape[1] // 2
    tokens = seqs * length
    lifted = jnp.broadcast_to(gain.astype(f32)[None], (8, gain.shape[0]))
    far_sems = pltpu.SemaphoreType.DMA((lax.axis_size("replica"),))
    return pl.pallas_call(
        front_kernel,
        in_specs=[VMEM_SPEC] * 3 + [ANY_SPEC] * 2,
        out_specs=[VMEM_SPEC] * 8,
        out_shape=[
            jax.ShapeDtypeStruct((seqs, length, model), bf16),
            jax.ShapeDtypeStruct((seqs, length, cols), bf16),
            jax.ShapeDtypeStruct((8 * group, gain.shape[0]), f32),
            jax.ShapeDtypeStruct((seqs, length, model), bf16),
            jax.ShapeDtypeStruct((2, seqs, length, model // 2), bf16),
            jax.ShapeDtypeStruct((2, seqs, length, width), bf16),
            jax.ShapeDtypeStruct((tokens, width), f32),
            jax.ShapeDtypeStruct((tokens, width), bf16),
        ],
        scratch_shapes=[
            pltpu.VMEM(w_in.shape, bf16),
            pltpu.VMEM(out_proj.shape, bf16),
            pltpu.VMEM((tokens // 2, model), bf16),
            pltpu.VMEM((2, 2, seqs, 2 * rows, width), bf16),
            pltpu.VMEM((2, tokens, width), bf16),
            pltpu.VMEM((2, tokens, width), bf16),
            pltpu.SemaphoreType.DMA((11,)), pltpu.SemaphoreType.DMA((11,)), pltpu.SemaphoreType.DMA((5,)),
            pltpu.SemaphoreType.DMA((4,)), pltpu.SemaphoreType.DMA((4,)), pltpu.SemaphoreType.DMA((2,)),
            far_sems, far_sems, far_sems,
        ],
        compiler_params=group_params(1, 48 << 20),
        name="front",
    )(x, cot, lifted, w_in, out_proj)


def pair_signal(barrier):
    home = lax.axis_index("replica")
    other = home + 1 - 2 * lax.rem(home, 2)
    pl.semaphore_signal(barrier, inc=1, device_id={"replica": other}, device_id_type=MESH)
    return other


def across(src, dst, sends, recvs, at, other):
    return pltpu.make_async_remote_copy(
        src_ref=src, dst_ref=dst, send_sem=sends.at[at], recv_sem=recvs.at[at],
        device_id={"replica": other}, device_id_type=MESH,
    )


def meet_group_and_pair():
    barrier = pltpu.get_barrier_semaphore()
    for hop in (1, 2, 3):
        pl.semaphore_signal(barrier, inc=1, device_id={"shard": peer(hop)}, device_id_type=MESH)
    other = pair_signal(barrier)
    pl.semaphore_wait(barrier, 4)
    return other


def collect_kernel(keep_ref, give_ref, gz_ref, keeps_ref, gives_ref, gz_both_ref, sends, recvs, local):
    me = lax.axis_index("shard")
    half = keep_ref.shape[1]
    other = meet_group_and_pair()

    def spot(ref, owner):
        return ref.at[:, pl.ds(pl.multiple_of(owner * half, 128), half)]

    k_chip = remote(keep_ref, spot(keeps_ref, me), sends, recvs, 0, 2)
    v_chip = remote(give_ref, spot(gives_ref, me), sends, recvs, 1, 2)
    k_core = remote(keep_ref, spot(keeps_ref, me), sends, recvs, 2, 1)
    v_core = remote(give_ref, spot(gives_ref, me), sends, recvs, 3, 1)
    gz_pair = across(gz_ref, gz_both_ref.at[1], sends, recvs, 4, other)
    own = [
        pltpu.make_async_copy(keep_ref, spot(keeps_ref, me), local.at[0]),
        pltpu.make_async_copy(give_ref, spot(gives_ref, me), local.at[1]),
        pltpu.make_async_copy(gz_ref, gz_both_ref.at[0], local.at[2]),
    ]
    for copy in [k_chip, v_chip, gz_pair, k_core, v_core] + own:
        copy.start()
    k_chip.wait_recv()
    k_on = remote(spot(keeps_ref, peer(2)), spot(keeps_ref, peer(2)), sends, recvs, 5, 1)
    k_on.start()
    v_chip.wait_recv()
    v_on = remote(spot(gives_ref, peer(2)), spot(gives_ref, peer(2)), sends, recvs, 6, 1)
    v_on.start()
    for copy in own + [k_core, v_core, gz_pair, k_on, v_on]:
        copy.wait()
    k_chip.wait_send()
    v_chip.wait_send()


def cost(microseconds):
    return pl.CostEstimate(flops=int(microseconds * 1e9), bytes_accessed=1 << 20, transcendentals=0)


def collect(keep, give, grad_z):
    tokens, half = keep.shape
    group = lax.axis_size("shard")
    wide = jax.ShapeDtypeStruct((tokens, half * group), bf16)
    return pl.pallas_call(
        collect_kernel,
        in_specs=[VMEM_SPEC] * 3,
        out_specs=[VMEM_SPEC] * 3,
        out_shape=[wide, wide, jax.ShapeDtypeStruct((2,) + grad_z.shape, bf16)],
        scratch_shapes=[
            pltpu.SemaphoreType.DMA((7,)), pltpu.SemaphoreType.DMA((7,)), pltpu.SemaphoreType.DMA((3,)),
        ],
        compiler_params=group_params(6, 16 << 20),
        cost_estimate=cost(25),
        name="collect",
    )(keep, give, grad_z)


def middle_kernel(
    keeps_ref, gives_ref, give_ref, cot_ref, x_hbm, o_hbm,
    both_ref, cots_ref, out_ref,
    o_ref, xcol, outs, sends, recvs, local, o_local,
):
    me = lax.axis_index("shard")
    side = lax.rem(lax.axis_index("replica"), 2)
    tokens, half = give_ref.shape
    gots_ref = both_ref.at[1]
    seqs, rows, _ = out_ref.shape
    cols = xcol.shape[1]
    piece = o_hbm.shape[0] // lax.axis_size("replica")
    per = half // piece
    loads = []
    for d in range(4):
        for q in range(2):
            for j in range(per):
                at = d * 2 * half + (2 * j) * piece + (side if q == 0 else 1 - side) * piece
                loads.append(
                    pltpu.make_async_copy(
                        o_hbm.at[pl.ds(pl.multiple_of(at, piece), piece), :],
                        o_ref.at[q, pl.ds(d * half + j * piece, piece), :],
                        o_local.at[len(loads)],
                    )
                )
    for copy in loads:
        copy.start()
    fetch = pltpu.make_async_copy(
        x_hbm.at[:, pl.ds(pl.multiple_of(me * cols, 128), cols)], xcol, local.at[0]
    )
    fetch.start()
    other = meet_group_and_pair()

    def spot(owner):
        return gots_ref.at[:, pl.ds(pl.multiple_of(owner * half, 128), half)]

    give_pair = across(give_ref, spot(me), sends, recvs, 0, other)
    cot_pair = across(cot_ref, cots_ref.at[1], sends, recvs, 1, other)
    own = [
        pltpu.make_async_copy(keeps_ref, both_ref.at[0], local.at[1]),
        pltpu.make_async_copy(cot_ref, cots_ref.at[0], local.at[2]),
    ]
    for copy in [give_pair, cot_pair] + own:
        copy.start()
    for copy in loads + [fetch]:
        copy.wait()
    tile = 256

    def product(t, carry):
        rows_at = pl.ds(pl.multiple_of(t * tile, tile), tile)
        value = (
            xcol[rows_at, :].astype(f32)
            + rows_dot(keeps_ref[rows_at, :], o_ref[0])
            + rows_dot(gives_ref[rows_at, :], o_ref[1])
        )
        outs[rows_at, :] = value.astype(bf16)
        return carry

    lax.fori_loop(0, tokens // tile, product, 0)
    length = tokens // seqs
    out_sends = []
    for seq in range(seqs):
        for n_hop, hop in enumerate((2, 3, 1)):
            src = outs.at[pl.ds(pl.multiple_of(seq * length + peer(hop) * rows, 16), rows), :]
            dst = out_ref.at[seq, :, pl.ds(pl.multiple_of(me * cols, 128), cols)]
            out_sends.append(remote(src, dst, sends, recvs, 2 + seq * 3 + n_hop, hop))
        own.append(
            pltpu.make_async_copy(
                outs.at[pl.ds(pl.multiple_of(seq * length + me * rows, 16), rows), :],
                out_ref.at[seq, :, pl.ds(pl.multiple_of(me * cols, 128), cols)],
                local.at[3 + seq],
            )
        )
        own[-1].start()
    for copy in out_sends:
        copy.start()
    base = 2 + seqs * 3
    give_pair.wait_recv()
    g_chip = remote(spot(me), spot(me), sends, recvs, base, 2)
    g_core = remote(spot(me), spot(me), sends, recvs, base + 1, 1)
    g_chip.start()
    g_core.start()
    g_chip.wait_recv()
    g_on = remote(spot(peer(2)), spot(peer(2)), sends, recvs, base + 2, 1)
    g_on.start()
    for copy in out_sends + [g_on, g_core, cot_pair] + own:
        copy.wait()
    g_chip.wait_send()
    give_pair.wait_send()


def middle(keeps, gives, give, cot, x_all, out_proj, seqs):
    tokens, half = give.shape
    group = lax.axis_size("shard")
    model = x_all.shape[1]
    cols = model // group
    pieces = 8 * max(1, half * lax.axis_size("replica") // out_proj.shape[0])
    return pl.pallas_call(
        middle_kernel,
        in_specs=[VMEM_SPEC] * 4 + [ANY_SPEC] * 2,
        out_specs=[VMEM_SPEC] * 3,
        out_shape=[
            jax.ShapeDtypeStruct((2, tokens, half * group), bf16),
            jax.ShapeDtypeStruct((2, tokens, cols), bf16),
            jax.ShapeDtypeStruct((seqs, tokens // seqs // group, model), bf16),
        ],
        scratch_shapes=[
            pltpu.VMEM((2, half * group, cols), bf16),
            pltpu.VMEM((tokens, cols), bf16),
            pltpu.VMEM((tokens, cols), bf16),
            pltpu.SemaphoreType.DMA((5 + 3 * seqs,)), pltpu.SemaphoreType.DMA((5 + 3 * seqs,)),
            pltpu.SemaphoreType.DMA((3 + seqs,)), pltpu.SemaphoreType.DMA((pieces,)),
        ],
        compiler_params=group_params(7, 20 << 20),
        cost_estimate=cost(25),
        name="middle",
    )(keeps, gives, give, cot, x_all, out_proj)


PARTS = 4


def finish_kernel(
    gx_ref, gz_ref, small_keep_ref, small_give_ref, wz_ref, norm_ref, w_hbm, x_ref, cot_ref, gain_ref,
    gw_ref, small_ref, dx_ref, ggain_ref,
    w_ref, got, cols_ref, turned, xb_ref, sb_ref, small_got, x_in, s_in, lhs, pairs, near, g_own, g_send, g_far,
    h_send, h_cols, s_own, gains, gain_near, gain_sum, gain_pair, gain_two, gain_in,
    sends, recvs, far_sends, far_recvs, home_sends, home_recvs, local,
):
    me = lax.axis_index("shard")
    home = lax.axis_index("replica")
    count = lax.axis_size("replica")
    height = count // 2
    mine = home // 2
    side = lax.rem(home, 2)
    seqs, rows, model = x_ref.shape
    tokens, width = gx_ref.shape
    length = tokens // seqs
    deep = wz_ref.shape[0]
    part = width // PARTS
    tile = 256
    span = seqs * rows
    load = pltpu.make_async_copy(w_hbm, w_ref, local.at[0])
    load.start()
    barrier = pltpu.get_barrier_semaphore()
    for hop in (1, 2, 3):
        pl.semaphore_signal(barrier, inc=1, device_id={"shard": peer(hop)}, device_id_type=MESH)
    other = pair_signal(barrier)

    def far(step):
        return lax.rem(home + 2 * step, count)

    for step in range(1, height):
        pl.semaphore_signal(barrier, inc=1, device_id={"replica": far(step)}, device_id_type=MESH)
    pl.semaphore_wait(barrier, 3 + height)

    def cut(p):
        return slice(p * part, (p + 1) * part)

    y_sends = [across(gx_ref.at[:, cut(p)], got.at[:, cut(p)], sends, recvs, p, other) for p in range(PARTS)]
    small_send = across(small_give_ref, small_got, sends, recvs, PARTS, other)
    y_sends[0].start()
    small_send.start()
    for copy in y_sends[1:]:
        copy.start()

    def goal(slot):
        return (4 * slot + me) // 2

    spot = pl.ds(pl.multiple_of(lax.rem(me, 2) * width, LANES), width)

    def home_pieces(at):
        if at == PARTS:
            return 1, wz_ref, h_cols.at[:, spot]
        if at == PARTS + 1:
            return 0, gx_ref, cols_ref.at[:, spot]
        if at == PARTS + 2:
            return 1, gz_ref, cols_ref.at[:, spot]
        place = pl.ds(pl.multiple_of(lax.rem(me, 2) * width + at * part, LANES), part)
        return 0, h_send.at[:, cut(at)], h_cols.at[:, place]

    def home_send(at):
        slot, src, dst = home_pieces(at)
        return part_copy(src, dst, home_sends.at[at], home_recvs.at[at * 2 + lax.rem(me, 2)], goal(slot))

    def home_keep(at):
        _, src, dst = home_pieces(at)
        return pltpu.make_async_copy(src, dst, local.at[1 + at])

    def home_start(at):
        slot = home_pieces(at)[0]
        pl.when(goal(slot) != me)(lambda: home_send(at).start())
        pl.when(goal(slot) == me)(lambda: home_keep(at).start())

    def home_wait(at):
        slot = home_pieces(at)[0]
        pl.when(goal(slot) != me)(lambda: home_send(at).wait_send())
        pl.when(goal(slot) == me)(lambda: home_keep(at).wait())
        for place in range(2):
            source = lax.rem(2 * me + place, 4)

            @pl.when((me // 2 == slot) & (source != me))
            def _(place=place):
                src = home_pieces(at)[1]
                part_copy(src, src, home_sends.at[at], home_recvs.at[at * 2 + place], peer(1)).wait_recv()

    for at in (PARTS + 1, PARTS + 2, PARTS):
        home_start(at)

    for i in range(2 * tokens // tile):
        for j in range(norm_ref.shape[1] // tile):
            turned[j * tile : (j + 1) * tile, i * tile : (i + 1) * tile] = norm_ref[
                i * tile : (i + 1) * tile, j * tile : (j + 1) * tile
            ].T

    def far_copy(src, dst, kind, step):
        return across(src, dst, far_sends, far_recvs, kind * height + step, far(step))

    def block(step):
        return lax.rem(mine + step, height)

    order = range(1, height)

    def lines(at):
        return pl.ds(pl.multiple_of(at * deep, 16), deep)

    def x_sends(p):
        return [
            far_copy(xb_ref.at[lines(block(step)), cut(p)], x_in.at[step - 1, :, cut(p)], p, step) for step in order
        ]

    def x_part(p):
        y_sends[p].wait_recv()

        def rows_of(t, carry):
            at = pl.ds(pl.multiple_of(t * tile, tile), tile)
            value = rows_dot(turned[at, :tokens], gx_ref[:, cut(p)]) + rows_dot(turned[at, tokens:], got[:, cut(p)])
            xb_ref[at, cut(p)] = value.astype(bf16)
            return carry

        lax.fori_loop(0, xb_ref.shape[0] // tile, rows_of, 0)
        for copy in x_sends(p):
            copy.start()

    x_part(0)
    small_send.wait_recv()
    for at in range(height):
        sb_ref[at] = (small_keep_ref[at] + small_got[at].astype(f32)).astype(bf16)
    s_sends = [far_copy(sb_ref.at[block(step)], s_in.at[step - 1], PARTS, step) for step in order]
    for copy in s_sends:
        copy.start()
    x_part(1)

    def stage(owners):
        for i, owner in enumerate(owners):
            for seq in range(seqs):
                at = pl.ds(pl.multiple_of(seq * length + owner * rows, 16), rows)
                lhs[i * span + seq * rows : i * span + (seq + 1) * rows, :] = cols_ref[at, :]

    def lanes(t):
        return pl.ds(pl.multiple_of(t * tile, tile), tile)

    def product(t):
        return outer_dot(lhs[...], w_ref[lanes(t), :])

    home_wait(PARTS + 1)
    home_wait(PARTS + 2)
    stage((peer(3), peer(1)))
    load.wait()

    def first(t, carry):
        value = product(t)
        pairs[0, :, lanes(t)] = value[:span].astype(bf16)
        pairs[1, :, lanes(t)] = value[span:].astype(bf16)
        return carry

    lax.fori_loop(0, model // tile, first, 0)
    near_send = remote(pairs, near, sends, recvs, PARTS + 1, 1)
    near_send.start()
    x_part(2)

    for copy in s_sends:
        copy.wait_recv()
    total = sb_ref[mine].astype(f32)
    for step in order:
        total = total + s_in[step - 1].astype(f32)
    s_own[...] = total.astype(bf16)
    small_ref[side, mine] = s_own[...]
    spread = [far_copy(s_own, small_ref.at[side, mine], PARTS + 1, step) for step in order]
    for copy in spread:
        copy.start()
    x_part(3)

    stage((peer(2), me))
    near_send.wait()

    def second(t, carry):
        value = product(t)
        g_send[:, lanes(t)] = (value[:span] + near[0, :, lanes(t)].astype(f32)).astype(bf16)
        g_own[:, lanes(t)] = value[span:] + near[1, :, lanes(t)].astype(f32)
        return carry

    lax.fori_loop(0, model // tile, second, 0)
    chip_send = remote(g_send, g_far, sends, recvs, PARTS + 2, 2)
    chip_send.start()

    def home_sum(p):
        for copy in x_sends(p):
            copy.wait_recv()
        total = xb_ref[lines(mine), cut(p)].astype(f32)
        for step in order:
            total = total + x_in[step - 1, :, cut(p)].astype(f32)
        h_send[:, cut(p)] = total.astype(bf16)
        home_start(p)

    home_sum(0)
    chip_send.wait()

    gains[...] = jnp.zeros_like(gains)
    for seq in range(seqs):

        def last(r, carry, seq=seq):
            at = pl.ds(pl.multiple_of(r * 16, 16), 16)
            flat = pl.ds(pl.multiple_of(seq * rows + r * 16, 16), 16)
            grad = g_own[flat, :] + g_far[flat, :].astype(f32)
            vals = x_ref[seq, at, :].astype(f32)
            inv = lax.rsqrt(jnp.mean(vals * vals, axis=1, keepdims=True) + EPS)
            scaled = grad * gain_ref[...]
            mean = jnp.mean(scaled * vals, axis=1, keepdims=True)
            out = inv * (scaled - vals * (inv * inv * mean))
            dx_ref[seq, at, :] = (cot_ref[seq, at, :].astype(f32) + out).astype(bf16)
            terms = grad * (vals * inv)
            gains[...] += terms[:8] + terms[8:]
            return carry

        lax.fori_loop(0, rows // 16, last, 0)
    gains[...] = jnp.broadcast_to(jnp.sum(gains[...], axis=0, keepdims=True), gains.shape)
    wide = model // 4

    def gain_part(owner):
        return gains.at[:, pl.ds(pl.multiple_of(owner * wide, LANES), wide)]

    gain_sends = [
        remote(gain_part(peer(hop)), gain_near.at[hop - 1], sends, recvs, PARTS + 2 + hop, hop) for hop in (1, 2, 3)
    ]
    for copy in gain_sends:
        copy.start()
    for copy in gain_sends:
        copy.wait()
    gain_sum[...] = gains[:, pl.ds(pl.multiple_of(me * wide, LANES), wide)] + gain_near[0] + gain_near[1] + gain_near[2]
    gain_copy = across(gain_sum, gain_pair, sends, recvs, PARTS + 6, other)
    gain_copy.start()
    home_sum(1)
    gain_copy.wait()
    gain_two[...] = gain_sum[...] + gain_pair[...]
    gain_far = [far_copy(gain_two, gain_in.at[step - 1], PARTS + 2, step) for step in order]
    for copy in gain_far:
        copy.start()
    home_sum(2)
    for copy in spread:
        copy.wait_recv()
    small_pair = across(small_ref.at[side], small_ref.at[side], sends, recvs, PARTS + 7, other)
    small_pair.start()
    home_sum(3)
    for copy in gain_far:
        copy.wait()
    total = gain_two[...]
    for step in order:
        total = total + gain_in[step - 1]
    ggain_ref[...] = total

    for at in (PARTS, 0, 1, 2, 3):
        home_wait(at)
    for r in range(0, deep, 32):
        gw_ref[r : r + 32, :] = h_cols[r : r + 32, :].astype(f32)
    small_pair.wait()
    small_send.wait_send()
    for p in range(PARTS):
        y_sends[p].wait_send()
        for copy in x_sends(p):
            copy.wait_send()
    for copy in s_sends + spread:
        copy.wait_send()


def finish(gx, gz, small_keep, small_give, wz, norm, w_in, x, cot, gain):
    tokens, width = gx.shape
    height, lines, _ = small_keep.shape
    deep = wz.shape[0]
    seqs, rows, model = x.shape
    span = seqs * rows
    wide = model // 4
    gain_tile = pltpu.VMEM((8, wide), f32)
    other = max(height - 1, 1)
    kinds = (PARTS + 3) * height
    return pl.pallas_call(
        finish_kernel,
        in_specs=[VMEM_SPEC] * 6 + [ANY_SPEC] + [VMEM_SPEC] * 3,
        out_specs=[VMEM_SPEC] * 4,
        out_shape=[
            jax.ShapeDtypeStruct((deep, 2 * width), f32),
            jax.ShapeDtypeStruct((2, height, lines, width), bf16),
            jax.ShapeDtypeStruct(x.shape, bf16),
            jax.ShapeDtypeStruct((8, wide), f32),
        ],
        scratch_shapes=[
            pltpu.VMEM(w_in.shape, bf16),
            pltpu.VMEM((tokens, width), bf16),
            pltpu.VMEM((tokens, 2 * width), bf16),
            pltpu.VMEM((height * deep, 2 * tokens), bf16),
            pltpu.VMEM((height * deep, width), bf16),
            pltpu.VMEM((height, lines, width), bf16),
            pltpu.VMEM((height, lines, width), bf16),
            pltpu.VMEM((other, deep, width), bf16),
            pltpu.VMEM((other, lines, width), bf16),
            pltpu.VMEM((2 * span, 2 * width), bf16),
            pltpu.VMEM((2, span, model), bf16),
            pltpu.VMEM((2, span, model), bf16),
            pltpu.VMEM((span, model), f32),
            pltpu.VMEM((span, model), bf16),
            pltpu.VMEM((span, model), bf16),
            pltpu.VMEM((deep, width), bf16),
            pltpu.VMEM((deep, 2 * width), bf16),
            pltpu.VMEM((lines, width), bf16),
            pltpu.VMEM((8, model), f32),
            pltpu.VMEM((3, 8, wide), f32),
            gain_tile, gain_tile, gain_tile,
            pltpu.VMEM((other, 8, wide), f32),
            pltpu.SemaphoreType.DMA((PARTS + 8,)), pltpu.SemaphoreType.DMA((PARTS + 8,)),
            pltpu.SemaphoreType.DMA((kinds,)), pltpu.SemaphoreType.DMA((kinds,)),
            pltpu.SemaphoreType.DMA((PARTS + 3,)), pltpu.SemaphoreType.DMA((2 * PARTS + 6,)),
            pltpu.SemaphoreType.DMA((PARTS + 4,)),
        ],
        compiler_params=group_params(8, 56 << 20),
        cost_estimate=cost(80),
        name="finish",
    )(gx, gz, small_keep, small_give, wz, norm, w_in, x, cot, gain)


def total_kernel(part_ref, out_ref, near, chip_sum, far, sends, recvs):
    me = lax.axis_index("shard")
    half = part_ref.shape[1] // 2
    mine = pl.ds(pl.multiple_of(lax.rem(me, 2) * half, 128), half)
    other = pl.ds(pl.multiple_of((1 - lax.rem(me, 2)) * half, 128), half)
    meet_group()
    first = remote(part_ref.at[:, other], near, sends, recvs, 0, 1)
    first.start()
    first.wait()
    chip_sum[...] = part_ref[:, mine] + near[...]
    second = remote(chip_sum, far, sends, recvs, 1, 2)
    second.start()
    second.wait()
    out_ref[:, mine] = chip_sum[...] + far[...]
    third = remote(out_ref.at[:, mine], out_ref.at[:, mine], sends, recvs, 2, 1)
    third.start()
    third.wait()


def group_total(part, collective_id):
    rows, cols = part.shape
    half = pltpu.VMEM((rows, cols // 2), f32)
    return pl.pallas_call(
        total_kernel,
        in_specs=[VMEM_SPEC],
        out_specs=VMEM_SPEC,
        out_shape=jax.ShapeDtypeStruct((rows, cols), f32),
        scratch_shapes=[half, half, half, pltpu.SemaphoreType.DMA((3,)), pltpu.SemaphoreType.DMA((3,))],
        compiler_params=group_params(collective_id, 16 << 20),
        name="group_total",
    )(part)


def by_hop(value, hop):
    return lax.ppermute(value, "shard", [(i, i ^ hop) for i in range(4)])


def pair(value):
    return lax.ppermute(value, "replica", [(i, i ^ 1) for i in range(lax.axis_size("replica"))])


def far_send(blocks):
    count = lax.axis_size("replica")
    height = count // 2
    mine = lax.axis_index("replica") // 2

    def pick(at):
        return lax.dynamic_index_in_dim(blocks, at, 0, False)

    sent = []
    for step in range(1, height):
        out = pick(lax.rem(mine + step, height)).astype(bf16)
        sent.append(lax.ppermute(out, "replica", [(i, (i + 2 * step) % count) for i in range(count)]))
    return pick(mine), tuple(sent)


def far_total(own, sent):
    total = own
    for value in sent:
        total = total + value.astype(f32)
    return total


def after(value, *others):
    return lax.optimization_barrier((value,) + others)[0]


def body(
    block_input, segment_ids, norm_gain, w_in, conv_weight, conv_bias, x_proj, dt_proj, dt_bias,
    d_skip, out_proj, out_grad,
):
    seqs, local, model = block_input.shape
    length = segment_ids.shape[1]
    tokens = seqs * length
    width = d_skip.shape[0]
    rank = dt_proj.shape[0]
    n = (x_proj.shape[0] - rank) // 2
    me = lax.axis_index("shard")
    count = lax.axis_size("replica")
    height = count // 2
    side = lax.rem(lax.axis_index("replica"), 2)

    def split(values):
        return values.reshape(seqs, length, -1)

    def halves(values, blocks):
        piece = values.shape[1] // blocks // 2
        cuts = [values[:, b * piece : (b + 1) * piece] for b in range(2 * blocks)]
        even = jnp.concatenate(cuts[0::2], axis=1)
        odd = jnp.concatenate(cuts[1::2], axis=1)
        return jnp.where(side == 0, even, odd), jnp.where(side == 0, odd, even)

    def both(keep, got):
        return jnp.concatenate([keep, got], axis=0)

    xs, cots, gains, normed, normed_pair, parts, gated_own, gated_send = front(
        block_input, out_grad, norm_gain, w_in, out_proj
    )
    gain = gains[::8].reshape(1, -1)
    x_all = xs.reshape(tokens, model)
    cot = cots.reshape(tokens, -1)
    if model // count % LANES == 0:
        normed_pair = normed_pair.reshape(2 * tokens, -1)
    else:
        normed_keep, normed_give = halves(normed.reshape(tokens, model), height)
        normed_pair = jnp.concatenate([normed_keep, pair(normed_give)], axis=0)
    x_part, z_part = parts[0], parts[1]

    seg_padded = jnp.pad(segment_ids, ((0, 0), (KW - 1, 0)), constant_values=-1)
    taps = [
        (seg_padded[:, KW - 1 - d : KW - 1 - d + length] == segment_ids).astype(f32) for d in range(KW)
    ]
    conv_w = conv_weight.astype(f32)
    xv = x_part.astype(f32)
    x_padded = jnp.pad(xv, ((0, 0), (KW - 1, 0), (0, 0)))
    conv_pre = conv_bias.astype(f32) + conv_w[KW - 1] * xv
    for j in range(KW - 1):
        d = KW - 1 - j
        conv_pre = conv_pre + conv_w[j] * x_padded[:, j : j + length] * taps[d][:, :, None]
    conv_out = jax.nn.silu(conv_pre).astype(bf16)
    conv_flat = conv_out.reshape(tokens, width)
    proj = group_total(outer_dot(x_proj, conv_flat), 3)
    gated_far = by_hop(after(gated_send, proj), 2)
    keep_lanes = jnp.broadcast_to(taps[1][:, :, None], (seqs, length, LANES))
    skip = d_skip.astype(f32)
    y_total, gated, rate, beta, states = recurrence_forward(
        conv_out, z_part, proj, keep_lanes, dt_proj, dt_bias.astype(f32)[None], skip[None]
    )
    y_total, gated, gated_far = lax.optimization_barrier((y_total, gated, gated_far))
    grad_gated = split(gated_own + gated_far.astype(f32))
    z_vals = z_part.astype(f32)
    dy = grad_gated * jax.nn.silu(z_vals)
    grad_z = (grad_gated * y_total * silu_slope(z_vals)).astype(bf16).reshape(tokens, width)

    gated_keep, gated_give = halves(gated.reshape(tokens, width), height // 4)
    cols = model // 4
    keeps, gives, grad_z_both = collect(gated_keep, gated_give, grad_z)
    z_blocks = inner_dot(normed_pair, grad_z_both.reshape(2 * tokens, -1)).astype(bf16).reshape(height, -1, width)
    z_own, z_sent = far_send(z_blocks)
    keeps, z_own = lax.optimization_barrier((keeps, z_own))
    gated_both, cot_both, block_output = middle(keeps, gives, gated_give, cot, x_all, out_proj, seqs)
    out_blocks = inner_dot(gated_both.reshape(2 * tokens, -1), cot_both.reshape(2 * tokens, -1))
    out_own, out_sent = far_send(out_blocks.astype(bf16).reshape(height, -1, cols))
    rate, out_own = lax.optimization_barrier((rate, out_own))

    grad_conv_rec, grad_dt_low, grad_proj, grad_dt_proj, grad_dt_bias, grad_d_skip = recurrence_backward(
        rate, beta, conv_out, dy, proj, keep_lanes, dt_proj, states
    )
    grad_proj, z_sent = lax.optimization_barrier((grad_proj, z_sent))
    grad_w_z = far_total(z_own.astype(f32), z_sent).astype(bf16)
    grad_proj = group_total(grad_proj, 4).astype(bf16)
    grad_x_proj = rows_dot(grad_proj, conv_flat)
    grad_conv = dy * skip + grad_conv_rec + split(inner_dot(grad_proj, x_proj))
    grad_pre = grad_conv * silu_slope(conv_pre)
    grad_conv_bias = jnp.sum(grad_pre, axis=(0, 1))
    grad_conv_weight = jnp.stack(
        [
            jnp.sum(grad_pre * x_padded[:, j : j + length] * taps[KW - 1 - j][:, :, None], axis=(0, 1))
            for j in range(KW)
        ]
    )
    grad_x = conv_w[KW - 1] * grad_pre
    for j in range(KW - 1):
        d = KW - 1 - j
        ahead = jnp.pad(grad_pre * taps[d][:, :, None], ((0, 0), (0, d), (0, 0)))[:, d:]
        grad_x = grad_x + conv_w[j] * ahead
    grad_x = grad_x.astype(bf16).reshape(tokens, width)

    small = jnp.concatenate(
        [grad_x_proj, grad_dt_proj, grad_conv_weight, grad_conv_bias[None], grad_dt_bias, grad_d_skip]
    )
    unit = 16 * count
    padded = -(-small.shape[0] // unit) * unit
    small = jnp.pad(small, ((0, padded - small.shape[0]), (0, 0))).reshape(height, 2, -1, width)
    small_keep = jnp.where(side == 0, small[:, 0], small[:, 1])
    small_give = jnp.where(side == 0, small[:, 1], small[:, 0]).astype(bf16)
    grad_x, out_sent = lax.optimization_barrier((grad_x, out_sent))
    grad_out_proj = far_total(out_own.astype(f32), out_sent)
    grad_w_in, small, input_grad, grad_gain = finish(
        grad_x, grad_z, small_keep, small_give, grad_w_z, normed_pair, w_in, block_input, out_grad, gain
    )
    small = small.transpose(1, 0, 2, 3).reshape(padded, width).astype(f32)

    top = x_proj.shape[0]
    return (
        block_output, input_grad, grad_gain[0], grad_w_in,
        small[top + rank : top + rank + KW], small[top + rank + KW], small[:top], small[top : top + rank],
        small[top + rank + KW + 1], small[top + rank + KW + 2], grad_out_proj,
    )


def solution(mesh):
    return jax.shard_map(
        body,
        mesh=mesh,
        in_specs=(
            P("replica", "shard", None), P("replica", None), P("shard"), P(None, "shard"), P(None, "shard"),
            P("shard"), P(None, "shard"), P(None, "shard"), P("shard"), P("shard"), P(None, "shard"),
            P("replica", "shard", None),
        ),
        out_specs=(
            P("replica", "shard", None), P("replica", "shard", None), P("shard"), P("replica", "shard"),
            P(None, "shard"), P("shard"), P(None, "shard"), P(None, "shard"), P("shard"), P("shard"),
            P("replica", "shard"),
        ),
        check_vma=False,
    )
```

```python
import functools

import jax
import jax.numpy as jnp
from jax import lax
from jax.experimental import pallas as pl
from jax.experimental.pallas import tpu as pltpu
from jax.sharding import PartitionSpec as P

KW = 4
EPS = 1e-05
CHUNK = 16
LANES = 128
f32 = jnp.float32
bf16 = jnp.bfloat16


def rows_dot(a, b):
    return jnp.dot(a, b, preferred_element_type=f32)


def inner_dot(a, b):
    return lax.dot_general(a, b, (((0,), (0,)), ((), ())), preferred_element_type=f32)


def outer_dot(a, b):
    return lax.dot_general(a, b, (((1,), (1,)), ((), ())), preferred_element_type=f32)


def silu_slope(values):
    sig_val = jax.nn.sigmoid(values)
    return sig_val + values * sig_val * (1.0 - sig_val)

MESH = pl.DeviceIdType.MESH
BLOCK = 128
PIECES = 1


def lane(g):
    return slice(g * LANES, (g + 1) * LANES)


def column(block, t):
    return jnp.broadcast_to(block[:, t : t + 1], (block.shape[0], LANES))


def row(ref, t, g, n):
    return jnp.broadcast_to(ref[t : t + 1, lane(g)], (n, LANES))


def prepare(base, rate_ref, conv_ref, keep_ref, rk, u, kept):
    rows = pl.ds(base, CHUNK)
    rate = rate_ref[0, rows, :]
    keep = keep_ref[0, rows, :]
    conv = conv_ref[0, rows, :].astype(f32)
    for g in range(rate.shape[1] // LANES):
        rk[:, lane(g)] = rate[:, lane(g)] * keep
    u[...] = rate * conv
    kept[...] = keep
    return rate, conv, keep


def shifted(cols, j):
    size = cols.shape[1]
    return pltpu.roll(cols, lax.rem(size - j * CHUNK, size), 1)


def spread_mask(n, size=CHUNK):
    shape = (size, size * n)
    return lax.broadcasted_iota(jnp.int32, shape, 1) // n == lax.broadcasted_iota(jnp.int32, shape, 0)


def picker(n, size=CHUNK):
    shape = (n, size * n)
    return (lax.broadcasted_iota(jnp.int32, shape, 1) % n == lax.broadcasted_iota(jnp.int32, shape, 0)).astype(bf16)


def diagonal(rows, mask, pick):
    return jnp.where(mask, rows_dot(rows.astype(bf16), pick), 0.0).astype(bf16)


def forward_kernel(
    conv_ref, z_ref, proj_ref, keep_ref, dt_proj_ref, dt_bias_ref, skip_ref,
    y_ref, gated_ref, rate_ref, beta_ref, state_ref,
    held_ref, rk, u, kept, query_rows,
):
    width = conv_ref.shape[2]
    rank = dt_proj_ref.shape[0]
    n = (proj_ref.shape[0] - rank) // 2
    groups = width // LANES
    span = CHUNK * n

    @pl.when(pl.program_id(1) == 0)
    def _():
        held_ref[...] = jnp.zeros_like(held_ref)

    dt_low = proj_ref[0:rank, :].astype(bf16)
    keys = proj_ref[rank : rank + n, :]
    query_rows[...] = proj_ref[rank + n :, :].T
    key_square = jnp.sum(keys.T * keys.T, axis=1, keepdims=True)
    beta = jax.nn.sigmoid(inner_dot(dt_low, dt_proj_ref[...]) + dt_bias_ref[...])
    beta_ref[0] = beta
    rate_ref[0] = beta / (1.0 + beta * key_square)
    mask, pick = spread_mask(n), picker(n)

    def chunk(j, held):
        base = pl.multiple_of(j * CHUNK, CHUNK)
        rows = pl.ds(base, CHUNK)
        _, conv, _ = prepare(base, rate_ref, conv_ref, keep_ref, rk, u, kept)
        near_keys = shifted(keys, j)
        held = list(held)
        for t in range(CHUNK):
            key = column(near_keys, t)
            key2 = key * key
            keep = jnp.broadcast_to(kept[t : t + 1, :], (n, LANES))
            at = pl.ds(pl.multiple_of((base + t) * n, n), n)
            for g in range(groups):
                decay = keep - row(rk, t, g, n) * key2
                held[g] = decay * held[g] + row(u, t, g, n) * key
                state_ref[0, at, lane(g)] = held[g].astype(bf16)
        block = state_ref[0, pl.ds(pl.multiple_of(base * n, span), span), :]
        total = rows_dot(diagonal(query_rows[rows, :], mask, pick), block) + skip_ref[...] * conv
        y_ref[0, rows, :] = total
        z = z_ref[0, rows, :].astype(f32)
        gated_ref[0, rows, :] = (total * (z * jax.nn.sigmoid(z))).astype(bf16)
        return tuple(held)

    start = tuple(held_ref[:, lane(g)] for g in range(groups))
    end = lax.fori_loop(0, conv_ref.shape[1] // CHUNK, chunk, start)
    for g in range(groups):
        held_ref[:, lane(g)] = end[g]


def backward_kernel(
    rate_ref, beta_ref, conv_ref, dy_ref, proj_ref, keep_ref, dt_proj_ref, state_ref, last_ref,
    gconv_ref, gdt_ref, gproj_ref, gdt_proj_ref, gdt_bias_ref, gskip_ref,
    held_ref, grate, rk, u, dys, kept, key_rows, adj, adj_state, sums,
):
    block_rows, width = rate_ref.shape[1:]
    rank = dt_proj_ref.shape[0]
    n = (proj_ref.shape[0] - rank) // 2
    groups = width // LANES
    chunks = block_rows // CHUNK

    @pl.when(pl.program_id(1) == 0)
    def _():
        held_ref[...] = jnp.zeros_like(held_ref)

    @pl.when((pl.program_id(0) == 0) & (pl.program_id(1) == 0))
    def _():
        gdt_proj_ref[...] = jnp.zeros_like(gdt_proj_ref)
        gdt_bias_ref[...] = jnp.zeros_like(gdt_bias_ref)
        gskip_ref[...] = jnp.zeros_like(gskip_ref)

    keys = proj_ref[rank : rank + n, :]
    queries = proj_ref[rank + n :, :]
    key_rows[...] = keys.T
    mask, pick = spread_mask(n, CHUNK // PIECES), picker(n, CHUNK // PIECES)

    spot = lax.broadcasted_iota(jnp.int32, (n, LANES), 1)
    sums[...] = jnp.zeros_like(sums)

    def chunk(step, held):
        j = chunks - 1 - step
        base = pl.multiple_of(j * CHUNK, CHUNK)
        rows = pl.ds(base, CHUNK)
        rate, conv, keeps = prepare(base, rate_ref, conv_ref, keep_ref, rk, u, kept)
        dys[...] = dy_ref[0, rows, :]
        near_keys = shifted(keys, j)
        near_queries = shifted(queries, j)
        held = list(held)
        after = [state_ref[0, pl.ds(pl.multiple_of((base + CHUNK - 1) * n, n), n), lane(g)] for g in range(groups)]
        found = [jnp.zeros((n, LANES), f32) for _ in range(3)]
        def settle(p):
            size = CHUNK // PIECES
            part = slice(p * size, (p + 1) * size)
            some = pl.ds(base + p * size, size)
            key_block = key_rows[some, :]
            w1 = rows_dot(diagonal(key_block, mask, pick), adj[p][...].astype(bf16))
            w2 = rows_dot(diagonal(key_block * key_block, mask, pick), adj_state[p][...].astype(bf16))
            for g in range(groups):
                grate[some, lane(g)] = conv[part, lane(g)] * w1[:, lane(g)] - keeps[part] * w2[:, lane(g)]
            gconv_ref[0, some, :] = rate[part] * w1

        for t in reversed(range(CHUNK)):
            piece, place = t // (CHUNK // PIECES), t % (CHUNK // PIECES)
            own = slice(place * n, (place + 1) * n)
            key = column(near_keys, t)
            key2 = key * key
            query = column(near_queries, t)
            keep = jnp.broadcast_to(kept[t : t + 1, :], (n, LANES))
            prior = jnp.maximum(base + t - 1, 0)
            at = pl.ds(pl.multiple_of(prior * n, n), n)
            parts = [None] * 3
            for g in range(groups):
                slope = row(dys, t, g, n)
                pace = row(rk, t, g, n)
                grad = held[g] + slope * query
                decay = keep - pace * key2
                held[g] = decay * grad
                before = state_ref[0, at, lane(g)]
                if t == 0:
                    before = jnp.where(j == 0, last_ref[0, :, lane(g)], before)
                cross = grad * before.astype(f32)
                adj[piece][own, lane(g)] = grad
                adj_state[piece][own, lane(g)] = cross
                terms = (grad * row(u, t, g, n), cross * pace, after[g].astype(f32) * slope)
                parts = [v if p is None else p + v for p, v in zip(parts, terms)]
                after[g] = before
            if place == 0:
                settle(piece)
            here = spot == base + t
            found = [jnp.where(here, jnp.sum(p, axis=1, keepdims=True), f) for p, f in zip(parts, found)]
        for i in range(3):
            sums[i] += found[i]
        return tuple(held)

    start = tuple(held_ref[:, lane(g)] for g in range(groups))
    end = lax.fori_loop(0, chunks, chunk, start)
    for g in range(groups):
        held_ref[:, lane(g)] = end[g]

    def picked(left, value):
        high = value.astype(bf16)
        low = (value - high.astype(f32)).astype(bf16)
        return outer_dot(left, high) + outer_dot(left, low)

    rate = rate_ref[0]
    beta = beta_ref[0]
    grad_rate = grate[...]
    self_term = picked(jnp.ones((n, width), bf16), grad_rate * rate * rate)
    key_square = jnp.sum(key_rows[...] * key_rows[...], axis=1, keepdims=True)
    denom_inv = 1.0 / (1.0 + beta * key_square)
    grad_dt = grad_rate * denom_inv * denom_inv * beta * (1.0 - beta)
    low = grad_dt.astype(bf16)
    gdt_ref[0] = low
    gdt_bias_ref[...] += jnp.sum(grad_dt, axis=0, keepdims=True)
    gskip_ref[...] += jnp.sum(dy_ref[0] * conv_ref[0].astype(f32), axis=0, keepdims=True)
    gdt_proj_ref[...] += rows_dot(proj_ref[0:rank, :].astype(bf16), low)
    gproj_ref[0:rank, :] = outer_dot(dt_proj_ref[...], low)
    gproj_ref[rank : rank + n, :] = sums[0] - 2.0 * keys * (sums[1] + self_term)
    gproj_ref[rank + n :, :] = sums[2]


def specs_for(length, reverse):
    blocks = length // BLOCK

    def place(b):
        return blocks - 1 - b if reverse else b

    def spec(*shape):
        return pl.BlockSpec((1,) + shape, lambda s, b: (s, place(b)) + (0,) * (len(shape) - 1))

    def across_spec(rows):
        return pl.BlockSpec((rows, BLOCK), lambda s, b: (0, s * blocks + place(b)))

    def whole(*shape):
        return pl.BlockSpec(shape, lambda s, b: (0,) * len(shape))

    return blocks, spec, across_spec, whole


def recurrence_forward(conv, z, proj, keep_lanes, dt_proj, dt_bias, skip):
    seqs, length, width = conv.shape
    rank = dt_proj.shape[0]
    n = (proj.shape[0] - rank) // 2
    blocks, spec, across_spec, whole = specs_for(length, False)
    wide = spec(BLOCK, width)
    full = jax.ShapeDtypeStruct((seqs, length, width), f32)
    return pl.pallas_call(
        forward_kernel,
        grid=(seqs, blocks),
        in_specs=[
            wide, wide, across_spec(proj.shape[0]), spec(BLOCK, LANES), whole(rank, width), whole(1, width),
            whole(1, width),
        ],
        out_specs=[wide, wide, wide, wide, spec(BLOCK * n, width)],
        out_shape=[
            full, jax.ShapeDtypeStruct((seqs, length, width), bf16), full, full,
            pltpu.HBM((seqs, length * n, width), bf16),
        ],
        scratch_shapes=[
            pltpu.VMEM((n, width), f32),
            pltpu.VMEM((CHUNK, width), f32),
            pltpu.VMEM((CHUNK, width), f32),
            pltpu.VMEM((CHUNK, LANES), f32),
            pltpu.VMEM((BLOCK, n), f32),
        ],
        compiler_params=pltpu.CompilerParams(vmem_limit_bytes=24 << 20),
        cost_estimate=pl.CostEstimate(flops=16_000_000_000, bytes_accessed=24 << 20, transcendentals=0),
        name="recurrence_forward",
    )(conv, z, proj, keep_lanes, dt_proj, dt_bias, skip)


def recurrence_backward(rate, beta, conv, dy, proj, keep_lanes, dt_proj, states):
    seqs, length, width = rate.shape
    rank = dt_proj.shape[0]
    n = (proj.shape[0] - rank) // 2
    span = CHUNK * n
    blocks, spec, across_spec, whole = specs_for(length, True)
    wide = spec(BLOCK, width)
    before = pl.BlockSpec((1, n, width), lambda s, b: (s, jnp.maximum((blocks - 1 - b) * BLOCK - 1, 0), 0))
    return pl.pallas_call(
        backward_kernel,
        grid=(seqs, blocks),
        in_specs=[
            wide, wide, wide, wide, across_spec(proj.shape[0]), spec(BLOCK, LANES), whole(rank, width),
            spec(BLOCK * n, width), before,
        ],
        out_specs=[wide, wide, across_spec(proj.shape[0]), whole(rank, width), whole(1, width), whole(1, width)],
        out_shape=[
            jax.ShapeDtypeStruct((seqs, length, width), f32),
            jax.ShapeDtypeStruct((seqs, length, width), bf16),
            jax.ShapeDtypeStruct(proj.shape, f32),
            jax.ShapeDtypeStruct((rank, width), f32),
            jax.ShapeDtypeStruct((1, width), f32),
            jax.ShapeDtypeStruct((1, width), f32),
        ],
        scratch_shapes=[
            pltpu.VMEM((n, width), f32),
            pltpu.VMEM((BLOCK, width), f32),
            pltpu.VMEM((CHUNK, width), f32),
            pltpu.VMEM((CHUNK, width), f32),
            pltpu.VMEM((CHUNK, width), f32),
            pltpu.VMEM((CHUNK, LANES), f32),
            pltpu.VMEM((BLOCK, n), f32),
            [pltpu.VMEM((span // PIECES, width), f32)] * PIECES,
            [pltpu.VMEM((span // PIECES, width), f32)] * PIECES,
            pltpu.VMEM((3, n, BLOCK), f32),
        ],
        compiler_params=pltpu.CompilerParams(vmem_limit_bytes=28 << 20),
        cost_estimate=pl.CostEstimate(flops=30_000_000_000, bytes_accessed=28 << 20, transcendentals=0),
        name="recurrence_backward",
    )(rate, beta, conv, dy, proj, keep_lanes, dt_proj, states, states)


def peer(hop):
    me = lax.axis_index("shard")
    core = lax.rem(me, 2)
    chip = me // 2
    if hop & 1:
        core = 1 - core
    if hop & 2:
        chip = 1 - chip
    return chip * 2 + core


def meet_group():
    barrier = pltpu.get_barrier_semaphore()
    for hop in (1, 2, 3):
        pl.semaphore_signal(barrier, inc=1, device_id={"shard": peer(hop)}, device_id_type=MESH)
    pl.semaphore_wait(barrier, 3)


def remote(src, dst, sends, recvs, at, hop):
    return pltpu.make_async_remote_copy(
        src_ref=src, dst_ref=dst, send_sem=sends.at[at], recv_sem=recvs.at[at],
        device_id={"shard": peer(hop)}, device_id_type=MESH,
    )


def group_params(collective_id, limit):
    return pltpu.CompilerParams(collective_id=collective_id, has_side_effects=True, vmem_limit_bytes=limit)


VMEM_SPEC = pl.BlockSpec(memory_space=pltpu.VMEM)


ANY_SPEC = pl.BlockSpec(memory_space=pl.ANY)


def part_copy(src, dst, send, recv, shard):
    return pltpu.make_async_remote_copy(
        src_ref=src, dst_ref=dst, send_sem=send, recv_sem=recv, device_id={"shard": shard}, device_id_type=MESH
    )


def front_kernel(
    x_ref, cot_ref, gain_ref, w_hbm, o_hbm,
    xs_ref, cots_ref, gains_ref, half_ref, parts_ref, own_ref, send_ref,
    w_ref, o_ref, normed_ref, lhs, mixed, pairs, near, sends, recvs, local, part_sends, part_recvs, part_local,
    pair_sends, pair_recvs, pair_local,
):
    me = lax.axis_index("shard")
    chip = me // 2
    slot = me // 2
    seqs, rows, model = x_ref.shape
    cols = cots_ref.shape[2]
    core = lax.rem(me, 2)
    width = parts_ref.shape[3]
    lift = gain_ref.shape[0]
    span = 2 * rows
    tile = 256
    loads = [
        pltpu.make_async_copy(w_hbm, w_ref, local.at[3]),
        pltpu.make_async_copy(o_hbm, o_ref, local.at[4]),
    ]
    for copy in loads:
        copy.start()
    meet([quad(1), quad(2)])

    def mine(ref, owner):
        return ref.at[:, pl.ds(pl.multiple_of(owner * rows, 16), rows), :]

    def part(owner):
        return cot_ref.at[:, :, pl.ds(pl.multiple_of(owner * cols, 128), cols)]

    def gain_rows(owner):
        return gains_ref.at[pl.ds(pl.multiple_of(owner * lift, 8), lift), :]

    gain_sends = [remote(gain_ref, gain_rows(me), sends, recvs, 5 + hop, hop) for hop in (1, 2, 3)]
    x_core = remote(x_ref, mine(xs_ref, me), sends, recvs, 0, 1)
    x_chip = remote(x_ref, mine(xs_ref, me), sends, recvs, 1, 2)
    cot_sends = [remote(part(peer(hop)), mine(cots_ref, me), sends, recvs, 2 + hop, hop) for hop in (1, 2, 3)]
    for copy in gain_sends + [x_core, x_chip] + cot_sends:
        copy.start()
    own = [
        pltpu.make_async_copy(x_ref, mine(xs_ref, me), local.at[0]),
        pltpu.make_async_copy(part(me), mine(cots_ref, me), local.at[1]),
        pltpu.make_async_copy(gain_ref, gain_rows(me), local.at[2]),
    ]
    for copy in own:
        copy.start()
    for copy in own:
        copy.wait()
    for copy in gain_sends:
        copy.wait()
    x_core.wait()
    gain = jnp.concatenate([gains_ref[lift * d : lift * d + 1, :] for d in range(4)], axis=1)
    loads[0].wait()

    def piece(half, i):
        where = jnp.bitwise_xor(chip, half)
        return parts_ref.at[slot, :, pl.ds(pl.multiple_of(where * span, 16), span), :]

    def away(i):
        return lax.rem(2 * me + i, 4) != me

    def send(half, i):
        return part_copy(
            mixed.at[half, i], piece(half, i), part_sends.at[2 * half + i], part_recvs.at[2 * slot + half],
            lax.rem(2 * me + i, 4),
        )

    def keep(half, i):
        return pltpu.make_async_copy(mixed.at[half, i], piece(half, i), part_local.at[half])

    def either(i, yes, no):
        pl.when(away(i))(yes)
        pl.when(jnp.logical_not(away(i)))(no)

    def run_half(half):
        where = jnp.bitwise_xor(chip, half) * span

        for seq in range(seqs):

            def norm(r, carry, seq=seq):
                at = pl.ds(pl.multiple_of(where + r * 16, 16), 16)
                vals = xs_ref[seq, at, :].astype(f32)
                inv = lax.rsqrt(jnp.mean(vals * vals, axis=1, keepdims=True) + EPS)
                out = (vals * inv * gain).astype(bf16)
                normed_ref[seq, at, :] = out
                lhs[pl.ds(pl.multiple_of(seq * span + r * 16, 16), 16), :] = out
                return carry

            lax.fori_loop(0, span // 16, norm, 0)
        for copy in normed_copies(half):
            copy.start()
        for i in range(2):

            def product(t, carry, i=i):
                value = rows_dot(lhs[...], w_ref[:, pl.ds(pl.multiple_of(i * width + t * tile, tile), tile)])
                for seq in range(seqs):
                    mixed[half, i, seq, :, pl.ds(pl.multiple_of(t * tile, tile), tile)] = value[
                        seq * span : (seq + 1) * span
                    ].astype(bf16)
                return carry

            lax.fori_loop(0, width // tile, product, 0)
            either(i, lambda i=i: send(half, i).start(), lambda i=i: keep(half, i).start())

    def normed_copies(half):
        where = pl.ds(pl.multiple_of(jnp.bitwise_xor(chip, half) * span, 16), span)
        src = normed_ref.at[:, where, pl.ds(pl.multiple_of(core * (model // 2), LANES), model // 2)]
        copies = [pltpu.make_async_copy(src, half_ref.at[0, :, where, :], pair_local.at[half])]
        for hop in (1, 2):
            at = 2 * half + hop - 1
            copies.append(across(src, half_ref.at[hop, :, where, :], pair_sends, pair_recvs, at, quad(hop)))
        return copies

    run_half(0)
    x_chip.wait_recv()
    onward = remote(mine(xs_ref, peer(2)), mine(xs_ref, peer(2)), sends, recvs, 2, 1)
    onward.start()
    onward.wait()
    run_half(1)

    for copy in cot_sends:
        copy.wait()
    loads[1].wait()

    def partial(block, t):
        return outer_dot(
            cots_ref[...].reshape(seqs * 4 * rows, cols),
            o_ref[pl.ds(pl.multiple_of(block * width + t * tile, tile), tile), :],
        )

    def lanes(t):
        return pl.ds(pl.multiple_of(t * tile, tile), tile)

    near_sends = []
    for at, hop in enumerate((3, 1)):

        def fill(t, carry, at=at, hop=hop):
            pairs[at, :, lanes(t)] = partial(peer(hop), t).astype(bf16)
            return carry

        lax.fori_loop(0, width // tile, fill, 0)
        copy = remote(pairs.at[at], near.at[at], sends, recvs, 9 + at, 1)
        copy.start()
        near_sends.append(copy)
    near_sends[0].wait()

    def to_send(t, carry):
        send_ref[:, lanes(t)] = (partial(peer(2), t) + near[0, :, lanes(t)].astype(f32)).astype(bf16)
        return carry

    lax.fori_loop(0, width // tile, to_send, 0)
    near_sends[1].wait()

    def to_own(t, carry):
        own_ref[:, lanes(t)] = partial(me, t) + near[1, :, lanes(t)].astype(f32)
        return carry

    lax.fori_loop(0, width // tile, to_own, 0)

    x_chip.wait_send()
    for copy in normed_copies(0) + normed_copies(1):
        copy.wait()
    for half in range(2):
        for i in range(2):
            either(i, lambda half=half, i=i: send(half, i).wait_send(), lambda half=half, i=i: keep(half, i).wait())
        for at in range(2):

            @pl.when(2 * at + me // 2 != me)
            def _(at=at, half=half):
                part_copy(
                    mixed.at[0, 0], mixed.at[0, 0], part_sends.at[0], part_recvs.at[2 * at + half], peer(1)
                ).wait_recv()


def front(x, cot, gain, w_in, out_proj):
    seqs, rows, model = x.shape
    group = lax.axis_size("shard")
    length = rows * group
    cols = model // group
    width = w_in.shape[1] // 2
    tokens = seqs * length
    lifted = jnp.broadcast_to(gain.astype(f32)[None], (8, gain.shape[0]))
    far_sems = pltpu.SemaphoreType.DMA((4,))
    return pl.pallas_call(
        front_kernel,
        in_specs=[VMEM_SPEC] * 3 + [ANY_SPEC] * 2,
        out_specs=[VMEM_SPEC] * 7,
        out_shape=[
            jax.ShapeDtypeStruct((seqs, length, model), bf16),
            jax.ShapeDtypeStruct((seqs, length, cols), bf16),
            jax.ShapeDtypeStruct((8 * group, gain.shape[0]), f32),
            jax.ShapeDtypeStruct((3, seqs, length, model // 2), bf16),
            jax.ShapeDtypeStruct((2, seqs, length, width), bf16),
            jax.ShapeDtypeStruct((tokens, width), f32),
            jax.ShapeDtypeStruct((tokens, width), bf16),
        ],
        scratch_shapes=[
            pltpu.VMEM(w_in.shape, bf16),
            pltpu.VMEM(out_proj.shape, bf16),
            pltpu.VMEM((seqs, length, model), bf16),
            pltpu.VMEM((tokens // 2, model), bf16),
            pltpu.VMEM((2, 2, seqs, 2 * rows, width), bf16),
            pltpu.VMEM((2, tokens, width), bf16),
            pltpu.VMEM((2, tokens, width), bf16),
            pltpu.SemaphoreType.DMA((11,)), pltpu.SemaphoreType.DMA((11,)), pltpu.SemaphoreType.DMA((5,)),
            pltpu.SemaphoreType.DMA((4,)), pltpu.SemaphoreType.DMA((4,)), pltpu.SemaphoreType.DMA((2,)),
            far_sems, far_sems, far_sems,
        ],
        compiler_params=group_params(1, 48 << 20),
        name="front",
    )(x, cot, lifted, w_in, out_proj)


def quad(hop):
    home = lax.axis_index("replica")
    if hop & 1:
        home = home + 1 - 2 * lax.rem(home, 2)
    if hop & 2:
        home = home + 2 - 4 * lax.rem(home // 2, 2)
    return home


def across(src, dst, sends, recvs, at, other):
    return pltpu.make_async_remote_copy(
        src_ref=src, dst_ref=dst, send_sem=sends.at[at], recv_sem=recvs.at[at],
        device_id={"replica": other}, device_id_type=MESH,
    )


def meet(replicas):
    barrier = pltpu.get_barrier_semaphore()
    for hop in (1, 2, 3):
        pl.semaphore_signal(barrier, inc=1, device_id={"shard": peer(hop)}, device_id_type=MESH)
    for other in replicas:
        pl.semaphore_signal(barrier, inc=1, device_id={"replica": other}, device_id_type=MESH)
    pl.semaphore_wait(barrier, 3 + len(replicas))


def ahead(step):
    count = lax.axis_size("replica")
    return lax.rem(lax.axis_index("replica") + step, count)


def collect_kernel(
    keep_ref, give_ref, gz_ref, half_ref, last_ref, cot_ref,
    keeps_ref, gives_ref, gz_ref4, norm_ref, cots_ref,
    sends, recvs, local,
):
    me = lax.axis_index("shard")
    half = keep_ref.shape[1]
    core = lax.rem(me, 2)
    member = lax.rem(lax.axis_index("replica"), 4)
    part = gz_ref4.shape[2]
    meet([quad(hop) for hop in (1, 2, 3)])

    def quarter(which):
        return gz_ref.at[:, pl.ds(pl.multiple_of(which * part, LANES), part)]

    def spot(ref, owner):
        return ref.at[:, pl.ds(pl.multiple_of(owner * half, 128), half)]

    k_chip = remote(keep_ref, spot(keeps_ref, me), sends, recvs, 0, 2)
    v_chip = remote(give_ref, spot(gives_ref, me), sends, recvs, 1, 2)
    k_core = remote(keep_ref, spot(keeps_ref, me), sends, recvs, 2, 1)
    v_core = remote(give_ref, spot(gives_ref, me), sends, recvs, 3, 1)
    quads = [
        across(quarter(lax.rem(quad(hop), 4)), gz_ref4.at[hop], sends, recvs, 6 + hop, quad(hop)) for hop in (3, 1, 2)
    ]
    cot_pair = across(cot_ref, cots_ref.at[1], sends, recvs, 11, quad(1))
    norms = [
        remote(half_ref, norm_ref.at[core, 0:3], sends, recvs, 10, 1),
        remote(last_ref, norm_ref.at[core, 3], sends, recvs, 4, 1),
    ]
    own = [
        pltpu.make_async_copy(keep_ref, spot(keeps_ref, me), local.at[0]),
        pltpu.make_async_copy(give_ref, spot(gives_ref, me), local.at[1]),
        pltpu.make_async_copy(quarter(member), gz_ref4.at[0], local.at[2]),
        pltpu.make_async_copy(half_ref, norm_ref.at[core, 0:3], local.at[3]),
        pltpu.make_async_copy(last_ref, norm_ref.at[core, 3], local.at[4]),
        pltpu.make_async_copy(cot_ref, cots_ref.at[0], local.at[5]),
    ]
    for copy in [k_chip, v_chip] + quads + [cot_pair, k_core, v_core] + norms + own:
        copy.start()
    k_chip.wait_recv()
    k_on = remote(spot(keeps_ref, peer(2)), spot(keeps_ref, peer(2)), sends, recvs, 5, 1)
    k_on.start()
    v_chip.wait_recv()
    v_on = remote(spot(gives_ref, peer(2)), spot(gives_ref, peer(2)), sends, recvs, 6, 1)
    v_on.start()
    for copy in own + quads + norms + [cot_pair, k_core, v_core, k_on, v_on]:
        copy.wait()
    k_chip.wait_send()
    v_chip.wait_send()


def cost(microseconds):
    return pl.CostEstimate(flops=int(microseconds * 1e9), bytes_accessed=1 << 20, transcendentals=0)


def collect(keep, give, grad_z, half_norm, last_norm, cot):
    tokens, half = keep.shape
    group = lax.axis_size("shard")
    wide = jax.ShapeDtypeStruct((tokens, half * group), bf16)
    return pl.pallas_call(
        collect_kernel,
        in_specs=[VMEM_SPEC] * 6,
        out_specs=[VMEM_SPEC] * 5,
        out_shape=[
            wide, wide, jax.ShapeDtypeStruct((4, tokens, grad_z.shape[1] // 4), bf16),
            jax.ShapeDtypeStruct((2, 4) + last_norm.shape, bf16),
            jax.ShapeDtypeStruct((2,) + cot.shape, bf16),
        ],
        scratch_shapes=[
            pltpu.SemaphoreType.DMA((12,)), pltpu.SemaphoreType.DMA((12,)), pltpu.SemaphoreType.DMA((6,)),
        ],
        compiler_params=group_params(6, 28 << 20),
        cost_estimate=cost(25),
        name="collect",
    )(keep, give, grad_z, half_norm, last_norm, cot)


def middle_kernel(
    keeps_ref, gives_ref, give_ref, z_ref, x_hbm, o_hbm,
    both_ref, out_ref, z_got_ref,
    o_ref, xcol, outs, sends, recvs, far_sends, far_recvs, local, o_local,
):
    me = lax.axis_index("shard")
    side = lax.rem(lax.axis_index("replica"), 2)
    tokens, half = give_ref.shape
    gots_ref = both_ref.at[1]
    seqs, rows, _ = out_ref.shape
    cols = xcol.shape[1]
    piece = o_hbm.shape[0] // lax.axis_size("replica")
    per = half // piece
    loads = []
    for d in range(4):
        for q in range(2):
            for j in range(per):
                at = d * 2 * half + (2 * j) * piece + (side if q == 0 else 1 - side) * piece
                loads.append(
                    pltpu.make_async_copy(
                        o_hbm.at[pl.ds(pl.multiple_of(at, piece), piece), :],
                        o_ref.at[q, pl.ds(d * half + j * piece, piece), :],
                        o_local.at[len(loads)],
                    )
                )
    for copy in loads:
        copy.start()
    fetch = pltpu.make_async_copy(
        x_hbm.at[:, pl.ds(pl.multiple_of(me * cols, 128), cols)], xcol, local.at[0]
    )
    fetch.start()
    home = lax.axis_index("replica")
    count = lax.axis_size("replica")
    other = quad(1)
    meet([ahead(step) for step in range(1, count)])

    def spot(owner):
        return gots_ref.at[:, pl.ds(pl.multiple_of(owner * half, 128), half)]

    give_pair = across(give_ref, spot(me), sends, recvs, 0, other)
    own = [
        pltpu.make_async_copy(keeps_ref, both_ref.at[0], local.at[1]),
    ]
    own.append(pltpu.make_async_copy(z_ref.at[home], z_got_ref.at[home], local.at[3 + seqs]))
    z_sends = [
        across(z_ref.at[ahead(step)], z_got_ref.at[home], far_sends, far_recvs, step, ahead(step))
        for step in range(1, count)
    ]
    for copy in [give_pair] + z_sends + own:
        copy.start()
    for copy in loads + [fetch]:
        copy.wait()
    tile = 256

    def product(t, carry):
        rows_at = pl.ds(pl.multiple_of(t * tile, tile), tile)
        value = (
            xcol[rows_at, :].astype(f32)
            + rows_dot(keeps_ref[rows_at, :], o_ref[0])
            + rows_dot(gives_ref[rows_at, :], o_ref[1])
        )
        outs[rows_at, :] = value.astype(bf16)
        return carry

    lax.fori_loop(0, tokens // tile, product, 0)
    length = tokens // seqs
    out_sends = []
    for seq in range(seqs):
        for n_hop, hop in enumerate((2, 3, 1)):
            src = outs.at[pl.ds(pl.multiple_of(seq * length + peer(hop) * rows, 16), rows), :]
            dst = out_ref.at[seq, :, pl.ds(pl.multiple_of(me * cols, 128), cols)]
            out_sends.append(remote(src, dst, sends, recvs, 2 + seq * 3 + n_hop, hop))
        own.append(
            pltpu.make_async_copy(
                outs.at[pl.ds(pl.multiple_of(seq * length + me * rows, 16), rows), :],
                out_ref.at[seq, :, pl.ds(pl.multiple_of(me * cols, 128), cols)],
                local.at[3 + seq],
            )
        )
        own[-1].start()
    for copy in out_sends:
        copy.start()
    base = 2 + seqs * 3
    give_pair.wait_recv()
    g_chip = remote(spot(me), spot(me), sends, recvs, base, 2)
    g_core = remote(spot(me), spot(me), sends, recvs, base + 1, 1)
    g_chip.start()
    g_core.start()
    g_chip.wait_recv()
    g_on = remote(spot(peer(2)), spot(peer(2)), sends, recvs, base + 2, 1)
    g_on.start()
    for copy in out_sends + [g_on, g_core] + own + z_sends:
        copy.wait()
    g_chip.wait_send()
    give_pair.wait_send()


def middle(keeps, gives, give, z_blocks, x_all, out_proj, seqs):
    tokens, half = give.shape
    group = lax.axis_size("shard")
    model = x_all.shape[1]
    cols = model // group
    far_sems = pltpu.SemaphoreType.DMA((lax.axis_size("replica"),))
    pieces = 8 * max(1, half * lax.axis_size("replica") // out_proj.shape[0])
    return pl.pallas_call(
        middle_kernel,
        in_specs=[VMEM_SPEC] * 4 + [ANY_SPEC] * 2,
        out_specs=[VMEM_SPEC] * 3,
        out_shape=[
            jax.ShapeDtypeStruct((2, tokens, half * group), bf16),
            jax.ShapeDtypeStruct((seqs, tokens // seqs // group, model), bf16),
            jax.ShapeDtypeStruct(z_blocks.shape, bf16),
        ],
        scratch_shapes=[
            pltpu.VMEM((2, half * group, cols), bf16),
            pltpu.VMEM((tokens, cols), bf16),
            pltpu.VMEM((tokens, cols), bf16),
            pltpu.SemaphoreType.DMA((5 + 3 * seqs,)), pltpu.SemaphoreType.DMA((5 + 3 * seqs,)),
            far_sems, far_sems, pltpu.SemaphoreType.DMA((4 + seqs,)), pltpu.SemaphoreType.DMA((pieces,)),
        ],
        compiler_params=group_params(7, 22 << 20),
        cost_estimate=cost(25),
        name="middle",
    )(keeps, gives, give, z_blocks, x_all, out_proj)


PARTS = 2


def finish_kernel(
    gx_ref, gz_ref, small_keep_ref, small_give_ref, wz_ref, norm_ref, w_hbm, x_ref, cot_ref, gain_ref,
    gw_ref, small_ref, dx_ref, ggain_ref,
    w_ref, gx4, cols_ref, turned, xb_ref, sb_ref, small_got, x_in, s_in, lhs, pairs, near, g_hold, g_own, g_send, g_far,
    h_send, h_cols, z_cols, s_own, gains, gain_near, gain_sum, gain_pair, gain_two, gain_in,
    sends, recvs, far_sends, far_recvs, home_sends, home_recvs, local,
):
    me = lax.axis_index("shard")
    home = lax.axis_index("replica")
    count = lax.axis_size("replica")
    height = count // 2
    mine = home // 2
    side = lax.rem(home, 2)
    seqs, rows, model = x_ref.shape
    tokens, width = gx_ref.shape
    length = tokens // seqs
    deep = wz_ref.shape[0]
    member = lax.rem(home, 4)
    quarter = width // 4
    part = quarter // PARTS
    tile = 256
    other = quad(1)
    load = pltpu.make_async_copy(w_hbm, w_ref, local.at[0])
    load.start()
    meet([ahead(step) for step in range(1, count)])

    def far(step):
        return ahead(2 * step)

    def cut(p):
        return slice(p * part, (p + 1) * part)

    def piece_of(which, p):
        return gx_ref.at[:, pl.ds(pl.multiple_of(which * quarter + p * part, LANES), part)]

    def spot_of(hop, p):
        return gx4.at[hop * tokens : (hop + 1) * tokens, cut(p)]

    def quad_sends(p):
        return [
            across(piece_of(lax.rem(quad(hop), 4), p), spot_of(hop, p), sends, recvs, 3 * p + hop - 1, quad(hop))
            for hop in (3, 1, 2)
        ]

    small_send = across(small_give_ref, small_got, sends, recvs, 3 * PARTS, other)
    quad_own = [
        pltpu.make_async_copy(piece_of(member, p), spot_of(0, p), local.at[PARTS + 2 + 2 * seqs + p]) for p in range(PARTS)
    ]
    for copy in quad_sends(0) + [small_send] + quad_sends(1) + quad_own:
        copy.start()

    def goal(slot):
        return (4 * slot + me) // 2

    spot = pl.ds(pl.multiple_of(lax.rem(me, 2) * width, LANES), width)

    def home_pieces(at):
        if at == PARTS:
            return 1, wz_ref, z_cols.at[:, spot]
        if at > PARTS:
            slot, seq = (at - PARTS - 1) % 2, (at - PARTS - 1) // 2
            some = slice(seq * length, (seq + 1) * length)
            return slot, (gx_ref, gz_ref)[slot].at[some], cols_ref.at[some, spot]
        some = 4 * part
        return 0, h_send.at[at], h_cols.at[at, :, pl.ds(pl.multiple_of(lax.rem(me, 2) * some, LANES), some)]

    def home_send(at):
        slot, src, dst = home_pieces(at)
        return part_copy(src, dst, home_sends.at[at], home_recvs.at[at * 2 + lax.rem(me, 2)], goal(slot))

    def home_keep(at):
        _, src, dst = home_pieces(at)
        return pltpu.make_async_copy(src, dst, local.at[1 + at])

    def home_start(at):
        slot = home_pieces(at)[0]
        pl.when(goal(slot) != me)(lambda: home_send(at).start())
        pl.when(goal(slot) == me)(lambda: home_keep(at).start())

    def home_wait(at):
        slot = home_pieces(at)[0]
        pl.when(goal(slot) != me)(lambda: home_send(at).wait_send())
        pl.when(goal(slot) == me)(lambda: home_keep(at).wait())
        for place in range(2):
            source = lax.rem(2 * me + place, 4)

            @pl.when((me // 2 == slot) & (source != me))
            def _(place=place):
                src = home_pieces(at)[1]
                part_copy(src, src, home_sends.at[at], home_recvs.at[at * 2 + place], peer(1)).wait_recv()

    for at in (*range(PARTS + 1, PARTS + 1 + 2 * seqs), PARTS):
        home_start(at)

    features = norm_ref.shape[2]

    def turn(i, carry):
        at = pl.ds(pl.multiple_of(i * tile, tile), tile)
        for side_half in range(2):
            for j in range(features // tile):
                low = side_half * features + j * tile
                turned[low : low + tile, at] = norm_ref[side_half, at, j * tile : (j + 1) * tile].T
        return carry

    lax.fori_loop(0, 4 * tokens // tile, turn, 0)

    def far_copy(src, dst, kind, step):
        return across(src, dst, far_sends, far_recvs, kind * count + step, far(step))

    def block(step):
        return lax.rem(mine + step, height)

    order = range(1, height)

    def lines(at):
        return pl.ds(pl.multiple_of(at * deep, 16), deep)

    def x_sends(p):
        return [
            across(
                xb_ref.at[lines(ahead(step)), cut(p)], x_in.at[home, :, cut(p)], far_sends, far_recvs,
                p * count + step, ahead(step),
            )
            for step in range(1, count)
        ]

    def x_part(p):
        for copy in quad_sends(p):
            copy.wait_recv()
        quad_own[p].wait()

        def rows_of(t, carry):
            at = pl.ds(pl.multiple_of(t * tile, tile), tile)
            xb_ref[at, cut(p)] = rows_dot(turned[at, :], gx4[:, cut(p)]).astype(bf16)
            return carry

        lax.fori_loop(0, xb_ref.shape[0] // tile, rows_of, 0)
        x_in[home, :, cut(p)] = xb_ref[lines(home), cut(p)]
        for copy in x_sends(p):
            copy.start()

    def lanes(t):
        return pl.ds(pl.multiple_of(t * tile, tile), tile)

    def near_send(seq):
        return remote(pairs.at[seq], near.at[seq], sends, recvs, 3 * PARTS + 8 + 2 * seq, 1)

    def chip_send(seq):
        return remote(g_send.at[seq], g_far.at[seq], sends, recvs, 3 * PARTS + 9 + 2 * seq, 2)

    def grads_of(seq):
        home_wait(PARTS + 1 + 2 * seq)
        home_wait(PARTS + 2 + 2 * seq)
        for i, owner in enumerate((peer(3), peer(1), peer(2), me)):
            at = pl.ds(pl.multiple_of(seq * length + owner * rows, 16), rows)
            lhs[i * rows : (i + 1) * rows, :] = cols_ref[at, :]

        def product(t, carry):
            value = outer_dot(lhs[...], w_ref[lanes(t), :])
            pairs[seq, :, lanes(t)] = value[: 2 * rows].astype(bf16)
            g_hold[:, lanes(t)] = value[2 * rows : 3 * rows]
            g_own[seq, :, lanes(t)] = value[3 * rows :]
            return carry

        lax.fori_loop(0, model // tile, product, 0)
        near_send(seq).start()

    def grads_on(seq):
        near_send(seq).wait()
        for low in range(0, model, tile):
            at = slice(low, low + tile)
            g_send[seq, :, at] = (g_hold[:, at] + near[seq, :rows, at].astype(f32)).astype(bf16)
            g_own[seq, :, at] += near[seq, rows:, at].astype(f32)
        chip_send(seq).start()

    def home_sum(p):
        for copy in x_sends(p):
            copy.wait_recv()
        for q in range(4):
            total = x_in[q, :, cut(p)].astype(f32)
            for group in range(1, count // 4):
                total = total + x_in[4 * group + q, :, cut(p)].astype(f32)
            h_send[p, :, q * part : (q + 1) * part] = total.astype(bf16)
        home_start(p)

    x_part(0)
    load.wait()
    grads_of(0)
    small_send.wait_recv()
    for at in range(height):
        sb_ref[at] = (small_keep_ref[at] + small_got[at].astype(f32)).astype(bf16)
    s_sends = [far_copy(sb_ref.at[block(step)], s_in.at[step - 1], PARTS, step) for step in order]
    for copy in s_sends:
        copy.start()
    grads_on(0)
    x_part(1)
    grads_of(1)
    home_sum(0)
    grads_on(1)

    for copy in s_sends:
        copy.wait_recv()
    total = sb_ref[mine].astype(f32)
    for step in order:
        total = total + s_in[step - 1].astype(f32)
    s_own[...] = total.astype(bf16)
    small_ref[side, mine] = s_own[...]
    spread = [far_copy(s_own, small_ref.at[side, mine], PARTS + 1, step) for step in order]
    for copy in spread:
        copy.start()

    gains[...] = jnp.zeros_like(gains)

    def finish_rows(seq):
        chip_send(seq).wait()

        def last(r, carry):
            at = pl.ds(pl.multiple_of(r * 16, 16), 16)
            grad = g_own[seq, at, :] + g_far[seq, at, :].astype(f32)
            vals = x_ref[seq, at, :].astype(f32)
            inv = lax.rsqrt(jnp.mean(vals * vals, axis=1, keepdims=True) + EPS)
            scaled = grad * gain_ref[...]
            mean = jnp.mean(scaled * vals, axis=1, keepdims=True)
            out = inv * (scaled - vals * (inv * inv * mean))
            dx_ref[seq, at, :] = (cot_ref[seq, at, :].astype(f32) + out).astype(bf16)
            terms = grad * (vals * inv)
            gains[...] += terms[:8] + terms[8:]
            return carry

        lax.fori_loop(0, rows // 16, last, 0)

    finish_rows(0)
    home_sum(1)
    finish_rows(1)
    gains[...] = jnp.broadcast_to(jnp.sum(gains[...], axis=0, keepdims=True), gains.shape)
    wide = model // 4

    def gain_part(owner):
        return gains.at[:, pl.ds(pl.multiple_of(owner * wide, LANES), wide)]

    gain_sends = [
        remote(gain_part(peer(hop)), gain_near.at[hop - 1], sends, recvs, 3 * PARTS + 2 + hop, hop) for hop in (1, 2, 3)
    ]
    for copy in gain_sends:
        copy.start()
    for copy in gain_sends:
        copy.wait()
    gain_sum[...] = gains[:, pl.ds(pl.multiple_of(me * wide, LANES), wide)] + gain_near[0] + gain_near[1] + gain_near[2]
    gain_copy = across(gain_sum, gain_pair, sends, recvs, 3 * PARTS + 6, other)
    gain_copy.start()
    for copy in spread:
        copy.wait_recv()
    small_pair = across(small_ref.at[side], small_ref.at[side], sends, recvs, 3 * PARTS + 7, other)
    small_pair.start()
    gain_copy.wait()
    gain_two[...] = gain_sum[...] + gain_pair[...]
    gain_far = [far_copy(gain_two, gain_in.at[step - 1], PARTS + 2, step) for step in order]
    for copy in gain_far:
        copy.start()
    for copy in gain_far:
        copy.wait()
    total = gain_two[...]
    for step in order:
        total = total + gain_in[step - 1]
    ggain_ref[...] = total

    for at in range(PARTS + 1):
        home_wait(at)

    @pl.when(me // 2 == 0)
    def _():
        for place in range(2):
            for q in range(4):
                for p in range(PARTS):
                    to = place * width + q * quarter + p * part
                    low = (place * 4 + q) * part
                    gw_ref[:, to : to + part] = h_cols[p, :, low : low + part].astype(f32)

    @pl.when(me // 2 == 1)
    def _():
        for low in range(0, 2 * width, quarter):
            gw_ref[:, low : low + quarter] = z_cols[:, low : low + quarter].astype(f32)

    small_pair.wait()
    small_send.wait_send()
    for p in range(PARTS):
        for copy in quad_sends(p) + x_sends(p):
            copy.wait_send()
    for copy in s_sends + spread:
        copy.wait_send()


def finish(gx, gz, small_keep, small_give, wz, norm, w_in, x, cot, gain):
    tokens, width = gx.shape
    height, lines, _ = small_keep.shape
    deep = wz.shape[0]
    seqs, rows, model = x.shape
    wide = model // 4
    gain_tile = pltpu.VMEM((8, wide), f32)
    other = max(height - 1, 1)
    count = 2 * height
    quarter = width // 4
    kinds = (PARTS + 3) * count
    homes = PARTS + 1 + 2 * seqs
    return pl.pallas_call(
        finish_kernel,
        in_specs=[VMEM_SPEC] * 6 + [ANY_SPEC] + [VMEM_SPEC] * 3,
        out_specs=[VMEM_SPEC] * 4,
        out_shape=[
            jax.ShapeDtypeStruct((deep, 2 * width), f32),
            jax.ShapeDtypeStruct((2, height, lines, width), bf16),
            jax.ShapeDtypeStruct(x.shape, bf16),
            jax.ShapeDtypeStruct((8, wide), f32),
        ],
        scratch_shapes=[
            pltpu.VMEM(w_in.shape, bf16),
            pltpu.VMEM((4 * tokens, quarter), bf16),
            pltpu.VMEM((tokens, 2 * width), bf16),
            pltpu.VMEM((count * deep, 4 * tokens), bf16),
            pltpu.VMEM((count * deep, quarter), bf16),
            pltpu.VMEM((height, lines, width), bf16),
            pltpu.VMEM((height, lines, width), bf16),
            pltpu.VMEM((count, deep, quarter), bf16),
            pltpu.VMEM((other, lines, width), bf16),
            pltpu.VMEM((4 * rows, 2 * width), bf16),
            pltpu.VMEM((seqs, 2 * rows, model), bf16),
            pltpu.VMEM((seqs, 2 * rows, model), bf16),
            pltpu.VMEM((rows, model), f32),
            pltpu.VMEM((seqs, rows, model), f32),
            pltpu.VMEM((seqs, rows, model), bf16),
            pltpu.VMEM((seqs, rows, model), bf16),
            pltpu.VMEM((PARTS, deep, width // PARTS), bf16),
            pltpu.VMEM((PARTS, deep, 2 * width // PARTS), bf16),
            pltpu.VMEM((deep, 2 * width), bf16),
            pltpu.VMEM((lines, width), bf16),
            pltpu.VMEM((8, model), f32),
            pltpu.VMEM((3, 8, wide), f32),
            gain_tile, gain_tile, gain_tile,
            pltpu.VMEM((other, 8, wide), f32),
            pltpu.SemaphoreType.DMA((3 * PARTS + 8 + 2 * seqs,)), pltpu.SemaphoreType.DMA((3 * PARTS + 8 + 2 * seqs,)),
            pltpu.SemaphoreType.DMA((kinds,)), pltpu.SemaphoreType.DMA((kinds,)),
            pltpu.SemaphoreType.DMA((homes,)), pltpu.SemaphoreType.DMA((2 * homes,)),
            pltpu.SemaphoreType.DMA((homes + 1 + PARTS,)),
        ],
        compiler_params=group_params(8, 58 << 20),
        cost_estimate=cost(80),
        name="finish",
    )(gx, gz, small_keep, small_give, wz, norm, w_in, x, cot, gain)


def total_kernel(part_ref, out_ref, near, chip_sum, far, sends, recvs):
    me = lax.axis_index("shard")
    half = part_ref.shape[1] // 2
    mine = pl.ds(pl.multiple_of(lax.rem(me, 2) * half, 128), half)
    other = pl.ds(pl.multiple_of((1 - lax.rem(me, 2)) * half, 128), half)
    meet_group()
    first = remote(part_ref.at[:, other], near, sends, recvs, 0, 1)
    first.start()
    first.wait()
    chip_sum[...] = part_ref[:, mine] + near[...]
    second = remote(chip_sum, far, sends, recvs, 1, 2)
    second.start()
    second.wait()
    out_ref[:, mine] = chip_sum[...] + far[...]
    third = remote(out_ref.at[:, mine], out_ref.at[:, mine], sends, recvs, 2, 1)
    third.start()
    third.wait()


def group_total(part, collective_id):
    rows, cols = part.shape
    half = pltpu.VMEM((rows, cols // 2), f32)
    return pl.pallas_call(
        total_kernel,
        in_specs=[VMEM_SPEC],
        out_specs=VMEM_SPEC,
        out_shape=jax.ShapeDtypeStruct((rows, cols), f32),
        scratch_shapes=[half, half, half, pltpu.SemaphoreType.DMA((3,)), pltpu.SemaphoreType.DMA((3,))],
        compiler_params=group_params(collective_id, 16 << 20),
        name="group_total",
    )(part)


def by_hop(value, hop):
    return lax.ppermute(value, "shard", [(i, i ^ hop) for i in range(4)])


def far_send(blocks):
    count = lax.axis_size("replica")
    height = count // 2
    mine = lax.axis_index("replica") // 2

    def pick(at):
        return lax.dynamic_index_in_dim(blocks, at, 0, False)

    sent = []
    for step in range(1, height):
        out = pick(lax.rem(mine + step, height)).astype(bf16)
        sent.append(lax.ppermute(out, "replica", [(i, (i + 2 * step) % count) for i in range(count)]))
    return pick(mine), tuple(sent)


def far_total(own, sent):
    total = own
    for value in sent:
        total = total + value.astype(f32)
    return total


def after(value, *others):
    return lax.optimization_barrier((value,) + others)[0]


def body(
    block_input, segment_ids, norm_gain, w_in, conv_weight, conv_bias, x_proj, dt_proj, dt_bias,
    d_skip, out_proj, out_grad,
):
    seqs, local, model = block_input.shape
    length = segment_ids.shape[1]
    tokens = seqs * length
    width = d_skip.shape[0]
    rank = dt_proj.shape[0]
    n = (x_proj.shape[0] - rank) // 2
    me = lax.axis_index("shard")
    count = lax.axis_size("replica")
    height = count // 2
    side = lax.rem(lax.axis_index("replica"), 2)

    def split(values):
        return values.reshape(seqs, length, -1)

    def halves(values, blocks):
        piece = values.shape[1] // blocks // 2
        cuts = [values[:, b * piece : (b + 1) * piece] for b in range(2 * blocks)]
        even = jnp.concatenate(cuts[0::2], axis=1)
        odd = jnp.concatenate(cuts[1::2], axis=1)
        return jnp.where(side == 0, even, odd), jnp.where(side == 0, odd, even)

    xs, cots, gains, half_norm, parts, gated_own, gated_send = front(
        block_input, out_grad, norm_gain, w_in, out_proj
    )
    gain = gains[::8].reshape(1, -1)
    x_all = xs.reshape(tokens, model)
    cot = cots.reshape(tokens, -1)
    x_part, z_part = parts[0], parts[1]

    seg_padded = jnp.pad(segment_ids, ((0, 0), (KW - 1, 0)), constant_values=-1)
    taps = [
        (seg_padded[:, KW - 1 - d : KW - 1 - d + length] == segment_ids).astype(f32) for d in range(KW)
    ]
    conv_w = conv_weight.astype(f32)
    xv = x_part.astype(f32)
    x_padded = jnp.pad(xv, ((0, 0), (KW - 1, 0), (0, 0)))
    conv_pre = conv_bias.astype(f32) + conv_w[KW - 1] * xv
    for j in range(KW - 1):
        d = KW - 1 - j
        conv_pre = conv_pre + conv_w[j] * x_padded[:, j : j + length] * taps[d][:, :, None]
    conv_out = jax.nn.silu(conv_pre).astype(bf16)
    conv_flat = conv_out.reshape(tokens, width)
    half_norm = half_norm.reshape(3, tokens, -1)
    last_norm = lax.ppermute(half_norm[0], "replica", [(i, i ^ 3) for i in range(count)])
    proj = group_total(outer_dot(x_proj, conv_flat), 3)
    gated_far = by_hop(after(gated_send, proj), 2)
    keep_lanes = jnp.broadcast_to(taps[1][:, :, None], (seqs, length, LANES))
    skip = d_skip.astype(f32)
    y_total, gated, rate, beta, states = recurrence_forward(
        conv_out, z_part, proj, keep_lanes, dt_proj, dt_bias.astype(f32)[None], skip[None]
    )
    y_total, gated, gated_far, last_norm = lax.optimization_barrier((y_total, gated, gated_far, last_norm))
    grad_gated = split(gated_own + gated_far.astype(f32))
    z_vals = z_part.astype(f32)
    dy = grad_gated * jax.nn.silu(z_vals)
    grad_z = (grad_gated * y_total * silu_slope(z_vals)).astype(bf16).reshape(tokens, width)

    gated_keep, gated_give = halves(gated.reshape(tokens, width), height // 4)
    cols = model // 4
    keeps, gives, grad_z_quad, norms, cot_both = collect(
        gated_keep, gated_give, grad_z, half_norm, last_norm, cot
    )
    norms = norms.reshape(2, 4 * tokens, -1)
    z_blocks = lax.dot_general(
        norms, grad_z_quad.reshape(4 * tokens, -1), (((1,), (0,)), ((), ())), preferred_element_type=f32
    )
    z_blocks = z_blocks.astype(bf16).reshape(count, -1, width // 4)
    gated_both, block_output, z_got = middle(keeps, gives, gated_give, z_blocks, x_all, out_proj, seqs)
    z_sum = jnp.sum(z_got.reshape((-1, 4) + z_got.shape[1:]).astype(f32), axis=0)
    grad_w_z = z_sum.transpose(1, 0, 2).reshape(-1, width).astype(bf16)
    out_blocks = inner_dot(gated_both.reshape(2 * tokens, -1), cot_both.reshape(2 * tokens, -1))
    out_own, out_sent = far_send(out_blocks.astype(bf16).reshape(height, -1, cols))
    rate, out_own = lax.optimization_barrier((rate, out_own))

    grad_conv_rec, grad_dt_low, grad_proj, grad_dt_proj, grad_dt_bias, grad_d_skip = recurrence_backward(
        rate, beta, conv_out, dy, proj, keep_lanes, dt_proj, states
    )
    grad_proj, out_sent = lax.optimization_barrier((group_total(grad_proj, 4), out_sent))
    grad_proj = grad_proj.astype(bf16)
    grad_out_proj = far_total(out_own.astype(f32), out_sent)
    grad_x_proj = rows_dot(grad_proj, conv_flat)
    grad_conv = dy * skip + grad_conv_rec + split(inner_dot(grad_proj, x_proj))
    grad_pre = grad_conv * silu_slope(conv_pre)
    grad_conv_bias = jnp.sum(grad_pre, axis=(0, 1))
    grad_conv_weight = jnp.stack(
        [
            jnp.sum(grad_pre * x_padded[:, j : j + length] * taps[KW - 1 - j][:, :, None], axis=(0, 1))
            for j in range(KW)
        ]
    )
    grad_x = conv_w[KW - 1] * grad_pre
    for j in range(KW - 1):
        d = KW - 1 - j
        ahead = jnp.pad(grad_pre * taps[d][:, :, None], ((0, 0), (0, d), (0, 0)))[:, d:]
        grad_x = grad_x + conv_w[j] * ahead
    grad_x = grad_x.astype(bf16).reshape(tokens, width)

    small = jnp.concatenate(
        [grad_x_proj, grad_dt_proj, grad_conv_weight, grad_conv_bias[None], grad_dt_bias, grad_d_skip]
    )
    unit = 16 * count
    padded = -(-small.shape[0] // unit) * unit
    small = jnp.pad(small, ((0, padded - small.shape[0]), (0, 0))).reshape(height, 2, -1, width)
    small_keep = jnp.where(side == 0, small[:, 0], small[:, 1])
    small_give = jnp.where(side == 0, small[:, 1], small[:, 0]).astype(bf16)
    grad_w_in, small, input_grad, grad_gain = finish(
        grad_x, grad_z, small_keep, small_give, grad_w_z, norms, w_in, block_input, out_grad, gain
    )
    small = small.transpose(1, 0, 2, 3).reshape(padded, width).astype(f32)

    top = x_proj.shape[0]
    return (
        block_output, input_grad, grad_gain[0], grad_w_in,
        small[top + rank : top + rank + KW], small[top + rank + KW], small[:top], small[top : top + rank],
        small[top + rank + KW + 1], small[top + rank + KW + 2], grad_out_proj,
    )


def solution(mesh):
    return jax.shard_map(
        body,
        mesh=mesh,
        in_specs=(
            P("replica", "shard", None), P("replica", None), P("shard"), P(None, "shard"), P(None, "shard"),
            P("shard"), P(None, "shard"), P(None, "shard"), P("shard"), P("shard"), P(None, "shard"),
            P("replica", "shard", None),
        ),
        out_specs=(
            P("replica", "shard", None), P("replica", "shard", None), P("shard"), P("replica", "shard"),
            P(None, "shard"), P("shard"), P(None, "shard"), P(None, "shard"), P("shard"), P("shard"),
            P("replica", "shard"),
        ),
        check_vma=False,
    )
```

```python
import functools

import jax
import jax.numpy as jnp
from jax import lax
from jax.experimental import pallas as pl
from jax.experimental.pallas import tpu as pltpu
from jax.sharding import PartitionSpec as P

KW = 4
EPS = 1e-05
CHUNK = 16
LANES = 128
f32 = jnp.float32
bf16 = jnp.bfloat16


def rows_dot(a, b):
    return jnp.dot(a, b, preferred_element_type=f32)


def inner_dot(a, b):
    return lax.dot_general(a, b, (((0,), (0,)), ((), ())), preferred_element_type=f32)


def outer_dot(a, b):
    return lax.dot_general(a, b, (((1,), (1,)), ((), ())), preferred_element_type=f32)


def silu_slope(values):
    sig_val = jax.nn.sigmoid(values)
    return sig_val + values * sig_val * (1.0 - sig_val)

MESH = pl.DeviceIdType.MESH
BLOCK = 128
PIECES = 1


def lane(g):
    return slice(g * LANES, (g + 1) * LANES)


def column(block, t):
    return jnp.broadcast_to(block[:, t : t + 1], (block.shape[0], LANES))


def row(ref, t, g, n):
    return jnp.broadcast_to(ref[t : t + 1, lane(g)], (n, LANES))


def prepare(base, rate_ref, conv_ref, keep_ref, rk, u, kept):
    rows = pl.ds(base, CHUNK)
    rate = rate_ref[0, rows, :]
    keep = keep_ref[0, rows, :]
    conv = conv_ref[0, rows, :].astype(f32)
    for g in range(rate.shape[1] // LANES):
        rk[:, lane(g)] = rate[:, lane(g)] * keep
    u[...] = rate * conv
    kept[...] = keep
    return rate, conv, keep


def shifted(cols, j):
    size = cols.shape[1]
    return pltpu.roll(cols, lax.rem(size - j * CHUNK, size), 1)


def spread_mask(n, size=CHUNK):
    shape = (size, size * n)
    return lax.broadcasted_iota(jnp.int32, shape, 1) // n == lax.broadcasted_iota(jnp.int32, shape, 0)


def picker(n, size=CHUNK):
    shape = (n, size * n)
    return (lax.broadcasted_iota(jnp.int32, shape, 1) % n == lax.broadcasted_iota(jnp.int32, shape, 0)).astype(bf16)


def diagonal(rows, mask, pick):
    return jnp.where(mask, rows_dot(rows.astype(bf16), pick), 0.0).astype(bf16)


def forward_kernel(
    conv_ref, z_ref, proj_ref, keep_ref, dt_proj_ref, dt_bias_ref, skip_ref,
    y_ref, gated_ref, rate_ref, beta_ref, state_ref,
    held_ref, rk, u, kept, query_rows,
):
    width = conv_ref.shape[2]
    rank = dt_proj_ref.shape[0]
    n = (proj_ref.shape[0] - rank) // 2
    groups = width // LANES
    span = CHUNK * n

    @pl.when(pl.program_id(1) == 0)
    def _():
        held_ref[...] = jnp.zeros_like(held_ref)

    dt_low = proj_ref[0:rank, :].astype(bf16)
    keys = proj_ref[rank : rank + n, :]
    query_rows[...] = proj_ref[rank + n :, :].T
    key_square = jnp.sum(keys.T * keys.T, axis=1, keepdims=True)
    beta = jax.nn.sigmoid(inner_dot(dt_low, dt_proj_ref[...]) + dt_bias_ref[...])
    beta_ref[0] = beta
    rate_ref[0] = beta / (1.0 + beta * key_square)
    mask, pick = spread_mask(n), picker(n)

    def chunk(j, held):
        base = pl.multiple_of(j * CHUNK, CHUNK)
        rows = pl.ds(base, CHUNK)
        _, conv, _ = prepare(base, rate_ref, conv_ref, keep_ref, rk, u, kept)
        near_keys = shifted(keys, j)
        held = list(held)
        for t in range(CHUNK):
            key = column(near_keys, t)
            key2 = key * key
            keep = jnp.broadcast_to(kept[t : t + 1, :], (n, LANES))
            at = pl.ds(pl.multiple_of((base + t) * n, n), n)
            for g in range(groups):
                decay = keep - row(rk, t, g, n) * key2
                held[g] = decay * held[g] + row(u, t, g, n) * key
                state_ref[0, at, lane(g)] = held[g].astype(bf16)
        block = state_ref[0, pl.ds(pl.multiple_of(base * n, span), span), :]
        total = rows_dot(diagonal(query_rows[rows, :], mask, pick), block) + skip_ref[...] * conv
        y_ref[0, rows, :] = total
        z = z_ref[0, rows, :].astype(f32)
        gated_ref[0, rows, :] = (total * (z * jax.nn.sigmoid(z))).astype(bf16)
        return tuple(held)

    start = tuple(held_ref[:, lane(g)] for g in range(groups))
    end = lax.fori_loop(0, conv_ref.shape[1] // CHUNK, chunk, start)
    for g in range(groups):
        held_ref[:, lane(g)] = end[g]


def backward_kernel(
    rate_ref, beta_ref, conv_ref, dy_ref, proj_ref, keep_ref, dt_proj_ref, state_ref, last_ref,
    gconv_ref, gdt_ref, gproj_ref, gdt_proj_ref, gdt_bias_ref, gskip_ref,
    held_ref, grate, rk, u, dys, kept, key_rows, adj, adj_state, sums,
):
    block_rows, width = rate_ref.shape[1:]
    rank = dt_proj_ref.shape[0]
    n = (proj_ref.shape[0] - rank) // 2
    groups = width // LANES
    chunks = block_rows // CHUNK

    @pl.when(pl.program_id(1) == 0)
    def _():
        held_ref[...] = jnp.zeros_like(held_ref)

    @pl.when((pl.program_id(0) == 0) & (pl.program_id(1) == 0))
    def _():
        gdt_proj_ref[...] = jnp.zeros_like(gdt_proj_ref)
        gdt_bias_ref[...] = jnp.zeros_like(gdt_bias_ref)
        gskip_ref[...] = jnp.zeros_like(gskip_ref)

    keys = proj_ref[rank : rank + n, :]
    queries = proj_ref[rank + n :, :]
    key_rows[...] = keys.T
    mask, pick = spread_mask(n, CHUNK // PIECES), picker(n, CHUNK // PIECES)

    spot = lax.broadcasted_iota(jnp.int32, (n, LANES), 1)
    sums[...] = jnp.zeros_like(sums)

    def chunk(step, held):
        j = chunks - 1 - step
        base = pl.multiple_of(j * CHUNK, CHUNK)
        rows = pl.ds(base, CHUNK)
        rate, conv, keeps = prepare(base, rate_ref, conv_ref, keep_ref, rk, u, kept)
        dys[...] = dy_ref[0, rows, :]
        near_keys = shifted(keys, j)
        near_queries = shifted(queries, j)
        held = list(held)
        after = [state_ref[0, pl.ds(pl.multiple_of((base + CHUNK - 1) * n, n), n), lane(g)] for g in range(groups)]
        found = [jnp.zeros((n, LANES), f32) for _ in range(3)]
        def settle(p):
            size = CHUNK // PIECES
            part = slice(p * size, (p + 1) * size)
            some = pl.ds(base + p * size, size)
            key_block = key_rows[some, :]
            w1 = rows_dot(diagonal(key_block, mask, pick), adj[p][...].astype(bf16))
            w2 = rows_dot(diagonal(key_block * key_block, mask, pick), adj_state[p][...].astype(bf16))
            for g in range(groups):
                grate[some, lane(g)] = conv[part, lane(g)] * w1[:, lane(g)] - keeps[part] * w2[:, lane(g)]
            gconv_ref[0, some, :] = rate[part] * w1

        for t in reversed(range(CHUNK)):
            piece, place = t // (CHUNK // PIECES), t % (CHUNK // PIECES)
            own = slice(place * n, (place + 1) * n)
            key = column(near_keys, t)
            key2 = key * key
            query = column(near_queries, t)
            keep = jnp.broadcast_to(kept[t : t + 1, :], (n, LANES))
            prior = jnp.maximum(base + t - 1, 0)
            at = pl.ds(pl.multiple_of(prior * n, n), n)
            parts = [None] * 3
            for g in range(groups):
                slope = row(dys, t, g, n)
                pace = row(rk, t, g, n)
                grad = held[g] + slope * query
                decay = keep - pace * key2
                held[g] = decay * grad
                before = state_ref[0, at, lane(g)]
                if t == 0:
                    before = jnp.where(j == 0, last_ref[0, :, lane(g)], before)
                cross = grad * before.astype(f32)
                adj[piece][own, lane(g)] = grad
                adj_state[piece][own, lane(g)] = cross
                terms = (grad * row(u, t, g, n), cross * pace, after[g].astype(f32) * slope)
                parts = [v if p is None else p + v for p, v in zip(parts, terms)]
                after[g] = before
            if place == 0:
                settle(piece)
            here = spot == base + t
            found = [jnp.where(here, jnp.sum(p, axis=1, keepdims=True), f) for p, f in zip(parts, found)]
        for i in range(3):
            sums[i] += found[i]
        return tuple(held)

    start = tuple(held_ref[:, lane(g)] for g in range(groups))
    end = lax.fori_loop(0, chunks, chunk, start)
    for g in range(groups):
        held_ref[:, lane(g)] = end[g]

    def picked(left, value):
        high = value.astype(bf16)
        low = (value - high.astype(f32)).astype(bf16)
        return outer_dot(left, high) + outer_dot(left, low)

    rate = rate_ref[0]
    beta = beta_ref[0]
    grad_rate = grate[...]
    self_term = picked(jnp.ones((n, width), bf16), grad_rate * rate * rate)
    key_square = jnp.sum(key_rows[...] * key_rows[...], axis=1, keepdims=True)
    denom_inv = 1.0 / (1.0 + beta * key_square)
    grad_dt = grad_rate * denom_inv * denom_inv * beta * (1.0 - beta)
    low = grad_dt.astype(bf16)
    gdt_ref[0] = low
    gdt_bias_ref[...] += jnp.sum(grad_dt, axis=0, keepdims=True)
    gskip_ref[...] += jnp.sum(dy_ref[0] * conv_ref[0].astype(f32), axis=0, keepdims=True)
    gdt_proj_ref[...] += rows_dot(proj_ref[0:rank, :].astype(bf16), low)
    gproj_ref[0:rank, :] = outer_dot(dt_proj_ref[...], low)
    gproj_ref[rank : rank + n, :] = sums[0] - 2.0 * keys * (sums[1] + self_term)
    gproj_ref[rank + n :, :] = sums[2]


def specs_for(length, reverse):
    blocks = length // BLOCK

    def place(b):
        return blocks - 1 - b if reverse else b

    def spec(*shape):
        return pl.BlockSpec((1,) + shape, lambda s, b: (s, place(b)) + (0,) * (len(shape) - 1))

    def across_spec(rows):
        return pl.BlockSpec((rows, BLOCK), lambda s, b: (0, s * blocks + place(b)))

    def whole(*shape):
        return pl.BlockSpec(shape, lambda s, b: (0,) * len(shape))

    return blocks, spec, across_spec, whole


def recurrence_forward(conv, z, proj, keep_lanes, dt_proj, dt_bias, skip):
    seqs, length, width = conv.shape
    rank = dt_proj.shape[0]
    n = (proj.shape[0] - rank) // 2
    blocks, spec, across_spec, whole = specs_for(length, False)
    wide = spec(BLOCK, width)
    full = jax.ShapeDtypeStruct((seqs, length, width), f32)
    return pl.pallas_call(
        forward_kernel,
        grid=(seqs, blocks),
        in_specs=[
            wide, wide, across_spec(proj.shape[0]), spec(BLOCK, LANES), whole(rank, width), whole(1, width),
            whole(1, width),
        ],
        out_specs=[wide, wide, wide, wide, spec(BLOCK * n, width)],
        out_shape=[
            full, jax.ShapeDtypeStruct((seqs, length, width), bf16), full, full,
            pltpu.HBM((seqs, length * n, width), bf16),
        ],
        scratch_shapes=[
            pltpu.VMEM((n, width), f32),
            pltpu.VMEM((CHUNK, width), f32),
            pltpu.VMEM((CHUNK, width), f32),
            pltpu.VMEM((CHUNK, LANES), f32),
            pltpu.VMEM((BLOCK, n), f32),
        ],
        compiler_params=pltpu.CompilerParams(vmem_limit_bytes=24 << 20),
        cost_estimate=pl.CostEstimate(flops=16_000_000_000, bytes_accessed=24 << 20, transcendentals=0),
        name="recurrence_forward",
    )(conv, z, proj, keep_lanes, dt_proj, dt_bias, skip)


def recurrence_backward(rate, beta, conv, dy, proj, keep_lanes, dt_proj, states):
    seqs, length, width = rate.shape
    rank = dt_proj.shape[0]
    n = (proj.shape[0] - rank) // 2
    span = CHUNK * n
    blocks, spec, across_spec, whole = specs_for(length, True)
    wide = spec(BLOCK, width)
    before = pl.BlockSpec((1, n, width), lambda s, b: (s, jnp.maximum((blocks - 1 - b) * BLOCK - 1, 0), 0))
    return pl.pallas_call(
        backward_kernel,
        grid=(seqs, blocks),
        in_specs=[
            wide, wide, wide, wide, across_spec(proj.shape[0]), spec(BLOCK, LANES), whole(rank, width),
            spec(BLOCK * n, width), before,
        ],
        out_specs=[wide, wide, across_spec(proj.shape[0]), whole(rank, width), whole(1, width), whole(1, width)],
        out_shape=[
            jax.ShapeDtypeStruct((seqs, length, width), f32),
            jax.ShapeDtypeStruct((seqs, length, width), bf16),
            jax.ShapeDtypeStruct(proj.shape, f32),
            jax.ShapeDtypeStruct((rank, width), f32),
            jax.ShapeDtypeStruct((1, width), f32),
            jax.ShapeDtypeStruct((1, width), f32),
        ],
        scratch_shapes=[
            pltpu.VMEM((n, width), f32),
            pltpu.VMEM((BLOCK, width), f32),
            pltpu.VMEM((CHUNK, width), f32),
            pltpu.VMEM((CHUNK, width), f32),
            pltpu.VMEM((CHUNK, width), f32),
            pltpu.VMEM((CHUNK, LANES), f32),
            pltpu.VMEM((BLOCK, n), f32),
            [pltpu.VMEM((span // PIECES, width), f32)] * PIECES,
            [pltpu.VMEM((span // PIECES, width), f32)] * PIECES,
            pltpu.VMEM((3, n, BLOCK), f32),
        ],
        compiler_params=pltpu.CompilerParams(vmem_limit_bytes=28 << 20),
        cost_estimate=pl.CostEstimate(flops=30_000_000_000, bytes_accessed=28 << 20, transcendentals=0),
        name="recurrence_backward",
    )(rate, beta, conv, dy, proj, keep_lanes, dt_proj, states, states)


def peer(hop):
    me = lax.axis_index("shard")
    core = lax.rem(me, 2)
    chip = me // 2
    if hop & 1:
        core = 1 - core
    if hop & 2:
        chip = 1 - chip
    return chip * 2 + core


def meet_group():
    barrier = pltpu.get_barrier_semaphore()
    for hop in (1, 2, 3):
        pl.semaphore_signal(barrier, inc=1, device_id={"shard": peer(hop)}, device_id_type=MESH)
    pl.semaphore_wait(barrier, 3)


def remote(src, dst, sends, recvs, at, hop):
    return pltpu.make_async_remote_copy(
        src_ref=src, dst_ref=dst, send_sem=sends.at[at], recv_sem=recvs.at[at],
        device_id={"shard": peer(hop)}, device_id_type=MESH,
    )


def group_params(collective_id, limit):
    return pltpu.CompilerParams(collective_id=collective_id, has_side_effects=True, vmem_limit_bytes=limit)


VMEM_SPEC = pl.BlockSpec(memory_space=pltpu.VMEM)


ANY_SPEC = pl.BlockSpec(memory_space=pl.ANY)


def part_copy(src, dst, send, recv, shard):
    return pltpu.make_async_remote_copy(
        src_ref=src, dst_ref=dst, send_sem=send, recv_sem=recv, device_id={"shard": shard}, device_id_type=MESH
    )


def front_kernel(
    x_ref, cot_ref, gain_ref, w_hbm, o_hbm,
    xs_ref, cots_ref, gains_ref, own_half_ref, half_ref, parts_ref, own_ref, send_ref,
    w_ref, o_ref, normed_ref, lhs, mixed, pairs, near, sends, recvs, local, part_sends, part_recvs, part_local,
    pair_sends, pair_recvs, pair_local,
):
    me = lax.axis_index("shard")
    chip = me // 2
    slot = me // 2
    seqs, rows, model = x_ref.shape
    cols = cots_ref.shape[2]
    core = lax.rem(me, 2)
    width = parts_ref.shape[3]
    lift = gain_ref.shape[0]
    span = 2 * rows
    tile = 256
    loads = [
        pltpu.make_async_copy(w_hbm, w_ref, local.at[3]),
        pltpu.make_async_copy(o_hbm, o_ref, local.at[4]),
    ]
    for copy in loads:
        copy.start()
    meet([quad(1), quad(2)])

    def mine(ref, owner):
        return ref.at[:, pl.ds(pl.multiple_of(owner * rows, 16), rows), :]

    def part(owner):
        return cot_ref.at[:, :, pl.ds(pl.multiple_of(owner * cols, 128), cols)]

    def gain_rows(owner):
        return gains_ref.at[pl.ds(pl.multiple_of(owner * lift, 8), lift), :]

    gain_sends = [remote(gain_ref, gain_rows(me), sends, recvs, 5 + hop, hop) for hop in (1, 2, 3)]
    x_core = remote(x_ref, mine(xs_ref, me), sends, recvs, 0, 1)
    x_chip = remote(x_ref, mine(xs_ref, me), sends, recvs, 1, 2)
    cot_sends = [remote(part(peer(hop)), mine(cots_ref, me), sends, recvs, 2 + hop, hop) for hop in (1, 2, 3)]
    for copy in gain_sends + [x_core, x_chip] + cot_sends:
        copy.start()
    own = [
        pltpu.make_async_copy(x_ref, mine(xs_ref, me), local.at[0]),
        pltpu.make_async_copy(part(me), mine(cots_ref, me), local.at[1]),
        pltpu.make_async_copy(gain_ref, gain_rows(me), local.at[2]),
    ]
    for copy in own:
        copy.start()
    for copy in own:
        copy.wait()
    for copy in gain_sends:
        copy.wait()
    x_core.wait()
    gain = jnp.concatenate([gains_ref[lift * d : lift * d + 1, :] for d in range(4)], axis=1)
    loads[0].wait()

    def piece(half, i):
        where = jnp.bitwise_xor(chip, half)
        return parts_ref.at[slot, :, pl.ds(pl.multiple_of(where * span, 16), span), :]

    def away(i):
        return lax.rem(2 * me + i, 4) != me

    def send(half, i):
        return part_copy(
            mixed.at[half, i], piece(half, i), part_sends.at[2 * half + i], part_recvs.at[2 * slot + half],
            lax.rem(2 * me + i, 4),
        )

    def keep(half, i):
        return pltpu.make_async_copy(mixed.at[half, i], piece(half, i), part_local.at[half])

    def either(i, yes, no):
        pl.when(away(i))(yes)
        pl.when(jnp.logical_not(away(i)))(no)

    def run_half(half):
        where = jnp.bitwise_xor(chip, half) * span

        for seq in range(seqs):

            def norm(r, carry, seq=seq):
                at = pl.ds(pl.multiple_of(where + r * 16, 16), 16)
                vals = xs_ref[seq, at, :].astype(f32)
                inv = lax.rsqrt(jnp.mean(vals * vals, axis=1, keepdims=True) + EPS)
                out = (vals * inv * gain).astype(bf16)
                normed_ref[seq, at, :] = out
                lhs[pl.ds(pl.multiple_of(seq * span + r * 16, 16), 16), :] = out
                return carry

            lax.fori_loop(0, span // 16, norm, 0)
        for copy in normed_copies(half):
            copy.start()
        for i in range(2):

            def product(t, carry, i=i):
                value = rows_dot(lhs[...], w_ref[:, pl.ds(pl.multiple_of(i * width + t * tile, tile), tile)])
                for seq in range(seqs):
                    mixed[half, i, seq, :, pl.ds(pl.multiple_of(t * tile, tile), tile)] = value[
                        seq * span : (seq + 1) * span
                    ].astype(bf16)
                return carry

            lax.fori_loop(0, width // tile, product, 0)
            either(i, lambda i=i: send(half, i).start(), lambda i=i: keep(half, i).start())

    def normed_copies(half):
        where = pl.ds(pl.multiple_of(jnp.bitwise_xor(chip, half) * span, 16), span)
        src = normed_ref.at[:, where, pl.ds(pl.multiple_of(core * (model // 2), LANES), model // 2)]
        copies = [pltpu.make_async_copy(src, own_half_ref.at[:, where, :], pair_local.at[half])]
        for hop in (1, 2):
            at = 2 * half + hop - 1
            copies.append(across(src, half_ref.at[hop - 1, :, where, :], pair_sends, pair_recvs, at, quad(hop)))
        return copies

    run_half(0)
    x_chip.wait_recv()
    onward = remote(mine(xs_ref, peer(2)), mine(xs_ref, peer(2)), sends, recvs, 2, 1)
    onward.start()
    onward.wait()
    run_half(1)

    for copy in cot_sends:
        copy.wait()
    loads[1].wait()

    def partial(block, t):
        return outer_dot(
            cots_ref[...].reshape(seqs * 4 * rows, cols),
            o_ref[pl.ds(pl.multiple_of(block * width + t * tile, tile), tile), :],
        )

    def lanes(t):
        return pl.ds(pl.multiple_of(t * tile, tile), tile)

    near_sends = []
    for at, hop in enumerate((3, 1)):

        def fill(t, carry, at=at, hop=hop):
            pairs[at, :, lanes(t)] = partial(peer(hop), t).astype(bf16)
            return carry

        lax.fori_loop(0, width // tile, fill, 0)
        copy = remote(pairs.at[at], near.at[at], sends, recvs, 9 + at, 1)
        copy.start()
        near_sends.append(copy)
    near_sends[0].wait()

    def to_send(t, carry):
        send_ref[:, lanes(t)] = (partial(peer(2), t) + near[0, :, lanes(t)].astype(f32)).astype(bf16)
        return carry

    lax.fori_loop(0, width // tile, to_send, 0)
    near_sends[1].wait()

    def to_own(t, carry):
        own_ref[:, lanes(t)] = partial(me, t) + near[1, :, lanes(t)].astype(f32)
        return carry

    lax.fori_loop(0, width // tile, to_own, 0)

    x_chip.wait_send()
    for copy in normed_copies(0) + normed_copies(1):
        copy.wait()
    for half in range(2):
        for i in range(2):
            either(i, lambda half=half, i=i: send(half, i).wait_send(), lambda half=half, i=i: keep(half, i).wait())
        for at in range(2):

            @pl.when(2 * at + me // 2 != me)
            def _(at=at, half=half):
                part_copy(
                    mixed.at[0, 0], mixed.at[0, 0], part_sends.at[0], part_recvs.at[2 * at + half], peer(1)
                ).wait_recv()


def front(x, cot, gain, w_in, out_proj):
    seqs, rows, model = x.shape
    group = lax.axis_size("shard")
    length = rows * group
    cols = model // group
    width = w_in.shape[1] // 2
    tokens = seqs * length
    lifted = jnp.broadcast_to(gain.astype(f32)[None], (8, gain.shape[0]))
    far_sems = pltpu.SemaphoreType.DMA((4,))
    return pl.pallas_call(
        front_kernel,
        in_specs=[VMEM_SPEC] * 3 + [ANY_SPEC] * 2,
        out_specs=[VMEM_SPEC] * 8,
        out_shape=[
            jax.ShapeDtypeStruct((seqs, length, model), bf16),
            jax.ShapeDtypeStruct((seqs, length, cols), bf16),
            jax.ShapeDtypeStruct((8 * group, gain.shape[0]), f32),
            jax.ShapeDtypeStruct((seqs, length, model // 2), bf16),
            jax.ShapeDtypeStruct((2, seqs, length, model // 2), bf16),
            jax.ShapeDtypeStruct((2, seqs, length, width), bf16),
            jax.ShapeDtypeStruct((tokens, width), f32),
            jax.ShapeDtypeStruct((tokens, width), bf16),
        ],
        scratch_shapes=[
            pltpu.VMEM(w_in.shape, bf16),
            pltpu.VMEM(out_proj.shape, bf16),
            pltpu.VMEM((seqs, length, model), bf16),
            pltpu.VMEM((tokens // 2, model), bf16),
            pltpu.VMEM((2, 2, seqs, 2 * rows, width), bf16),
            pltpu.VMEM((2, tokens, width), bf16),
            pltpu.VMEM((2, tokens, width), bf16),
            pltpu.SemaphoreType.DMA((11,)), pltpu.SemaphoreType.DMA((11,)), pltpu.SemaphoreType.DMA((5,)),
            pltpu.SemaphoreType.DMA((4,)), pltpu.SemaphoreType.DMA((4,)), pltpu.SemaphoreType.DMA((2,)),
            far_sems, far_sems, far_sems,
        ],
        compiler_params=group_params(1, 48 << 20),
        name="front",
    )(x, cot, lifted, w_in, out_proj)


def quad(hop):
    home = lax.axis_index("replica")
    if hop & 1:
        home = home + 1 - 2 * lax.rem(home, 2)
    if hop & 2:
        home = home + 2 - 4 * lax.rem(home // 2, 2)
    return home


def across(src, dst, sends, recvs, at, other):
    return pltpu.make_async_remote_copy(
        src_ref=src, dst_ref=dst, send_sem=sends.at[at], recv_sem=recvs.at[at],
        device_id={"replica": other}, device_id_type=MESH,
    )


def meet(replicas):
    barrier = pltpu.get_barrier_semaphore()
    for hop in (1, 2, 3):
        pl.semaphore_signal(barrier, inc=1, device_id={"shard": peer(hop)}, device_id_type=MESH)
    for other in replicas:
        pl.semaphore_signal(barrier, inc=1, device_id={"replica": other}, device_id_type=MESH)
    pl.semaphore_wait(barrier, 3 + len(replicas))


def ahead(step):
    count = lax.axis_size("replica")
    return lax.rem(lax.axis_index("replica") + step, count)


def collect_kernel(
    keep_ref, give_ref, gz_ref, own_half_ref, half_ref, last_ref,
    keeps_ref, gives_ref, gz_ref4, norm_ref, got_ref,
    sends, recvs, local,
):
    me = lax.axis_index("shard")
    half = keep_ref.shape[1]
    core = lax.rem(me, 2)
    member = lax.rem(lax.axis_index("replica"), 4)
    part = gz_ref4.shape[2]
    meet([quad(hop) for hop in (1, 2, 3)])

    def quarter(which):
        return gz_ref.at[:, pl.ds(pl.multiple_of(which * part, LANES), part)]

    def spot(ref, owner):
        return ref.at[:, pl.ds(pl.multiple_of(owner * half, 128), half)]

    k_chip = remote(keep_ref, spot(keeps_ref, me), sends, recvs, 0, 2)
    v_chip = remote(give_ref, spot(gives_ref, me), sends, recvs, 1, 2)
    k_core = remote(keep_ref, spot(keeps_ref, me), sends, recvs, 2, 1)
    v_core = remote(give_ref, spot(gives_ref, me), sends, recvs, 3, 1)
    quads = [
        across(quarter(lax.rem(quad(hop), 4)), gz_ref4.at[hop], sends, recvs, 6 + hop, quad(hop)) for hop in (3, 1, 2)
    ]
    give_pair = across(give_ref, got_ref, sends, recvs, 11, quad(1))
    norms = [
        remote(own_half_ref, norm_ref.at[core, 0], sends, recvs, 12, 1),
        remote(half_ref, norm_ref.at[core, 1:3], sends, recvs, 10, 1),
        remote(last_ref, norm_ref.at[core, 3], sends, recvs, 4, 1),
    ]
    own = [
        pltpu.make_async_copy(keep_ref, spot(keeps_ref, me), local.at[0]),
        pltpu.make_async_copy(give_ref, spot(gives_ref, me), local.at[1]),
        pltpu.make_async_copy(quarter(member), gz_ref4.at[0], local.at[2]),
        pltpu.make_async_copy(own_half_ref, norm_ref.at[core, 0], local.at[5]),
        pltpu.make_async_copy(half_ref, norm_ref.at[core, 1:3], local.at[3]),
        pltpu.make_async_copy(last_ref, norm_ref.at[core, 3], local.at[4]),
    ]
    for copy in [k_chip, v_chip] + quads + [give_pair, k_core, v_core] + norms + own:
        copy.start()
    k_chip.wait_recv()
    k_on = remote(spot(keeps_ref, peer(2)), spot(keeps_ref, peer(2)), sends, recvs, 5, 1)
    k_on.start()
    v_chip.wait_recv()
    v_on = remote(spot(gives_ref, peer(2)), spot(gives_ref, peer(2)), sends, recvs, 6, 1)
    v_on.start()
    for copy in own + quads + norms + [give_pair, k_core, v_core, k_on, v_on]:
        copy.wait()
    k_chip.wait_send()
    v_chip.wait_send()


def cost(microseconds):
    return pl.CostEstimate(flops=int(microseconds * 1e9), bytes_accessed=1 << 20, transcendentals=0)


def collect(keep, give, grad_z, own_half, half_norm, last_norm):
    tokens, half = keep.shape
    group = lax.axis_size("shard")
    wide = jax.ShapeDtypeStruct((tokens, half * group), bf16)
    return pl.pallas_call(
        collect_kernel,
        in_specs=[VMEM_SPEC] * 6,
        out_specs=[VMEM_SPEC] * 5,
        out_shape=[
            wide, wide, jax.ShapeDtypeStruct((4, tokens, grad_z.shape[1] // 4), bf16),
            jax.ShapeDtypeStruct((2, 4) + last_norm.shape, bf16),
            jax.ShapeDtypeStruct(give.shape, bf16),
        ],
        scratch_shapes=[
            pltpu.SemaphoreType.DMA((13,)), pltpu.SemaphoreType.DMA((13,)), pltpu.SemaphoreType.DMA((6,)),
        ],
        compiler_params=group_params(6, 28 << 20),
        cost_estimate=cost(25),
        name="collect",
    )(keep, give, grad_z, own_half, half_norm, last_norm)


def middle_kernel(
    keeps_ref, gives_ref, got_ref, z_ref, x_hbm, o_hbm,
    both_ref, out_ref, wz_ref,
    z_got_ref, o_ref, xcol, outs, sends, recvs, far_sends, far_recvs, local, o_local,
):
    me = lax.axis_index("shard")
    side = lax.rem(lax.axis_index("replica"), 2)
    tokens, half = got_ref.shape
    gots_ref = both_ref.at[1]
    seqs, rows, _ = out_ref.shape
    cols = xcol.shape[1]
    piece = o_hbm.shape[0] // lax.axis_size("replica")
    per = half // piece
    loads = []
    for d in range(4):
        for q in range(2):
            for j in range(per):
                at = d * 2 * half + (2 * j) * piece + (side if q == 0 else 1 - side) * piece
                loads.append(
                    pltpu.make_async_copy(
                        o_hbm.at[pl.ds(pl.multiple_of(at, piece), piece), :],
                        o_ref.at[q, pl.ds(d * half + j * piece, piece), :],
                        o_local.at[len(loads)],
                    )
                )
    for copy in loads:
        copy.start()
    fetch = pltpu.make_async_copy(
        x_hbm.at[:, pl.ds(pl.multiple_of(me * cols, 128), cols)], xcol, local.at[0]
    )
    fetch.start()
    home = lax.axis_index("replica")
    count = lax.axis_size("replica")
    meet([ahead(step) for step in range(1, count)])

    def spot(owner):
        return gots_ref.at[:, pl.ds(pl.multiple_of(owner * half, 128), half)]

    g_own = pltpu.make_async_copy(got_ref, spot(me), local.at[2])
    g_chip = remote(got_ref, spot(me), sends, recvs, 0, 2)
    g_core = remote(got_ref, spot(me), sends, recvs, 1, 1)
    own = [
        pltpu.make_async_copy(keeps_ref, both_ref.at[0], local.at[1]),
    ]
    own.append(pltpu.make_async_copy(z_ref.at[home], z_got_ref.at[home], local.at[3 + seqs]))
    z_sends = [
        across(z_ref.at[ahead(step)], z_got_ref.at[home], far_sends, far_recvs, step, ahead(step))
        for step in range(1, count)
    ]
    own.append(g_own)
    for copy in [g_chip] + z_sends + [g_core] + own:
        copy.start()
    for copy in loads + [fetch]:
        copy.wait()
    tile = 256

    def product(t, carry):
        rows_at = pl.ds(pl.multiple_of(t * tile, tile), tile)
        value = (
            xcol[rows_at, :].astype(f32)
            + rows_dot(keeps_ref[rows_at, :], o_ref[0])
            + rows_dot(gives_ref[rows_at, :], o_ref[1])
        )
        outs[rows_at, :] = value.astype(bf16)
        return carry

    lax.fori_loop(0, tokens // tile, product, 0)
    length = tokens // seqs
    out_sends = []
    for seq in range(seqs):
        for n_hop, hop in enumerate((2, 3, 1)):
            src = outs.at[pl.ds(pl.multiple_of(seq * length + peer(hop) * rows, 16), rows), :]
            dst = out_ref.at[seq, :, pl.ds(pl.multiple_of(me * cols, 128), cols)]
            out_sends.append(remote(src, dst, sends, recvs, 2 + seq * 3 + n_hop, hop))
        own.append(
            pltpu.make_async_copy(
                outs.at[pl.ds(pl.multiple_of(seq * length + me * rows, 16), rows), :],
                out_ref.at[seq, :, pl.ds(pl.multiple_of(me * cols, 128), cols)],
                local.at[3 + seq],
            )
        )
        own[-1].start()
    for copy in out_sends:
        copy.start()
    base = 2 + seqs * 3
    g_chip.wait_recv()
    g_on = remote(spot(peer(2)), spot(peer(2)), sends, recvs, base + 2, 1)
    g_on.start()
    for copy in out_sends + [g_on, g_core] + own + z_sends:
        copy.wait()
    g_chip.wait_send()
    quarter = z_got_ref.shape[2]
    for q in range(4):
        total = z_got_ref[q].astype(f32)
        for group in range(1, count // 4):
            total = total + z_got_ref[4 * group + q].astype(f32)
        wz_ref[:, q * quarter : (q + 1) * quarter] = total.astype(bf16)


def middle(keeps, gives, got, z_blocks, x_all, out_proj, seqs):
    tokens, half = got.shape
    group = lax.axis_size("shard")
    model = x_all.shape[1]
    cols = model // group
    far_sems = pltpu.SemaphoreType.DMA((lax.axis_size("replica"),))
    pieces = 8 * max(1, half * lax.axis_size("replica") // out_proj.shape[0])
    return pl.pallas_call(
        middle_kernel,
        in_specs=[VMEM_SPEC] * 4 + [ANY_SPEC] * 2,
        out_specs=[VMEM_SPEC] * 3,
        out_shape=[
            jax.ShapeDtypeStruct((2, tokens, half * group), bf16),
            jax.ShapeDtypeStruct((seqs, tokens // seqs // group, model), bf16),
            jax.ShapeDtypeStruct((z_blocks.shape[1], 4 * z_blocks.shape[2]), bf16),
        ],
        scratch_shapes=[
            pltpu.VMEM(z_blocks.shape, bf16),
            pltpu.VMEM((2, half * group, cols), bf16),
            pltpu.VMEM((tokens, cols), bf16),
            pltpu.VMEM((tokens, cols), bf16),
            pltpu.SemaphoreType.DMA((5 + 3 * seqs,)), pltpu.SemaphoreType.DMA((5 + 3 * seqs,)),
            far_sems, far_sems, pltpu.SemaphoreType.DMA((4 + seqs,)), pltpu.SemaphoreType.DMA((pieces,)),
        ],
        compiler_params=group_params(7, 22 << 20),
        cost_estimate=cost(25),
        name="middle",
    )(keeps, gives, got, z_blocks, x_all, out_proj)


PARTS = 2


def finish_kernel(
    gx_ref, gz_ref, small_keep_ref, small_give_ref, wz_ref, norm_hbm, w_hbm, x_ref, cot_ref, gain_ref,
    gw_ref, gxp_ref, gdp_ref, rest_ref, dx_ref, ggain_ref,
    small_ref, norm_ref, w_ref, gx4, cols_ref, turned, xb_ref, sb_ref, small_got, x_in, s_in, lhs, pairs, near, g_hold, g_own, g_send, g_far,
    h_send, h_cols, z_cols, s_own, gains, gain_near, gain_sum, gain_pair, gain_two, gain_in,
    sends, recvs, far_sends, far_recvs, home_sends, home_recvs, local,
):
    me = lax.axis_index("shard")
    home = lax.axis_index("replica")
    count = lax.axis_size("replica")
    height = count // 2
    mine = home // 2
    side = lax.rem(home, 2)
    seqs, rows, model = x_ref.shape
    tokens, width = gx_ref.shape
    length = tokens // seqs
    deep = wz_ref.shape[0]
    member = lax.rem(home, 4)
    quarter = width // 4
    part = quarter // PARTS
    tile = 256
    other = quad(1)
    load = pltpu.make_async_copy(w_hbm, w_ref, local.at[0])
    load_norm = pltpu.make_async_copy(norm_hbm, norm_ref, local.at[1])
    load_norm.start()
    load.start()
    meet([ahead(step) for step in range(1, count)])

    def far(step):
        return ahead(2 * step)

    def cut(p):
        return slice(p * part, (p + 1) * part)

    def piece_of(which, p):
        return gx_ref.at[:, pl.ds(pl.multiple_of(which * quarter + p * part, LANES), part)]

    def spot_of(hop, p):
        return gx4.at[hop * tokens : (hop + 1) * tokens, cut(p)]

    def quad_sends(p):
        return [
            across(piece_of(lax.rem(quad(hop), 4), p), spot_of(hop, p), sends, recvs, 3 * p + hop - 1, quad(hop))
            for hop in (3, 1, 2)
        ]

    small_send = across(small_give_ref, small_got, sends, recvs, 3 * PARTS, other)
    quad_own = [
        pltpu.make_async_copy(piece_of(member, p), spot_of(0, p), local.at[PARTS + 3 + 2 * seqs + p]) for p in range(PARTS)
    ]
    for copy in quad_sends(0) + [small_send] + quad_sends(1) + quad_own:
        copy.start()

    def goal(slot):
        return (4 * slot + me) // 2

    spot = pl.ds(pl.multiple_of(lax.rem(me, 2) * width, LANES), width)

    def home_pieces(at):
        if at == PARTS:
            return 1, wz_ref, z_cols.at[:, spot]
        if at > PARTS:
            slot, seq = (at - PARTS - 1) % 2, (at - PARTS - 1) // 2
            some = slice(seq * length, (seq + 1) * length)
            return slot, (gx_ref, gz_ref)[slot].at[some], cols_ref.at[some, spot]
        some = 4 * part
        return 0, h_send.at[at], h_cols.at[at, :, pl.ds(pl.multiple_of(lax.rem(me, 2) * some, LANES), some)]

    def home_send(at):
        slot, src, dst = home_pieces(at)
        return part_copy(src, dst, home_sends.at[at], home_recvs.at[at * 2 + lax.rem(me, 2)], goal(slot))

    def home_keep(at):
        _, src, dst = home_pieces(at)
        return pltpu.make_async_copy(src, dst, local.at[2 + at])

    def home_start(at):
        slot = home_pieces(at)[0]
        pl.when(goal(slot) != me)(lambda: home_send(at).start())
        pl.when(goal(slot) == me)(lambda: home_keep(at).start())

    def home_wait(at):
        slot = home_pieces(at)[0]
        pl.when(goal(slot) != me)(lambda: home_send(at).wait_send())
        pl.when(goal(slot) == me)(lambda: home_keep(at).wait())
        for place in range(2):
            source = lax.rem(2 * me + place, 4)

            @pl.when((me // 2 == slot) & (source != me))
            def _(place=place):
                src = home_pieces(at)[1]
                part_copy(src, src, home_sends.at[at], home_recvs.at[at * 2 + place], peer(1)).wait_recv()

    for at in (*range(PARTS + 1, PARTS + 1 + 2 * seqs), PARTS):
        home_start(at)

    features = norm_ref.shape[2]

    def turn(i, carry):
        at = pl.ds(pl.multiple_of(i * tile, tile), tile)
        for side_half in range(2):
            for j in range(features // tile):
                low = side_half * features + j * tile
                turned[low : low + tile, at] = norm_ref[side_half, at, j * tile : (j + 1) * tile].T
        return carry

    load_norm.wait()
    lax.fori_loop(0, 4 * tokens // tile, turn, 0)

    def far_copy(src, dst, kind, step):
        return across(src, dst, far_sends, far_recvs, kind * count + step, far(step))

    def block(step):
        return lax.rem(mine + step, height)

    order = range(1, height)

    def lines(at):
        return pl.ds(pl.multiple_of(at * deep, 16), deep)

    def x_sends(p):
        return [
            across(
                xb_ref.at[lines(ahead(step)), cut(p)], x_in.at[home, :, cut(p)], far_sends, far_recvs,
                p * count + step, ahead(step),
            )
            for step in range(1, count)
        ]

    def x_part(p):
        for copy in quad_sends(p):
            copy.wait_recv()
        quad_own[p].wait()

        def rows_of(t, carry):
            at = pl.ds(pl.multiple_of(t * tile, tile), tile)
            xb_ref[at, cut(p)] = rows_dot(turned[at, :], gx4[:, cut(p)]).astype(bf16)
            return carry

        lax.fori_loop(0, xb_ref.shape[0] // tile, rows_of, 0)
        x_in[home, :, cut(p)] = xb_ref[lines(home), cut(p)]
        for copy in x_sends(p):
            copy.start()

    def lanes(t):
        return pl.ds(pl.multiple_of(t * tile, tile), tile)

    def near_send(seq):
        return remote(pairs.at[seq], near.at[seq], sends, recvs, 3 * PARTS + 8 + 2 * seq, 1)

    def chip_send(seq):
        return remote(g_send.at[seq], g_far.at[seq], sends, recvs, 3 * PARTS + 9 + 2 * seq, 2)

    def grads_of(seq):
        home_wait(PARTS + 1 + 2 * seq)
        home_wait(PARTS + 2 + 2 * seq)
        for i, owner in enumerate((peer(3), peer(1), peer(2), me)):
            at = pl.ds(pl.multiple_of(seq * length + owner * rows, 16), rows)
            lhs[i * rows : (i + 1) * rows, :] = cols_ref[at, :]

        def product(t, carry):
            value = outer_dot(lhs[...], w_ref[lanes(t), :])
            pairs[seq, :, lanes(t)] = value[: 2 * rows].astype(bf16)
            g_hold[:, lanes(t)] = value[2 * rows : 3 * rows]
            g_own[seq, :, lanes(t)] = value[3 * rows :]
            return carry

        lax.fori_loop(0, model // tile, product, 0)
        near_send(seq).start()

    def grads_on(seq):
        near_send(seq).wait()
        for low in range(0, model, tile):
            at = slice(low, low + tile)
            g_send[seq, :, at] = (g_hold[:, at] + near[seq, :rows, at].astype(f32)).astype(bf16)
            g_own[seq, :, at] += near[seq, rows:, at].astype(f32)
        chip_send(seq).start()

    def home_sum(p):
        for copy in x_sends(p):
            copy.wait_recv()
        for q in range(4):
            total = x_in[q, :, cut(p)].astype(f32)
            for group in range(1, count // 4):
                total = total + x_in[4 * group + q, :, cut(p)].astype(f32)
            h_send[p, :, q * part : (q + 1) * part] = total.astype(bf16)
        home_start(p)

    x_part(0)
    load.wait()
    grads_of(0)
    small_send.wait_recv()
    for at in range(height):
        sb_ref[at] = (small_keep_ref[at] + small_got[at].astype(f32)).astype(bf16)
    s_sends = [far_copy(sb_ref.at[block(step)], s_in.at[step - 1], PARTS, step) for step in order]
    for copy in s_sends:
        copy.start()
    grads_on(0)
    x_part(1)
    grads_of(1)
    for copy in s_sends:
        copy.wait_recv()
    total = sb_ref[mine].astype(f32)
    for step in order:
        total = total + s_in[step - 1].astype(f32)
    s_own[...] = total.astype(bf16)
    small_ref[side, mine] = s_own[...]
    spread = [far_copy(s_own, small_ref.at[side, mine], PARTS + 1, step) for step in order]
    for copy in spread:
        copy.start()

    def pass_on(step):
        at = lax.rem(mine + height - step, height)
        return across(
            small_ref.at[side, at], small_ref.at[side, at], far_sends, far_recvs, (PARTS + 3) * count + step, other
        )

    pass_on(0).start()
    home_sum(0)
    grads_on(1)


    gains[...] = jnp.zeros_like(gains)

    def finish_rows(seq):
        chip_send(seq).wait()

        def last(r, carry):
            at = pl.ds(pl.multiple_of(r * 16, 16), 16)
            grad = g_own[seq, at, :] + g_far[seq, at, :].astype(f32)
            vals = x_ref[seq, at, :].astype(f32)
            inv = lax.rsqrt(jnp.mean(vals * vals, axis=1, keepdims=True) + EPS)
            scaled = grad * gain_ref[...]
            mean = jnp.mean(scaled * vals, axis=1, keepdims=True)
            out = inv * (scaled - vals * (inv * inv * mean))
            dx_ref[seq, at, :] = (cot_ref[seq, at, :].astype(f32) + out).astype(bf16)
            terms = grad * (vals * inv)
            gains[...] += terms[:8] + terms[8:]
            return carry

        lax.fori_loop(0, rows // 16, last, 0)

    finish_rows(0)
    home_sum(1)
    for step in order:
        spread[step - 1].wait_recv()
        pass_on(step).start()
    finish_rows(1)
    gains[...] = jnp.broadcast_to(jnp.sum(gains[...], axis=0, keepdims=True), gains.shape)
    wide = model // 4

    def gain_part(owner):
        return gains.at[:, pl.ds(pl.multiple_of(owner * wide, LANES), wide)]

    gain_sends = [
        remote(gain_part(peer(hop)), gain_near.at[hop - 1], sends, recvs, 3 * PARTS + 2 + hop, hop) for hop in (1, 2, 3)
    ]
    for copy in gain_sends:
        copy.start()
    for copy in gain_sends:
        copy.wait()
    gain_sum[...] = gains[:, pl.ds(pl.multiple_of(me * wide, LANES), wide)] + gain_near[0] + gain_near[1] + gain_near[2]
    gain_copy = across(gain_sum, gain_pair, sends, recvs, 3 * PARTS + 6, other)
    gain_copy.start()
    gain_copy.wait()
    gain_two[...] = gain_sum[...] + gain_pair[...]
    gain_far = [far_copy(gain_two, gain_in.at[step - 1], PARTS + 2, step) for step in order]
    for copy in gain_far:
        copy.start()
    for copy in gain_far:
        copy.wait()
    total = gain_two[...]
    for step in order:
        total = total + gain_in[step - 1]
    ggain_ref[...] = total

    for at in range(PARTS + 1):
        home_wait(at)

    @pl.when(me // 2 == 0)
    def _():
        for place in range(2):
            for q in range(4):
                for p in range(PARTS):
                    to = place * width + q * quarter + p * part
                    low = (place * 4 + q) * part
                    gw_ref[:, to : to + part] = h_cols[p, :, low : low + part].astype(f32)

    @pl.when(me // 2 == 1)
    def _():
        for low in range(0, 2 * width, quarter):
            gw_ref[:, low : low + quarter] = z_cols[:, low : low + quarter].astype(f32)

    for step in range(height):
        pass_on(step).wait()
    lined = small_keep_ref.shape[1]
    first, second = gxp_ref.shape[0], gxp_ref.shape[0] + gdp_ref.shape[0]
    for at in range(count):
        low, high = at * lined, (at + 1) * lined
        for ref, start, stop in ((gxp_ref, 0, first), (gdp_ref, first, second), (rest_ref, second, second + 8)):
            a, b = max(low, start), min(high, stop)
            if a < b:
                ref[a - start : b - start, :] = small_ref[at % 2, at // 2, a - low : b - low, :].astype(f32)
    small_send.wait_send()
    for p in range(PARTS):
        for copy in quad_sends(p) + x_sends(p):
            copy.wait_send()
    for copy in s_sends + spread:
        copy.wait_send()


def finish(gx, gz, small_keep, small_give, wz, norm, w_in, x, cot, gain, tops):
    tokens, width = gx.shape
    height, lines, _ = small_keep.shape
    deep = wz.shape[0]
    seqs, rows, model = x.shape
    wide = model // 4
    gain_tile = pltpu.VMEM((8, wide), f32)
    other = max(height - 1, 1)
    count = 2 * height
    quarter = width // 4
    kinds = (PARTS + 4) * count
    homes = PARTS + 1 + 2 * seqs
    return pl.pallas_call(
        finish_kernel,
        in_specs=[VMEM_SPEC] * 5 + [ANY_SPEC] * 2 + [VMEM_SPEC] * 3,
        out_specs=[VMEM_SPEC] * 6,
        out_shape=[
            jax.ShapeDtypeStruct((deep, 2 * width), f32),
            jax.ShapeDtypeStruct((tops[0], width), f32),
            jax.ShapeDtypeStruct((tops[1], width), f32),
            jax.ShapeDtypeStruct((8, width), f32),
            jax.ShapeDtypeStruct(x.shape, bf16),
            jax.ShapeDtypeStruct((8, wide), f32),
        ],
        scratch_shapes=[
            pltpu.VMEM((2, height, lines, width), bf16),
            pltpu.VMEM(norm.shape, bf16),
            pltpu.VMEM(w_in.shape, bf16),
            pltpu.VMEM((4 * tokens, quarter), bf16),
            pltpu.VMEM((tokens, 2 * width), bf16),
            pltpu.VMEM((count * deep, 4 * tokens), bf16),
            pltpu.VMEM((count * deep, quarter), bf16),
            pltpu.VMEM((height, lines, width), bf16),
            pltpu.VMEM((height, lines, width), bf16),
            pltpu.VMEM((count, deep, quarter), bf16),
            pltpu.VMEM((other, lines, width), bf16),
            pltpu.VMEM((4 * rows, 2 * width), bf16),
            pltpu.VMEM((seqs, 2 * rows, model), bf16),
            pltpu.VMEM((seqs, 2 * rows, model), bf16),
            pltpu.VMEM((rows, model), f32),
            pltpu.VMEM((seqs, rows, model), f32),
            pltpu.VMEM((seqs, rows, model), bf16),
            pltpu.VMEM((seqs, rows, model), bf16),
            pltpu.VMEM((PARTS, deep, width // PARTS), bf16),
            pltpu.VMEM((PARTS, deep, 2 * width // PARTS), bf16),
            pltpu.VMEM((deep, 2 * width), bf16),
            pltpu.VMEM((lines, width), bf16),
            pltpu.VMEM((8, model), f32),
            pltpu.VMEM((3, 8, wide), f32),
            gain_tile, gain_tile, gain_tile,
            pltpu.VMEM((other, 8, wide), f32),
            pltpu.SemaphoreType.DMA((3 * PARTS + 8 + 2 * seqs,)), pltpu.SemaphoreType.DMA((3 * PARTS + 8 + 2 * seqs,)),
            pltpu.SemaphoreType.DMA((kinds,)), pltpu.SemaphoreType.DMA((kinds,)),
            pltpu.SemaphoreType.DMA((homes,)), pltpu.SemaphoreType.DMA((2 * homes,)),
            pltpu.SemaphoreType.DMA((homes + 2 + PARTS,)),
        ],
        compiler_params=group_params(8, 58 << 20),
        cost_estimate=cost(80),
        name="finish",
    )(gx, gz, small_keep, small_give, wz, norm, w_in, x, cot, gain)


def total_kernel(part_ref, out_ref, near, chip_sum, far, sends, recvs):
    me = lax.axis_index("shard")
    half = part_ref.shape[1] // 2
    mine = pl.ds(pl.multiple_of(lax.rem(me, 2) * half, 128), half)
    other = pl.ds(pl.multiple_of((1 - lax.rem(me, 2)) * half, 128), half)
    meet_group()
    first = remote(part_ref.at[:, other], near, sends, recvs, 0, 1)
    first.start()
    first.wait()
    chip_sum[...] = part_ref[:, mine] + near[...]
    second = remote(chip_sum, far, sends, recvs, 1, 2)
    second.start()
    second.wait()
    out_ref[:, mine] = chip_sum[...] + far[...]
    third = remote(out_ref.at[:, mine], out_ref.at[:, mine], sends, recvs, 2, 1)
    third.start()
    third.wait()


def group_total(part, collective_id):
    rows, cols = part.shape
    half = pltpu.VMEM((rows, cols // 2), f32)
    return pl.pallas_call(
        total_kernel,
        in_specs=[VMEM_SPEC],
        out_specs=VMEM_SPEC,
        out_shape=jax.ShapeDtypeStruct((rows, cols), f32),
        scratch_shapes=[half, half, half, pltpu.SemaphoreType.DMA((3,)), pltpu.SemaphoreType.DMA((3,))],
        compiler_params=group_params(collective_id, 16 << 20),
        name="group_total",
    )(part)


def by_hop(value, hop):
    return lax.ppermute(value, "shard", [(i, i ^ hop) for i in range(4)])


def far_send(blocks):
    count = lax.axis_size("replica")
    height = count // 2
    mine = lax.axis_index("replica") // 2

    def pick(at):
        return lax.dynamic_index_in_dim(blocks, at, 0, False)

    sent = []
    for step in range(1, height):
        out = pick(lax.rem(mine + step, height)).astype(bf16)
        sent.append(lax.ppermute(out, "replica", [(i, (i + 2 * step) % count) for i in range(count)]))
    return pick(mine), tuple(sent)


def far_total(own, sent):
    total = own
    for value in sent:
        total = total + value.astype(f32)
    return total


def after(value, *others):
    return lax.optimization_barrier((value,) + others)[0]


def body(
    block_input, segment_ids, norm_gain, w_in, conv_weight, conv_bias, x_proj, dt_proj, dt_bias,
    d_skip, out_proj, out_grad,
):
    seqs, local, model = block_input.shape
    length = segment_ids.shape[1]
    tokens = seqs * length
    width = d_skip.shape[0]
    rank = dt_proj.shape[0]
    n = (x_proj.shape[0] - rank) // 2
    me = lax.axis_index("shard")
    count = lax.axis_size("replica")
    height = count // 2
    side = lax.rem(lax.axis_index("replica"), 2)

    def split(values):
        return values.reshape(seqs, length, -1)

    def halves(values, blocks):
        piece = values.shape[1] // blocks // 2
        cuts = [values[:, b * piece : (b + 1) * piece] for b in range(2 * blocks)]
        even = jnp.concatenate(cuts[0::2], axis=1)
        odd = jnp.concatenate(cuts[1::2], axis=1)
        return jnp.where(side == 0, even, odd), jnp.where(side == 0, odd, even)

    xs, cots, gains, own_half, half_norm, parts, gated_own, gated_send = front(
        block_input, out_grad, norm_gain, w_in, out_proj
    )
    gain = gains[::8].reshape(1, -1)
    x_all = xs.reshape(tokens, model)
    cot = cots.reshape(tokens, -1)
    x_part, z_part = parts[0], parts[1]

    seg_padded = jnp.pad(segment_ids, ((0, 0), (KW - 1, 0)), constant_values=-1)
    taps = [
        (seg_padded[:, KW - 1 - d : KW - 1 - d + length] == segment_ids).astype(f32) for d in range(KW)
    ]
    conv_w = conv_weight.astype(f32)
    xv = x_part.astype(f32)
    x_padded = jnp.pad(xv, ((0, 0), (KW - 1, 0), (0, 0)))
    conv_pre = conv_bias.astype(f32) + conv_w[KW - 1] * xv
    for j in range(KW - 1):
        d = KW - 1 - j
        conv_pre = conv_pre + conv_w[j] * x_padded[:, j : j + length] * taps[d][:, :, None]
    conv_out = jax.nn.silu(conv_pre).astype(bf16)
    conv_flat = conv_out.reshape(tokens, width)
    half_norm = half_norm.reshape(2, tokens, -1)
    own_half = own_half.reshape(tokens, -1)
    last_norm = lax.ppermute(own_half, "replica", [(i, i ^ 3) for i in range(count)])
    cot_got = lax.ppermute(cot, "replica", [(i, i ^ 1) for i in range(count)])
    proj = group_total(outer_dot(x_proj, conv_flat), 3)
    gated_far = by_hop(after(gated_send, proj), 2)
    keep_lanes = jnp.broadcast_to(taps[1][:, :, None], (seqs, length, LANES))
    skip = d_skip.astype(f32)
    y_total, gated, rate, beta, states = recurrence_forward(
        conv_out, z_part, proj, keep_lanes, dt_proj, dt_bias.astype(f32)[None], skip[None]
    )
    y_total, gated, gated_far, last_norm, cot_got = lax.optimization_barrier(
        (y_total, gated, gated_far, last_norm, cot_got)
    )
    cot_both = jnp.concatenate([cot, cot_got], axis=0)
    grad_gated = split(gated_own + gated_far.astype(f32))
    z_vals = z_part.astype(f32)
    dy = grad_gated * jax.nn.silu(z_vals)
    grad_z = (grad_gated * y_total * silu_slope(z_vals)).astype(bf16).reshape(tokens, width)

    gated_keep, gated_give = halves(gated.reshape(tokens, width), height // 4)
    cols = model // 4
    keeps, gives, grad_z_quad, norms, gated_got = collect(
        gated_keep, gated_give, grad_z, own_half, half_norm, last_norm
    )
    norms = norms.reshape(2, 4 * tokens, -1)
    z_blocks = lax.dot_general(
        norms, grad_z_quad.reshape(4 * tokens, -1), (((1,), (0,)), ((), ())), preferred_element_type=f32
    )
    z_blocks = z_blocks.astype(bf16).reshape(count, -1, width // 4)
    gated_both, block_output, grad_w_z = middle(keeps, gives, gated_got, z_blocks, x_all, out_proj, seqs)
    out_blocks = inner_dot(gated_both.reshape(2 * tokens, -1), cot_both)
    out_own, out_sent = far_send(out_blocks.astype(bf16).reshape(height, -1, cols))
    rate, out_own = lax.optimization_barrier((rate, out_own))

    grad_conv_rec, grad_dt_low, grad_proj, grad_dt_proj, grad_dt_bias, grad_d_skip = recurrence_backward(
        rate, beta, conv_out, dy, proj, keep_lanes, dt_proj, states
    )
    grad_proj, out_sent = lax.optimization_barrier((group_total(grad_proj, 4), out_sent))
    grad_proj = grad_proj.astype(bf16)
    grad_out_proj = far_total(out_own.astype(f32), out_sent)
    grad_x_proj = rows_dot(grad_proj, conv_flat)
    grad_conv = dy * skip + grad_conv_rec + split(inner_dot(grad_proj, x_proj))
    grad_pre = grad_conv * silu_slope(conv_pre)
    grad_conv_bias = jnp.sum(grad_pre, axis=(0, 1))
    grad_conv_weight = jnp.stack(
        [
            jnp.sum(grad_pre * x_padded[:, j : j + length] * taps[KW - 1 - j][:, :, None], axis=(0, 1))
            for j in range(KW)
        ]
    )
    grad_x = conv_w[KW - 1] * grad_pre
    for j in range(KW - 1):
        d = KW - 1 - j
        ahead = jnp.pad(grad_pre * taps[d][:, :, None], ((0, 0), (0, d), (0, 0)))[:, d:]
        grad_x = grad_x + conv_w[j] * ahead
    grad_x = grad_x.astype(bf16).reshape(tokens, width)

    small = jnp.concatenate(
        [grad_x_proj, grad_dt_proj, grad_conv_weight, grad_conv_bias[None], grad_dt_bias, grad_d_skip]
    )
    unit = 8 * count
    padded = -(-small.shape[0] // unit) * unit
    small = jnp.pad(small, ((0, padded - small.shape[0]), (0, 0))).reshape(height, 2, -1, width)
    small_keep = jnp.where(side == 0, small[:, 0], small[:, 1])
    small_give = jnp.where(side == 0, small[:, 1], small[:, 0]).astype(bf16)
    top = x_proj.shape[0]
    grad_w_in, grad_x_proj, grad_dt_proj, rest, input_grad, grad_gain = finish(
        grad_x, grad_z, small_keep, small_give, grad_w_z, norms, w_in, block_input, out_grad, gain,
        (top, rank),
    )
    return (
        block_output, input_grad, grad_gain[0], grad_w_in, rest[:KW], rest[KW], grad_x_proj, grad_dt_proj,
        rest[KW + 1], rest[KW + 2], grad_out_proj,
    )


def solution(mesh):
    return jax.shard_map(
        body,
        mesh=mesh,
        in_specs=(
            P("replica", "shard", None), P("replica", None), P("shard"), P(None, "shard"), P(None, "shard"),
            P("shard"), P(None, "shard"), P(None, "shard"), P("shard"), P("shard"), P(None, "shard"),
            P("replica", "shard", None),
        ),
        out_specs=(
            P("replica", "shard", None), P("replica", "shard", None), P("shard"), P("replica", "shard"),
            P(None, "shard"), P("shard"), P(None, "shard"), P(None, "shard"), P("shard"), P("shard"),
            P("replica", "shard"),
        ),
        check_vma=False,
    )
```

```python
import functools

import jax
import jax.numpy as jnp
from jax import lax
from jax.experimental import pallas as pl
from jax.experimental.pallas import tpu as pltpu
from jax.sharding import PartitionSpec as P

KW = 4
EPS = 1e-05
CHUNK = 16
LANES = 128
f32 = jnp.float32
bf16 = jnp.bfloat16


def rows_dot(a, b):
    return jnp.dot(a, b, preferred_element_type=f32)


def inner_dot(a, b):
    return lax.dot_general(a, b, (((0,), (0,)), ((), ())), preferred_element_type=f32)


def outer_dot(a, b):
    return lax.dot_general(a, b, (((1,), (1,)), ((), ())), preferred_element_type=f32)


def silu_slope(values):
    sig_val = jax.nn.sigmoid(values)
    return sig_val + values * sig_val * (1.0 - sig_val)

MESH = pl.DeviceIdType.MESH
BLOCK = 128
UNROLL = 4
PIECES = 1


def lane(g):
    return slice(g * LANES, (g + 1) * LANES)


def column(block, t):
    return jnp.broadcast_to(block[:, t : t + 1], (block.shape[0], LANES))


def row(ref, t, g, n):
    return jnp.broadcast_to(ref[t : t + 1, lane(g)], (n, LANES))


def prepare(base, rate_ref, conv_ref, keep_ref, rk, u, kept):
    rows = pl.ds(base, CHUNK)
    rate = rate_ref[0, rows, :]
    keep = keep_ref[0, rows, :]
    conv = conv_ref[0, rows, :].astype(f32)
    for g in range(rate.shape[1] // LANES):
        rk[:, lane(g)] = rate[:, lane(g)] * keep
    u[...] = rate * conv
    kept[...] = keep
    return rate, conv, keep


def shifted(cols, j):
    size = cols.shape[1]
    return pltpu.roll(cols, lax.rem(size - j * CHUNK, size), 1)


def spread_mask(n, size=CHUNK):
    shape = (size, size * n)
    return lax.broadcasted_iota(jnp.int32, shape, 1) // n == lax.broadcasted_iota(jnp.int32, shape, 0)


def picker(n, size=CHUNK):
    shape = (n, size * n)
    return (lax.broadcasted_iota(jnp.int32, shape, 1) % n == lax.broadcasted_iota(jnp.int32, shape, 0)).astype(bf16)


def diagonal(rows, mask, pick):
    return jnp.where(mask, rows_dot(rows.astype(bf16), pick), 0.0).astype(bf16)


def forward_kernel(
    conv_ref, z_ref, proj_ref, keep_ref, dt_proj_ref, dt_bias_ref, skip_ref,
    y_ref, gated_ref, rate_ref, beta_ref, state_ref,
    held_ref, rk, u, kept, query_rows, fresh,
):
    width = conv_ref.shape[2]
    rank = dt_proj_ref.shape[0]
    n = (proj_ref.shape[0] - rank) // 2
    groups = width // LANES
    span = CHUNK * n

    @pl.when(pl.program_id(1) == 0)
    def _():
        held_ref[...] = jnp.zeros_like(held_ref)

    dt_low = proj_ref[0:rank, :].astype(bf16)
    keys = proj_ref[rank : rank + n, :]
    query_rows[...] = proj_ref[rank + n :, :].T
    key_square = jnp.sum(keys.T * keys.T, axis=1, keepdims=True)
    beta = jax.nn.sigmoid(inner_dot(dt_low, dt_proj_ref[...]) + dt_bias_ref[...])
    beta_ref[0] = beta
    rate_ref[0] = beta / (1.0 + beta * key_square)
    mask, pick = spread_mask(n), picker(n)

    def states_of(j, held, rk, u, kept, fresh):
        base = pl.multiple_of(j * CHUNK, CHUNK)
        prepare(base, rate_ref, conv_ref, keep_ref, rk, u, kept)
        near_keys = shifted(keys, j)
        for t in range(CHUNK):
            key = column(near_keys, t)
            key2 = key * key
            keep = jnp.broadcast_to(kept[t : t + 1, :], (n, LANES))
            at = slice(t * n, (t + 1) * n)
            for g in range(groups):
                decay = keep - row(rk, t, g, n) * key2
                held[g] = decay * held[g] + row(u, t, g, n) * key
                fresh[at, lane(g)] = held[g].astype(fresh.dtype)

    def outputs_of(j, fresh):
        base = pl.multiple_of(j * CHUNK, CHUNK)
        rows = pl.ds(base, CHUNK)
        block = fresh[...].astype(bf16)
        state_ref[0, pl.ds(pl.multiple_of(base * n, span), span), :] = block
        conv = conv_ref[0, rows, :].astype(f32)
        total = rows_dot(diagonal(query_rows[rows, :], mask, pick), block) + skip_ref[...] * conv
        y_ref[0, rows, :] = total
        z = z_ref[0, rows, :].astype(f32)
        gated_ref[0, rows, :] = (total * (z * jax.nn.sigmoid(z))).astype(bf16)

    def step(i, held):
        held = list(held)
        for k in range(UNROLL):
            states_of(i * UNROLL + k, held, rk[k], u[k], kept[k], fresh[k])
            if k > 0:
                outputs_of(i * UNROLL + k - 1, fresh[k - 1])
        outputs_of(i * UNROLL + UNROLL - 1, fresh[UNROLL - 1])
        return tuple(held)

    start = tuple(held_ref[:, lane(g)] for g in range(groups))
    end = lax.fori_loop(0, conv_ref.shape[1] // CHUNK // UNROLL, step, start)
    for g in range(groups):
        held_ref[:, lane(g)] = end[g]


def backward_kernel(
    rate_ref, beta_ref, conv_ref, dy_ref, proj_ref, keep_ref, dt_proj_ref, state_ref, last_ref,
    gconv_ref, gdt_ref, gproj_ref, gdt_proj_ref, gdt_bias_ref, gskip_ref,
    held_ref, grate, rk, u, dys, kept, key_rows, adj, adj_state, sums,
):
    block_rows, width = rate_ref.shape[1:]
    rank = dt_proj_ref.shape[0]
    n = (proj_ref.shape[0] - rank) // 2
    groups = width // LANES
    chunks = block_rows // CHUNK

    @pl.when(pl.program_id(1) == 0)
    def _():
        held_ref[...] = jnp.zeros_like(held_ref)

    @pl.when((pl.program_id(0) == 0) & (pl.program_id(1) == 0))
    def _():
        gdt_proj_ref[...] = jnp.zeros_like(gdt_proj_ref)
        gdt_bias_ref[...] = jnp.zeros_like(gdt_bias_ref)
        gskip_ref[...] = jnp.zeros_like(gskip_ref)

    keys = proj_ref[rank : rank + n, :]
    queries = proj_ref[rank + n :, :]
    key_rows[...] = keys.T
    mask, pick = spread_mask(n, CHUNK // PIECES), picker(n, CHUNK // PIECES)

    spot = lax.broadcasted_iota(jnp.int32, (n, LANES), 1)
    sums[...] = jnp.zeros_like(sums)

    def chunk(step, held):
        j = chunks - 1 - step
        base = pl.multiple_of(j * CHUNK, CHUNK)
        rows = pl.ds(base, CHUNK)
        rate, conv, keeps = prepare(base, rate_ref, conv_ref, keep_ref, rk, u, kept)
        dys[...] = dy_ref[0, rows, :]
        near_keys = shifted(keys, j)
        near_queries = shifted(queries, j)
        held = list(held)
        after = [state_ref[0, pl.ds(pl.multiple_of((base + CHUNK - 1) * n, n), n), lane(g)] for g in range(groups)]
        found = [jnp.zeros((n, LANES), f32) for _ in range(3)]
        def settle(p):
            size = CHUNK // PIECES
            part = slice(p * size, (p + 1) * size)
            some = pl.ds(base + p * size, size)
            key_block = key_rows[some, :]
            w1 = rows_dot(diagonal(key_block, mask, pick), adj[p][...].astype(bf16))
            w2 = rows_dot(diagonal(key_block * key_block, mask, pick), adj_state[p][...].astype(bf16))
            for g in range(groups):
                grate[some, lane(g)] = conv[part, lane(g)] * w1[:, lane(g)] - keeps[part] * w2[:, lane(g)]
            gconv_ref[0, some, :] = rate[part] * w1

        for t in reversed(range(CHUNK)):
            piece, place = t // (CHUNK // PIECES), t % (CHUNK // PIECES)
            own = slice(place * n, (place + 1) * n)
            key = column(near_keys, t)
            key2 = key * key
            query = column(near_queries, t)
            keep = jnp.broadcast_to(kept[t : t + 1, :], (n, LANES))
            prior = jnp.maximum(base + t - 1, 0)
            at = pl.ds(pl.multiple_of(prior * n, n), n)
            parts = [None] * 3
            for g in range(groups):
                slope = row(dys, t, g, n)
                pace = row(rk, t, g, n)
                grad = held[g] + slope * query
                decay = keep - pace * key2
                held[g] = decay * grad
                before = state_ref[0, at, lane(g)]
                if t == 0:
                    before = jnp.where(j == 0, last_ref[0, :, lane(g)], before)
                cross = grad * before.astype(f32)
                adj[piece][own, lane(g)] = grad
                adj_state[piece][own, lane(g)] = cross
                terms = (grad * row(u, t, g, n), cross * pace, after[g].astype(f32) * slope)
                parts = [v if p is None else p + v for p, v in zip(parts, terms)]
                after[g] = before
            if place == 0:
                settle(piece)
            here = spot == base + t
            found = [jnp.where(here, jnp.sum(p, axis=1, keepdims=True), f) for p, f in zip(parts, found)]
        for i in range(3):
            sums[i] += found[i]
        return tuple(held)

    start = tuple(held_ref[:, lane(g)] for g in range(groups))
    end = lax.fori_loop(0, chunks, chunk, start)
    for g in range(groups):
        held_ref[:, lane(g)] = end[g]

    def picked(left, value):
        high = value.astype(bf16)
        low = (value - high.astype(f32)).astype(bf16)
        return outer_dot(left, high) + outer_dot(left, low)

    rate = rate_ref[0]
    beta = beta_ref[0]
    grad_rate = grate[...]
    self_term = picked(jnp.ones((n, width), bf16), grad_rate * rate * rate)
    key_square = jnp.sum(key_rows[...] * key_rows[...], axis=1, keepdims=True)
    denom_inv = 1.0 / (1.0 + beta * key_square)
    grad_dt = grad_rate * denom_inv * denom_inv * beta * (1.0 - beta)
    low = grad_dt.astype(bf16)
    gdt_ref[0] = low
    gdt_bias_ref[...] += jnp.sum(grad_dt, axis=0, keepdims=True)
    gskip_ref[...] += jnp.sum(dy_ref[0] * conv_ref[0].astype(f32), axis=0, keepdims=True)
    gdt_proj_ref[...] += rows_dot(proj_ref[0:rank, :].astype(bf16), low)
    gproj_ref[0:rank, :] = outer_dot(dt_proj_ref[...], low)
    gproj_ref[rank : rank + n, :] = sums[0] - 2.0 * keys * (sums[1] + self_term)
    gproj_ref[rank + n :, :] = sums[2]


def specs_for(length, reverse):
    blocks = length // BLOCK

    def place(b):
        return blocks - 1 - b if reverse else b

    def spec(*shape):
        return pl.BlockSpec((1,) + shape, lambda s, b: (s, place(b)) + (0,) * (len(shape) - 1))

    def across_spec(rows):
        return pl.BlockSpec((rows, BLOCK), lambda s, b: (0, s * blocks + place(b)))

    def whole(*shape):
        return pl.BlockSpec(shape, lambda s, b: (0,) * len(shape))

    return blocks, spec, across_spec, whole


def recurrence_forward(conv, z, proj, keep_lanes, dt_proj, dt_bias, skip):
    seqs, length, width = conv.shape
    rank = dt_proj.shape[0]
    n = (proj.shape[0] - rank) // 2
    blocks, spec, across_spec, whole = specs_for(length, False)
    span = CHUNK * n
    wide = spec(BLOCK, width)
    full = jax.ShapeDtypeStruct((seqs, length, width), f32)
    return pl.pallas_call(
        forward_kernel,
        grid=(seqs, blocks),
        in_specs=[
            wide, wide, across_spec(proj.shape[0]), spec(BLOCK, LANES), whole(rank, width), whole(1, width),
            whole(1, width),
        ],
        out_specs=[wide, wide, wide, wide, spec(BLOCK * n, width)],
        out_shape=[
            full, jax.ShapeDtypeStruct((seqs, length, width), bf16),
            pltpu.HBM((seqs, length, width), f32), pltpu.HBM((seqs, length, width), f32),
            pltpu.HBM((seqs, length * n, width), bf16),
        ],
        scratch_shapes=[
            pltpu.VMEM((n, width), f32),
            [pltpu.VMEM((CHUNK, width), f32)] * UNROLL,
            [pltpu.VMEM((CHUNK, width), f32)] * UNROLL,
            [pltpu.VMEM((CHUNK, LANES), f32)] * UNROLL,
            pltpu.VMEM((BLOCK, n), f32),
            [pltpu.VMEM((span, width), f32)] * UNROLL,
        ],
        compiler_params=pltpu.CompilerParams(vmem_limit_bytes=24 << 20),
        cost_estimate=pl.CostEstimate(flops=16_000_000_000, bytes_accessed=24 << 20, transcendentals=0),
        name="recurrence_forward",
    )(conv, z, proj, keep_lanes, dt_proj, dt_bias, skip)


def recurrence_backward(rate, beta, conv, dy, proj, keep_lanes, dt_proj, states):
    seqs, length, width = rate.shape
    rank = dt_proj.shape[0]
    n = (proj.shape[0] - rank) // 2
    span = CHUNK * n
    blocks, spec, across_spec, whole = specs_for(length, True)
    wide = spec(BLOCK, width)
    before = pl.BlockSpec((1, n, width), lambda s, b: (s, jnp.maximum((blocks - 1 - b) * BLOCK - 1, 0), 0))
    return pl.pallas_call(
        backward_kernel,
        grid=(seqs, blocks),
        in_specs=[
            wide, wide, wide, wide, across_spec(proj.shape[0]), spec(BLOCK, LANES), whole(rank, width),
            spec(BLOCK * n, width), before,
        ],
        out_specs=[wide, wide, across_spec(proj.shape[0]), whole(rank, width), whole(1, width), whole(1, width)],
        out_shape=[
            jax.ShapeDtypeStruct((seqs, length, width), f32),
            jax.ShapeDtypeStruct((seqs, length, width), bf16),
            jax.ShapeDtypeStruct(proj.shape, f32),
            jax.ShapeDtypeStruct((rank, width), f32),
            jax.ShapeDtypeStruct((1, width), f32),
            jax.ShapeDtypeStruct((1, width), f32),
        ],
        scratch_shapes=[
            pltpu.VMEM((n, width), f32),
            pltpu.VMEM((BLOCK, width), f32),
            pltpu.VMEM((CHUNK, width), f32),
            pltpu.VMEM((CHUNK, width), f32),
            pltpu.VMEM((CHUNK, width), f32),
            pltpu.VMEM((CHUNK, LANES), f32),
            pltpu.VMEM((BLOCK, n), f32),
            [pltpu.VMEM((span // PIECES, width), f32)] * PIECES,
            [pltpu.VMEM((span // PIECES, width), f32)] * PIECES,
            pltpu.VMEM((3, n, BLOCK), f32),
        ],
        compiler_params=pltpu.CompilerParams(vmem_limit_bytes=28 << 20),
        cost_estimate=pl.CostEstimate(flops=30_000_000_000, bytes_accessed=28 << 20, transcendentals=0),
        name="recurrence_backward",
    )(rate, beta, conv, dy, proj, keep_lanes, dt_proj, states, states)


def peer(hop):
    me = lax.axis_index("shard")
    core = lax.rem(me, 2)
    chip = me // 2
    if hop & 1:
        core = 1 - core
    if hop & 2:
        chip = 1 - chip
    return chip * 2 + core


def meet_group():
    barrier = pltpu.get_barrier_semaphore()
    for hop in (1, 2, 3):
        pl.semaphore_signal(barrier, inc=1, device_id={"shard": peer(hop)}, device_id_type=MESH)
    pl.semaphore_wait(barrier, 3)


def remote(src, dst, sends, recvs, at, hop):
    return pltpu.make_async_remote_copy(
        src_ref=src, dst_ref=dst, send_sem=sends.at[at], recv_sem=recvs.at[at],
        device_id={"shard": peer(hop)}, device_id_type=MESH,
    )


def group_params(collective_id, limit):
    return pltpu.CompilerParams(collective_id=collective_id, has_side_effects=True, vmem_limit_bytes=limit)


VMEM_SPEC = pl.BlockSpec(memory_space=pltpu.VMEM)


ANY_SPEC = pl.BlockSpec(memory_space=pl.ANY)


def part_copy(src, dst, send, recv, shard):
    return pltpu.make_async_remote_copy(
        src_ref=src, dst_ref=dst, send_sem=send, recv_sem=recv, device_id={"shard": shard}, device_id_type=MESH
    )


def front_kernel(
    x_ref, cot_ref, gain_ref, w_hbm, o_hbm,
    xs_ref, inv_ref, cots_ref, gain_row_ref, own_half_ref, half_ref, parts_ref, own_ref, send_ref, send_more_ref,
    gains_ref, w_ref, o_ref, normed_ref, lhs, mixed, pairs, near, sends, recvs, local, part_sends, part_recvs, part_local,
    pair_sends, pair_recvs, pair_local,
):
    me = lax.axis_index("shard")
    chip = me // 2
    slot = me // 2
    seqs, rows, model = x_ref.shape
    cols = cots_ref.shape[2]
    core = lax.rem(me, 2)
    width = parts_ref.shape[3]
    lift = gain_ref.shape[0]
    span = 2 * rows
    tile = 256
    loads = [
        pltpu.make_async_copy(w_hbm, w_ref, local.at[3]),
        pltpu.make_async_copy(o_hbm, o_ref, local.at[4]),
    ]
    for copy in loads:
        copy.start()
    meet([quad(1), quad(2)])

    def mine(ref, owner):
        return ref.at[:, pl.ds(pl.multiple_of(owner * rows, 16), rows), :]

    def part(owner):
        return cot_ref.at[:, :, pl.ds(pl.multiple_of(owner * cols, 128), cols)]

    def gain_rows(owner):
        return gains_ref.at[pl.ds(pl.multiple_of(owner * lift, 8), lift), :]

    gain_sends = [remote(gain_ref, gain_rows(me), sends, recvs, 5 + hop, hop) for hop in (1, 2, 3)]
    x_core = remote(x_ref, mine(xs_ref, me), sends, recvs, 0, 1)
    x_chip = remote(x_ref, mine(xs_ref, me), sends, recvs, 1, 2)
    cot_sends = [remote(part(peer(hop)), mine(cots_ref, me), sends, recvs, 2 + hop, hop) for hop in (1, 2, 3)]
    for copy in gain_sends + [x_core, x_chip] + cot_sends:
        copy.start()
    own = [
        pltpu.make_async_copy(x_ref, mine(xs_ref, me), local.at[0]),
        pltpu.make_async_copy(part(me), mine(cots_ref, me), local.at[1]),
        pltpu.make_async_copy(gain_ref, gain_rows(me), local.at[2]),
    ]
    for copy in own:
        copy.start()
    for copy in own:
        copy.wait()
    for copy in gain_sends:
        copy.wait()
    x_core.wait()
    gain = jnp.concatenate([gains_ref[lift * d : lift * d + 1, :] for d in range(4)], axis=1)
    gain_row_ref[...] = jnp.broadcast_to(gain, gain_row_ref.shape)
    loads[0].wait()

    def piece(half, i):
        where = jnp.bitwise_xor(chip, half)
        return parts_ref.at[slot, :, pl.ds(pl.multiple_of(where * span, 16), span), :]

    def away(i):
        return lax.rem(2 * me + i, 4) != me

    def send(half, i):
        return part_copy(
            mixed.at[half, i], piece(half, i), part_sends.at[2 * half + i], part_recvs.at[2 * slot + half],
            lax.rem(2 * me + i, 4),
        )

    def keep(half, i):
        return pltpu.make_async_copy(mixed.at[half, i], piece(half, i), part_local.at[half])

    def either(i, yes, no):
        pl.when(away(i))(yes)
        pl.when(jnp.logical_not(away(i)))(no)

    def run_half(half):
        where = jnp.bitwise_xor(chip, half) * span

        for seq in range(seqs):

            def norm(r, carry, seq=seq):
                at = pl.ds(pl.multiple_of(where + r * 16, 16), 16)
                vals = xs_ref[seq, at, :].astype(f32)
                inv = lax.rsqrt(jnp.mean(vals * vals, axis=1, keepdims=True) + EPS)
                inv_ref[seq, at, :] = jnp.broadcast_to(inv, (16, LANES))
                out = (vals * inv * gain).astype(bf16)
                normed_ref[seq, at, :] = out
                lhs[pl.ds(pl.multiple_of(seq * span + r * 16, 16), 16), :] = out
                return carry

            lax.fori_loop(0, span // 16, norm, 0)
        for copy in normed_copies(half):
            copy.start()
        for i in range(2):

            def product(t, carry, i=i):
                value = rows_dot(lhs[...], w_ref[:, pl.ds(pl.multiple_of(i * width + t * tile, tile), tile)])
                for seq in range(seqs):
                    mixed[half, i, seq, :, pl.ds(pl.multiple_of(t * tile, tile), tile)] = value[
                        seq * span : (seq + 1) * span
                    ].astype(bf16)
                return carry

            lax.fori_loop(0, width // tile, product, 0)
            either(i, lambda i=i: send(half, i).start(), lambda i=i: keep(half, i).start())

    def normed_copies(half):
        where = pl.ds(pl.multiple_of(jnp.bitwise_xor(chip, half) * span, 16), span)
        src = normed_ref.at[:, where, pl.ds(pl.multiple_of(core * (model // 2), LANES), model // 2)]
        copies = [pltpu.make_async_copy(src, own_half_ref.at[:, where, :], pair_local.at[half])]
        for hop in (1, 2):
            at = 2 * half + hop - 1
            copies.append(across(src, half_ref.at[hop - 1, :, where, :], pair_sends, pair_recvs, at, quad(hop)))
        return copies

    run_half(0)
    x_chip.wait_recv()
    onward = remote(mine(xs_ref, peer(2)), mine(xs_ref, peer(2)), sends, recvs, 2, 1)
    onward.start()
    onward.wait()
    run_half(1)

    for copy in cot_sends:
        copy.wait()
    loads[1].wait()

    def partial(block, t):
        return outer_dot(
            cots_ref[...].reshape(seqs * 4 * rows, cols),
            o_ref[pl.ds(pl.multiple_of(block * width + t * tile, tile), tile), :],
        )

    def lanes(t):
        return pl.ds(pl.multiple_of(t * tile, tile), tile)

    near_sends = []
    for at, hop in enumerate((3, 1)):

        def fill(t, carry, at=at, hop=hop):
            pairs[at, :, lanes(t)] = partial(peer(hop), t).astype(bf16)
            return carry

        lax.fori_loop(0, width // tile, fill, 0)
        copy = remote(pairs.at[at], near.at[at], sends, recvs, 9 + at, 1)
        copy.start()
        near_sends.append(copy)
    near_sends[0].wait()

    pieces = width // tile // 2
    for first, ref in ((0, send_ref), (pieces, send_more_ref)):

        def to_send(t, carry, first=first, ref=ref):
            ref[:, lanes(t)] = (
                partial(peer(2), first + t) + near[0, :, lanes(first + t)].astype(f32)
            ).astype(bf16)
            return carry

        lax.fori_loop(0, pieces, to_send, 0)
    near_sends[1].wait()

    def to_own(t, carry):
        own_ref[:, lanes(t)] = partial(me, t) + near[1, :, lanes(t)].astype(f32)
        return carry

    lax.fori_loop(0, width // tile, to_own, 0)

    x_chip.wait_send()
    for copy in normed_copies(0) + normed_copies(1):
        copy.wait()
    for half in range(2):
        for i in range(2):
            either(i, lambda half=half, i=i: send(half, i).wait_send(), lambda half=half, i=i: keep(half, i).wait())
        for at in range(2):

            @pl.when(2 * at + me // 2 != me)
            def _(at=at, half=half):
                part_copy(
                    mixed.at[0, 0], mixed.at[0, 0], part_sends.at[0], part_recvs.at[2 * at + half], peer(1)
                ).wait_recv()


def front(x, cot, gain, w_in, out_proj):
    seqs, rows, model = x.shape
    group = lax.axis_size("shard")
    length = rows * group
    cols = model // group
    width = w_in.shape[1] // 2
    tokens = seqs * length
    lifted = jnp.broadcast_to(gain.astype(f32)[None], (8, gain.shape[0]))
    far_sems = pltpu.SemaphoreType.DMA((4,))
    return pl.pallas_call(
        front_kernel,
        in_specs=[VMEM_SPEC] * 3 + [ANY_SPEC] * 2,
        out_specs=[VMEM_SPEC] * 10,
        out_shape=[
            jax.ShapeDtypeStruct((seqs, length, model), bf16),
            jax.ShapeDtypeStruct((seqs, length, LANES), f32),
            jax.ShapeDtypeStruct((seqs, length, cols), bf16),
            jax.ShapeDtypeStruct((8, model), f32),
            jax.ShapeDtypeStruct((seqs, length, model // 2), bf16),
            jax.ShapeDtypeStruct((2, seqs, length, model // 2), bf16),
            jax.ShapeDtypeStruct((2, seqs, length, width), bf16),
            jax.ShapeDtypeStruct((tokens, width), f32),
            jax.ShapeDtypeStruct((tokens, width // 2), bf16),
            jax.ShapeDtypeStruct((tokens, width // 2), bf16),
        ],
        scratch_shapes=[
            pltpu.VMEM((8 * group, gain.shape[0]), f32),
            pltpu.VMEM(w_in.shape, bf16),
            pltpu.VMEM(out_proj.shape, bf16),
            pltpu.VMEM((seqs, length, model), bf16),
            pltpu.VMEM((tokens // 2, model), bf16),
            pltpu.VMEM((2, 2, seqs, 2 * rows, width), bf16),
            pltpu.VMEM((2, tokens, width), bf16),
            pltpu.VMEM((2, tokens, width), bf16),
            pltpu.SemaphoreType.DMA((11,)), pltpu.SemaphoreType.DMA((11,)), pltpu.SemaphoreType.DMA((5,)),
            pltpu.SemaphoreType.DMA((4,)), pltpu.SemaphoreType.DMA((4,)), pltpu.SemaphoreType.DMA((2,)),
            far_sems, far_sems, far_sems,
        ],
        compiler_params=group_params(1, 48 << 20),
        name="front",
    )(x, cot, lifted, w_in, out_proj)


def quad(hop):
    home = lax.axis_index("replica")
    if hop & 1:
        home = home + 1 - 2 * lax.rem(home, 2)
    if hop & 2:
        home = home + 2 - 4 * lax.rem(home // 2, 2)
    return home


def across(src, dst, sends, recvs, at, other):
    return pltpu.make_async_remote_copy(
        src_ref=src, dst_ref=dst, send_sem=sends.at[at], recv_sem=recvs.at[at],
        device_id={"replica": other}, device_id_type=MESH,
    )


def meet(replicas):
    barrier = pltpu.get_barrier_semaphore()
    for hop in (1, 2, 3):
        pl.semaphore_signal(barrier, inc=1, device_id={"shard": peer(hop)}, device_id_type=MESH)
    for other in replicas:
        pl.semaphore_signal(barrier, inc=1, device_id={"replica": other}, device_id_type=MESH)
    pl.semaphore_wait(barrier, 3 + len(replicas))


def ahead(step):
    count = lax.axis_size("replica")
    return lax.rem(lax.axis_index("replica") + step, count)


def collect_kernel(
    keep_ref, give_ref, gz_ref, own_half_ref, half_ref, last_ref,
    keeps_ref, gives_ref, gz_ref4, norm_ref, got_ref,
    sends, recvs, local,
):
    me = lax.axis_index("shard")
    half = keep_ref.shape[1]
    core = lax.rem(me, 2)
    member = lax.rem(lax.axis_index("replica"), 4)
    part = gz_ref4.shape[2]
    meet([quad(hop) for hop in (1, 2, 3)])

    def quarter(which):
        return gz_ref.at[:, pl.ds(pl.multiple_of(which * part, LANES), part)]

    def spot(ref, owner):
        return ref.at[:, pl.ds(pl.multiple_of(owner * half, 128), half)]

    k_chip = remote(keep_ref, spot(keeps_ref, me), sends, recvs, 0, 2)
    v_chip = remote(give_ref, spot(gives_ref, me), sends, recvs, 1, 2)
    k_core = remote(keep_ref, spot(keeps_ref, me), sends, recvs, 2, 1)
    v_core = remote(give_ref, spot(gives_ref, me), sends, recvs, 3, 1)
    quads = [
        across(quarter(lax.rem(quad(hop), 4)), gz_ref4.at[hop], sends, recvs, 6 + hop, quad(hop)) for hop in (3, 1, 2)
    ]
    give_pair = across(give_ref, got_ref, sends, recvs, 11, quad(1))
    norms = [
        remote(own_half_ref, norm_ref.at[core, 0], sends, recvs, 12, 1),
        remote(half_ref, norm_ref.at[core, 1:3], sends, recvs, 10, 1),
        remote(last_ref, norm_ref.at[core, 3], sends, recvs, 4, 1),
    ]
    own = [
        pltpu.make_async_copy(keep_ref, spot(keeps_ref, me), local.at[0]),
        pltpu.make_async_copy(give_ref, spot(gives_ref, me), local.at[1]),
        pltpu.make_async_copy(quarter(member), gz_ref4.at[0], local.at[2]),
        pltpu.make_async_copy(own_half_ref, norm_ref.at[core, 0], local.at[5]),
        pltpu.make_async_copy(half_ref, norm_ref.at[core, 1:3], local.at[3]),
        pltpu.make_async_copy(last_ref, norm_ref.at[core, 3], local.at[4]),
    ]
    for copy in [k_chip, v_chip] + quads + [give_pair, k_core, v_core] + norms + own:
        copy.start()
    k_chip.wait_recv()
    k_on = remote(spot(keeps_ref, peer(2)), spot(keeps_ref, peer(2)), sends, recvs, 5, 1)
    k_on.start()
    v_chip.wait_recv()
    v_on = remote(spot(gives_ref, peer(2)), spot(gives_ref, peer(2)), sends, recvs, 6, 1)
    v_on.start()
    for copy in own + quads + norms + [give_pair, k_core, v_core, k_on, v_on]:
        copy.wait()
    k_chip.wait_send()
    v_chip.wait_send()


def cost(microseconds):
    return pl.CostEstimate(flops=int(microseconds * 1e9), bytes_accessed=1 << 20, transcendentals=0)


def collect(keep, give, grad_z, own_half, half_norm, last_norm):
    tokens, half = keep.shape
    group = lax.axis_size("shard")
    wide = jax.ShapeDtypeStruct((tokens, half * group), bf16)
    return pl.pallas_call(
        collect_kernel,
        in_specs=[VMEM_SPEC] * 6,
        out_specs=[VMEM_SPEC] * 3 + [ANY_SPEC, VMEM_SPEC],
        out_shape=[
            wide, wide, jax.ShapeDtypeStruct((4, tokens, grad_z.shape[1] // 4), bf16),
            pltpu.HBM((2, 4) + last_norm.shape, bf16),
            jax.ShapeDtypeStruct(give.shape, bf16),
        ],
        scratch_shapes=[
            pltpu.SemaphoreType.DMA((13,)), pltpu.SemaphoreType.DMA((13,)), pltpu.SemaphoreType.DMA((6,)),
        ],
        compiler_params=group_params(6, 28 << 20),
        cost_estimate=cost(25),
        name="collect",
    )(keep, give, grad_z, own_half, half_norm, last_norm)


def middle_kernel(
    keeps_ref, gives_ref, got_ref, z_ref, x_hbm, o_hbm,
    both_ref, out_ref, wz_ref,
    z_got_ref, o_ref, xcol, outs, sends, recvs, far_sends, far_recvs, local, o_local,
):
    me = lax.axis_index("shard")
    side = lax.rem(lax.axis_index("replica"), 2)
    tokens, half = got_ref.shape
    gots_ref = both_ref.at[1]
    seqs, rows, _ = out_ref.shape
    cols = xcol.shape[1]
    piece = o_hbm.shape[0] // lax.axis_size("replica")
    per = half // piece
    loads = []
    for d in range(4):
        for q in range(2):
            for j in range(per):
                at = d * 2 * half + (2 * j) * piece + (side if q == 0 else 1 - side) * piece
                loads.append(
                    pltpu.make_async_copy(
                        o_hbm.at[pl.ds(pl.multiple_of(at, piece), piece), :],
                        o_ref.at[q, pl.ds(d * half + j * piece, piece), :],
                        o_local.at[len(loads)],
                    )
                )
    for copy in loads:
        copy.start()
    fetch = pltpu.make_async_copy(
        x_hbm.at[:, pl.ds(pl.multiple_of(me * cols, 128), cols)], xcol, local.at[0]
    )
    fetch.start()
    home = lax.axis_index("replica")
    count = lax.axis_size("replica")
    meet([ahead(step) for step in range(1, count)])

    def spot(owner):
        return gots_ref.at[:, pl.ds(pl.multiple_of(owner * half, 128), half)]

    g_own = pltpu.make_async_copy(got_ref, spot(me), local.at[2])
    g_chip = remote(got_ref, spot(me), sends, recvs, 0, 2)
    g_core = remote(got_ref, spot(me), sends, recvs, 1, 1)
    own = [
        pltpu.make_async_copy(keeps_ref, both_ref.at[0], local.at[1]),
    ]
    own.append(pltpu.make_async_copy(z_ref.at[home], z_got_ref.at[home], local.at[3 + seqs]))
    z_sends = [
        across(z_ref.at[ahead(step)], z_got_ref.at[home], far_sends, far_recvs, step, ahead(step))
        for step in range(1, count)
    ]
    own.append(g_own)
    for copy in [g_chip] + z_sends + [g_core] + own:
        copy.start()
    for copy in loads + [fetch]:
        copy.wait()
    tile = 256

    def product(t, carry):
        rows_at = pl.ds(pl.multiple_of(t * tile, tile), tile)
        value = (
            xcol[rows_at, :].astype(f32)
            + rows_dot(keeps_ref[rows_at, :], o_ref[0])
            + rows_dot(gives_ref[rows_at, :], o_ref[1])
        )
        outs[rows_at, :] = value.astype(bf16)
        return carry

    lax.fori_loop(0, tokens // tile, product, 0)
    length = tokens // seqs
    out_sends = []
    for seq in range(seqs):
        for n_hop, hop in enumerate((2, 3, 1)):
            src = outs.at[pl.ds(pl.multiple_of(seq * length + peer(hop) * rows, 16), rows), :]
            dst = out_ref.at[seq, :, pl.ds(pl.multiple_of(me * cols, 128), cols)]
            out_sends.append(remote(src, dst, sends, recvs, 2 + seq * 3 + n_hop, hop))
        own.append(
            pltpu.make_async_copy(
                outs.at[pl.ds(pl.multiple_of(seq * length + me * rows, 16), rows), :],
                out_ref.at[seq, :, pl.ds(pl.multiple_of(me * cols, 128), cols)],
                local.at[3 + seq],
            )
        )
        own[-1].start()
    for copy in out_sends:
        copy.start()
    base = 2 + seqs * 3
    g_chip.wait_recv()
    g_on = remote(spot(peer(2)), spot(peer(2)), sends, recvs, base + 2, 1)
    g_on.start()
    for copy in out_sends + [g_on, g_core] + own + z_sends:
        copy.wait()
    g_chip.wait_send()
    quarter = z_got_ref.shape[2]
    for q in range(4):
        total = z_got_ref[q].astype(f32)
        for group in range(1, count // 4):
            total = total + z_got_ref[4 * group + q].astype(f32)
        wz_ref[:, q * quarter : (q + 1) * quarter] = total.astype(bf16)


def middle(keeps, gives, got, z_blocks, x_all, out_proj, seqs):
    tokens, half = got.shape
    group = lax.axis_size("shard")
    model = x_all.shape[1]
    cols = model // group
    far_sems = pltpu.SemaphoreType.DMA((lax.axis_size("replica"),))
    pieces = 8 * max(1, half * lax.axis_size("replica") // out_proj.shape[0])
    return pl.pallas_call(
        middle_kernel,
        in_specs=[VMEM_SPEC] * 4 + [ANY_SPEC] * 2,
        out_specs=[VMEM_SPEC] * 3,
        out_shape=[
            jax.ShapeDtypeStruct((2, tokens, half * group), bf16),
            jax.ShapeDtypeStruct((seqs, tokens // seqs // group, model), bf16),
            jax.ShapeDtypeStruct((z_blocks.shape[1], 4 * z_blocks.shape[2]), bf16),
        ],
        scratch_shapes=[
            pltpu.VMEM(z_blocks.shape, bf16),
            pltpu.VMEM((2, half * group, cols), bf16),
            pltpu.VMEM((tokens, cols), bf16),
            pltpu.VMEM((tokens, cols), bf16),
            pltpu.SemaphoreType.DMA((5 + 3 * seqs,)), pltpu.SemaphoreType.DMA((5 + 3 * seqs,)),
            far_sems, far_sems, pltpu.SemaphoreType.DMA((4 + seqs,)), pltpu.SemaphoreType.DMA((pieces,)),
        ],
        compiler_params=group_params(7, 22 << 20),
        cost_estimate=cost(25),
        name="middle",
    )(keeps, gives, got, z_blocks, x_all, out_proj)


PARTS = 2


def finish_kernel(
    gx_ref, gz_ref, small_keep_ref, small_give_ref, wz_ref, norm_hbm, w_hbm, x_ref, cot_ref, gain_ref, xs_ref, inv_ref,
    gw_ref, gxp_ref, gdp_ref, gcw_ref, gcb_ref, gdb_ref, gsk_ref, dx_ref, ggain_ref,
    small_ref, norm_ref, w_ref, gx4, cols_ref, turned, xb_ref, sb_ref, small_got, x_in, s_in, lhs, pairs, near, g_hold, g_own, g_send, g_far,
    h_send, h_cols, z_cols, s_own, gains, gain_near, gain_sum, gain_in, unit_x,
    sends, recvs, far_sends, far_recvs, home_sends, home_recvs, local,
):
    me = lax.axis_index("shard")
    home = lax.axis_index("replica")
    count = lax.axis_size("replica")
    height = count // 2
    mine = home // 2
    side = lax.rem(home, 2)
    seqs, rows, model = x_ref.shape
    tokens, width = gx_ref.shape
    length = tokens // seqs
    deep = wz_ref.shape[0]
    member = lax.rem(home, 4)
    quarter = width // 4
    part = quarter // PARTS
    tile = 256
    other = quad(1)
    load = pltpu.make_async_copy(w_hbm, w_ref, local.at[0])
    load_norm = pltpu.make_async_copy(norm_hbm, norm_ref, local.at[1])
    load_norm.start()
    load.start()
    meet([ahead(step) for step in range(1, count)])

    def far(step):
        return ahead(2 * step)

    def cut(p):
        return slice(p * part, (p + 1) * part)

    def piece_of(which, p):
        return gx_ref.at[:, pl.ds(pl.multiple_of(which * quarter + p * part, LANES), part)]

    def spot_of(hop, p):
        return gx4.at[hop * tokens : (hop + 1) * tokens, cut(p)]

    def quad_sends(p):
        return [
            across(piece_of(lax.rem(quad(hop), 4), p), spot_of(hop, p), sends, recvs, 3 * p + hop - 1, quad(hop))
            for hop in (3, 1, 2)
        ]

    small_send = across(small_give_ref, small_got, sends, recvs, 3 * PARTS, other)
    quad_own = [
        pltpu.make_async_copy(piece_of(member, p), spot_of(0, p), local.at[PARTS + 3 + 2 * seqs + p]) for p in range(PARTS)
    ]
    for copy in quad_sends(0) + [small_send] + quad_sends(1) + quad_own:
        copy.start()

    def goal(slot):
        return (4 * slot + me) // 2

    spot = pl.ds(pl.multiple_of(lax.rem(me, 2) * width, LANES), width)

    def home_pieces(at):
        if at == PARTS:
            return 1, wz_ref, z_cols.at[:, spot]
        if at > PARTS:
            slot, seq = (at - PARTS - 1) % 2, (at - PARTS - 1) // 2
            some = slice(seq * length, (seq + 1) * length)
            return slot, (gx_ref, gz_ref)[slot].at[some], cols_ref.at[some, spot]
        some = 4 * part
        return 0, h_send.at[at], h_cols.at[at, :, pl.ds(pl.multiple_of(lax.rem(me, 2) * some, LANES), some)]

    def home_send(at):
        slot, src, dst = home_pieces(at)
        return part_copy(src, dst, home_sends.at[at], home_recvs.at[at * 2 + lax.rem(me, 2)], goal(slot))

    def home_keep(at):
        _, src, dst = home_pieces(at)
        return pltpu.make_async_copy(src, dst, local.at[2 + at])

    def home_start(at):
        slot = home_pieces(at)[0]
        pl.when(goal(slot) != me)(lambda: home_send(at).start())
        pl.when(goal(slot) == me)(lambda: home_keep(at).start())

    def home_wait(at):
        slot = home_pieces(at)[0]
        pl.when(goal(slot) != me)(lambda: home_send(at).wait_send())
        pl.when(goal(slot) == me)(lambda: home_keep(at).wait())
        for place in range(2):
            source = lax.rem(2 * me + place, 4)

            @pl.when((me // 2 == slot) & (source != me))
            def _(place=place):
                src = home_pieces(at)[1]
                part_copy(src, src, home_sends.at[at], home_recvs.at[at * 2 + place], peer(1)).wait_recv()

    for at in (*range(PARTS + 1, PARTS + 1 + 2 * seqs), PARTS):
        home_start(at)

    def far_copy(src, dst, kind, step):
        return across(src, dst, far_sends, far_recvs, kind * count + step, far(step))

    def block(step):
        return lax.rem(mine + step, height)

    order = range(1, height)

    def lines(at):
        return pl.ds(pl.multiple_of(at * deep, 16), deep)

    def x_sends(p):
        return [
            across(
                xb_ref.at[lines(ahead(step)), cut(p)], x_in.at[home, :, cut(p)], far_sends, far_recvs,
                p * count + step, ahead(step),
            )
            for step in range(1, count)
        ]

    def x_part(p):
        for copy in quad_sends(p):
            copy.wait_recv()
        quad_own[p].wait()

        for at in range(0, 4 * tokens, tile):
            turned[:, at : at + tile] = gx4[at : at + tile, cut(p)].T
        wide = norm_ref.shape[2] // tile

        def rows_of(t, carry):
            feature = pl.ds(pl.multiple_of(lax.rem(t, wide) * tile, tile), tile)
            value = rows_dot(turned[...], norm_ref[t // wide, :, feature])
            xb_ref[pl.ds(pl.multiple_of(t * tile, tile), tile), cut(p)] = value.astype(bf16).T
            return carry

        lax.fori_loop(0, xb_ref.shape[0] // tile, rows_of, 0)
        x_in[home, :, cut(p)] = xb_ref[lines(home), cut(p)]
        for copy in x_sends(p):
            copy.start()

    def lanes(t):
        return pl.ds(pl.multiple_of(t * tile, tile), tile)

    def near_send(seq):
        return remote(pairs.at[seq], near.at[seq], sends, recvs, 3 * PARTS + 8 + 2 * seq, 1)

    def chip_send(seq):
        return remote(g_send.at[seq], g_far.at[seq], sends, recvs, 3 * PARTS + 9 + 2 * seq, 2)

    def grads_of(seq):
        home_wait(PARTS + 1 + 2 * seq)
        home_wait(PARTS + 2 + 2 * seq)
        for i, owner in enumerate((peer(3), peer(1), peer(2), me)):
            at = pl.ds(pl.multiple_of(seq * length + owner * rows, 16), rows)
            lhs[i * rows : (i + 1) * rows, :] = cols_ref[at, :]
            here = pl.ds(pl.multiple_of(owner * rows, 16), rows)
            inv = inv_ref[seq, here, :]
            for low in range(0, model, LANES):
                unit_x[i * rows : (i + 1) * rows, low : low + LANES] = xs_ref[seq, here, low : low + LANES].astype(f32) * inv

        def product(t, carry):
            value = outer_dot(lhs[...], w_ref[lanes(t), :])
            pairs[seq, :, lanes(t)] = value[: 2 * rows].astype(bf16)
            g_hold[:, lanes(t)] = value[2 * rows : 3 * rows]
            g_own[seq, :, lanes(t)] = value[3 * rows :]
            terms = value * unit_x[:, lanes(t)]
            gains[:, lanes(t)] += jnp.sum(terms.reshape(rows // 2, 8, tile), axis=0)
            return carry

        lax.fori_loop(0, model // tile, product, 0)
        near_send(seq).start()

    def grads_on(seq):
        near_send(seq).wait()
        for low in range(0, model, tile):
            at = slice(low, low + tile)
            g_send[seq, :, at] = (g_hold[:, at] + near[seq, :rows, at].astype(f32)).astype(bf16)
            g_own[seq, :, at] += near[seq, rows:, at].astype(f32)
        chip_send(seq).start()

    def home_sum(p):
        for copy in x_sends(p):
            copy.wait_recv()
        for q in range(4):
            total = x_in[q, :, cut(p)].astype(f32)
            for group in range(1, count // 4):
                total = total + x_in[4 * group + q, :, cut(p)].astype(f32)
            h_send[p, :, q * part : (q + 1) * part] = total.astype(bf16)
        home_start(p)

    gains[...] = jnp.zeros_like(gains)
    load_norm.wait()
    x_part(0)
    load.wait()
    grads_of(0)
    small_send.wait_recv()
    for at in range(height):
        sb_ref[at] = (small_keep_ref[at] + small_got[at].astype(f32)).astype(bf16)
    s_sends = [far_copy(sb_ref.at[block(step)], s_in.at[step - 1], PARTS, step) for step in order]
    for copy in s_sends:
        copy.start()
    grads_on(0)
    x_part(1)
    grads_of(1)
    wide = model // 4

    def gain_part(owner):
        return gains.at[:, pl.ds(pl.multiple_of(owner * wide, LANES), wide)]

    gain_sends = [
        remote(gain_part(peer(hop)), gain_near.at[hop - 1], sends, recvs, 3 * PARTS + 2 + hop, hop) for hop in (1, 2, 3)
    ]
    for copy in gain_sends:
        copy.start()
    for copy in s_sends:
        copy.wait_recv()
    total = sb_ref[mine].astype(f32)
    for step in order:
        total = total + s_in[step - 1].astype(f32)
    s_own[...] = total.astype(bf16)
    small_ref[side, mine] = s_own[...]
    spread = [far_copy(s_own, small_ref.at[side, mine], PARTS + 1, step) for step in order]
    for copy in spread:
        copy.start()

    def pass_on(step):
        at = lax.rem(mine + height - step, height)
        return across(
            small_ref.at[side, at], small_ref.at[side, at], far_sends, far_recvs, (PARTS + 3) * count + step, other
        )

    pass_on(0).start()
    home_sum(0)
    grads_on(1)
    for copy in gain_sends:
        copy.wait()
    gain_sum[...] = gains[:, pl.ds(pl.multiple_of(me * wide, LANES), wide)] + gain_near[0] + gain_near[1] + gain_near[2]
    gain_far = [
        across(gain_sum, gain_in.at[step - 1], far_sends, far_recvs, (PARTS + 2) * count + step, ahead(step))
        for step in range(1, count)
    ]
    for copy in gain_far:
        copy.start()


    def finish_rows(seq):
        chip_send(seq).wait()

        def last(r, carry):
            at = pl.ds(pl.multiple_of(r * 16, 16), 16)
            grad = g_own[seq, at, :] + g_far[seq, at, :].astype(f32)
            vals = x_ref[seq, at, :].astype(f32)
            inv = lax.rsqrt(jnp.mean(vals * vals, axis=1, keepdims=True) + EPS)
            scaled = grad * gain_ref[0:1, :]
            mean = jnp.mean(scaled * vals, axis=1, keepdims=True)
            out = inv * (scaled - vals * (inv * inv * mean))
            dx_ref[seq, at, :] = (cot_ref[seq, at, :].astype(f32) + out).astype(bf16)
            return carry

        lax.fori_loop(0, rows // 16, last, 0)

    finish_rows(0)
    home_sum(1)
    for step in order:
        spread[step - 1].wait_recv()
        pass_on(step).start()
    finish_rows(1)
    for at in range(PARTS + 1):
        home_wait(at)

    @pl.when(me // 2 == 0)
    def _():
        for place in range(2):
            for q in range(4):
                for p in range(PARTS):
                    to = place * width + q * quarter + p * part
                    low = (place * 4 + q) * part
                    gw_ref[:, to : to + part] = h_cols[p, :, low : low + part].astype(f32)

    @pl.when(me // 2 == 1)
    def _():
        for low in range(0, 2 * width, quarter):
            gw_ref[:, low : low + quarter] = z_cols[:, low : low + quarter].astype(f32)

    for copy in gain_far:
        copy.wait()
    total = gain_sum[...]
    for step in range(1, count):
        total = total + gain_in[step - 1]
    ggain_ref[...] = jnp.broadcast_to(jnp.sum(total, axis=0, keepdims=True), total.shape)
    for step in range(height):
        pass_on(step).wait()
    lined = small_keep_ref.shape[1]
    goals, start = [], 0
    for ref in (gxp_ref, gdp_ref, gcw_ref, gcb_ref, gdb_ref, gsk_ref):
        goals.append((ref, start, start + ref.shape[0]))
        start += ref.shape[0]
    for at in range(count):
        low, high = at * lined, (at + 1) * lined
        if low < start:
            value = small_ref[at % 2, at // 2].astype(f32)
        for ref, begin, stop in goals:
            a, b = max(low, begin), min(high, stop)
            if a < b:
                ref[a - begin : b - begin, :] = value[a - low : b - low]
    small_send.wait_send()
    for p in range(PARTS):
        for copy in quad_sends(p) + x_sends(p):
            copy.wait_send()
    for copy in s_sends + spread:
        copy.wait_send()


def finish(gx, gz, small_keep, small_give, wz, norm, w_in, x, cot, gain, xs, inv, tops):
    tokens, width = gx.shape
    height, lines, _ = small_keep.shape
    deep = wz.shape[0]
    seqs, rows, model = x.shape
    wide = model // 4
    gain_tile = pltpu.VMEM((8, wide), f32)
    other = max(height - 1, 1)
    count = 2 * height
    quarter = width // 4
    kinds = (PARTS + 4) * count
    homes = PARTS + 1 + 2 * seqs
    line = jax.ShapeDtypeStruct((1, width), f32)
    return pl.pallas_call(
        finish_kernel,
        in_specs=[VMEM_SPEC] * 5 + [ANY_SPEC] * 2 + [VMEM_SPEC] * 5,
        out_specs=[VMEM_SPEC] * 9,
        out_shape=[
            jax.ShapeDtypeStruct((deep, 2 * width), f32),
            jax.ShapeDtypeStruct((tops[0], width), f32),
            jax.ShapeDtypeStruct((tops[1], width), f32),
            jax.ShapeDtypeStruct((KW, width), f32),
            line, line, line,
            jax.ShapeDtypeStruct(x.shape, bf16),
            jax.ShapeDtypeStruct((8, wide), f32),
        ],
        scratch_shapes=[
            pltpu.VMEM((2, height, lines, width), bf16),
            pltpu.VMEM(norm.shape, bf16),
            pltpu.VMEM(w_in.shape, bf16),
            pltpu.VMEM((4 * tokens, quarter), bf16),
            pltpu.VMEM((tokens, 2 * width), bf16),
            pltpu.VMEM((quarter // PARTS, 4 * tokens), bf16),
            pltpu.VMEM((count * deep, quarter), bf16),
            pltpu.VMEM((height, lines, width), bf16),
            pltpu.VMEM((height, lines, width), bf16),
            pltpu.VMEM((count, deep, quarter), bf16),
            pltpu.VMEM((other, lines, width), bf16),
            pltpu.VMEM((4 * rows, 2 * width), bf16),
            pltpu.VMEM((seqs, 2 * rows, model), bf16),
            pltpu.VMEM((seqs, 2 * rows, model), bf16),
            pltpu.VMEM((rows, model), f32),
            pltpu.VMEM((seqs, rows, model), f32),
            pltpu.VMEM((seqs, rows, model), bf16),
            pltpu.VMEM((seqs, rows, model), bf16),
            pltpu.VMEM((PARTS, deep, width // PARTS), bf16),
            pltpu.VMEM((PARTS, deep, 2 * width // PARTS), bf16),
            pltpu.VMEM((deep, 2 * width), bf16),
            pltpu.VMEM((lines, width), bf16),
            pltpu.VMEM((8, model), f32),
            pltpu.VMEM((3, 8, wide), f32),
            gain_tile,
            pltpu.VMEM((count - 1, 8, wide), f32),
            pltpu.VMEM((4 * rows, model), f32),
            pltpu.SemaphoreType.DMA((3 * PARTS + 8 + 2 * seqs,)), pltpu.SemaphoreType.DMA((3 * PARTS + 8 + 2 * seqs,)),
            pltpu.SemaphoreType.DMA((kinds,)), pltpu.SemaphoreType.DMA((kinds,)),
            pltpu.SemaphoreType.DMA((homes,)), pltpu.SemaphoreType.DMA((2 * homes,)),
            pltpu.SemaphoreType.DMA((homes + 2 + PARTS,)),
        ],
        compiler_params=group_params(8, 58 << 20),
        cost_estimate=cost(80),
        name="finish",
    )(gx, gz, small_keep, small_give, wz, norm, w_in, x, cot, gain, xs, inv)


def total_kernel(part_ref, out_ref, near, chip_sum, far, sends, recvs):
    me = lax.axis_index("shard")
    half = part_ref.shape[1] // 2
    mine = pl.ds(pl.multiple_of(lax.rem(me, 2) * half, 128), half)
    other = pl.ds(pl.multiple_of((1 - lax.rem(me, 2)) * half, 128), half)
    meet_group()
    first = remote(part_ref.at[:, other], near, sends, recvs, 0, 1)
    first.start()
    first.wait()
    chip_sum[...] = part_ref[:, mine] + near[...]
    second = remote(chip_sum, far, sends, recvs, 1, 2)
    second.start()
    second.wait()
    out_ref[:, mine] = chip_sum[...] + far[...]
    third = remote(out_ref.at[:, mine], out_ref.at[:, mine], sends, recvs, 2, 1)
    third.start()
    third.wait()


def group_total(part, collective_id):
    rows, cols = part.shape
    half = pltpu.VMEM((rows, cols // 2), f32)
    return pl.pallas_call(
        total_kernel,
        in_specs=[VMEM_SPEC],
        out_specs=VMEM_SPEC,
        out_shape=jax.ShapeDtypeStruct((rows, cols), f32),
        scratch_shapes=[half, half, half, pltpu.SemaphoreType.DMA((3,)), pltpu.SemaphoreType.DMA((3,))],
        compiler_params=group_params(collective_id, 16 << 20),
        name="group_total",
    )(part)


def by_hop(value, hop):
    return lax.ppermute(value, "shard", [(i, i ^ hop) for i in range(4)])


def far_send(blocks):
    count = lax.axis_size("replica")
    height = count // 2
    mine = lax.axis_index("replica") // 2

    def pick(at):
        return lax.dynamic_index_in_dim(blocks, at, 0, False)

    sent = []
    for step in range(1, height):
        out = pick(lax.rem(mine + step, height)).astype(bf16)
        sent.append(lax.ppermute(out, "replica", [(i, (i + 2 * step) % count) for i in range(count)]))
    return pick(mine), tuple(sent)


def far_total(own, sent):
    total = own
    for value in sent:
        total = total + value.astype(f32)
    return total


def after(value, *others):
    return lax.optimization_barrier((value,) + others)[0]


def body(
    block_input, segment_ids, norm_gain, w_in, conv_weight, conv_bias, x_proj, dt_proj, dt_bias,
    d_skip, out_proj, out_grad,
):
    seqs, local, model = block_input.shape
    length = segment_ids.shape[1]
    tokens = seqs * length
    width = d_skip.shape[0]
    rank = dt_proj.shape[0]
    n = (x_proj.shape[0] - rank) // 2
    me = lax.axis_index("shard")
    count = lax.axis_size("replica")
    height = count // 2
    side = lax.rem(lax.axis_index("replica"), 2)

    def split(values):
        return values.reshape(seqs, length, -1)

    def halves(values, blocks):
        piece = values.shape[1] // blocks // 2
        cuts = [values[:, b * piece : (b + 1) * piece] for b in range(2 * blocks)]
        even = jnp.concatenate(cuts[0::2], axis=1)
        odd = jnp.concatenate(cuts[1::2], axis=1)
        return jnp.where(side == 0, even, odd), jnp.where(side == 0, odd, even)

    xs, inv, cots, gain, own_half, half_norm, parts, gated_own, gated_send, gated_more = front(
        block_input, out_grad, norm_gain, w_in, out_proj
    )
    x_all = xs.reshape(tokens, model)
    cot = cots.reshape(tokens, -1)
    x_part, z_part = parts[0], parts[1]

    seg_padded = jnp.pad(segment_ids, ((0, 0), (KW - 1, 0)), constant_values=-1)
    taps = [
        (seg_padded[:, KW - 1 - d : KW - 1 - d + length] == segment_ids).astype(f32) for d in range(KW)
    ]
    conv_w = conv_weight.astype(f32)
    xv = x_part.astype(f32)
    x_padded = jnp.pad(xv, ((0, 0), (KW - 1, 0), (0, 0)))
    conv_pre = conv_bias.astype(f32) + conv_w[KW - 1] * xv
    for j in range(KW - 1):
        d = KW - 1 - j
        conv_pre = conv_pre + conv_w[j] * x_padded[:, j : j + length] * taps[d][:, :, None]
    conv_out = jax.nn.silu(conv_pre).astype(bf16)
    conv_flat = conv_out.reshape(tokens, width)
    half_norm = half_norm.reshape(2, tokens, -1)
    own_half = own_half.reshape(tokens, -1)
    last_norm = lax.ppermute(own_half, "replica", [(i, i ^ 3) for i in range(count)])
    cot_got = lax.ppermute(cot, "replica", [(i, i ^ 1) for i in range(count)])
    proj = group_total(outer_dot(x_proj, conv_flat), 3)
    gated_far = by_hop(gated_send, 2)
    proj, gated_far = lax.optimization_barrier((proj, gated_far))
    gated_rest = by_hop(after(gated_more, proj), 2)
    keep_lanes = jnp.broadcast_to(taps[1][:, :, None], (seqs, length, LANES))
    skip = d_skip.astype(f32)
    y_total, gated, rate, beta, states = recurrence_forward(
        conv_out, z_part, proj, keep_lanes, dt_proj, dt_bias.astype(f32)[None], skip[None]
    )
    y_total, gated, gated_rest, last_norm, cot_got = lax.optimization_barrier(
        (y_total, gated, gated_rest, last_norm, cot_got)
    )
    cot_both = jnp.concatenate([cot, cot_got], axis=0)
    grad_gated = split(gated_own + jnp.concatenate([gated_far, gated_rest], axis=1).astype(f32))
    z_vals = z_part.astype(f32)
    dy = grad_gated * jax.nn.silu(z_vals)
    grad_z = (grad_gated * y_total * silu_slope(z_vals)).astype(bf16).reshape(tokens, width)

    gated_keep, gated_give = halves(gated.reshape(tokens, width), height // 4)
    cols = model // 4
    keeps, gives, grad_z_quad, norms, gated_got = collect(
        gated_keep, gated_give, grad_z, own_half, half_norm, last_norm
    )
    norms = norms.reshape(2, 4 * tokens, -1)
    z_blocks = lax.dot_general(
        norms, grad_z_quad.reshape(4 * tokens, -1), (((1,), (0,)), ((), ())), preferred_element_type=f32
    )
    z_blocks = z_blocks.astype(bf16).reshape(count, -1, width // 4)
    gated_both, block_output, grad_w_z = middle(keeps, gives, gated_got, z_blocks, x_all, out_proj, seqs)
    out_blocks = inner_dot(gated_both.reshape(2 * tokens, -1), cot_both)
    out_own, out_sent = far_send(out_blocks.astype(bf16).reshape(height, -1, cols))
    rate, out_own = lax.optimization_barrier((rate, out_own))

    grad_conv_rec, grad_dt_low, grad_proj, grad_dt_proj, grad_dt_bias, grad_d_skip = recurrence_backward(
        rate, beta, conv_out, dy, proj, keep_lanes, dt_proj, states
    )
    grad_proj, out_sent = lax.optimization_barrier((group_total(grad_proj, 4), out_sent))
    grad_proj = grad_proj.astype(bf16)
    grad_out_proj = far_total(out_own.astype(f32), out_sent)
    grad_x_proj = rows_dot(grad_proj, conv_flat)
    grad_conv = dy * skip + grad_conv_rec + split(inner_dot(grad_proj, x_proj))
    grad_pre = grad_conv * silu_slope(conv_pre)
    grad_conv_bias = jnp.sum(grad_pre, axis=(0, 1))
    grad_conv_weight = jnp.stack(
        [
            jnp.sum(grad_pre * x_padded[:, j : j + length] * taps[KW - 1 - j][:, :, None], axis=(0, 1))
            for j in range(KW)
        ]
    )
    grad_x = conv_w[KW - 1] * grad_pre
    for j in range(KW - 1):
        d = KW - 1 - j
        ahead = jnp.pad(grad_pre * taps[d][:, :, None], ((0, 0), (0, d), (0, 0)))[:, d:]
        grad_x = grad_x + conv_w[j] * ahead
    grad_x = grad_x.astype(bf16).reshape(tokens, width)

    small = jnp.concatenate(
        [grad_x_proj, grad_dt_proj, grad_conv_weight, grad_conv_bias[None], grad_dt_bias, grad_d_skip]
    )
    unit = 8 * count
    padded = -(-small.shape[0] // unit) * unit
    small = jnp.pad(small, ((0, padded - small.shape[0]), (0, 0))).reshape(height, 2, -1, width)
    small_keep = jnp.where(side == 0, small[:, 0], small[:, 1])
    small_give = jnp.where(side == 0, small[:, 1], small[:, 0]).astype(bf16)
    top = x_proj.shape[0]
    grad_w_in, grad_x_proj, grad_dt_proj, grad_conv_weight, conv_line, bias_line, skip_line, input_grad, grad_gain = finish(
        grad_x, grad_z, small_keep, small_give, grad_w_z, norms, w_in, block_input, out_grad, gain, xs, inv,
        (top, rank),
    )
    return (
        block_output, input_grad, grad_gain[0], grad_w_in, grad_conv_weight, conv_line[0], grad_x_proj, grad_dt_proj,
        bias_line[0], skip_line[0], grad_out_proj,
    )


def solution(mesh):
    return jax.shard_map(
        body,
        mesh=mesh,
        in_specs=(
            P("replica", "shard", None), P("replica", None), P("shard"), P(None, "shard"), P(None, "shard"),
            P("shard"), P(None, "shard"), P(None, "shard"), P("shard"), P("shard"), P(None, "shard"),
            P("replica", "shard", None),
        ),
        out_specs=(
            P("replica", "shard", None), P("replica", "shard", None), P("shard"), P("replica", "shard"),
            P(None, "shard"), P("shard"), P(None, "shard"), P(None, "shard"), P("shard"), P("shard"),
            P("replica", "shard"),
        ),
        check_vma=False,
    )
```

```python
import functools

import jax
import jax.numpy as jnp
from jax import lax
from jax.experimental import pallas as pl
from jax.experimental.pallas import tpu as pltpu
from jax.sharding import PartitionSpec as P

KW = 4
EPS = 1e-05
CHUNK = 16
LANES = 128
f32 = jnp.float32
bf16 = jnp.bfloat16


def rows_dot(a, b):
    return jnp.dot(a, b, preferred_element_type=f32)


def inner_dot(a, b):
    return lax.dot_general(a, b, (((0,), (0,)), ((), ())), preferred_element_type=f32)


def outer_dot(a, b):
    return lax.dot_general(a, b, (((1,), (1,)), ((), ())), preferred_element_type=f32)


def silu_slope(values):
    sig_val = jax.nn.sigmoid(values)
    return sig_val + values * sig_val * (1.0 - sig_val)

MESH = pl.DeviceIdType.MESH
BLOCK = 128
UNROLL = 4
BACK_UNROLL = 4


def lane(g):
    return slice(g * LANES, (g + 1) * LANES)


def column(block, t):
    return jnp.broadcast_to(block[:, t : t + 1], (block.shape[0], LANES))


def row(ref, t, g, n):
    return jnp.broadcast_to(ref[t : t + 1, lane(g)], (n, LANES))


def prepare(base, rate_ref, conv_ref, keep_ref, rk, u, kept):
    rows = pl.ds(base, CHUNK)
    rate = rate_ref[0, rows, :]
    keep = keep_ref[0, rows, :]
    conv = conv_ref[0, rows, :].astype(f32)
    for g in range(rate.shape[1] // LANES):
        rk[:, lane(g)] = rate[:, lane(g)] * keep
    u[...] = rate * conv
    kept[...] = keep
    return rate, conv, keep


def shifted(cols, j):
    size = cols.shape[1]
    return pltpu.roll(cols, lax.rem(size - j * CHUNK, size), 1)


def spread_mask(n, size=CHUNK):
    shape = (size, size * n)
    return lax.broadcasted_iota(jnp.int32, shape, 1) // n == lax.broadcasted_iota(jnp.int32, shape, 0)


def picker(n, size=CHUNK):
    shape = (n, size * n)
    return (lax.broadcasted_iota(jnp.int32, shape, 1) % n == lax.broadcasted_iota(jnp.int32, shape, 0)).astype(bf16)


def diagonal(rows, mask, pick):
    return jnp.where(mask, rows_dot(rows.astype(bf16), pick), 0.0).astype(bf16)


def forward_kernel(
    conv_ref, z_ref, proj_ref, keep_ref, dt_proj_ref, dt_bias_ref, skip_ref,
    y_ref, gated_ref, rate_ref, beta_ref, state_ref,
    held_ref, rk, u, kept, query_rows, fresh,
):
    width = conv_ref.shape[2]
    rank = dt_proj_ref.shape[0]
    n = (proj_ref.shape[0] - rank) // 2
    groups = width // LANES
    span = CHUNK * n

    @pl.when(pl.program_id(1) == 0)
    def _():
        held_ref[...] = jnp.zeros_like(held_ref)

    dt_low = proj_ref[0:rank, :].astype(bf16)
    keys = proj_ref[rank : rank + n, :]
    query_rows[...] = proj_ref[rank + n :, :].T
    key_square = jnp.sum(keys.T * keys.T, axis=1, keepdims=True)
    beta = jax.nn.sigmoid(inner_dot(dt_low, dt_proj_ref[...]) + dt_bias_ref[...])
    beta_ref[0] = beta
    rate_ref[0] = beta / (1.0 + beta * key_square)
    mask, pick = spread_mask(n), picker(n)

    def states_of(j, held, rk, u, kept, fresh):
        base = pl.multiple_of(j * CHUNK, CHUNK)
        prepare(base, rate_ref, conv_ref, keep_ref, rk, u, kept)
        near_keys = shifted(keys, j)
        for t in range(CHUNK):
            key = column(near_keys, t)
            key2 = key * key
            keep = jnp.broadcast_to(kept[t : t + 1, :], (n, LANES))
            at = slice(t * n, (t + 1) * n)
            for g in range(groups):
                decay = keep - row(rk, t, g, n) * key2
                held[g] = decay * held[g] + row(u, t, g, n) * key
                fresh[at, lane(g)] = held[g].astype(fresh.dtype)

    def outputs_of(j, fresh):
        base = pl.multiple_of(j * CHUNK, CHUNK)
        rows = pl.ds(base, CHUNK)
        block = fresh[...].astype(bf16)
        state_ref[0, pl.ds(pl.multiple_of(base * n, span), span), :] = block
        conv = conv_ref[0, rows, :].astype(f32)
        total = rows_dot(diagonal(query_rows[rows, :], mask, pick), block) + skip_ref[...] * conv
        y_ref[0, rows, :] = total
        z = z_ref[0, rows, :].astype(f32)
        gated_ref[0, rows, :] = (total * (z * jax.nn.sigmoid(z))).astype(bf16)

    def step(i, held):
        held = list(held)
        for k in range(UNROLL):
            states_of(i * UNROLL + k, held, rk[k], u[k], kept[k], fresh[k])
            if k > 0:
                outputs_of(i * UNROLL + k - 1, fresh[k - 1])
        outputs_of(i * UNROLL + UNROLL - 1, fresh[UNROLL - 1])
        return tuple(held)

    start = tuple(held_ref[:, lane(g)] for g in range(groups))
    end = lax.fori_loop(0, conv_ref.shape[1] // CHUNK // UNROLL, step, start)
    for g in range(groups):
        held_ref[:, lane(g)] = end[g]


def backward_kernel(
    rate_ref, beta_ref, conv_ref, dy_ref, proj_ref, keep_ref, dt_proj_ref, state_ref, last_ref,
    gconv_ref, gdt_ref, gproj_ref, gdt_proj_ref, gdt_bias_ref, gskip_ref,
    held_ref, grate, rk, u, dys, kept, key_rows, adj, adj_state, totals, lined,
):
    block_rows, width = rate_ref.shape[1:]
    rank = dt_proj_ref.shape[0]
    n = (proj_ref.shape[0] - rank) // 2
    groups = width // LANES
    chunks = block_rows // CHUNK

    @pl.when(pl.program_id(1) == 0)
    def _():
        held_ref[...] = jnp.zeros_like(held_ref)

    @pl.when((pl.program_id(0) == 0) & (pl.program_id(1) == 0))
    def _():
        gdt_proj_ref[...] = jnp.zeros_like(gdt_proj_ref)
        gdt_bias_ref[...] = jnp.zeros_like(gdt_bias_ref)
        gskip_ref[...] = jnp.zeros_like(gskip_ref)

    keys = proj_ref[rank : rank + n, :]
    queries = proj_ref[rank + n :, :]
    key_rows[...] = keys.T
    mask, pick = spread_mask(n), picker(n)

    ones = jnp.ones((CHUNK, LANES), bf16)

    def walk(j, held, rk, u, dys, kept, adj, adj_state, totals):
        base = pl.multiple_of(j * CHUNK, CHUNK)
        rows = pl.ds(base, CHUNK)
        prepare(base, rate_ref, conv_ref, keep_ref, rk, u, kept)
        dys[...] = dy_ref[0, rows, :]
        near_keys = shifted(keys, j)
        near_queries = shifted(queries, j)
        late = pl.ds(pl.multiple_of((base + CHUNK - 1) * n, n), n)
        after = [state_ref[0, late, lane(g)] for g in range(groups)]
        for t in reversed(range(CHUNK)):
            own = slice(t * n, (t + 1) * n)
            key = column(near_keys, t)
            key2 = key * key
            query = column(near_queries, t)
            keep = jnp.broadcast_to(kept[t : t + 1, :], (n, LANES))
            prior = jnp.maximum(base + t - 1, 0)
            at = pl.ds(pl.multiple_of(prior * n, n), n)
            parts = [None] * 3
            for g in range(groups):
                slope = row(dys, t, g, n)
                pace = row(rk, t, g, n)
                grad = held[g] + slope * query
                decay = keep - pace * key2
                held[g] = decay * grad
                before = state_ref[0, at, lane(g)]
                if t == 0:
                    before = jnp.where(j == 0, last_ref[0, :, lane(g)], before)
                cross = grad * before.astype(f32)
                adj[own, lane(g)] = grad
                adj_state[own, lane(g)] = cross
                terms = (grad * row(u, t, g, n), cross * pace, after[g].astype(f32) * slope)
                parts = [v if p is None else p + v for p, v in zip(parts, terms)]
                after[g] = before
            for i in range(3):
                totals[i, own, :] = parts[i]

    def settle(j, adj, adj_state, totals):
        base = pl.multiple_of(j * CHUNK, CHUNK)
        rows = pl.ds(base, CHUNK)
        key_block = key_rows[rows, :]
        w1 = rows_dot(diagonal(key_block, mask, pick), adj[...].astype(bf16))
        w2 = rows_dot(diagonal(key_block * key_block, mask, pick), adj_state[...].astype(bf16))
        for i in range(3):
            lined[i, rows, :] = jnp.where(mask, outer_dot(ones, totals[i].astype(bf16)), 0.0)
        keeps = keep_ref[0, rows, :]
        for g in range(groups):
            conv = conv_ref[0, rows, lane(g)].astype(f32)
            grate[rows, lane(g)] = conv * w1[:, lane(g)] - keeps * w2[:, lane(g)]
        gconv_ref[0, rows, :] = rate_ref[0, rows, :] * w1

    def step(i, held):
        held = list(held)
        first = chunks - 1 - i * BACK_UNROLL
        for k in range(BACK_UNROLL):
            walk(first - k, held, rk[k], u[k], dys[k], kept[k], adj[k], adj_state[k], totals[k])
            if k > 0:
                settle(first - k + 1, adj[k - 1], adj_state[k - 1], totals[k - 1])
        last = BACK_UNROLL - 1
        settle(first - last, adj[last], adj_state[last], totals[last])
        return tuple(held)

    start = tuple(held_ref[:, lane(g)] for g in range(groups))
    end = lax.fori_loop(0, chunks // BACK_UNROLL, step, start)
    for g in range(groups):
        held_ref[:, lane(g)] = end[g]

    def picked(left, value):
        high = value.astype(bf16)
        low = (value - high.astype(f32)).astype(bf16)
        return outer_dot(left, high) + outer_dot(left, low)

    rate = rate_ref[0]
    beta = beta_ref[0]
    grad_rate = grate[...]
    self_term = picked(jnp.ones((n, width), bf16), grad_rate * rate * rate)
    key_square = jnp.sum(key_rows[...] * key_rows[...], axis=1, keepdims=True)
    denom_inv = 1.0 / (1.0 + beta * key_square)
    grad_dt = grad_rate * denom_inv * denom_inv * beta * (1.0 - beta)
    low = grad_dt.astype(bf16)
    gdt_ref[0] = low
    gdt_bias_ref[...] += jnp.sum(grad_dt, axis=0, keepdims=True)
    gskip_ref[...] += jnp.sum(dy_ref[0] * conv_ref[0].astype(f32), axis=0, keepdims=True)
    gdt_proj_ref[...] += rows_dot(proj_ref[0:rank, :].astype(bf16), low)
    gproj_ref[0:rank, :] = outer_dot(dt_proj_ref[...], low)
    gproj_ref[rank : rank + n, :] = picked(pick, lined[0]) - 2.0 * keys * (picked(pick, lined[1]) + self_term)
    gproj_ref[rank + n :, :] = picked(pick, lined[2])


def specs_for(length, reverse):
    blocks = length // BLOCK

    def place(b):
        return blocks - 1 - b if reverse else b

    def spec(*shape):
        return pl.BlockSpec((1,) + shape, lambda s, b: (s, place(b)) + (0,) * (len(shape) - 1))

    def across_spec(rows):
        return pl.BlockSpec((rows, BLOCK), lambda s, b: (0, s * blocks + place(b)))

    def whole(*shape):
        return pl.BlockSpec(shape, lambda s, b: (0,) * len(shape))

    return blocks, spec, across_spec, whole


def recurrence_forward(conv, z, proj, keep_lanes, dt_proj, dt_bias, skip):
    seqs, length, width = conv.shape
    rank = dt_proj.shape[0]
    n = (proj.shape[0] - rank) // 2
    blocks, spec, across_spec, whole = specs_for(length, False)
    span = CHUNK * n
    wide = spec(BLOCK, width)
    full = jax.ShapeDtypeStruct((seqs, length, width), f32)
    return pl.pallas_call(
        forward_kernel,
        grid=(seqs, blocks),
        in_specs=[
            wide, wide, across_spec(proj.shape[0]), spec(BLOCK, LANES), whole(rank, width), whole(1, width),
            whole(1, width),
        ],
        out_specs=[wide, wide, wide, wide, spec(BLOCK * n, width)],
        out_shape=[
            full, jax.ShapeDtypeStruct((seqs, length, width), bf16),
            pltpu.HBM((seqs, length, width), f32), pltpu.HBM((seqs, length, width), f32),
            pltpu.HBM((seqs, length * n, width), bf16),
        ],
        scratch_shapes=[
            pltpu.VMEM((n, width), f32),
            [pltpu.VMEM((CHUNK, width), f32)] * UNROLL,
            [pltpu.VMEM((CHUNK, width), f32)] * UNROLL,
            [pltpu.VMEM((CHUNK, LANES), f32)] * UNROLL,
            pltpu.VMEM((BLOCK, n), f32),
            [pltpu.VMEM((span, width), f32)] * UNROLL,
        ],
        compiler_params=pltpu.CompilerParams(vmem_limit_bytes=24 << 20),
        cost_estimate=pl.CostEstimate(flops=16_000_000_000, bytes_accessed=24 << 20, transcendentals=0),
        name="recurrence_forward",
    )(conv, z, proj, keep_lanes, dt_proj, dt_bias, skip)


def recurrence_backward(rate, beta, conv, dy, proj, keep_lanes, dt_proj, states):
    seqs, length, width = rate.shape
    rank = dt_proj.shape[0]
    n = (proj.shape[0] - rank) // 2
    span = CHUNK * n
    blocks, spec, across_spec, whole = specs_for(length, True)
    wide = spec(BLOCK, width)
    before = pl.BlockSpec((1, n, width), lambda s, b: (s, jnp.maximum((blocks - 1 - b) * BLOCK - 1, 0), 0))
    return pl.pallas_call(
        backward_kernel,
        grid=(seqs, blocks),
        in_specs=[
            wide, wide, wide, wide, across_spec(proj.shape[0]), spec(BLOCK, LANES), whole(rank, width),
            spec(BLOCK * n, width), before,
        ],
        out_specs=[wide, wide, across_spec(proj.shape[0]), whole(rank, width), whole(1, width), whole(1, width)],
        out_shape=[
            jax.ShapeDtypeStruct((seqs, length, width), f32),
            jax.ShapeDtypeStruct((seqs, length, width), bf16),
            jax.ShapeDtypeStruct(proj.shape, f32),
            jax.ShapeDtypeStruct((rank, width), f32),
            jax.ShapeDtypeStruct((1, width), f32),
            jax.ShapeDtypeStruct((1, width), f32),
        ],
        scratch_shapes=[
            pltpu.VMEM((n, width), f32),
            pltpu.VMEM((BLOCK, width), f32),
            [pltpu.VMEM((CHUNK, width), f32)] * BACK_UNROLL,
            [pltpu.VMEM((CHUNK, width), f32)] * BACK_UNROLL,
            [pltpu.VMEM((CHUNK, width), f32)] * BACK_UNROLL,
            [pltpu.VMEM((CHUNK, LANES), f32)] * BACK_UNROLL,
            pltpu.VMEM((BLOCK, n), f32),
            [pltpu.VMEM((span, width), f32)] * BACK_UNROLL,
            [pltpu.VMEM((span, width), f32)] * BACK_UNROLL,
            [pltpu.VMEM((3, span, LANES), f32)] * BACK_UNROLL,
            pltpu.VMEM((3, BLOCK, span), f32),
        ],
        compiler_params=pltpu.CompilerParams(vmem_limit_bytes=36 << 20),
        cost_estimate=pl.CostEstimate(flops=30_000_000_000, bytes_accessed=28 << 20, transcendentals=0),
        name="recurrence_backward",
    )(rate, beta, conv, dy, proj, keep_lanes, dt_proj, states, states)


def peer(hop):
    me = lax.axis_index("shard")
    core = lax.rem(me, 2)
    chip = me // 2
    if hop & 1:
        core = 1 - core
    if hop & 2:
        chip = 1 - chip
    return chip * 2 + core


def meet_group():
    barrier = pltpu.get_barrier_semaphore()
    for hop in (1, 2, 3):
        pl.semaphore_signal(barrier, inc=1, device_id={"shard": peer(hop)}, device_id_type=MESH)
    pl.semaphore_wait(barrier, 3)


def remote(src, dst, sends, recvs, at, hop):
    return pltpu.make_async_remote_copy(
        src_ref=src, dst_ref=dst, send_sem=sends.at[at], recv_sem=recvs.at[at],
        device_id={"shard": peer(hop)}, device_id_type=MESH,
    )


def group_params(collective_id, limit):
    return pltpu.CompilerParams(collective_id=collective_id, has_side_effects=True, vmem_limit_bytes=limit)


VMEM_SPEC = pl.BlockSpec(memory_space=pltpu.VMEM)


ANY_SPEC = pl.BlockSpec(memory_space=pl.ANY)


def part_copy(src, dst, send, recv, shard):
    return pltpu.make_async_remote_copy(
        src_ref=src, dst_ref=dst, send_sem=send, recv_sem=recv, device_id={"shard": shard}, device_id_type=MESH
    )


def front_kernel(
    x_ref, cot_ref, gain_ref, w_hbm, o_hbm,
    xs_ref, inv_ref, cots_ref, gain_row_ref, own_half_ref, half_ref, parts_ref, own_ref, send_ref, send_more_ref,
    gains_ref, w_ref, o_ref, normed_ref, lhs, mixed, pairs, near, sends, recvs, local, part_sends, part_recvs, part_local,
    pair_sends, pair_recvs, pair_local,
):
    me = lax.axis_index("shard")
    chip = me // 2
    slot = me // 2
    seqs, rows, model = x_ref.shape
    cols = cots_ref.shape[2]
    core = lax.rem(me, 2)
    width = parts_ref.shape[3]
    lift = gain_ref.shape[0]
    span = 2 * rows
    tile = 256
    loads = [
        pltpu.make_async_copy(w_hbm, w_ref, local.at[3]),
        pltpu.make_async_copy(o_hbm, o_ref, local.at[4]),
    ]
    for copy in loads:
        copy.start()
    meet([quad(1), quad(2)])

    def mine(ref, owner):
        return ref.at[:, pl.ds(pl.multiple_of(owner * rows, 16), rows), :]

    def part(owner):
        return cot_ref.at[:, :, pl.ds(pl.multiple_of(owner * cols, 128), cols)]

    def gain_rows(owner):
        return gains_ref.at[pl.ds(pl.multiple_of(owner * lift, 8), lift), :]

    gain_sends = [remote(gain_ref, gain_rows(me), sends, recvs, 5 + hop, hop) for hop in (1, 2, 3)]
    x_core = remote(x_ref, mine(xs_ref, me), sends, recvs, 0, 1)
    x_chip = remote(x_ref, mine(xs_ref, me), sends, recvs, 1, 2)
    cot_sends = [remote(part(peer(hop)), mine(cots_ref, me), sends, recvs, 2 + hop, hop) for hop in (1, 2, 3)]
    for copy in gain_sends + [x_core, x_chip] + cot_sends:
        copy.start()
    own = [
        pltpu.make_async_copy(x_ref, mine(xs_ref, me), local.at[0]),
        pltpu.make_async_copy(part(me), mine(cots_ref, me), local.at[1]),
        pltpu.make_async_copy(gain_ref, gain_rows(me), local.at[2]),
    ]
    for copy in own:
        copy.start()
    for copy in own:
        copy.wait()
    for copy in gain_sends:
        copy.wait()
    x_core.wait()
    gain = jnp.concatenate([gains_ref[lift * d : lift * d + 1, :] for d in range(4)], axis=1)
    gain_row_ref[...] = jnp.broadcast_to(gain, gain_row_ref.shape)
    loads[0].wait()

    def piece(half, i):
        where = jnp.bitwise_xor(chip, half)
        return parts_ref.at[slot, :, pl.ds(pl.multiple_of(where * span, 16), span), :]

    def away(i):
        return lax.rem(2 * me + i, 4) != me

    def send(half, i):
        return part_copy(
            mixed.at[half, i], piece(half, i), part_sends.at[2 * half + i], part_recvs.at[2 * slot + half],
            lax.rem(2 * me + i, 4),
        )

    def keep(half, i):
        return pltpu.make_async_copy(mixed.at[half, i], piece(half, i), part_local.at[half])

    def either(i, yes, no):
        pl.when(away(i))(yes)
        pl.when(jnp.logical_not(away(i)))(no)

    def run_half(half):
        where = jnp.bitwise_xor(chip, half) * span

        for seq in range(seqs):

            def norm(r, carry, seq=seq):
                at = pl.ds(pl.multiple_of(where + r * 16, 16), 16)
                vals = xs_ref[seq, at, :].astype(f32)
                inv = lax.rsqrt(jnp.mean(vals * vals, axis=1, keepdims=True) + EPS)
                inv_ref[seq, at, :] = jnp.broadcast_to(inv, (16, LANES))
                out = (vals * inv * gain).astype(bf16)
                normed_ref[seq, at, :] = out
                lhs[pl.ds(pl.multiple_of(seq * span + r * 16, 16), 16), :] = out
                return carry

            lax.fori_loop(0, span // 16, norm, 0)
        for copy in normed_copies(half):
            copy.start()
        for i in range(2):

            def product(t, carry, i=i):
                value = rows_dot(lhs[...], w_ref[:, pl.ds(pl.multiple_of(i * width + t * tile, tile), tile)])
                for seq in range(seqs):
                    mixed[half, i, seq, :, pl.ds(pl.multiple_of(t * tile, tile), tile)] = value[
                        seq * span : (seq + 1) * span
                    ].astype(bf16)
                return carry

            lax.fori_loop(0, width // tile, product, 0)
            either(i, lambda i=i: send(half, i).start(), lambda i=i: keep(half, i).start())

    def normed_copies(half):
        where = pl.ds(pl.multiple_of(jnp.bitwise_xor(chip, half) * span, 16), span)
        src = normed_ref.at[:, where, pl.ds(pl.multiple_of(core * (model // 2), LANES), model // 2)]
        copies = [pltpu.make_async_copy(src, own_half_ref.at[:, where, :], pair_local.at[half])]
        for hop in (1, 2):
            at = 2 * half + hop - 1
            copies.append(across(src, half_ref.at[hop - 1, :, where, :], pair_sends, pair_recvs, at, quad(hop)))
        return copies

    run_half(0)
    x_chip.wait_recv()
    onward = remote(mine(xs_ref, peer(2)), mine(xs_ref, peer(2)), sends, recvs, 2, 1)
    onward.start()
    onward.wait()
    run_half(1)

    for copy in cot_sends:
        copy.wait()
    loads[1].wait()

    def partial(block, t):
        return outer_dot(
            cots_ref[...].reshape(seqs * 4 * rows, cols),
            o_ref[pl.ds(pl.multiple_of(block * width + t * tile, tile), tile), :],
        )

    def lanes(t):
        return pl.ds(pl.multiple_of(t * tile, tile), tile)

    near_sends = []
    for at, hop in enumerate((3, 1)):

        def fill(t, carry, at=at, hop=hop):
            pairs[at, :, lanes(t)] = partial(peer(hop), t).astype(bf16)
            return carry

        lax.fori_loop(0, width // tile, fill, 0)
        copy = remote(pairs.at[at], near.at[at], sends, recvs, 9 + at, 1)
        copy.start()
        near_sends.append(copy)
    near_sends[0].wait()

    pieces = width // tile // 2
    for first, ref in ((0, send_ref), (pieces, send_more_ref)):

        def to_send(t, carry, first=first, ref=ref):
            ref[:, lanes(t)] = (
                partial(peer(2), first + t) + near[0, :, lanes(first + t)].astype(f32)
            ).astype(bf16)
            return carry

        lax.fori_loop(0, pieces, to_send, 0)
    near_sends[1].wait()

    def to_own(t, carry):
        own_ref[:, lanes(t)] = partial(me, t) + near[1, :, lanes(t)].astype(f32)
        return carry

    lax.fori_loop(0, width // tile, to_own, 0)

    x_chip.wait_send()
    for copy in normed_copies(0) + normed_copies(1):
        copy.wait()
    for half in range(2):
        for i in range(2):
            either(i, lambda half=half, i=i: send(half, i).wait_send(), lambda half=half, i=i: keep(half, i).wait())
        for at in range(2):

            @pl.when(2 * at + me // 2 != me)
            def _(at=at, half=half):
                part_copy(
                    mixed.at[0, 0], mixed.at[0, 0], part_sends.at[0], part_recvs.at[2 * at + half], peer(1)
                ).wait_recv()


def front(x, cot, gain, w_in, out_proj):
    seqs, rows, model = x.shape
    group = lax.axis_size("shard")
    length = rows * group
    cols = model // group
    width = w_in.shape[1] // 2
    tokens = seqs * length
    lifted = jnp.broadcast_to(gain.astype(f32)[None], (8, gain.shape[0]))
    far_sems = pltpu.SemaphoreType.DMA((4,))
    return pl.pallas_call(
        front_kernel,
        in_specs=[VMEM_SPEC] * 3 + [ANY_SPEC] * 2,
        out_specs=[VMEM_SPEC] * 10,
        out_shape=[
            jax.ShapeDtypeStruct((seqs, length, model), bf16),
            jax.ShapeDtypeStruct((seqs, length, LANES), f32),
            jax.ShapeDtypeStruct((seqs, length, cols), bf16),
            jax.ShapeDtypeStruct((8, model), f32),
            jax.ShapeDtypeStruct((seqs, length, model // 2), bf16),
            jax.ShapeDtypeStruct((2, seqs, length, model // 2), bf16),
            jax.ShapeDtypeStruct((2, seqs, length, width), bf16),
            jax.ShapeDtypeStruct((tokens, width), f32),
            jax.ShapeDtypeStruct((tokens, width // 2), bf16),
            jax.ShapeDtypeStruct((tokens, width // 2), bf16),
        ],
        scratch_shapes=[
            pltpu.VMEM((8 * group, gain.shape[0]), f32),
            pltpu.VMEM(w_in.shape, bf16),
            pltpu.VMEM(out_proj.shape, bf16),
            pltpu.VMEM((seqs, length, model), bf16),
            pltpu.VMEM((tokens // 2, model), bf16),
            pltpu.VMEM((2, 2, seqs, 2 * rows, width), bf16),
            pltpu.VMEM((2, tokens, width), bf16),
            pltpu.VMEM((2, tokens, width), bf16),
            pltpu.SemaphoreType.DMA((11,)), pltpu.SemaphoreType.DMA((11,)), pltpu.SemaphoreType.DMA((5,)),
            pltpu.SemaphoreType.DMA((4,)), pltpu.SemaphoreType.DMA((4,)), pltpu.SemaphoreType.DMA((2,)),
            far_sems, far_sems, far_sems,
        ],
        compiler_params=group_params(1, 48 << 20),
        name="front",
    )(x, cot, lifted, w_in, out_proj)


def quad(hop):
    home = lax.axis_index("replica")
    if hop & 1:
        home = home + 1 - 2 * lax.rem(home, 2)
    if hop & 2:
        home = home + 2 - 4 * lax.rem(home // 2, 2)
    return home


def across(src, dst, sends, recvs, at, other):
    return pltpu.make_async_remote_copy(
        src_ref=src, dst_ref=dst, send_sem=sends.at[at], recv_sem=recvs.at[at],
        device_id={"replica": other}, device_id_type=MESH,
    )


def meet(replicas):
    barrier = pltpu.get_barrier_semaphore()
    for hop in (1, 2, 3):
        pl.semaphore_signal(barrier, inc=1, device_id={"shard": peer(hop)}, device_id_type=MESH)
    for other in replicas:
        pl.semaphore_signal(barrier, inc=1, device_id={"replica": other}, device_id_type=MESH)
    pl.semaphore_wait(barrier, 3 + len(replicas))


def ahead(step):
    count = lax.axis_size("replica")
    return lax.rem(lax.axis_index("replica") + step, count)


def collect_kernel(
    keep_ref, give_ref, gz_ref, own_half_ref, half_ref, last_ref,
    keeps_ref, gives_ref, gz_ref4, norm_ref, got_ref,
    sends, recvs, local,
):
    me = lax.axis_index("shard")
    half = keep_ref.shape[1]
    core = lax.rem(me, 2)
    member = lax.rem(lax.axis_index("replica"), 4)
    part = gz_ref4.shape[2]
    meet([quad(hop) for hop in (1, 2, 3)])

    def quarter(which):
        return gz_ref.at[:, pl.ds(pl.multiple_of(which * part, LANES), part)]

    def spot(ref, owner):
        return ref.at[:, pl.ds(pl.multiple_of(owner * half, 128), half)]

    k_chip = remote(keep_ref, spot(keeps_ref, me), sends, recvs, 0, 2)
    v_chip = remote(give_ref, spot(gives_ref, me), sends, recvs, 1, 2)
    k_core = remote(keep_ref, spot(keeps_ref, me), sends, recvs, 2, 1)
    v_core = remote(give_ref, spot(gives_ref, me), sends, recvs, 3, 1)
    quads = [
        across(quarter(lax.rem(quad(hop), 4)), gz_ref4.at[hop], sends, recvs, 6 + hop, quad(hop)) for hop in (3, 1, 2)
    ]
    give_pair = across(give_ref, got_ref, sends, recvs, 11, quad(1))
    norms = [
        remote(own_half_ref, norm_ref.at[core, 0], sends, recvs, 12, 1),
        remote(half_ref, norm_ref.at[core, 1:3], sends, recvs, 10, 1),
        remote(last_ref, norm_ref.at[core, 3], sends, recvs, 4, 1),
    ]
    own = [
        pltpu.make_async_copy(keep_ref, spot(keeps_ref, me), local.at[0]),
        pltpu.make_async_copy(give_ref, spot(gives_ref, me), local.at[1]),
        pltpu.make_async_copy(quarter(member), gz_ref4.at[0], local.at[2]),
        pltpu.make_async_copy(own_half_ref, norm_ref.at[core, 0], local.at[5]),
        pltpu.make_async_copy(half_ref, norm_ref.at[core, 1:3], local.at[3]),
        pltpu.make_async_copy(last_ref, norm_ref.at[core, 3], local.at[4]),
    ]
    for copy in [k_chip, v_chip] + quads + [give_pair, k_core, v_core] + norms + own:
        copy.start()
    k_chip.wait_recv()
    k_on = remote(spot(keeps_ref, peer(2)), spot(keeps_ref, peer(2)), sends, recvs, 5, 1)
    k_on.start()
    v_chip.wait_recv()
    v_on = remote(spot(gives_ref, peer(2)), spot(gives_ref, peer(2)), sends, recvs, 6, 1)
    v_on.start()
    for copy in own + quads + norms + [give_pair, k_core, v_core, k_on, v_on]:
        copy.wait()
    k_chip.wait_send()
    v_chip.wait_send()


def cost(microseconds):
    return pl.CostEstimate(flops=int(microseconds * 1e9), bytes_accessed=1 << 20, transcendentals=0)


def collect(keep, give, grad_z, own_half, half_norm, last_norm):
    tokens, half = keep.shape
    group = lax.axis_size("shard")
    wide = jax.ShapeDtypeStruct((tokens, half * group), bf16)
    return pl.pallas_call(
        collect_kernel,
        in_specs=[VMEM_SPEC] * 6,
        out_specs=[VMEM_SPEC] * 3 + [ANY_SPEC, VMEM_SPEC],
        out_shape=[
            wide, wide, jax.ShapeDtypeStruct((4, tokens, grad_z.shape[1] // 4), bf16),
            pltpu.HBM((2, 4) + last_norm.shape, bf16),
            jax.ShapeDtypeStruct(give.shape, bf16),
        ],
        scratch_shapes=[
            pltpu.SemaphoreType.DMA((13,)), pltpu.SemaphoreType.DMA((13,)), pltpu.SemaphoreType.DMA((6,)),
        ],
        compiler_params=group_params(6, 28 << 20),
        cost_estimate=cost(25),
        name="collect",
    )(keep, give, grad_z, own_half, half_norm, last_norm)


def middle_kernel(
    keeps_ref, gives_ref, got_ref, z_ref, x_hbm, o_hbm,
    both_ref, out_ref, wz_ref,
    z_got_ref, o_ref, xcol, outs, sends, recvs, far_sends, far_recvs, local, o_local,
):
    me = lax.axis_index("shard")
    side = lax.rem(lax.axis_index("replica"), 2)
    tokens, half = got_ref.shape
    gots_ref = both_ref.at[1]
    seqs, rows, _ = out_ref.shape
    cols = xcol.shape[1]
    piece = o_hbm.shape[0] // lax.axis_size("replica")
    per = half // piece
    loads = []
    for d in range(4):
        for q in range(2):
            for j in range(per):
                at = d * 2 * half + (2 * j) * piece + (side if q == 0 else 1 - side) * piece
                loads.append(
                    pltpu.make_async_copy(
                        o_hbm.at[pl.ds(pl.multiple_of(at, piece), piece), :],
                        o_ref.at[q, pl.ds(d * half + j * piece, piece), :],
                        o_local.at[len(loads)],
                    )
                )
    for copy in loads:
        copy.start()
    fetch = pltpu.make_async_copy(
        x_hbm.at[:, pl.ds(pl.multiple_of(me * cols, 128), cols)], xcol, local.at[0]
    )
    fetch.start()
    home = lax.axis_index("replica")
    count = lax.axis_size("replica")
    meet([ahead(step) for step in range(1, count)])

    def spot(owner):
        return gots_ref.at[:, pl.ds(pl.multiple_of(owner * half, 128), half)]

    g_own = pltpu.make_async_copy(got_ref, spot(me), local.at[2])
    g_chip = remote(got_ref, spot(me), sends, recvs, 0, 2)
    g_core = remote(got_ref, spot(me), sends, recvs, 1, 1)
    own = [
        pltpu.make_async_copy(keeps_ref, both_ref.at[0], local.at[1]),
    ]
    own.append(pltpu.make_async_copy(z_ref.at[home], z_got_ref.at[home], local.at[3 + seqs]))
    z_sends = [
        across(z_ref.at[ahead(step)], z_got_ref.at[home], far_sends, far_recvs, step, ahead(step))
        for step in range(1, count)
    ]
    own.append(g_own)
    for copy in [g_chip] + z_sends + [g_core] + own:
        copy.start()
    for copy in loads + [fetch]:
        copy.wait()
    tile = 256

    def product(t, carry):
        rows_at = pl.ds(pl.multiple_of(t * tile, tile), tile)
        value = (
            xcol[rows_at, :].astype(f32)
            + rows_dot(keeps_ref[rows_at, :], o_ref[0])
            + rows_dot(gives_ref[rows_at, :], o_ref[1])
        )
        outs[rows_at, :] = value.astype(bf16)
        return carry

    lax.fori_loop(0, tokens // tile, product, 0)
    length = tokens // seqs
    out_sends = []
    for seq in range(seqs):
        for n_hop, hop in enumerate((2, 3, 1)):
            src = outs.at[pl.ds(pl.multiple_of(seq * length + peer(hop) * rows, 16), rows), :]
            dst = out_ref.at[seq, :, pl.ds(pl.multiple_of(me * cols, 128), cols)]
            out_sends.append(remote(src, dst, sends, recvs, 2 + seq * 3 + n_hop, hop))
        own.append(
            pltpu.make_async_copy(
                outs.at[pl.ds(pl.multiple_of(seq * length + me * rows, 16), rows), :],
                out_ref.at[seq, :, pl.ds(pl.multiple_of(me * cols, 128), cols)],
                local.at[3 + seq],
            )
        )
        own[-1].start()
    for copy in out_sends:
        copy.start()
    base = 2 + seqs * 3
    g_chip.wait_recv()
    g_on = remote(spot(peer(2)), spot(peer(2)), sends, recvs, base + 2, 1)
    g_on.start()
    for copy in out_sends + [g_on, g_core] + own + z_sends:
        copy.wait()
    g_chip.wait_send()
    quarter = z_got_ref.shape[2]
    for q in range(4):
        total = z_got_ref[q].astype(f32)
        for group in range(1, count // 4):
            total = total + z_got_ref[4 * group + q].astype(f32)
        wz_ref[:, q * quarter : (q + 1) * quarter] = total.astype(bf16)


def middle(keeps, gives, got, z_blocks, x_all, out_proj, seqs):
    tokens, half = got.shape
    group = lax.axis_size("shard")
    model = x_all.shape[1]
    cols = model // group
    far_sems = pltpu.SemaphoreType.DMA((lax.axis_size("replica"),))
    pieces = 8 * max(1, half * lax.axis_size("replica") // out_proj.shape[0])
    return pl.pallas_call(
        middle_kernel,
        in_specs=[VMEM_SPEC] * 4 + [ANY_SPEC] * 2,
        out_specs=[VMEM_SPEC] * 3,
        out_shape=[
            jax.ShapeDtypeStruct((2, tokens, half * group), bf16),
            jax.ShapeDtypeStruct((seqs, tokens // seqs // group, model), bf16),
            jax.ShapeDtypeStruct((z_blocks.shape[1], 4 * z_blocks.shape[2]), bf16),
        ],
        scratch_shapes=[
            pltpu.VMEM(z_blocks.shape, bf16),
            pltpu.VMEM((2, half * group, cols), bf16),
            pltpu.VMEM((tokens, cols), bf16),
            pltpu.VMEM((tokens, cols), bf16),
            pltpu.SemaphoreType.DMA((5 + 3 * seqs,)), pltpu.SemaphoreType.DMA((5 + 3 * seqs,)),
            far_sems, far_sems, pltpu.SemaphoreType.DMA((4 + seqs,)), pltpu.SemaphoreType.DMA((pieces,)),
        ],
        compiler_params=group_params(7, 22 << 20),
        cost_estimate=cost(25),
        name="middle",
    )(keeps, gives, got, z_blocks, x_all, out_proj)


PARTS = 2


def finish_kernel(
    gx_ref, gz_ref, xp_ref, dp_ref, cw_ref, cb_ref, db_ref, sk_ref, wz_ref, norm_hbm, w_hbm, x_ref, cot_ref, gain_ref, xs_ref, inv_ref,
    gw_ref, gxp_ref, gdp_ref, gcw_ref, gcb_ref, gdb_ref, gsk_ref, dx_ref, ggain_ref,
    small_keep_ref, small_give_ref, small_ref, norm_ref, w_ref, gx4, cols_ref, turned, xb_ref, sb_ref, small_got, x_in, s_in, lhs, pairs, near, g_hold, g_own, g_send, g_far,
    h_send, h_cols, z_cols, s_own, gains, gain_near, gain_sum, gain_in, unit_x,
    sends, recvs, far_sends, far_recvs, home_sends, home_recvs, local,
):
    me = lax.axis_index("shard")
    home = lax.axis_index("replica")
    count = lax.axis_size("replica")
    height = count // 2
    mine = home // 2
    side = lax.rem(home, 2)
    seqs, rows, model = x_ref.shape
    tokens, width = gx_ref.shape
    length = tokens // seqs
    deep = wz_ref.shape[0]
    member = lax.rem(home, 4)
    quarter = width // 4
    part = quarter // PARTS
    tile = 256
    other = quad(1)
    load = pltpu.make_async_copy(w_hbm, w_ref, local.at[0])
    load_norm = pltpu.make_async_copy(norm_hbm, norm_ref, local.at[1])
    load_norm.start()
    load.start()
    meet([ahead(step) for step in range(1, count)])

    def far(step):
        return ahead(2 * step)

    def cut(p):
        return slice(p * part, (p + 1) * part)

    def piece_of(which, p):
        return gx_ref.at[:, pl.ds(pl.multiple_of(which * quarter + p * part, LANES), part)]

    def spot_of(hop, p):
        return gx4.at[hop * tokens : (hop + 1) * tokens, cut(p)]

    def quad_sends(p):
        return [
            across(piece_of(lax.rem(quad(hop), 4), p), spot_of(hop, p), sends, recvs, 3 * p + hop - 1, quad(hop))
            for hop in (3, 1, 2)
        ]

    small_send = across(small_give_ref, small_got, sends, recvs, 3 * PARTS, other)
    quad_own = [
        pltpu.make_async_copy(piece_of(member, p), spot_of(0, p), local.at[PARTS + 3 + 2 * seqs + p]) for p in range(PARTS)
    ]
    for copy in quad_sends(0):
        copy.start()
    lined = small_keep_ref.shape[1]

    def fill(at, put):
        low, high, begin = at * lined, (at + 1) * lined, 0
        for ref in (xp_ref, dp_ref, cw_ref, cb_ref, db_ref, sk_ref):
            stop = begin + ref.shape[0]
            a, b = max(low, begin), min(high, stop)
            if a < b:
                put(at // 2, slice(a - low, b - low), ref[a - begin : b - begin, :])
            begin = stop
        if high > begin:
            a = max(low, begin)
            put(at // 2, slice(a - low, lined), jnp.zeros((high - a, width), f32))

    def keep_rows(at, rows_at, value):
        small_keep_ref[at, rows_at, :] = value

    for at in range(count):
        pl.when(side == at % 2)(lambda at=at: fill(at, keep_rows))

        @pl.when(side != at % 2)
        def _(at=at):
            values = []
            fill(at, lambda where, rows_at, value: values.append(value))
            small_give_ref[at // 2] = jnp.concatenate(values, axis=0).astype(bf16)

    for copy in [small_send] + quad_sends(1) + quad_own:
        copy.start()

    def goal(slot):
        return (4 * slot + me) // 2

    spot = pl.ds(pl.multiple_of(lax.rem(me, 2) * width, LANES), width)

    def home_pieces(at):
        if at == PARTS:
            return 1, wz_ref, z_cols.at[:, spot]
        if at > PARTS:
            slot, seq = (at - PARTS - 1) % 2, (at - PARTS - 1) // 2
            some = slice(seq * length, (seq + 1) * length)
            return slot, (gx_ref, gz_ref)[slot].at[some], cols_ref.at[some, spot]
        some = 4 * part
        return 0, h_send.at[at], h_cols.at[at, :, pl.ds(pl.multiple_of(lax.rem(me, 2) * some, LANES), some)]

    def home_send(at):
        slot, src, dst = home_pieces(at)
        return part_copy(src, dst, home_sends.at[at], home_recvs.at[at * 2 + lax.rem(me, 2)], goal(slot))

    def home_keep(at):
        _, src, dst = home_pieces(at)
        return pltpu.make_async_copy(src, dst, local.at[2 + at])

    def home_start(at):
        slot = home_pieces(at)[0]
        pl.when(goal(slot) != me)(lambda: home_send(at).start())
        pl.when(goal(slot) == me)(lambda: home_keep(at).start())

    def home_wait(at):
        slot = home_pieces(at)[0]
        pl.when(goal(slot) != me)(lambda: home_send(at).wait_send())
        pl.when(goal(slot) == me)(lambda: home_keep(at).wait())
        for place in range(2):
            source = lax.rem(2 * me + place, 4)

            @pl.when((me // 2 == slot) & (source != me))
            def _(place=place):
                src = home_pieces(at)[1]
                part_copy(src, src, home_sends.at[at], home_recvs.at[at * 2 + place], peer(1)).wait_recv()

    for at in (*range(PARTS + 1, PARTS + 1 + 2 * seqs), PARTS):
        home_start(at)

    def far_copy(src, dst, kind, step):
        return across(src, dst, far_sends, far_recvs, kind * count + step, far(step))

    def block(step):
        return lax.rem(mine + step, height)

    order = range(1, height)

    def lines(at):
        return pl.ds(pl.multiple_of(at * deep, 16), deep)

    def x_sends(p):
        return [
            across(
                xb_ref.at[lines(ahead(step)), cut(p)], x_in.at[home, :, cut(p)], far_sends, far_recvs,
                p * count + step, ahead(step),
            )
            for step in range(1, count)
        ]

    def x_part(p):
        for copy in quad_sends(p):
            copy.wait_recv()
        quad_own[p].wait()

        for at in range(0, 4 * tokens, tile):
            turned[:, at : at + tile] = gx4[at : at + tile, cut(p)].T
        wide = norm_ref.shape[2] // tile

        def rows_of(t, carry):
            feature = pl.ds(pl.multiple_of(lax.rem(t, wide) * tile, tile), tile)
            value = rows_dot(turned[...], norm_ref[t // wide, :, feature])
            xb_ref[pl.ds(pl.multiple_of(t * tile, tile), tile), cut(p)] = value.astype(bf16).T
            return carry

        lax.fori_loop(0, xb_ref.shape[0] // tile, rows_of, 0)
        x_in[home, :, cut(p)] = xb_ref[lines(home), cut(p)]
        for copy in x_sends(p):
            copy.start()

    def lanes(t):
        return pl.ds(pl.multiple_of(t * tile, tile), tile)

    def near_send(seq):
        return remote(pairs.at[seq], near.at[seq], sends, recvs, 3 * PARTS + 8 + 2 * seq, 1)

    def chip_send(seq):
        return remote(g_send.at[seq], g_far.at[seq], sends, recvs, 3 * PARTS + 9 + 2 * seq, 2)

    def grads_of(seq):
        home_wait(PARTS + 1 + 2 * seq)
        home_wait(PARTS + 2 + 2 * seq)
        for i, owner in enumerate((peer(3), peer(1), peer(2), me)):
            at = pl.ds(pl.multiple_of(seq * length + owner * rows, 16), rows)
            lhs[i * rows : (i + 1) * rows, :] = cols_ref[at, :]
            here = pl.ds(pl.multiple_of(owner * rows, 16), rows)
            inv = inv_ref[seq, here, :]
            for low in range(0, model, LANES):
                unit_x[i * rows : (i + 1) * rows, low : low + LANES] = xs_ref[seq, here, low : low + LANES].astype(f32) * inv

        def product(t, carry):
            value = outer_dot(lhs[...], w_ref[lanes(t), :])
            pairs[seq, :, lanes(t)] = value[: 2 * rows].astype(bf16)
            g_hold[:, lanes(t)] = value[2 * rows : 3 * rows]
            g_own[seq, :, lanes(t)] = value[3 * rows :]
            terms = value * unit_x[:, lanes(t)]
            gains[:, lanes(t)] += jnp.sum(terms.reshape(rows // 2, 8, tile), axis=0)
            return carry

        lax.fori_loop(0, model // tile, product, 0)
        near_send(seq).start()

    def grads_on(seq):
        near_send(seq).wait()
        for low in range(0, model, tile):
            at = slice(low, low + tile)
            g_send[seq, :, at] = (g_hold[:, at] + near[seq, :rows, at].astype(f32)).astype(bf16)
            g_own[seq, :, at] += near[seq, rows:, at].astype(f32)
        chip_send(seq).start()

    def home_sum(p):
        for copy in x_sends(p):
            copy.wait_recv()
        for q in range(4):
            total = x_in[q, :, cut(p)].astype(f32)
            for group in range(1, count // 4):
                total = total + x_in[4 * group + q, :, cut(p)].astype(f32)
            h_send[p, :, q * part : (q + 1) * part] = total.astype(bf16)
        home_start(p)

    gains[...] = jnp.zeros_like(gains)
    load_norm.wait()
    x_part(0)
    small_send.wait_recv()
    for at in range(height):
        sb_ref[at] = (small_keep_ref[at] + small_got[at].astype(f32)).astype(bf16)
    s_sends = [far_copy(sb_ref.at[block(step)], s_in.at[step - 1], PARTS, step) for step in order]
    for copy in s_sends:
        copy.start()
    load.wait()
    grads_of(0)
    x_part(1)
    grads_on(0)
    grads_of(1)
    wide = model // 4

    def gain_part(owner):
        return gains.at[:, pl.ds(pl.multiple_of(owner * wide, LANES), wide)]

    gain_sends = [
        remote(gain_part(peer(hop)), gain_near.at[hop - 1], sends, recvs, 3 * PARTS + 2 + hop, hop) for hop in (1, 2, 3)
    ]
    for copy in gain_sends:
        copy.start()
    for copy in s_sends:
        copy.wait_recv()
    total = sb_ref[mine].astype(f32)
    for step in order:
        total = total + s_in[step - 1].astype(f32)
    s_own[...] = total.astype(bf16)
    small_ref[side, mine] = s_own[...]
    spread = [far_copy(s_own, small_ref.at[side, mine], PARTS + 1, step) for step in order]
    for copy in spread:
        copy.start()

    def pass_on(step):
        at = lax.rem(mine + height - step, height)
        return across(
            small_ref.at[side, at], small_ref.at[side, at], far_sends, far_recvs, (PARTS + 3) * count + step, other
        )

    pass_on(0).start()
    home_sum(0)
    grads_on(1)
    for copy in gain_sends:
        copy.wait()
    gain_sum[...] = gains[:, pl.ds(pl.multiple_of(me * wide, LANES), wide)] + gain_near[0] + gain_near[1] + gain_near[2]
    gain_far = [
        across(gain_sum, gain_in.at[step - 1], far_sends, far_recvs, (PARTS + 2) * count + step, ahead(step))
        for step in range(1, count)
    ]
    for copy in gain_far:
        copy.start()


    def finish_rows(seq):
        chip_send(seq).wait()

        def last(r, carry):
            at = pl.ds(pl.multiple_of(r * 16, 16), 16)
            grad = g_own[seq, at, :] + g_far[seq, at, :].astype(f32)
            vals = x_ref[seq, at, :].astype(f32)
            inv = lax.rsqrt(jnp.mean(vals * vals, axis=1, keepdims=True) + EPS)
            scaled = grad * gain_ref[0:1, :]
            mean = jnp.mean(scaled * vals, axis=1, keepdims=True)
            out = inv * (scaled - vals * (inv * inv * mean))
            dx_ref[seq, at, :] = (cot_ref[seq, at, :].astype(f32) + out).astype(bf16)
            return carry

        lax.fori_loop(0, rows // 16, last, 0)

    finish_rows(0)
    home_sum(1)
    for step in order:
        spread[step - 1].wait_recv()
        pass_on(step).start()
    finish_rows(1)
    for at in range(PARTS + 1):
        home_wait(at)

    @pl.when(me // 2 == 0)
    def _():
        for place in range(2):
            for q in range(4):
                for p in range(PARTS):
                    to = place * width + q * quarter + p * part
                    low = (place * 4 + q) * part
                    gw_ref[:, to : to + part] = h_cols[p, :, low : low + part].astype(f32)

    @pl.when(me // 2 == 1)
    def _():
        for low in range(0, 2 * width, quarter):
            gw_ref[:, low : low + quarter] = z_cols[:, low : low + quarter].astype(f32)

    for copy in gain_far:
        copy.wait()
    total = gain_sum[...]
    for step in range(1, count):
        total = total + gain_in[step - 1]
    ggain_ref[...] = jnp.broadcast_to(jnp.sum(total, axis=0, keepdims=True), total.shape)
    for step in range(height):
        pass_on(step).wait()
    goals, start = [], 0
    for ref in (gxp_ref, gdp_ref, gcw_ref, gcb_ref, gdb_ref, gsk_ref):
        goals.append((ref, start, start + ref.shape[0]))
        start += ref.shape[0]
    for at in range(count):
        low, high = at * lined, (at + 1) * lined
        if low < start:
            value = small_ref[at % 2, at // 2].astype(f32)
        for ref, begin, stop in goals:
            a, b = max(low, begin), min(high, stop)
            if a < b:
                ref[a - begin : b - begin, :] = value[a - low : b - low]
    small_send.wait_send()
    for p in range(PARTS):
        for copy in quad_sends(p) + x_sends(p):
            copy.wait_send()
    for copy in s_sends + spread:
        copy.wait_send()


def finish(gx, gz, smalls, wz, norm, w_in, x, cot, gain, xs, inv):
    tokens, width = gx.shape
    height = lax.axis_size("replica") // 2
    lines = -(-sum(value.shape[0] for value in smalls) // (16 * height)) * 8
    deep = wz.shape[0]
    seqs, rows, model = x.shape
    wide = model // 4
    gain_tile = pltpu.VMEM((8, wide), f32)
    other = max(height - 1, 1)
    count = 2 * height
    quarter = width // 4
    kinds = (PARTS + 4) * count
    homes = PARTS + 1 + 2 * seqs
    line = jax.ShapeDtypeStruct((1, width), f32)
    return pl.pallas_call(
        finish_kernel,
        in_specs=[VMEM_SPEC] * 9 + [ANY_SPEC] * 2 + [VMEM_SPEC] * 5,
        out_specs=[VMEM_SPEC] * 9,
        out_shape=[
            jax.ShapeDtypeStruct((deep, 2 * width), f32),
            jax.ShapeDtypeStruct(smalls[0].shape, f32),
            jax.ShapeDtypeStruct(smalls[1].shape, f32),
            jax.ShapeDtypeStruct((KW, width), f32),
            line, line, line,
            jax.ShapeDtypeStruct(x.shape, bf16),
            jax.ShapeDtypeStruct((8, wide), f32),
        ],
        scratch_shapes=[
            pltpu.VMEM((height, lines, width), f32),
            pltpu.VMEM((height, lines, width), bf16),
            pltpu.VMEM((2, height, lines, width), bf16),
            pltpu.VMEM(norm.shape, bf16),
            pltpu.VMEM(w_in.shape, bf16),
            pltpu.VMEM((4 * tokens, quarter), bf16),
            pltpu.VMEM((tokens, 2 * width), bf16),
            pltpu.VMEM((quarter // PARTS, 4 * tokens), bf16),
            pltpu.VMEM((count * deep, quarter), bf16),
            pltpu.VMEM((height, lines, width), bf16),
            pltpu.VMEM((height, lines, width), bf16),
            pltpu.VMEM((count, deep, quarter), bf16),
            pltpu.VMEM((other, lines, width), bf16),
            pltpu.VMEM((4 * rows, 2 * width), bf16),
            pltpu.VMEM((seqs, 2 * rows, model), bf16),
            pltpu.VMEM((seqs, 2 * rows, model), bf16),
            pltpu.VMEM((rows, model), f32),
            pltpu.VMEM((seqs, rows, model), f32),
            pltpu.VMEM((seqs, rows, model), bf16),
            pltpu.VMEM((seqs, rows, model), bf16),
            pltpu.VMEM((PARTS, deep, width // PARTS), bf16),
            pltpu.VMEM((PARTS, deep, 2 * width // PARTS), bf16),
            pltpu.VMEM((deep, 2 * width), bf16),
            pltpu.VMEM((lines, width), bf16),
            pltpu.VMEM((8, model), f32),
            pltpu.VMEM((3, 8, wide), f32),
            gain_tile,
            pltpu.VMEM((count - 1, 8, wide), f32),
            pltpu.VMEM((4 * rows, model), f32),
            pltpu.SemaphoreType.DMA((3 * PARTS + 8 + 2 * seqs,)), pltpu.SemaphoreType.DMA((3 * PARTS + 8 + 2 * seqs,)),
            pltpu.SemaphoreType.DMA((kinds,)), pltpu.SemaphoreType.DMA((kinds,)),
            pltpu.SemaphoreType.DMA((homes,)), pltpu.SemaphoreType.DMA((2 * homes,)),
            pltpu.SemaphoreType.DMA((homes + 2 + PARTS,)),
        ],
        compiler_params=group_params(8, 58 << 20),
        cost_estimate=cost(80),
        name="finish",
    )(gx, gz, *smalls, wz, norm, w_in, x, cot, gain, xs, inv)


def total_kernel(part_ref, out_ref, near, chip_sum, far, sends, recvs):
    me = lax.axis_index("shard")
    half = part_ref.shape[1] // 2
    mine = pl.ds(pl.multiple_of(lax.rem(me, 2) * half, 128), half)
    other = pl.ds(pl.multiple_of((1 - lax.rem(me, 2)) * half, 128), half)
    meet_group()
    first = remote(part_ref.at[:, other], near, sends, recvs, 0, 1)
    first.start()
    first.wait()
    chip_sum[...] = part_ref[:, mine] + near[...]
    second = remote(chip_sum, far, sends, recvs, 1, 2)
    second.start()
    second.wait()
    out_ref[:, mine] = chip_sum[...] + far[...]
    third = remote(out_ref.at[:, mine], out_ref.at[:, mine], sends, recvs, 2, 1)
    third.start()
    third.wait()


def group_total(part, collective_id):
    rows, cols = part.shape
    half = pltpu.VMEM((rows, cols // 2), f32)
    return pl.pallas_call(
        total_kernel,
        in_specs=[VMEM_SPEC],
        out_specs=VMEM_SPEC,
        out_shape=jax.ShapeDtypeStruct((rows, cols), f32),
        scratch_shapes=[half, half, half, pltpu.SemaphoreType.DMA((3,)), pltpu.SemaphoreType.DMA((3,))],
        compiler_params=group_params(collective_id, 16 << 20),
        name="group_total",
    )(part)


def by_hop(value, hop):
    return lax.ppermute(value, "shard", [(i, i ^ hop) for i in range(4)])


def far_send(blocks):
    count = lax.axis_size("replica")
    height = count // 2
    mine = lax.axis_index("replica") // 2

    def pick(at):
        return lax.dynamic_index_in_dim(blocks, at, 0, False)

    sent = []
    for step in range(1, height):
        out = pick(lax.rem(mine + step, height)).astype(bf16)
        sent.append(lax.ppermute(out, "replica", [(i, (i + 2 * step) % count) for i in range(count)]))
    return pick(mine), tuple(sent)


def far_total(own, sent):
    total = own
    for value in sent:
        total = total + value.astype(f32)
    return total


def after(value, *others):
    return lax.optimization_barrier((value,) + others)[0]


def body(
    block_input, segment_ids, norm_gain, w_in, conv_weight, conv_bias, x_proj, dt_proj, dt_bias,
    d_skip, out_proj, out_grad,
):
    seqs, local, model = block_input.shape
    length = segment_ids.shape[1]
    tokens = seqs * length
    width = d_skip.shape[0]
    rank = dt_proj.shape[0]
    n = (x_proj.shape[0] - rank) // 2
    me = lax.axis_index("shard")
    count = lax.axis_size("replica")
    height = count // 2
    side = lax.rem(lax.axis_index("replica"), 2)

    def split(values):
        return values.reshape(seqs, length, -1)

    def halves(values, blocks):
        piece = values.shape[1] // blocks // 2
        cuts = [values[:, b * piece : (b + 1) * piece] for b in range(2 * blocks)]
        even = jnp.concatenate(cuts[0::2], axis=1)
        odd = jnp.concatenate(cuts[1::2], axis=1)
        return jnp.where(side == 0, even, odd), jnp.where(side == 0, odd, even)

    xs, inv, cots, gain, own_half, half_norm, parts, gated_own, gated_send, gated_more = front(
        block_input, out_grad, norm_gain, w_in, out_proj
    )
    x_all = xs.reshape(tokens, model)
    cot = cots.reshape(tokens, -1)
    x_part, z_part = parts[0], parts[1]

    seg_padded = jnp.pad(segment_ids, ((0, 0), (KW - 1, 0)), constant_values=-1)
    taps = [
        (seg_padded[:, KW - 1 - d : KW - 1 - d + length] == segment_ids).astype(f32) for d in range(KW)
    ]
    conv_w = conv_weight.astype(f32)
    xv = x_part.astype(f32)
    x_padded = jnp.pad(xv, ((0, 0), (KW - 1, 0), (0, 0)))
    conv_pre = conv_bias.astype(f32) + conv_w[KW - 1] * xv
    for j in range(KW - 1):
        d = KW - 1 - j
        conv_pre = conv_pre + conv_w[j] * x_padded[:, j : j + length] * taps[d][:, :, None]
    conv_out = jax.nn.silu(conv_pre).astype(bf16)
    conv_flat = conv_out.reshape(tokens, width)
    half_norm = half_norm.reshape(2, tokens, -1)
    own_half = own_half.reshape(tokens, -1)
    last_norm = lax.ppermute(own_half, "replica", [(i, i ^ 3) for i in range(count)])
    cot_got = lax.ppermute(cot, "replica", [(i, i ^ 1) for i in range(count)])
    proj = group_total(outer_dot(x_proj, conv_flat), 3)
    gated_far = by_hop(gated_send, 2)
    proj, gated_far = lax.optimization_barrier((proj, gated_far))
    gated_rest = by_hop(after(gated_more, proj), 2)
    keep_lanes = jnp.broadcast_to(taps[1][:, :, None], (seqs, length, LANES))
    skip = d_skip.astype(f32)
    y_total, gated, rate, beta, states = recurrence_forward(
        conv_out, z_part, proj, keep_lanes, dt_proj, dt_bias.astype(f32)[None], skip[None]
    )
    y_total, gated, gated_rest, last_norm, cot_got = lax.optimization_barrier(
        (y_total, gated, gated_rest, last_norm, cot_got)
    )
    cot_both = jnp.concatenate([cot, cot_got], axis=0)
    grad_gated = split(gated_own + jnp.concatenate([gated_far, gated_rest], axis=1).astype(f32))
    z_vals = z_part.astype(f32)
    dy = grad_gated * jax.nn.silu(z_vals)
    grad_z = (grad_gated * y_total * silu_slope(z_vals)).astype(bf16).reshape(tokens, width)

    gated_keep, gated_give = halves(gated.reshape(tokens, width), height // 4)
    cols = model // 4
    keeps, gives, grad_z_quad, norms, gated_got = collect(
        gated_keep, gated_give, grad_z, own_half, half_norm, last_norm
    )
    norms = norms.reshape(2, 4 * tokens, -1)
    z_blocks = lax.dot_general(
        norms, grad_z_quad.reshape(4 * tokens, -1), (((1,), (0,)), ((), ())), preferred_element_type=f32
    )
    z_blocks = z_blocks.astype(bf16).reshape(count, -1, width // 4)
    gated_both, block_output, grad_w_z = middle(keeps, gives, gated_got, z_blocks, x_all, out_proj, seqs)
    out_blocks = inner_dot(gated_both.reshape(2 * tokens, -1), cot_both)
    out_own, out_sent = far_send(out_blocks.astype(bf16).reshape(height, -1, cols))
    rate, out_own = lax.optimization_barrier((rate, out_own))

    grad_conv_rec, grad_dt_low, grad_proj, grad_dt_proj, grad_dt_bias, grad_d_skip = recurrence_backward(
        rate, beta, conv_out, dy, proj, keep_lanes, dt_proj, states
    )
    grad_proj, out_sent = lax.optimization_barrier((group_total(grad_proj, 4), out_sent))
    grad_proj = grad_proj.astype(bf16)
    grad_out_proj = far_total(out_own.astype(f32), out_sent)
    grad_x_proj = rows_dot(grad_proj, conv_flat)
    grad_conv = dy * skip + grad_conv_rec + split(inner_dot(grad_proj, x_proj))
    grad_pre = grad_conv * silu_slope(conv_pre)
    grad_conv_bias = jnp.sum(grad_pre, axis=(0, 1))
    grad_conv_weight = jnp.stack(
        [
            jnp.sum(grad_pre * x_padded[:, j : j + length] * taps[KW - 1 - j][:, :, None], axis=(0, 1))
            for j in range(KW)
        ]
    )
    grad_x = conv_w[KW - 1] * grad_pre
    for j in range(KW - 1):
        d = KW - 1 - j
        ahead = jnp.pad(grad_pre * taps[d][:, :, None], ((0, 0), (0, d), (0, 0)))[:, d:]
        grad_x = grad_x + conv_w[j] * ahead
    grad_x = grad_x.astype(bf16).reshape(tokens, width)

    smalls = (grad_x_proj, grad_dt_proj, grad_conv_weight, grad_conv_bias[None], grad_dt_bias, grad_d_skip)
    grad_w_in, grad_x_proj, grad_dt_proj, grad_conv_weight, conv_line, bias_line, skip_line, input_grad, grad_gain = finish(
        grad_x, grad_z, smalls, grad_w_z, norms, w_in, block_input, out_grad, gain, xs, inv
    )
    return (
        block_output, input_grad, grad_gain[0], grad_w_in, grad_conv_weight, conv_line[0], grad_x_proj, grad_dt_proj,
        bias_line[0], skip_line[0], grad_out_proj,
    )


def solution(mesh):
    return jax.shard_map(
        body,
        mesh=mesh,
        in_specs=(
            P("replica", "shard", None), P("replica", None), P("shard"), P(None, "shard"), P(None, "shard"),
            P("shard"), P(None, "shard"), P(None, "shard"), P("shard"), P("shard"), P(None, "shard"),
            P("replica", "shard", None),
        ),
        out_specs=(
            P("replica", "shard", None), P("replica", "shard", None), P("shard"), P("replica", "shard"),
            P(None, "shard"), P("shard"), P(None, "shard"), P(None, "shard"), P("shard"), P("shard"),
            P("replica", "shard"),
        ),
        check_vma=False,
    )
```

```python
import functools

import jax
import jax.numpy as jnp
from jax import lax
from jax.experimental import pallas as pl
from jax.experimental.pallas import tpu as pltpu
from jax.sharding import PartitionSpec as P

KW = 4
EPS = 1e-05
CHUNK = 16
LANES = 128
f32 = jnp.float32
bf16 = jnp.bfloat16


def rows_dot(a, b):
    return jnp.dot(a, b, preferred_element_type=f32)


def inner_dot(a, b):
    return lax.dot_general(a, b, (((0,), (0,)), ((), ())), preferred_element_type=f32)


def outer_dot(a, b):
    return lax.dot_general(a, b, (((1,), (1,)), ((), ())), preferred_element_type=f32)


def silu_slope(values):
    sig_val = jax.nn.sigmoid(values)
    return sig_val + values * sig_val * (1.0 - sig_val)

MESH = pl.DeviceIdType.MESH
BLOCK = 128
UNROLL = 4
BACK_UNROLL = 4


def lane(g):
    return slice(g * LANES, (g + 1) * LANES)


def column(block, t):
    return jnp.broadcast_to(block[:, t : t + 1], (block.shape[0], LANES))


def row(ref, t, g, n):
    return jnp.broadcast_to(ref[t : t + 1, lane(g)], (n, LANES))


def prepare(base, rate_ref, conv_ref, keep_ref, rk, u, kept):
    rows = pl.ds(base, CHUNK)
    rate = rate_ref[0, rows, :]
    keep = keep_ref[0, rows, :]
    conv = conv_ref[0, rows, :].astype(f32)
    for g in range(rate.shape[1] // LANES):
        rk[:, lane(g)] = rate[:, lane(g)] * keep
    u[...] = rate * conv
    kept[...] = keep
    return rate, conv, keep


def shifted(cols, j):
    size = cols.shape[1]
    return pltpu.roll(cols, lax.rem(size - j * CHUNK, size), 1)


def spread_mask(n, size=CHUNK):
    shape = (size, size * n)
    return lax.broadcasted_iota(jnp.int32, shape, 1) // n == lax.broadcasted_iota(jnp.int32, shape, 0)


def picker(n, size=CHUNK):
    shape = (n, size * n)
    return (lax.broadcasted_iota(jnp.int32, shape, 1) % n == lax.broadcasted_iota(jnp.int32, shape, 0)).astype(bf16)


def diagonal(rows, mask, pick):
    return jnp.where(mask, rows_dot(rows.astype(bf16), pick), 0.0).astype(bf16)


def forward_kernel(
    conv_ref, z_ref, proj_ref, keep_ref, dt_proj_ref, dt_bias_ref, skip_ref,
    y_ref, gated_ref, rate_ref, beta_ref, state_ref,
    held_ref, rk, u, kept, query_rows, fresh,
):
    width = conv_ref.shape[2]
    rank = dt_proj_ref.shape[0]
    n = (proj_ref.shape[0] - rank) // 2
    groups = width // LANES
    span = CHUNK * n

    @pl.when(pl.program_id(1) == 0)
    def _():
        held_ref[...] = jnp.zeros_like(held_ref)

    dt_low = proj_ref[0:rank, :].astype(bf16)
    keys = proj_ref[rank : rank + n, :]
    query_rows[...] = proj_ref[rank + n :, :].T
    key_square = jnp.sum(keys.T * keys.T, axis=1, keepdims=True)
    beta = jax.nn.sigmoid(inner_dot(dt_low, dt_proj_ref[...]) + dt_bias_ref[...])
    beta_ref[0] = beta
    rate_ref[0] = beta / (1.0 + beta * key_square)
    mask, pick = spread_mask(n), picker(n)

    def states_of(j, held, rk, u, kept, fresh):
        base = pl.multiple_of(j * CHUNK, CHUNK)
        prepare(base, rate_ref, conv_ref, keep_ref, rk, u, kept)
        near_keys = shifted(keys, j)
        for t in range(CHUNK):
            key = column(near_keys, t)
            key2 = key * key
            keep = jnp.broadcast_to(kept[t : t + 1, :], (n, LANES))
            at = slice(t * n, (t + 1) * n)
            for g in range(groups):
                decay = keep - row(rk, t, g, n) * key2
                held[g] = decay * held[g] + row(u, t, g, n) * key
                fresh[at, lane(g)] = held[g].astype(fresh.dtype)

    def outputs_of(j, fresh):
        base = pl.multiple_of(j * CHUNK, CHUNK)
        rows = pl.ds(base, CHUNK)
        block = fresh[...].astype(bf16)
        state_ref[0, pl.ds(pl.multiple_of(base * n, span), span), :] = block
        conv = conv_ref[0, rows, :].astype(f32)
        total = rows_dot(diagonal(query_rows[rows, :], mask, pick), block) + skip_ref[...] * conv
        y_ref[0, rows, :] = total
        z = z_ref[0, rows, :].astype(f32)
        gated_ref[0, rows, :] = (total * (z * jax.nn.sigmoid(z))).astype(bf16)

    def step(i, held):
        held = list(held)
        for k in range(UNROLL):
            states_of(i * UNROLL + k, held, rk[k], u[k], kept[k], fresh[k])
            if k > 0:
                outputs_of(i * UNROLL + k - 1, fresh[k - 1])
        outputs_of(i * UNROLL + UNROLL - 1, fresh[UNROLL - 1])
        return tuple(held)

    start = tuple(held_ref[:, lane(g)] for g in range(groups))
    end = lax.fori_loop(0, conv_ref.shape[1] // CHUNK // UNROLL, step, start)
    for g in range(groups):
        held_ref[:, lane(g)] = end[g]


def backward_kernel(
    rate_ref, beta_ref, conv_ref, dy_ref, proj_ref, keep_ref, dt_proj_ref, state_ref, last_ref,
    gconv_ref, gdt_ref, gproj_ref, gdt_proj_ref, gdt_bias_ref, gskip_ref,
    held_ref, grate, rk, u, dys, kept, key_rows, adj, adj_state, totals, lined,
):
    block_rows, width = rate_ref.shape[1:]
    rank = dt_proj_ref.shape[0]
    n = (proj_ref.shape[0] - rank) // 2
    groups = width // LANES
    chunks = block_rows // CHUNK

    @pl.when(pl.program_id(1) == 0)
    def _():
        held_ref[...] = jnp.zeros_like(held_ref)

    @pl.when((pl.program_id(0) == 0) & (pl.program_id(1) == 0))
    def _():
        gdt_proj_ref[...] = jnp.zeros_like(gdt_proj_ref)
        gdt_bias_ref[...] = jnp.zeros_like(gdt_bias_ref)
        gskip_ref[...] = jnp.zeros_like(gskip_ref)

    keys = proj_ref[rank : rank + n, :]
    queries = proj_ref[rank + n :, :]
    key_rows[...] = keys.T
    mask, pick = spread_mask(n), picker(n)

    ones = jnp.ones((CHUNK, LANES), bf16)

    def walk(j, held, rk, u, dys, kept, adj, adj_state, totals):
        base = pl.multiple_of(j * CHUNK, CHUNK)
        rows = pl.ds(base, CHUNK)
        prepare(base, rate_ref, conv_ref, keep_ref, rk, u, kept)
        dys[...] = dy_ref[0, rows, :]
        near_keys = shifted(keys, j)
        near_queries = shifted(queries, j)
        late = pl.ds(pl.multiple_of((base + CHUNK - 1) * n, n), n)
        after = [state_ref[0, late, lane(g)] for g in range(groups)]
        for t in reversed(range(CHUNK)):
            own = slice(t * n, (t + 1) * n)
            key = column(near_keys, t)
            key2 = key * key
            query = column(near_queries, t)
            keep = jnp.broadcast_to(kept[t : t + 1, :], (n, LANES))
            prior = jnp.maximum(base + t - 1, 0)
            at = pl.ds(pl.multiple_of(prior * n, n), n)
            parts = [None] * 3
            for g in range(groups):
                slope = row(dys, t, g, n)
                pace = row(rk, t, g, n)
                grad = held[g] + slope * query
                decay = keep - pace * key2
                held[g] = decay * grad
                before = state_ref[0, at, lane(g)]
                if t == 0:
                    before = jnp.where(j == 0, last_ref[0, :, lane(g)], before)
                cross = grad * before.astype(f32)
                adj[own, lane(g)] = grad
                adj_state[own, lane(g)] = cross
                terms = (grad * row(u, t, g, n), cross * pace, after[g].astype(f32) * slope)
                parts = [v if p is None else p + v for p, v in zip(parts, terms)]
                after[g] = before
            for i in range(3):
                totals[i, own, :] = parts[i]

    def settle(j, adj, adj_state, totals):
        base = pl.multiple_of(j * CHUNK, CHUNK)
        rows = pl.ds(base, CHUNK)
        key_block = key_rows[rows, :]
        w1 = rows_dot(diagonal(key_block, mask, pick), adj[...].astype(bf16))
        w2 = rows_dot(diagonal(key_block * key_block, mask, pick), adj_state[...].astype(bf16))
        for i in range(3):
            lined[i, rows, :] = jnp.where(mask, outer_dot(ones, totals[i].astype(bf16)), 0.0)
        keeps = keep_ref[0, rows, :]
        for g in range(groups):
            conv = conv_ref[0, rows, lane(g)].astype(f32)
            grate[rows, lane(g)] = conv * w1[:, lane(g)] - keeps * w2[:, lane(g)]
        gconv_ref[0, rows, :] = rate_ref[0, rows, :] * w1

    def step(i, held):
        held = list(held)
        first = chunks - 1 - i * BACK_UNROLL
        for k in range(BACK_UNROLL):
            walk(first - k, held, rk[k], u[k], dys[k], kept[k], adj[k], adj_state[k], totals[k])
            if k > 0:
                settle(first - k + 1, adj[k - 1], adj_state[k - 1], totals[k - 1])
        last = BACK_UNROLL - 1
        settle(first - last, adj[last], adj_state[last], totals[last])
        return tuple(held)

    start = tuple(held_ref[:, lane(g)] for g in range(groups))
    end = lax.fori_loop(0, chunks // BACK_UNROLL, step, start)
    for g in range(groups):
        held_ref[:, lane(g)] = end[g]

    def picked(left, value):
        high = value.astype(bf16)
        low = (value - high.astype(f32)).astype(bf16)
        return outer_dot(left, high) + outer_dot(left, low)

    rate = rate_ref[0]
    beta = beta_ref[0]
    grad_rate = grate[...]
    self_term = picked(jnp.ones((n, width), bf16), grad_rate * rate * rate)
    key_square = jnp.sum(key_rows[...] * key_rows[...], axis=1, keepdims=True)
    denom_inv = 1.0 / (1.0 + beta * key_square)
    grad_dt = grad_rate * denom_inv * denom_inv * beta * (1.0 - beta)
    low = grad_dt.astype(bf16)
    gdt_ref[0] = low
    gdt_bias_ref[...] += jnp.sum(grad_dt, axis=0, keepdims=True)
    gskip_ref[...] += jnp.sum(dy_ref[0] * conv_ref[0].astype(f32), axis=0, keepdims=True)
    gdt_proj_ref[...] += rows_dot(proj_ref[0:rank, :].astype(bf16), low)
    gproj_ref[0:rank, :] = outer_dot(dt_proj_ref[...], low)
    gproj_ref[rank : rank + n, :] = picked(pick, lined[0]) - 2.0 * keys * (picked(pick, lined[1]) + self_term)
    gproj_ref[rank + n :, :] = picked(pick, lined[2])


def specs_for(length, reverse):
    blocks = length // BLOCK

    def place(b):
        return blocks - 1 - b if reverse else b

    def spec(*shape):
        return pl.BlockSpec((1,) + shape, lambda s, b: (s, place(b)) + (0,) * (len(shape) - 1))

    def across_spec(rows):
        return pl.BlockSpec((rows, BLOCK), lambda s, b: (0, s * blocks + place(b)))

    def whole(*shape):
        return pl.BlockSpec(shape, lambda s, b: (0,) * len(shape))

    return blocks, spec, across_spec, whole


def recurrence_forward(conv, z, proj, keep_lanes, dt_proj, dt_bias, skip):
    seqs, length, width = conv.shape
    rank = dt_proj.shape[0]
    n = (proj.shape[0] - rank) // 2
    blocks, spec, across_spec, whole = specs_for(length, False)
    span = CHUNK * n
    wide = spec(BLOCK, width)
    full = jax.ShapeDtypeStruct((seqs, length, width), f32)
    return pl.pallas_call(
        forward_kernel,
        grid=(seqs, blocks),
        in_specs=[
            wide, wide, across_spec(proj.shape[0]), spec(BLOCK, LANES), whole(rank, width), whole(1, width),
            whole(1, width),
        ],
        out_specs=[wide, wide, wide, wide, spec(BLOCK * n, width)],
        out_shape=[
            full, jax.ShapeDtypeStruct((seqs, length, width), bf16),
            pltpu.HBM((seqs, length, width), f32), pltpu.HBM((seqs, length, width), f32),
            pltpu.HBM((seqs, length * n, width), bf16),
        ],
        scratch_shapes=[
            pltpu.VMEM((n, width), f32),
            [pltpu.VMEM((CHUNK, width), f32)] * UNROLL,
            [pltpu.VMEM((CHUNK, width), f32)] * UNROLL,
            [pltpu.VMEM((CHUNK, LANES), f32)] * UNROLL,
            pltpu.VMEM((BLOCK, n), f32),
            [pltpu.VMEM((span, width), f32)] * UNROLL,
        ],
        compiler_params=pltpu.CompilerParams(vmem_limit_bytes=24 << 20),
        cost_estimate=pl.CostEstimate(flops=16_000_000_000, bytes_accessed=24 << 20, transcendentals=0),
        name="recurrence_forward",
    )(conv, z, proj, keep_lanes, dt_proj, dt_bias, skip)


def recurrence_backward(rate, beta, conv, dy, proj, keep_lanes, dt_proj, states):
    seqs, length, width = rate.shape
    rank = dt_proj.shape[0]
    n = (proj.shape[0] - rank) // 2
    span = CHUNK * n
    blocks, spec, across_spec, whole = specs_for(length, True)
    wide = spec(BLOCK, width)
    before = pl.BlockSpec((1, n, width), lambda s, b: (s, jnp.maximum((blocks - 1 - b) * BLOCK - 1, 0), 0))
    return pl.pallas_call(
        backward_kernel,
        grid=(seqs, blocks),
        in_specs=[
            wide, wide, wide, wide, across_spec(proj.shape[0]), spec(BLOCK, LANES), whole(rank, width),
            spec(BLOCK * n, width), before,
        ],
        out_specs=[wide, wide, across_spec(proj.shape[0]), whole(rank, width), whole(1, width), whole(1, width)],
        out_shape=[
            jax.ShapeDtypeStruct((seqs, length, width), f32),
            jax.ShapeDtypeStruct((seqs, length, width), bf16),
            jax.ShapeDtypeStruct(proj.shape, f32),
            jax.ShapeDtypeStruct((rank, width), f32),
            jax.ShapeDtypeStruct((1, width), f32),
            jax.ShapeDtypeStruct((1, width), f32),
        ],
        scratch_shapes=[
            pltpu.VMEM((n, width), f32),
            pltpu.VMEM((BLOCK, width), f32),
            [pltpu.VMEM((CHUNK, width), f32)] * BACK_UNROLL,
            [pltpu.VMEM((CHUNK, width), f32)] * BACK_UNROLL,
            [pltpu.VMEM((CHUNK, width), f32)] * BACK_UNROLL,
            [pltpu.VMEM((CHUNK, LANES), f32)] * BACK_UNROLL,
            pltpu.VMEM((BLOCK, n), f32),
            [pltpu.VMEM((span, width), f32)] * BACK_UNROLL,
            [pltpu.VMEM((span, width), f32)] * BACK_UNROLL,
            [pltpu.VMEM((3, span, LANES), f32)] * BACK_UNROLL,
            pltpu.VMEM((3, BLOCK, span), f32),
        ],
        compiler_params=pltpu.CompilerParams(vmem_limit_bytes=36 << 20),
        cost_estimate=pl.CostEstimate(flops=30_000_000_000, bytes_accessed=28 << 20, transcendentals=0),
        name="recurrence_backward",
    )(rate, beta, conv, dy, proj, keep_lanes, dt_proj, states, states)


def peer(hop):
    me = lax.axis_index("shard")
    core = lax.rem(me, 2)
    chip = me // 2
    if hop & 1:
        core = 1 - core
    if hop & 2:
        chip = 1 - chip
    return chip * 2 + core


def meet_group():
    barrier = pltpu.get_barrier_semaphore()
    for hop in (1, 2, 3):
        pl.semaphore_signal(barrier, inc=1, device_id={"shard": peer(hop)}, device_id_type=MESH)
    pl.semaphore_wait(barrier, 3)


def remote(src, dst, sends, recvs, at, hop):
    return pltpu.make_async_remote_copy(
        src_ref=src, dst_ref=dst, send_sem=sends.at[at], recv_sem=recvs.at[at],
        device_id={"shard": peer(hop)}, device_id_type=MESH,
    )


def group_params(collective_id, limit):
    return pltpu.CompilerParams(collective_id=collective_id, has_side_effects=True, vmem_limit_bytes=limit)


VMEM_SPEC = pl.BlockSpec(memory_space=pltpu.VMEM)


ANY_SPEC = pl.BlockSpec(memory_space=pl.ANY)


def part_copy(src, dst, send, recv, shard):
    return pltpu.make_async_remote_copy(
        src_ref=src, dst_ref=dst, send_sem=send, recv_sem=recv, device_id={"shard": shard}, device_id_type=MESH
    )


def front_kernel(
    x_ref, cot_ref, gain_ref, w_hbm, o_hbm,
    xs_ref, inv_ref, cots_ref, gain_row_ref, own_half_ref, y_half_ref, z_half_ref, x_part_ref, z_part_ref, own_ref, send_ref, send_more_ref,
    gains_ref, w_ref, o_ref, normed_ref, lhs, mixed, pairs, near, sends, recvs, local, part_sends, part_recvs, part_local,
    pair_sends, pair_recvs, pair_local,
):
    me = lax.axis_index("shard")
    chip = me // 2
    slot = me // 2
    seqs, rows, model = x_ref.shape
    cols = cots_ref.shape[2]
    core = lax.rem(me, 2)
    width = x_part_ref.shape[2]
    lift = gain_ref.shape[0]
    span = 2 * rows
    tile = 256
    loads = [
        pltpu.make_async_copy(w_hbm, w_ref, local.at[3]),
        pltpu.make_async_copy(o_hbm, o_ref, local.at[4]),
    ]
    for copy in loads:
        copy.start()
    meet([quad(1), quad(2)])

    def mine(ref, owner):
        return ref.at[:, pl.ds(pl.multiple_of(owner * rows, 16), rows), :]

    def part(owner):
        return cot_ref.at[:, :, pl.ds(pl.multiple_of(owner * cols, 128), cols)]

    def gain_rows(owner):
        return gains_ref.at[pl.ds(pl.multiple_of(owner * lift, 8), lift), :]

    gain_sends = [remote(gain_ref, gain_rows(me), sends, recvs, 5 + hop, hop) for hop in (1, 2, 3)]
    x_core = remote(x_ref, mine(xs_ref, me), sends, recvs, 0, 1)
    x_chip = remote(x_ref, mine(xs_ref, me), sends, recvs, 1, 2)
    cot_sends = [remote(part(peer(hop)), mine(cots_ref, me), sends, recvs, 2 + hop, hop) for hop in (1, 2, 3)]
    for copy in gain_sends + [x_core, x_chip] + cot_sends:
        copy.start()
    own = [
        pltpu.make_async_copy(x_ref, mine(xs_ref, me), local.at[0]),
        pltpu.make_async_copy(part(me), mine(cots_ref, me), local.at[1]),
        pltpu.make_async_copy(gain_ref, gain_rows(me), local.at[2]),
    ]
    for copy in own:
        copy.start()
    for copy in own:
        copy.wait()
    for copy in gain_sends:
        copy.wait()
    x_core.wait()
    gain = jnp.concatenate([gains_ref[lift * d : lift * d + 1, :] for d in range(4)], axis=1)
    gain_row_ref[...] = jnp.broadcast_to(gain, gain_row_ref.shape)
    loads[0].wait()

    def piece(half, kind):
        where = jnp.bitwise_xor(chip, half)
        return (x_part_ref, z_part_ref)[kind].at[:, pl.ds(pl.multiple_of(where * span, 16), span), :]

    def away(i):
        return lax.rem(2 * me + i, 4) != me

    def send(half, i, kind):
        return part_copy(
            mixed.at[half, i], piece(half, kind), part_sends.at[2 * half + i], part_recvs.at[2 * kind + half],
            lax.rem(2 * me + i, 4),
        )

    def keep(half, i, kind):
        return pltpu.make_async_copy(mixed.at[half, i], piece(half, kind), part_local.at[half])

    def either(half, i, send_does, keep_does):
        for kind in range(2):
            pl.when(away(i) & (slot == kind))(lambda kind=kind: send_does(send(half, i, kind)))
            pl.when(jnp.logical_not(away(i)) & (slot == kind))(lambda kind=kind: keep_does(keep(half, i, kind)))

    def run_half(half):
        where = jnp.bitwise_xor(chip, half) * span

        for seq in range(seqs):

            def norm(r, carry, seq=seq):
                at = pl.ds(pl.multiple_of(where + r * 16, 16), 16)
                vals = xs_ref[seq, at, :].astype(f32)
                inv = lax.rsqrt(jnp.mean(vals * vals, axis=1, keepdims=True) + EPS)
                inv_ref[seq, at, :] = jnp.broadcast_to(inv, (16, LANES))
                out = (vals * inv * gain).astype(bf16)
                normed_ref[seq, at, :] = out
                lhs[pl.ds(pl.multiple_of(seq * span + r * 16, 16), 16), :] = out
                return carry

            lax.fori_loop(0, span // 16, norm, 0)
        for copy in normed_copies(half):
            copy.start()
        for i in range(2):

            def product(t, carry, i=i):
                value = rows_dot(lhs[...], w_ref[:, pl.ds(pl.multiple_of(i * width + t * tile, tile), tile)])
                for seq in range(seqs):
                    mixed[half, i, seq, :, pl.ds(pl.multiple_of(t * tile, tile), tile)] = value[
                        seq * span : (seq + 1) * span
                    ].astype(bf16)
                return carry

            lax.fori_loop(0, width // tile, product, 0)
            either(half, i, lambda copy: copy.start(), lambda copy: copy.start())

    def normed_copies(half):
        where = pl.ds(pl.multiple_of(jnp.bitwise_xor(chip, half) * span, 16), span)
        src = normed_ref.at[:, where, pl.ds(pl.multiple_of(core * (model // 2), LANES), model // 2)]
        copies = [pltpu.make_async_copy(src, own_half_ref.at[:, where, :], pair_local.at[half])]
        for hop in (1, 2):
            at = 2 * half + hop - 1
            half_ref = (y_half_ref, z_half_ref)[hop - 1]
            copies.append(across(src, half_ref.at[:, where, :], pair_sends, pair_recvs, at, quad(hop)))
        return copies

    run_half(0)
    x_chip.wait_recv()
    onward = remote(mine(xs_ref, peer(2)), mine(xs_ref, peer(2)), sends, recvs, 2, 1)
    onward.start()
    onward.wait()
    run_half(1)

    for copy in cot_sends:
        copy.wait()
    loads[1].wait()

    def partial(block, t):
        return outer_dot(
            cots_ref[...].reshape(seqs * 4 * rows, cols),
            o_ref[pl.ds(pl.multiple_of(block * width + t * tile, tile), tile), :],
        )

    def lanes(t):
        return pl.ds(pl.multiple_of(t * tile, tile), tile)

    near_sends = []
    for at, hop in enumerate((3, 1)):

        def fill(t, carry, at=at, hop=hop):
            pairs[at, :, lanes(t)] = partial(peer(hop), t).astype(bf16)
            return carry

        lax.fori_loop(0, width // tile, fill, 0)
        copy = remote(pairs.at[at], near.at[at], sends, recvs, 9 + at, 1)
        copy.start()
        near_sends.append(copy)
    near_sends[0].wait()

    pieces = width // tile // 2
    for first, ref in ((0, send_ref), (pieces, send_more_ref)):

        def to_send(t, carry, first=first, ref=ref):
            ref[:, lanes(t)] = (
                partial(peer(2), first + t) + near[0, :, lanes(first + t)].astype(f32)
            ).astype(bf16)
            return carry

        lax.fori_loop(0, pieces, to_send, 0)
    near_sends[1].wait()

    def to_own(t, carry):
        own_ref[:, lanes(t)] = partial(me, t) + near[1, :, lanes(t)].astype(f32)
        return carry

    lax.fori_loop(0, width // tile, to_own, 0)

    x_chip.wait_send()
    for copy in normed_copies(0) + normed_copies(1):
        copy.wait()
    for half in range(2):
        for i in range(2):
            either(half, i, lambda copy: copy.wait_send(), lambda copy: copy.wait())
        for at in range(2):

            @pl.when(2 * at + me // 2 != me)
            def _(at=at, half=half):
                part_copy(
                    mixed.at[0, 0], mixed.at[0, 0], part_sends.at[0], part_recvs.at[2 * at + half], peer(1)
                ).wait_recv()


def front(x, cot, gain, w_in, out_proj):
    seqs, rows, model = x.shape
    group = lax.axis_size("shard")
    length = rows * group
    cols = model // group
    width = w_in.shape[1] // 2
    tokens = seqs * length
    lifted = jnp.broadcast_to(gain.astype(f32)[None], (8, gain.shape[0]))
    far_sems = pltpu.SemaphoreType.DMA((4,))
    return pl.pallas_call(
        front_kernel,
        in_specs=[VMEM_SPEC] * 3 + [ANY_SPEC] * 2,
        out_specs=[VMEM_SPEC] * 12,
        out_shape=[
            jax.ShapeDtypeStruct((seqs, length, model), bf16),
            jax.ShapeDtypeStruct((seqs, length, LANES), f32),
            jax.ShapeDtypeStruct((seqs, length, cols), bf16),
            jax.ShapeDtypeStruct((8, model), f32),
            jax.ShapeDtypeStruct((seqs, length, model // 2), bf16),
            jax.ShapeDtypeStruct((seqs, length, model // 2), bf16),
            jax.ShapeDtypeStruct((seqs, length, model // 2), bf16),
            jax.ShapeDtypeStruct((seqs, length, width), bf16),
            jax.ShapeDtypeStruct((seqs, length, width), bf16),
            jax.ShapeDtypeStruct((tokens, width), f32),
            jax.ShapeDtypeStruct((tokens, width // 2), bf16),
            jax.ShapeDtypeStruct((tokens, width // 2), bf16),
        ],
        scratch_shapes=[
            pltpu.VMEM((8 * group, gain.shape[0]), f32),
            pltpu.VMEM(w_in.shape, bf16),
            pltpu.VMEM(out_proj.shape, bf16),
            pltpu.VMEM((seqs, length, model), bf16),
            pltpu.VMEM((tokens // 2, model), bf16),
            pltpu.VMEM((2, 2, seqs, 2 * rows, width), bf16),
            pltpu.VMEM((2, tokens, width), bf16),
            pltpu.VMEM((2, tokens, width), bf16),
            pltpu.SemaphoreType.DMA((11,)), pltpu.SemaphoreType.DMA((11,)), pltpu.SemaphoreType.DMA((5,)),
            pltpu.SemaphoreType.DMA((4,)), pltpu.SemaphoreType.DMA((4,)), pltpu.SemaphoreType.DMA((2,)),
            far_sems, far_sems, far_sems,
        ],
        compiler_params=group_params(1, 48 << 20),
        name="front",
    )(x, cot, lifted, w_in, out_proj)


def quad(hop):
    home = lax.axis_index("replica")
    if hop & 1:
        home = home + 1 - 2 * lax.rem(home, 2)
    if hop & 2:
        home = home + 2 - 4 * lax.rem(home // 2, 2)
    return home


def across(src, dst, sends, recvs, at, other):
    return pltpu.make_async_remote_copy(
        src_ref=src, dst_ref=dst, send_sem=sends.at[at], recv_sem=recvs.at[at],
        device_id={"replica": other}, device_id_type=MESH,
    )


def meet(replicas):
    barrier = pltpu.get_barrier_semaphore()
    for hop in (1, 2, 3):
        pl.semaphore_signal(barrier, inc=1, device_id={"shard": peer(hop)}, device_id_type=MESH)
    for other in replicas:
        pl.semaphore_signal(barrier, inc=1, device_id={"replica": other}, device_id_type=MESH)
    pl.semaphore_wait(barrier, 3 + len(replicas))


def ahead(step):
    count = lax.axis_size("replica")
    return lax.rem(lax.axis_index("replica") + step, count)


def collect_kernel(
    keep_ref, give_ref, gz_ref, own_half_ref, y_half_ref, z_half_ref, last_ref,
    keeps_ref, gives_ref, gz_ref4, norm_ref, got_ref,
    sends, recvs, local,
):
    me = lax.axis_index("shard")
    half = keep_ref.shape[1]
    core = lax.rem(me, 2)
    member = lax.rem(lax.axis_index("replica"), 4)
    part = gz_ref4.shape[2]
    meet([quad(hop) for hop in (1, 2, 3)])

    def quarter(which):
        return gz_ref.at[:, pl.ds(pl.multiple_of(which * part, LANES), part)]

    def spot(ref, owner):
        return ref.at[:, pl.ds(pl.multiple_of(owner * half, 128), half)]

    k_chip = remote(keep_ref, spot(keeps_ref, me), sends, recvs, 0, 2)
    v_chip = remote(give_ref, spot(gives_ref, me), sends, recvs, 1, 2)
    k_core = remote(keep_ref, spot(keeps_ref, me), sends, recvs, 2, 1)
    v_core = remote(give_ref, spot(gives_ref, me), sends, recvs, 3, 1)
    quads = [
        across(quarter(lax.rem(quad(hop), 4)), gz_ref4.at[hop], sends, recvs, 6 + hop, quad(hop)) for hop in (3, 1, 2)
    ]
    give_pair = across(give_ref, got_ref, sends, recvs, 11, quad(1))
    norms = [
        remote(own_half_ref, norm_ref.at[core, 0], sends, recvs, 12, 1),
        remote(y_half_ref, norm_ref.at[core, 1], sends, recvs, 10, 1),
        remote(z_half_ref, norm_ref.at[core, 2], sends, recvs, 13, 1),
        remote(last_ref, norm_ref.at[core, 3], sends, recvs, 4, 1),
    ]
    own = [
        pltpu.make_async_copy(keep_ref, spot(keeps_ref, me), local.at[0]),
        pltpu.make_async_copy(give_ref, spot(gives_ref, me), local.at[1]),
        pltpu.make_async_copy(quarter(member), gz_ref4.at[0], local.at[2]),
        pltpu.make_async_copy(own_half_ref, norm_ref.at[core, 0], local.at[5]),
        pltpu.make_async_copy(y_half_ref, norm_ref.at[core, 1], local.at[3]),
        pltpu.make_async_copy(z_half_ref, norm_ref.at[core, 2], local.at[6]),
        pltpu.make_async_copy(last_ref, norm_ref.at[core, 3], local.at[4]),
    ]
    for copy in [k_chip, v_chip] + quads + [give_pair, k_core, v_core] + norms + own:
        copy.start()
    k_chip.wait_recv()
    k_on = remote(spot(keeps_ref, peer(2)), spot(keeps_ref, peer(2)), sends, recvs, 5, 1)
    k_on.start()
    v_chip.wait_recv()
    v_on = remote(spot(gives_ref, peer(2)), spot(gives_ref, peer(2)), sends, recvs, 6, 1)
    v_on.start()
    for copy in own + quads + norms + [give_pair, k_core, v_core, k_on, v_on]:
        copy.wait()
    k_chip.wait_send()
    v_chip.wait_send()


def cost(microseconds):
    return pl.CostEstimate(flops=int(microseconds * 1e9), bytes_accessed=1 << 20, transcendentals=0)


def collect(keep, give, grad_z, own_half, y_half, z_half, last_norm):
    tokens, half = keep.shape
    group = lax.axis_size("shard")
    wide = jax.ShapeDtypeStruct((tokens, half * group), bf16)
    return pl.pallas_call(
        collect_kernel,
        in_specs=[VMEM_SPEC] * 7,
        out_specs=[VMEM_SPEC] * 3 + [ANY_SPEC, VMEM_SPEC],
        out_shape=[
            wide, wide, jax.ShapeDtypeStruct((4, tokens, grad_z.shape[1] // 4), bf16),
            pltpu.HBM((2, 4) + last_norm.shape, bf16),
            jax.ShapeDtypeStruct(give.shape, bf16),
        ],
        scratch_shapes=[
            pltpu.SemaphoreType.DMA((14,)), pltpu.SemaphoreType.DMA((14,)), pltpu.SemaphoreType.DMA((7,)),
        ],
        compiler_params=group_params(6, 28 << 20),
        cost_estimate=cost(25),
        name="collect",
    )(keep, give, grad_z, own_half, y_half, z_half, last_norm)


def middle_kernel(
    keeps_ref, gives_ref, got_ref, z_ref, x_hbm, o_hbm,
    both_ref, out_ref, wz_ref,
    z_got_ref, o_ref, xcol, outs, sends, recvs, far_sends, far_recvs, local, o_local,
):
    me = lax.axis_index("shard")
    side = lax.rem(lax.axis_index("replica"), 2)
    tokens, half = got_ref.shape
    gots_ref = both_ref.at[1]
    seqs, rows, _ = out_ref.shape
    cols = xcol.shape[1]
    piece = o_hbm.shape[0] // lax.axis_size("replica")
    per = half // piece
    loads = []
    for d in range(4):
        for q in range(2):
            for j in range(per):
                at = d * 2 * half + (2 * j) * piece + (side if q == 0 else 1 - side) * piece
                loads.append(
                    pltpu.make_async_copy(
                        o_hbm.at[pl.ds(pl.multiple_of(at, piece), piece), :],
                        o_ref.at[q, pl.ds(d * half + j * piece, piece), :],
                        o_local.at[len(loads)],
                    )
                )
    for copy in loads:
        copy.start()
    fetch = pltpu.make_async_copy(
        x_hbm.at[:, pl.ds(pl.multiple_of(me * cols, 128), cols)], xcol, local.at[0]
    )
    fetch.start()
    home = lax.axis_index("replica")
    count = lax.axis_size("replica")
    meet([ahead(step) for step in range(1, count)])

    def spot(owner):
        return gots_ref.at[:, pl.ds(pl.multiple_of(owner * half, 128), half)]

    g_own = pltpu.make_async_copy(got_ref, spot(me), local.at[2])
    g_chip = remote(got_ref, spot(me), sends, recvs, 0, 2)
    g_core = remote(got_ref, spot(me), sends, recvs, 1, 1)
    own = [
        pltpu.make_async_copy(keeps_ref, both_ref.at[0], local.at[1]),
    ]
    own.append(pltpu.make_async_copy(z_ref.at[home], z_got_ref.at[home], local.at[3 + seqs]))
    z_sends = [
        across(z_ref.at[ahead(step)], z_got_ref.at[home], far_sends, far_recvs, step, ahead(step))
        for step in range(1, count)
    ]
    own.append(g_own)
    for copy in [g_chip] + z_sends + [g_core] + own:
        copy.start()
    for copy in loads + [fetch]:
        copy.wait()
    tile = 256

    def product(t, carry):
        rows_at = pl.ds(pl.multiple_of(t * tile, tile), tile)
        value = (
            xcol[rows_at, :].astype(f32)
            + rows_dot(keeps_ref[rows_at, :], o_ref[0])
            + rows_dot(gives_ref[rows_at, :], o_ref[1])
        )
        outs[rows_at, :] = value.astype(bf16)
        return carry

    lax.fori_loop(0, tokens // tile, product, 0)
    length = tokens // seqs
    out_sends = []
    for seq in range(seqs):
        for n_hop, hop in enumerate((2, 3, 1)):
            src = outs.at[pl.ds(pl.multiple_of(seq * length + peer(hop) * rows, 16), rows), :]
            dst = out_ref.at[seq, :, pl.ds(pl.multiple_of(me * cols, 128), cols)]
            out_sends.append(remote(src, dst, sends, recvs, 2 + seq * 3 + n_hop, hop))
        own.append(
            pltpu.make_async_copy(
                outs.at[pl.ds(pl.multiple_of(seq * length + me * rows, 16), rows), :],
                out_ref.at[seq, :, pl.ds(pl.multiple_of(me * cols, 128), cols)],
                local.at[3 + seq],
            )
        )
        own[-1].start()
    for copy in out_sends:
        copy.start()
    base = 2 + seqs * 3
    g_chip.wait_recv()
    g_on = remote(spot(peer(2)), spot(peer(2)), sends, recvs, base + 2, 1)
    g_on.start()
    for copy in out_sends + [g_on, g_core] + own + z_sends:
        copy.wait()
    g_chip.wait_send()
    quarter = z_got_ref.shape[2]
    for q in range(4):
        total = z_got_ref[q].astype(f32)
        for group in range(1, count // 4):
            total = total + z_got_ref[4 * group + q].astype(f32)
        wz_ref[:, q * quarter : (q + 1) * quarter] = total.astype(bf16)


def middle(keeps, gives, got, z_blocks, x_all, out_proj, seqs):
    tokens, half = got.shape
    group = lax.axis_size("shard")
    model = x_all.shape[1]
    cols = model // group
    far_sems = pltpu.SemaphoreType.DMA((lax.axis_size("replica"),))
    pieces = 8 * max(1, half * lax.axis_size("replica") // out_proj.shape[0])
    return pl.pallas_call(
        middle_kernel,
        in_specs=[VMEM_SPEC] * 4 + [ANY_SPEC] * 2,
        out_specs=[VMEM_SPEC] * 3,
        out_shape=[
            jax.ShapeDtypeStruct((2, tokens, half * group), bf16),
            jax.ShapeDtypeStruct((seqs, tokens // seqs // group, model), bf16),
            jax.ShapeDtypeStruct((z_blocks.shape[1], 4 * z_blocks.shape[2]), bf16),
        ],
        scratch_shapes=[
            pltpu.VMEM(z_blocks.shape, bf16),
            pltpu.VMEM((2, half * group, cols), bf16),
            pltpu.VMEM((tokens, cols), bf16),
            pltpu.VMEM((tokens, cols), bf16),
            pltpu.SemaphoreType.DMA((5 + 3 * seqs,)), pltpu.SemaphoreType.DMA((5 + 3 * seqs,)),
            far_sems, far_sems, pltpu.SemaphoreType.DMA((4 + seqs,)), pltpu.SemaphoreType.DMA((pieces,)),
        ],
        compiler_params=group_params(7, 22 << 20),
        cost_estimate=cost(25),
        name="middle",
    )(keeps, gives, got, z_blocks, x_all, out_proj)


PARTS = 2


def finish_kernel(
    gx_ref, gz_ref, xp_ref, dp_ref, cw_ref, cb_ref, db_ref, sk_ref, wz_ref, norm_hbm, w_hbm, x_ref, cot_ref, gain_ref, xs_ref, inv_ref,
    gw_ref, gxp_ref, gdp_ref, gcw_ref, gcb_ref, gdb_ref, gsk_ref, dx_ref, ggain_ref,
    small_keep_ref, small_give_ref, small_ref, norm_ref, w_ref, gx4, cols_ref, turned, xb_ref, sb_ref, small_got, x_in, s_in, lhs, pairs, near, g_hold, g_own, g_send, g_far,
    h_send, h_cols, z_cols, s_own, gains, gain_near, gain_sum, gain_in, unit_x,
    sends, recvs, far_sends, far_recvs, home_sends, home_recvs, local,
):
    me = lax.axis_index("shard")
    home = lax.axis_index("replica")
    count = lax.axis_size("replica")
    height = count // 2
    mine = home // 2
    side = lax.rem(home, 2)
    seqs, rows, model = x_ref.shape
    tokens, width = gx_ref.shape
    length = tokens // seqs
    deep = wz_ref.shape[0]
    member = lax.rem(home, 4)
    quarter = width // 4
    part = quarter // PARTS
    tile = 256
    other = quad(1)
    load = pltpu.make_async_copy(w_hbm, w_ref, local.at[0])
    load_norm = pltpu.make_async_copy(norm_hbm, norm_ref, local.at[1])
    load_norm.start()
    load.start()
    meet([ahead(step) for step in range(1, count)])

    def far(step):
        return ahead(2 * step)

    def cut(p):
        return slice(p * part, (p + 1) * part)

    def piece_of(which, p):
        return gx_ref.at[:, pl.ds(pl.multiple_of(which * quarter + p * part, LANES), part)]

    def spot_of(hop, p):
        return gx4.at[hop * tokens : (hop + 1) * tokens, cut(p)]

    def quad_sends(p):
        return [
            across(piece_of(lax.rem(quad(hop), 4), p), spot_of(hop, p), sends, recvs, 3 * p + hop - 1, quad(hop))
            for hop in (3, 1, 2)
        ]

    small_send = across(small_give_ref, small_got, sends, recvs, 3 * PARTS, other)
    quad_own = [
        pltpu.make_async_copy(piece_of(member, p), spot_of(0, p), local.at[PARTS + 3 + 2 * seqs + p]) for p in range(PARTS)
    ]
    for copy in quad_sends(0):
        copy.start()
    lined = small_keep_ref.shape[1]

    def fill(at, put):
        low, high, begin = at * lined, (at + 1) * lined, 0
        for ref in (xp_ref, dp_ref, cw_ref, cb_ref, db_ref, sk_ref):
            stop = begin + ref.shape[0]
            a, b = max(low, begin), min(high, stop)
            if a < b:
                put(at // 2, slice(a - low, b - low), ref[a - begin : b - begin, :])
            begin = stop
        if high > begin:
            a = max(low, begin)
            put(at // 2, slice(a - low, lined), jnp.zeros((high - a, width), f32))

    def keep_rows(at, rows_at, value):
        small_keep_ref[at, rows_at, :] = value

    for at in range(count):
        pl.when(side == at % 2)(lambda at=at: fill(at, keep_rows))

        @pl.when(side != at % 2)
        def _(at=at):
            values = []
            fill(at, lambda where, rows_at, value: values.append(value))
            small_give_ref[at // 2] = jnp.concatenate(values, axis=0).astype(bf16)

    for copy in [small_send] + quad_sends(1) + quad_own:
        copy.start()

    def goal(slot):
        return (4 * slot + me) // 2

    spot = pl.ds(pl.multiple_of(lax.rem(me, 2) * width, LANES), width)

    def home_pieces(at):
        if at == PARTS:
            return 1, wz_ref, z_cols.at[:, spot]
        if at > PARTS:
            slot, seq = (at - PARTS - 1) % 2, (at - PARTS - 1) // 2
            some = slice(seq * length, (seq + 1) * length)
            return slot, (gx_ref, gz_ref)[slot].at[some], cols_ref.at[some, spot]
        some = 4 * part
        return 0, h_send.at[at], h_cols.at[at, :, pl.ds(pl.multiple_of(lax.rem(me, 2) * some, LANES), some)]

    def home_send(at):
        slot, src, dst = home_pieces(at)
        return part_copy(src, dst, home_sends.at[at], home_recvs.at[at * 2 + lax.rem(me, 2)], goal(slot))

    def home_keep(at):
        _, src, dst = home_pieces(at)
        return pltpu.make_async_copy(src, dst, local.at[2 + at])

    def home_start(at):
        slot = home_pieces(at)[0]
        pl.when(goal(slot) != me)(lambda: home_send(at).start())
        pl.when(goal(slot) == me)(lambda: home_keep(at).start())

    def home_wait(at):
        slot = home_pieces(at)[0]
        pl.when(goal(slot) != me)(lambda: home_send(at).wait_send())
        pl.when(goal(slot) == me)(lambda: home_keep(at).wait())
        for place in range(2):
            source = lax.rem(2 * me + place, 4)

            @pl.when((me // 2 == slot) & (source != me))
            def _(place=place):
                src = home_pieces(at)[1]
                part_copy(src, src, home_sends.at[at], home_recvs.at[at * 2 + place], peer(1)).wait_recv()

    for at in (*range(PARTS + 1, PARTS + 1 + 2 * seqs), PARTS):
        home_start(at)

    def far_copy(src, dst, kind, step):
        return across(src, dst, far_sends, far_recvs, kind * count + step, far(step))

    def block(step):
        return lax.rem(mine + step, height)

    order = range(1, height)

    def lines(at):
        return pl.ds(pl.multiple_of(at * deep, 16), deep)

    def x_sends(p):
        return [
            across(
                xb_ref.at[lines(ahead(step)), cut(p)], x_in.at[home, :, cut(p)], far_sends, far_recvs,
                p * count + step, ahead(step),
            )
            for step in range(1, count)
        ]

    def x_part(p):
        for copy in quad_sends(p):
            copy.wait_recv()
        quad_own[p].wait()

        for at in range(0, 4 * tokens, tile):
            turned[:, at : at + tile] = gx4[at : at + tile, cut(p)].T
        wide = norm_ref.shape[2] // tile

        def rows_of(t, carry):
            feature = pl.ds(pl.multiple_of(lax.rem(t, wide) * tile, tile), tile)
            value = rows_dot(turned[...], norm_ref[t // wide, :, feature])
            xb_ref[pl.ds(pl.multiple_of(t * tile, tile), tile), cut(p)] = value.astype(bf16).T
            return carry

        lax.fori_loop(0, xb_ref.shape[0] // tile, rows_of, 0)
        x_in[home, :, cut(p)] = xb_ref[lines(home), cut(p)]
        for copy in x_sends(p):
            copy.start()

    def lanes(t):
        return pl.ds(pl.multiple_of(t * tile, tile), tile)

    def near_send(seq):
        return remote(pairs.at[seq], near.at[seq], sends, recvs, 3 * PARTS + 8 + 2 * seq, 1)

    def chip_send(seq):
        return remote(g_send.at[seq], g_far.at[seq], sends, recvs, 3 * PARTS + 9 + 2 * seq, 2)

    def grads_of(seq):
        home_wait(PARTS + 1 + 2 * seq)
        home_wait(PARTS + 2 + 2 * seq)
        for i, owner in enumerate((peer(3), peer(1), peer(2), me)):
            at = pl.ds(pl.multiple_of(seq * length + owner * rows, 16), rows)
            lhs[i * rows : (i + 1) * rows, :] = cols_ref[at, :]
            here = pl.ds(pl.multiple_of(owner * rows, 16), rows)
            inv = inv_ref[seq, here, :]
            for low in range(0, model, LANES):
                unit_x[i * rows : (i + 1) * rows, low : low + LANES] = xs_ref[seq, here, low : low + LANES].astype(f32) * inv

        def product(t, carry):
            value = outer_dot(lhs[...], w_ref[lanes(t), :])
            pairs[seq, :, lanes(t)] = value[: 2 * rows].astype(bf16)
            g_hold[:, lanes(t)] = value[2 * rows : 3 * rows]
            g_own[seq, :, lanes(t)] = value[3 * rows :]
            terms = value * unit_x[:, lanes(t)]
            gains[:, lanes(t)] += jnp.sum(terms.reshape(rows // 2, 8, tile), axis=0)
            return carry

        lax.fori_loop(0, model // tile, product, 0)
        near_send(seq).start()

    def grads_on(seq):
        near_send(seq).wait()
        for low in range(0, model, tile):
            at = slice(low, low + tile)
            g_send[seq, :, at] = (g_hold[:, at] + near[seq, :rows, at].astype(f32)).astype(bf16)
            g_own[seq, :, at] += near[seq, rows:, at].astype(f32)
        chip_send(seq).start()

    def home_sum(p):
        for copy in x_sends(p):
            copy.wait_recv()
        for q in range(4):
            total = x_in[q, :, cut(p)].astype(f32)
            for group in range(1, count // 4):
                total = total + x_in[4 * group + q, :, cut(p)].astype(f32)
            h_send[p, :, q * part : (q + 1) * part] = total.astype(bf16)
        home_start(p)

    gains[...] = jnp.zeros_like(gains)
    load_norm.wait()
    x_part(0)
    small_send.wait_recv()
    for at in range(height):
        sb_ref[at] = (small_keep_ref[at] + small_got[at].astype(f32)).astype(bf16)
    s_sends = [far_copy(sb_ref.at[block(step)], s_in.at[step - 1], PARTS, step) for step in order]
    for copy in s_sends:
        copy.start()
    load.wait()
    grads_of(0)
    x_part(1)
    grads_on(0)
    grads_of(1)
    wide = model // 4

    def gain_part(owner):
        return gains.at[:, pl.ds(pl.multiple_of(owner * wide, LANES), wide)]

    gain_sends = [
        remote(gain_part(peer(hop)), gain_near.at[hop - 1], sends, recvs, 3 * PARTS + 2 + hop, hop) for hop in (1, 2, 3)
    ]
    for copy in gain_sends:
        copy.start()
    for copy in s_sends:
        copy.wait_recv()
    total = sb_ref[mine].astype(f32)
    for step in order:
        total = total + s_in[step - 1].astype(f32)
    s_own[...] = total.astype(bf16)
    small_ref[side, mine] = s_own[...]
    spread = [far_copy(s_own, small_ref.at[side, mine], PARTS + 1, step) for step in order]
    for copy in spread:
        copy.start()

    def pass_on(step):
        at = lax.rem(mine + height - step, height)
        return across(
            small_ref.at[side, at], small_ref.at[side, at], far_sends, far_recvs, (PARTS + 3) * count + step, other
        )

    pass_on(0).start()
    home_sum(0)
    grads_on(1)
    for copy in gain_sends:
        copy.wait()
    gain_sum[...] = gains[:, pl.ds(pl.multiple_of(me * wide, LANES), wide)] + gain_near[0] + gain_near[1] + gain_near[2]
    gain_far = [
        across(gain_sum, gain_in.at[step - 1], far_sends, far_recvs, (PARTS + 2) * count + step, ahead(step))
        for step in range(1, count)
    ]
    for copy in gain_far:
        copy.start()


    def finish_rows(seq):
        chip_send(seq).wait()

        def last(r, carry):
            at = pl.ds(pl.multiple_of(r * 16, 16), 16)
            grad = g_own[seq, at, :] + g_far[seq, at, :].astype(f32)
            vals = x_ref[seq, at, :].astype(f32)
            inv = lax.rsqrt(jnp.mean(vals * vals, axis=1, keepdims=True) + EPS)
            scaled = grad * gain_ref[0:1, :]
            mean = jnp.mean(scaled * vals, axis=1, keepdims=True)
            out = inv * (scaled - vals * (inv * inv * mean))
            dx_ref[seq, at, :] = (cot_ref[seq, at, :].astype(f32) + out).astype(bf16)
            return carry

        lax.fori_loop(0, rows // 16, last, 0)

    finish_rows(0)
    home_sum(1)
    for step in order:
        spread[step - 1].wait_recv()
        pass_on(step).start()
    finish_rows(1)
    for at in range(PARTS + 1):
        home_wait(at)

    @pl.when(me // 2 == 0)
    def _():
        for place in range(2):
            for q in range(4):
                for p in range(PARTS):
                    to = place * width + q * quarter + p * part
                    low = (place * 4 + q) * part
                    gw_ref[:, to : to + part] = h_cols[p, :, low : low + part].astype(f32)

    @pl.when(me // 2 == 1)
    def _():
        for low in range(0, 2 * width, quarter):
            gw_ref[:, low : low + quarter] = z_cols[:, low : low + quarter].astype(f32)

    for copy in gain_far:
        copy.wait()
    total = gain_sum[...]
    for step in range(1, count):
        total = total + gain_in[step - 1]
    ggain_ref[...] = jnp.sum(total, axis=0, keepdims=True)
    for step in range(height):
        pass_on(step).wait()
    goals, start = [], 0
    for ref in (gxp_ref, gdp_ref, gcw_ref, gcb_ref, gdb_ref, gsk_ref):
        goals.append((ref, start, start + ref.shape[0]))
        start += ref.shape[0]
    for at in range(count):
        low, high = at * lined, (at + 1) * lined
        if low < start:
            value = small_ref[at % 2, at // 2].astype(f32)
        for ref, begin, stop in goals:
            a, b = max(low, begin), min(high, stop)
            if a < b:
                ref[a - begin : b - begin, :] = value[a - low : b - low]
    small_send.wait_send()
    for p in range(PARTS):
        for copy in quad_sends(p) + x_sends(p):
            copy.wait_send()
    for copy in s_sends + spread:
        copy.wait_send()


def finish(gx, gz, smalls, wz, norm, w_in, x, cot, gain, xs, inv):
    tokens, width = gx.shape
    height = lax.axis_size("replica") // 2
    lines = -(-sum(value.shape[0] for value in smalls) // (16 * height)) * 8
    deep = wz.shape[0]
    seqs, rows, model = x.shape
    wide = model // 4
    gain_tile = pltpu.VMEM((8, wide), f32)
    other = max(height - 1, 1)
    count = 2 * height
    quarter = width // 4
    kinds = (PARTS + 4) * count
    homes = PARTS + 1 + 2 * seqs
    line = jax.ShapeDtypeStruct((1, width), f32)
    return pl.pallas_call(
        finish_kernel,
        in_specs=[VMEM_SPEC] * 9 + [ANY_SPEC] * 2 + [VMEM_SPEC] * 5,
        out_specs=[VMEM_SPEC] * 9,
        out_shape=[
            jax.ShapeDtypeStruct((deep, 2 * width), f32),
            jax.ShapeDtypeStruct(smalls[0].shape, f32),
            jax.ShapeDtypeStruct(smalls[1].shape, f32),
            jax.ShapeDtypeStruct((KW, width), f32),
            line, line, line,
            jax.ShapeDtypeStruct(x.shape, bf16),
            jax.ShapeDtypeStruct((1, wide), f32),
        ],
        scratch_shapes=[
            pltpu.VMEM((height, lines, width), f32),
            pltpu.VMEM((height, lines, width), bf16),
            pltpu.VMEM((2, height, lines, width), bf16),
            pltpu.VMEM(norm.shape, bf16),
            pltpu.VMEM(w_in.shape, bf16),
            pltpu.VMEM((4 * tokens, quarter), bf16),
            pltpu.VMEM((tokens, 2 * width), bf16),
            pltpu.VMEM((quarter // PARTS, 4 * tokens), bf16),
            pltpu.VMEM((count * deep, quarter), bf16),
            pltpu.VMEM((height, lines, width), bf16),
            pltpu.VMEM((height, lines, width), bf16),
            pltpu.VMEM((count, deep, quarter), bf16),
            pltpu.VMEM((other, lines, width), bf16),
            pltpu.VMEM((4 * rows, 2 * width), bf16),
            pltpu.VMEM((seqs, 2 * rows, model), bf16),
            pltpu.VMEM((seqs, 2 * rows, model), bf16),
            pltpu.VMEM((rows, model), f32),
            pltpu.VMEM((seqs, rows, model), f32),
            pltpu.VMEM((seqs, rows, model), bf16),
            pltpu.VMEM((seqs, rows, model), bf16),
            pltpu.VMEM((PARTS, deep, width // PARTS), bf16),
            pltpu.VMEM((PARTS, deep, 2 * width // PARTS), bf16),
            pltpu.VMEM((deep, 2 * width), bf16),
            pltpu.VMEM((lines, width), bf16),
            pltpu.VMEM((8, model), f32),
            pltpu.VMEM((3, 8, wide), f32),
            gain_tile,
            pltpu.VMEM((count - 1, 8, wide), f32),
            pltpu.VMEM((4 * rows, model), f32),
            pltpu.SemaphoreType.DMA((3 * PARTS + 8 + 2 * seqs,)), pltpu.SemaphoreType.DMA((3 * PARTS + 8 + 2 * seqs,)),
            pltpu.SemaphoreType.DMA((kinds,)), pltpu.SemaphoreType.DMA((kinds,)),
            pltpu.SemaphoreType.DMA((homes,)), pltpu.SemaphoreType.DMA((2 * homes,)),
            pltpu.SemaphoreType.DMA((homes + 2 + PARTS,)),
        ],
        compiler_params=group_params(8, 58 << 20),
        cost_estimate=cost(80),
        name="finish",
    )(gx, gz, *smalls, wz, norm, w_in, x, cot, gain, xs, inv)


def total_kernel(part_ref, out_ref, near, chip_sum, far, sends, recvs):
    me = lax.axis_index("shard")
    half = part_ref.shape[1] // 2
    mine = pl.ds(pl.multiple_of(lax.rem(me, 2) * half, 128), half)
    other = pl.ds(pl.multiple_of((1 - lax.rem(me, 2)) * half, 128), half)
    meet_group()
    first = remote(part_ref.at[:, other], near, sends, recvs, 0, 1)
    first.start()
    first.wait()
    chip_sum[...] = part_ref[:, mine] + near[...]
    second = remote(chip_sum, far, sends, recvs, 1, 2)
    second.start()
    second.wait()
    out_ref[:, mine] = chip_sum[...] + far[...]
    third = remote(out_ref.at[:, mine], out_ref.at[:, mine], sends, recvs, 2, 1)
    third.start()
    third.wait()


def group_total(part, collective_id):
    rows, cols = part.shape
    half = pltpu.VMEM((rows, cols // 2), f32)
    return pl.pallas_call(
        total_kernel,
        in_specs=[VMEM_SPEC],
        out_specs=VMEM_SPEC,
        out_shape=jax.ShapeDtypeStruct((rows, cols), f32),
        scratch_shapes=[half, half, half, pltpu.SemaphoreType.DMA((3,)), pltpu.SemaphoreType.DMA((3,))],
        compiler_params=group_params(collective_id, 16 << 20),
        name="group_total",
    )(part)


def by_hop(value, hop):
    return lax.ppermute(value, "shard", [(i, i ^ hop) for i in range(4)])


def far_send(blocks):
    count = lax.axis_size("replica")
    height = count // 2
    mine = lax.axis_index("replica") // 2

    def pick(at):
        return lax.dynamic_index_in_dim(blocks, at, 0, False)

    sent = []
    for step in range(1, height):
        out = pick(lax.rem(mine + step, height)).astype(bf16)
        sent.append(lax.ppermute(out, "replica", [(i, (i + 2 * step) % count) for i in range(count)]))
    return pick(mine), tuple(sent)


def far_total(own, sent):
    total = own
    for value in sent:
        total = total + value.astype(f32)
    return total


def after(value, *others):
    return lax.optimization_barrier((value,) + others)[0]


def body(
    block_input, segment_ids, norm_gain, w_in, conv_weight, conv_bias, x_proj, dt_proj, dt_bias,
    d_skip, out_proj, out_grad,
):
    seqs, local, model = block_input.shape
    length = segment_ids.shape[1]
    tokens = seqs * length
    width = d_skip.shape[0]
    rank = dt_proj.shape[0]
    n = (x_proj.shape[0] - rank) // 2
    me = lax.axis_index("shard")
    count = lax.axis_size("replica")
    height = count // 2
    side = lax.rem(lax.axis_index("replica"), 2)

    def split(values):
        return values.reshape(seqs, length, -1)

    def halves(values, blocks):
        piece = values.shape[1] // blocks // 2
        cuts = [values[:, b * piece : (b + 1) * piece] for b in range(2 * blocks)]
        even = jnp.concatenate(cuts[0::2], axis=1)
        odd = jnp.concatenate(cuts[1::2], axis=1)
        return jnp.where(side == 0, even, odd), jnp.where(side == 0, odd, even)

    xs, inv, cots, gain, own_half, y_half, z_half, x_part, z_part, gated_own, gated_send, gated_more = front(
        block_input, out_grad, norm_gain, w_in, out_proj
    )
    x_all = xs.reshape(tokens, model)
    cot = cots.reshape(tokens, -1)

    seg_padded = jnp.pad(segment_ids, ((0, 0), (KW - 1, 0)), constant_values=-1)
    taps = [
        (seg_padded[:, KW - 1 - d : KW - 1 - d + length] == segment_ids).astype(f32) for d in range(KW)
    ]
    conv_w = conv_weight.astype(f32)
    xv = x_part.astype(f32)
    x_padded = jnp.pad(xv, ((0, 0), (KW - 1, 0), (0, 0)))
    conv_pre = conv_bias.astype(f32) + conv_w[KW - 1] * xv
    for j in range(KW - 1):
        d = KW - 1 - j
        conv_pre = conv_pre + conv_w[j] * x_padded[:, j : j + length] * taps[d][:, :, None]
    conv_out = jax.nn.silu(conv_pre).astype(bf16)
    conv_flat = conv_out.reshape(tokens, width)
    own_half, y_half, z_half = (value.reshape(tokens, -1) for value in (own_half, y_half, z_half))
    last_norm = lax.ppermute(y_half, "replica", [(i, i ^ 2) for i in range(count)])
    cot_got = lax.ppermute(cot, "replica", [(i, i ^ 1) for i in range(count)])
    proj = group_total(outer_dot(x_proj, conv_flat), 3)
    gated_far = by_hop(gated_send, 2)
    proj, gated_far = lax.optimization_barrier((proj, gated_far))
    gated_rest = by_hop(after(gated_more, proj), 2)
    keep_lanes = jnp.broadcast_to(taps[1][:, :, None], (seqs, length, LANES))
    skip = d_skip.astype(f32)
    y_total, gated, rate, beta, states = recurrence_forward(
        conv_out, z_part, proj, keep_lanes, dt_proj, dt_bias.astype(f32)[None], skip[None]
    )
    y_total, gated, gated_rest, last_norm, cot_got = lax.optimization_barrier(
        (y_total, gated, gated_rest, last_norm, cot_got)
    )
    cot_both = jnp.concatenate([cot, cot_got], axis=0)
    grad_gated = split(gated_own + jnp.concatenate([gated_far, gated_rest], axis=1).astype(f32))
    z_vals = z_part.astype(f32)
    dy = grad_gated * jax.nn.silu(z_vals)
    grad_z = (grad_gated * y_total * silu_slope(z_vals)).astype(bf16).reshape(tokens, width)

    gated_keep, gated_give = halves(gated.reshape(tokens, width), height // 4)
    cols = model // 4
    keeps, gives, grad_z_quad, norms, gated_got = collect(
        gated_keep, gated_give, grad_z, own_half, y_half, z_half, last_norm
    )
    norms = norms.reshape(2, 4 * tokens, -1)
    z_blocks = lax.dot_general(
        norms, grad_z_quad.reshape(4 * tokens, -1), (((1,), (0,)), ((), ())), preferred_element_type=f32
    )
    z_blocks = z_blocks.astype(bf16).reshape(count, -1, width // 4)
    gated_both, block_output, grad_w_z = middle(keeps, gives, gated_got, z_blocks, x_all, out_proj, seqs)
    out_blocks = inner_dot(gated_both.reshape(2 * tokens, -1), cot_both)
    out_own, out_sent = far_send(out_blocks.astype(bf16).reshape(height, -1, cols))
    rate, out_own = lax.optimization_barrier((rate, out_own))

    grad_conv_rec, grad_dt_low, grad_proj, grad_dt_proj, grad_dt_bias, grad_d_skip = recurrence_backward(
        rate, beta, conv_out, dy, proj, keep_lanes, dt_proj, states
    )
    grad_proj, out_sent = lax.optimization_barrier((group_total(grad_proj, 4), out_sent))
    grad_proj = grad_proj.astype(bf16)
    grad_out_proj = far_total(out_own.astype(f32), out_sent)
    grad_x_proj = rows_dot(grad_proj, conv_flat)
    grad_conv = dy * skip + grad_conv_rec + split(inner_dot(grad_proj, x_proj))
    grad_pre = grad_conv * silu_slope(conv_pre)
    grad_conv_bias = jnp.sum(grad_pre, axis=(0, 1))
    grad_conv_weight = jnp.stack(
        [
            jnp.sum(grad_pre * x_padded[:, j : j + length] * taps[KW - 1 - j][:, :, None], axis=(0, 1))
            for j in range(KW)
        ]
    )
    grad_x = conv_w[KW - 1] * grad_pre
    for j in range(KW - 1):
        d = KW - 1 - j
        ahead = jnp.pad(grad_pre * taps[d][:, :, None], ((0, 0), (0, d), (0, 0)))[:, d:]
        grad_x = grad_x + conv_w[j] * ahead
    grad_x = grad_x.astype(bf16).reshape(tokens, width)

    smalls = (grad_x_proj, grad_dt_proj, grad_conv_weight, grad_conv_bias[None], grad_dt_bias, grad_d_skip)
    grad_w_in, grad_x_proj, grad_dt_proj, grad_conv_weight, conv_line, bias_line, skip_line, input_grad, grad_gain = finish(
        grad_x, grad_z, smalls, grad_w_z, norms, w_in, block_input, out_grad, gain, xs, inv
    )
    return (
        block_output, input_grad, grad_gain[0], grad_w_in, grad_conv_weight, conv_line[0], grad_x_proj, grad_dt_proj,
        bias_line[0], skip_line[0], grad_out_proj,
    )


def solution(mesh):
    return jax.shard_map(
        body,
        mesh=mesh,
        in_specs=(
            P("replica", "shard", None), P("replica", None), P("shard"), P(None, "shard"), P(None, "shard"),
            P("shard"), P(None, "shard"), P(None, "shard"), P("shard"), P("shard"), P(None, "shard"),
            P("replica", "shard", None),
        ),
        out_specs=(
            P("replica", "shard", None), P("replica", "shard", None), P("shard"), P("replica", "shard"),
            P(None, "shard"), P("shard"), P(None, "shard"), P(None, "shard"), P("shard"), P("shard"),
            P("replica", "shard"),
        ),
        check_vma=False,
    )
```

```python
import functools

import jax
import jax.numpy as jnp
from jax import lax
from jax.experimental import pallas as pl
from jax.experimental.pallas import tpu as pltpu
from jax.sharding import PartitionSpec as P

KW = 4
EPS = 1e-05
CHUNK = 16
LANES = 128
f32 = jnp.float32
bf16 = jnp.bfloat16


def rows_dot(a, b):
    return jnp.dot(a, b, preferred_element_type=f32)


def inner_dot(a, b):
    return lax.dot_general(a, b, (((0,), (0,)), ((), ())), preferred_element_type=f32)


def outer_dot(a, b):
    return lax.dot_general(a, b, (((1,), (1,)), ((), ())), preferred_element_type=f32)


def silu_slope(values):
    sig_val = jax.nn.sigmoid(values)
    return sig_val + values * sig_val * (1.0 - sig_val)

MESH = pl.DeviceIdType.MESH
BLOCK = 128
UNROLL = 4
BACK_UNROLL = 4


def lane(g):
    return slice(g * LANES, (g + 1) * LANES)


def column(block, t):
    return jnp.broadcast_to(block[:, t : t + 1], (block.shape[0], LANES))


def row(ref, t, g, n):
    return jnp.broadcast_to(ref[t : t + 1, lane(g)], (n, LANES))


def prepare(base, rate_ref, conv_ref, keep_ref, rk, u, kept):
    rows = pl.ds(base, CHUNK)
    rate = rate_ref[0, rows, :]
    keep = keep_ref[0, rows, :]
    conv = conv_ref[0, rows, :].astype(f32)
    for g in range(rate.shape[1] // LANES):
        rk[:, lane(g)] = rate[:, lane(g)] * keep
    u[...] = rate * conv
    kept[...] = keep
    return rate, conv, keep


def shifted(cols, j):
    size = cols.shape[1]
    return pltpu.roll(cols, lax.rem(size - j * CHUNK, size), 1)


def spread_mask(n, size=CHUNK):
    shape = (size, size * n)
    return lax.broadcasted_iota(jnp.int32, shape, 1) // n == lax.broadcasted_iota(jnp.int32, shape, 0)


def picker(n, size=CHUNK):
    shape = (n, size * n)
    return (lax.broadcasted_iota(jnp.int32, shape, 1) % n == lax.broadcasted_iota(jnp.int32, shape, 0)).astype(bf16)


def diagonal(rows, mask, pick):
    return jnp.where(mask, rows_dot(rows.astype(bf16), pick), 0.0).astype(bf16)


def forward_kernel(
    conv_ref, z_ref, proj_ref, keep_ref, dt_proj_ref, dt_bias_ref, skip_ref,
    y_ref, gated_ref, rate_ref, beta_ref, state_ref,
    held_ref, rk, u, kept, query_rows, fresh,
):
    width = conv_ref.shape[2]
    rank = dt_proj_ref.shape[0]
    n = (proj_ref.shape[0] - rank) // 2
    groups = width // LANES
    span = CHUNK * n

    @pl.when(pl.program_id(1) == 0)
    def _():
        held_ref[...] = jnp.zeros_like(held_ref)

    dt_low = proj_ref[0:rank, :].astype(bf16)
    keys = proj_ref[rank : rank + n, :]
    query_rows[...] = proj_ref[rank + n :, :].T
    key_square = jnp.sum(keys.T * keys.T, axis=1, keepdims=True)
    beta = jax.nn.sigmoid(inner_dot(dt_low, dt_proj_ref[...]) + dt_bias_ref[...])
    beta_ref[0] = beta
    rate_ref[0] = beta / (1.0 + beta * key_square)
    mask, pick = spread_mask(n), picker(n)

    def states_of(j, held, rk, u, kept, fresh):
        base = pl.multiple_of(j * CHUNK, CHUNK)
        prepare(base, rate_ref, conv_ref, keep_ref, rk, u, kept)
        near_keys = shifted(keys, j)
        for t in range(CHUNK):
            key = column(near_keys, t)
            key2 = key * key
            keep = jnp.broadcast_to(kept[t : t + 1, :], (n, LANES))
            at = slice(t * n, (t + 1) * n)
            for g in range(groups):
                decay = keep - row(rk, t, g, n) * key2
                held[g] = decay * held[g] + row(u, t, g, n) * key
                fresh[at, lane(g)] = held[g].astype(fresh.dtype)

    def outputs_of(j, fresh):
        base = pl.multiple_of(j * CHUNK, CHUNK)
        rows = pl.ds(base, CHUNK)
        block = fresh[...].astype(bf16)
        state_ref[0, pl.ds(pl.multiple_of(base * n, span), span), :] = block
        conv = conv_ref[0, rows, :].astype(f32)
        total = rows_dot(diagonal(query_rows[rows, :], mask, pick), block) + skip_ref[...] * conv
        y_ref[0, rows, :] = total
        z = z_ref[0, rows, :].astype(f32)
        gated_ref[0, rows, :] = (total * (z * jax.nn.sigmoid(z))).astype(bf16)

    def step(i, held):
        held = list(held)
        for k in range(UNROLL):
            states_of(i * UNROLL + k, held, rk[k], u[k], kept[k], fresh[k])
            if k > 0:
                outputs_of(i * UNROLL + k - 1, fresh[k - 1])
        outputs_of(i * UNROLL + UNROLL - 1, fresh[UNROLL - 1])
        return tuple(held)

    start = tuple(held_ref[:, lane(g)] for g in range(groups))
    end = lax.fori_loop(0, conv_ref.shape[1] // CHUNK // UNROLL, step, start)
    for g in range(groups):
        held_ref[:, lane(g)] = end[g]


def backward_kernel(
    rate_ref, beta_ref, conv_ref, dy_ref, proj_ref, keep_ref, dt_proj_ref, state_ref, last_ref,
    gconv_ref, gdt_ref, gproj_ref, gdt_proj_ref, gdt_bias_ref, gskip_ref,
    held_ref, grate, rk, u, dys, kept, key_rows, adj, adj_state, totals, lined,
):
    block_rows, width = rate_ref.shape[1:]
    rank = dt_proj_ref.shape[0]
    n = (proj_ref.shape[0] - rank) // 2
    groups = width // LANES
    chunks = block_rows // CHUNK

    @pl.when(pl.program_id(1) == 0)
    def _():
        held_ref[...] = jnp.zeros_like(held_ref)

    @pl.when((pl.program_id(0) == 0) & (pl.program_id(1) == 0))
    def _():
        gdt_proj_ref[...] = jnp.zeros_like(gdt_proj_ref)
        gdt_bias_ref[...] = jnp.zeros_like(gdt_bias_ref)
        gskip_ref[...] = jnp.zeros_like(gskip_ref)

    keys = proj_ref[rank : rank + n, :]
    queries = proj_ref[rank + n :, :]
    key_rows[...] = keys.T
    mask, pick = spread_mask(n), picker(n)

    ones = jnp.ones((CHUNK, LANES), bf16)

    def walk(j, held, rk, u, dys, kept, adj, adj_state, totals):
        base = pl.multiple_of(j * CHUNK, CHUNK)
        rows = pl.ds(base, CHUNK)
        prepare(base, rate_ref, conv_ref, keep_ref, rk, u, kept)
        dys[...] = dy_ref[0, rows, :]
        near_keys = shifted(keys, j)
        near_queries = shifted(queries, j)
        late = pl.ds(pl.multiple_of((base + CHUNK - 1) * n, n), n)
        after = [state_ref[0, late, lane(g)] for g in range(groups)]
        for t in reversed(range(CHUNK)):
            own = slice(t * n, (t + 1) * n)
            key = column(near_keys, t)
            key2 = key * key
            query = column(near_queries, t)
            keep = jnp.broadcast_to(kept[t : t + 1, :], (n, LANES))
            prior = jnp.maximum(base + t - 1, 0)
            at = pl.ds(pl.multiple_of(prior * n, n), n)
            parts = [None] * 3
            for g in range(groups):
                slope = row(dys, t, g, n)
                pace = row(rk, t, g, n)
                grad = held[g] + slope * query
                decay = keep - pace * key2
                held[g] = decay * grad
                before = state_ref[0, at, lane(g)]
                if t == 0:
                    before = jnp.where(j == 0, last_ref[0, :, lane(g)], before)
                cross = grad * before.astype(f32)
                adj[own, lane(g)] = grad
                adj_state[own, lane(g)] = cross
                terms = (grad * row(u, t, g, n), cross * pace, after[g].astype(f32) * slope)
                parts = [v if p is None else p + v for p, v in zip(parts, terms)]
                after[g] = before
            for i in range(3):
                totals[i, own, :] = parts[i]

    def settle(j, adj, adj_state, totals):
        base = pl.multiple_of(j * CHUNK, CHUNK)
        rows = pl.ds(base, CHUNK)
        key_block = key_rows[rows, :]
        w1 = rows_dot(diagonal(key_block, mask, pick), adj[...].astype(bf16))
        w2 = rows_dot(diagonal(key_block * key_block, mask, pick), adj_state[...].astype(bf16))
        for i in range(3):
            lined[i, rows, :] = jnp.where(mask, outer_dot(ones, totals[i].astype(bf16)), 0.0)
        keeps = keep_ref[0, rows, :]
        for g in range(groups):
            conv = conv_ref[0, rows, lane(g)].astype(f32)
            grate[rows, lane(g)] = conv * w1[:, lane(g)] - keeps * w2[:, lane(g)]
        gconv_ref[0, rows, :] = rate_ref[0, rows, :] * w1

    def step(i, held):
        held = list(held)
        first = chunks - 1 - i * BACK_UNROLL
        for k in range(BACK_UNROLL):
            walk(first - k, held, rk[k], u[k], dys[k], kept[k], adj[k], adj_state[k], totals[k])
            if k > 0:
                settle(first - k + 1, adj[k - 1], adj_state[k - 1], totals[k - 1])
        last = BACK_UNROLL - 1
        settle(first - last, adj[last], adj_state[last], totals[last])
        return tuple(held)

    start = tuple(held_ref[:, lane(g)] for g in range(groups))
    end = lax.fori_loop(0, chunks // BACK_UNROLL, step, start)
    for g in range(groups):
        held_ref[:, lane(g)] = end[g]

    def picked(left, value):
        high = value.astype(bf16)
        low = (value - high.astype(f32)).astype(bf16)
        return outer_dot(left, high) + outer_dot(left, low)

    rate = rate_ref[0]
    beta = beta_ref[0]
    grad_rate = grate[...]
    self_term = picked(jnp.ones((n, width), bf16), grad_rate * rate * rate)
    key_square = jnp.sum(key_rows[...] * key_rows[...], axis=1, keepdims=True)
    denom_inv = 1.0 / (1.0 + beta * key_square)
    grad_dt = grad_rate * denom_inv * denom_inv * beta * (1.0 - beta)
    low = grad_dt.astype(bf16)
    gdt_ref[0] = low
    gdt_bias_ref[...] += jnp.sum(grad_dt, axis=0, keepdims=True)
    gskip_ref[...] += jnp.sum(dy_ref[0] * conv_ref[0].astype(f32), axis=0, keepdims=True)
    gdt_proj_ref[...] += rows_dot(proj_ref[0:rank, :].astype(bf16), low)
    gproj_ref[0:rank, :] = outer_dot(dt_proj_ref[...], low)
    gproj_ref[rank : rank + n, :] = picked(pick, lined[0]) - 2.0 * keys * (picked(pick, lined[1]) + self_term)
    gproj_ref[rank + n :, :] = picked(pick, lined[2])


def specs_for(length, reverse):
    blocks = length // BLOCK

    def place(b):
        return blocks - 1 - b if reverse else b

    def spec(*shape):
        return pl.BlockSpec((1,) + shape, lambda s, b: (s, place(b)) + (0,) * (len(shape) - 1))

    def across_spec(rows):
        return pl.BlockSpec((rows, BLOCK), lambda s, b: (0, s * blocks + place(b)))

    def whole(*shape):
        return pl.BlockSpec(shape, lambda s, b: (0,) * len(shape))

    return blocks, spec, across_spec, whole


def recurrence_forward(conv, z, proj, keep_lanes, dt_proj, dt_bias, skip):
    seqs, length, width = conv.shape
    rank = dt_proj.shape[0]
    n = (proj.shape[0] - rank) // 2
    blocks, spec, across_spec, whole = specs_for(length, False)
    span = CHUNK * n
    wide = spec(BLOCK, width)
    full = jax.ShapeDtypeStruct((seqs, length, width), f32)
    return pl.pallas_call(
        forward_kernel,
        grid=(seqs, blocks),
        in_specs=[
            wide, wide, across_spec(proj.shape[0]), spec(BLOCK, LANES), whole(rank, width), whole(1, width),
            whole(1, width),
        ],
        out_specs=[wide, wide, wide, wide, spec(BLOCK * n, width)],
        out_shape=[
            full, jax.ShapeDtypeStruct((seqs, length, width), bf16),
            pltpu.HBM((seqs, length, width), f32), pltpu.HBM((seqs, length, width), f32),
            pltpu.HBM((seqs, length * n, width), bf16),
        ],
        scratch_shapes=[
            pltpu.VMEM((n, width), f32),
            [pltpu.VMEM((CHUNK, width), f32)] * UNROLL,
            [pltpu.VMEM((CHUNK, width), f32)] * UNROLL,
            [pltpu.VMEM((CHUNK, LANES), f32)] * UNROLL,
            pltpu.VMEM((BLOCK, n), f32),
            [pltpu.VMEM((span, width), f32)] * UNROLL,
        ],
        compiler_params=pltpu.CompilerParams(vmem_limit_bytes=24 << 20),
        cost_estimate=pl.CostEstimate(flops=16_000_000_000, bytes_accessed=24 << 20, transcendentals=0),
        name="recurrence_forward",
    )(conv, z, proj, keep_lanes, dt_proj, dt_bias, skip)


def recurrence_backward(rate, beta, conv, dy, proj, keep_lanes, dt_proj, states):
    seqs, length, width = rate.shape
    rank = dt_proj.shape[0]
    n = (proj.shape[0] - rank) // 2
    span = CHUNK * n
    blocks, spec, across_spec, whole = specs_for(length, True)
    wide = spec(BLOCK, width)
    before = pl.BlockSpec((1, n, width), lambda s, b: (s, jnp.maximum((blocks - 1 - b) * BLOCK - 1, 0), 0))
    return pl.pallas_call(
        backward_kernel,
        grid=(seqs, blocks),
        in_specs=[
            wide, wide, wide, wide, across_spec(proj.shape[0]), spec(BLOCK, LANES), whole(rank, width),
            spec(BLOCK * n, width), before,
        ],
        out_specs=[wide, wide, across_spec(proj.shape[0]), whole(rank, width), whole(1, width), whole(1, width)],
        out_shape=[
            jax.ShapeDtypeStruct((seqs, length, width), f32),
            jax.ShapeDtypeStruct((seqs, length, width), bf16),
            jax.ShapeDtypeStruct(proj.shape, f32),
            jax.ShapeDtypeStruct((rank, width), f32),
            jax.ShapeDtypeStruct((1, width), f32),
            jax.ShapeDtypeStruct((1, width), f32),
        ],
        scratch_shapes=[
            pltpu.VMEM((n, width), f32),
            pltpu.VMEM((BLOCK, width), f32),
            [pltpu.VMEM((CHUNK, width), f32)] * BACK_UNROLL,
            [pltpu.VMEM((CHUNK, width), f32)] * BACK_UNROLL,
            [pltpu.VMEM((CHUNK, width), f32)] * BACK_UNROLL,
            [pltpu.VMEM((CHUNK, LANES), f32)] * BACK_UNROLL,
            pltpu.VMEM((BLOCK, n), f32),
            [pltpu.VMEM((span, width), f32)] * BACK_UNROLL,
            [pltpu.VMEM((span, width), f32)] * BACK_UNROLL,
            [pltpu.VMEM((3, span, LANES), f32)] * BACK_UNROLL,
            pltpu.VMEM((3, BLOCK, span), f32),
        ],
        compiler_params=pltpu.CompilerParams(vmem_limit_bytes=36 << 20),
        cost_estimate=pl.CostEstimate(flops=30_000_000_000, bytes_accessed=28 << 20, transcendentals=0),
        name="recurrence_backward",
    )(rate, beta, conv, dy, proj, keep_lanes, dt_proj, states, states)


def peer(hop):
    me = lax.axis_index("shard")
    core = lax.rem(me, 2)
    chip = me // 2
    if hop & 1:
        core = 1 - core
    if hop & 2:
        chip = 1 - chip
    return chip * 2 + core


def meet_group():
    barrier = pltpu.get_barrier_semaphore()
    for hop in (1, 2, 3):
        pl.semaphore_signal(barrier, inc=1, device_id={"shard": peer(hop)}, device_id_type=MESH)
    pl.semaphore_wait(barrier, 3)


def remote(src, dst, sends, recvs, at, hop):
    return pltpu.make_async_remote_copy(
        src_ref=src, dst_ref=dst, send_sem=sends.at[at], recv_sem=recvs.at[at],
        device_id={"shard": peer(hop)}, device_id_type=MESH,
    )


def group_params(collective_id, limit):
    return pltpu.CompilerParams(collective_id=collective_id, has_side_effects=True, vmem_limit_bytes=limit)


VMEM_SPEC = pl.BlockSpec(memory_space=pltpu.VMEM)


ANY_SPEC = pl.BlockSpec(memory_space=pl.ANY)


def part_copy(src, dst, send, recv, shard):
    return pltpu.make_async_remote_copy(
        src_ref=src, dst_ref=dst, send_sem=send, recv_sem=recv, device_id={"shard": shard}, device_id_type=MESH
    )


def front_kernel(
    x_ref, cot_ref, gain_ref, w_hbm, o_hbm,
    xs_ref, inv_ref, cots_ref, gain_row_ref, own_half_ref, y_half_ref, z_half_ref, x_part_ref, z_part_ref, own_ref, send_ref, send_more_ref,
    gains_ref, w_ref, o_ref, normed_ref, lhs, mixed, pairs, near, sends, recvs, local, part_sends, part_recvs, part_local,
    pair_sends, pair_recvs, pair_local,
):
    me = lax.axis_index("shard")
    chip = me // 2
    slot = me // 2
    seqs, rows, model = x_ref.shape
    cols = cots_ref.shape[2]
    core = lax.rem(me, 2)
    width = x_part_ref.shape[2]
    lift = gain_ref.shape[0]
    span = 2 * rows
    tile = 256
    loads = [
        pltpu.make_async_copy(w_hbm, w_ref, local.at[3]),
        pltpu.make_async_copy(o_hbm, o_ref, local.at[4]),
    ]
    for copy in loads:
        copy.start()
    meet([quad(1), quad(2)])

    def mine(ref, owner):
        return ref.at[:, pl.ds(pl.multiple_of(owner * rows, 16), rows), :]

    def part(owner):
        return cot_ref.at[:, :, pl.ds(pl.multiple_of(owner * cols, 128), cols)]

    def gain_rows(owner):
        return gains_ref.at[pl.ds(pl.multiple_of(owner * lift, 8), lift), :]

    gain_sends = [remote(gain_ref, gain_rows(me), sends, recvs, 5 + hop, hop) for hop in (1, 2, 3)]
    x_core = remote(x_ref, mine(xs_ref, me), sends, recvs, 0, 1)
    x_chip = remote(x_ref, mine(xs_ref, me), sends, recvs, 1, 2)
    cot_sends = [remote(part(peer(hop)), mine(cots_ref, me), sends, recvs, 2 + hop, hop) for hop in (1, 2, 3)]
    for copy in gain_sends + [x_core, x_chip] + cot_sends:
        copy.start()
    own = [
        pltpu.make_async_copy(x_ref, mine(xs_ref, me), local.at[0]),
        pltpu.make_async_copy(part(me), mine(cots_ref, me), local.at[1]),
        pltpu.make_async_copy(gain_ref, gain_rows(me), local.at[2]),
    ]
    for copy in own:
        copy.start()
    for copy in own:
        copy.wait()
    for copy in gain_sends:
        copy.wait()
    x_core.wait()
    gain = jnp.concatenate([gains_ref[lift * d : lift * d + 1, :] for d in range(4)], axis=1)
    gain_row_ref[...] = jnp.broadcast_to(gain, gain_row_ref.shape)
    loads[0].wait()

    def piece(half, kind):
        where = jnp.bitwise_xor(chip, half)
        return (x_part_ref, z_part_ref)[kind].at[:, pl.ds(pl.multiple_of(where * span, 16), span), :]

    def away(i):
        return lax.rem(2 * me + i, 4) != me

    def send(half, i, kind):
        return part_copy(
            mixed.at[half, i], piece(half, kind), part_sends.at[2 * half + i], part_recvs.at[2 * kind + half],
            lax.rem(2 * me + i, 4),
        )

    def keep(half, i, kind):
        return pltpu.make_async_copy(mixed.at[half, i], piece(half, kind), part_local.at[half])

    def either(half, i, send_does, keep_does):
        for kind in range(2):
            pl.when(away(i) & (slot == kind))(lambda kind=kind: send_does(send(half, i, kind)))
            pl.when(jnp.logical_not(away(i)) & (slot == kind))(lambda kind=kind: keep_does(keep(half, i, kind)))

    def run_half(half):
        where = jnp.bitwise_xor(chip, half) * span

        for seq in range(seqs):

            def norm(r, carry, seq=seq):
                at = pl.ds(pl.multiple_of(where + r * 16, 16), 16)
                vals = xs_ref[seq, at, :].astype(f32)
                inv = lax.rsqrt(jnp.mean(vals * vals, axis=1, keepdims=True) + EPS)
                inv_ref[seq, at, :] = jnp.broadcast_to(inv, (16, LANES))
                out = (vals * inv * gain).astype(bf16)
                normed_ref[seq, at, :] = out
                lhs[pl.ds(pl.multiple_of(seq * span + r * 16, 16), 16), :] = out
                return carry

            lax.fori_loop(0, span // 16, norm, 0)
        for copy in normed_copies(half):
            copy.start()
        for i in range(2):

            def product(t, carry, i=i):
                value = rows_dot(lhs[...], w_ref[:, pl.ds(pl.multiple_of(i * width + t * tile, tile), tile)])
                for seq in range(seqs):
                    mixed[half, i, seq, :, pl.ds(pl.multiple_of(t * tile, tile), tile)] = value[
                        seq * span : (seq + 1) * span
                    ].astype(bf16)
                return carry

            lax.fori_loop(0, width // tile, product, 0)
            either(half, i, lambda copy: copy.start(), lambda copy: copy.start())

    def normed_copies(half):
        where = pl.ds(pl.multiple_of(jnp.bitwise_xor(chip, half) * span, 16), span)
        src = normed_ref.at[:, where, pl.ds(pl.multiple_of(core * (model // 2), LANES), model // 2)]
        copies = [pltpu.make_async_copy(src, own_half_ref.at[:, where, :], pair_local.at[half])]
        for hop in (1, 2):
            at = 2 * half + hop - 1
            half_ref = (y_half_ref, z_half_ref)[hop - 1]
            copies.append(across(src, half_ref.at[:, where, :], pair_sends, pair_recvs, at, quad(hop)))
        return copies

    run_half(0)
    x_chip.wait_recv()
    onward = remote(mine(xs_ref, peer(2)), mine(xs_ref, peer(2)), sends, recvs, 2, 1)
    onward.start()
    onward.wait()
    run_half(1)

    for copy in cot_sends:
        copy.wait()
    loads[1].wait()

    def partial(block, t):
        return outer_dot(
            cots_ref[...].reshape(seqs * 4 * rows, cols),
            o_ref[pl.ds(pl.multiple_of(block * width + t * tile, tile), tile), :],
        )

    def lanes(t):
        return pl.ds(pl.multiple_of(t * tile, tile), tile)

    near_sends = []
    for at, hop in enumerate((3, 1)):

        def fill(t, carry, at=at, hop=hop):
            pairs[at, :, lanes(t)] = partial(peer(hop), t).astype(bf16)
            return carry

        lax.fori_loop(0, width // tile, fill, 0)
        copy = remote(pairs.at[at], near.at[at], sends, recvs, 9 + at, 1)
        copy.start()
        near_sends.append(copy)
    near_sends[0].wait()

    pieces = width // tile // 2
    for first, ref in ((0, send_ref), (pieces, send_more_ref)):

        def to_send(t, carry, first=first, ref=ref):
            ref[:, lanes(t)] = (
                partial(peer(2), first + t) + near[0, :, lanes(first + t)].astype(f32)
            ).astype(bf16)
            return carry

        lax.fori_loop(0, pieces, to_send, 0)
    near_sends[1].wait()

    def to_own(t, carry):
        own_ref[:, lanes(t)] = partial(me, t) + near[1, :, lanes(t)].astype(f32)
        return carry

    lax.fori_loop(0, width // tile, to_own, 0)

    x_chip.wait_send()
    for copy in normed_copies(0) + normed_copies(1):
        copy.wait()
    for half in range(2):
        for i in range(2):
            either(half, i, lambda copy: copy.wait_send(), lambda copy: copy.wait())
        for at in range(2):

            @pl.when(2 * at + me // 2 != me)
            def _(at=at, half=half):
                part_copy(
                    mixed.at[0, 0], mixed.at[0, 0], part_sends.at[0], part_recvs.at[2 * at + half], peer(1)
                ).wait_recv()


def front(x, cot, gain, w_in, out_proj):
    seqs, rows, model = x.shape
    group = lax.axis_size("shard")
    length = rows * group
    cols = model // group
    width = w_in.shape[1] // 2
    tokens = seqs * length
    lifted = jnp.broadcast_to(gain.astype(f32)[None], (8, gain.shape[0]))
    far_sems = pltpu.SemaphoreType.DMA((4,))
    return pl.pallas_call(
        front_kernel,
        in_specs=[VMEM_SPEC] * 3 + [ANY_SPEC] * 2,
        out_specs=[VMEM_SPEC] * 12,
        out_shape=[
            jax.ShapeDtypeStruct((seqs, length, model), bf16),
            jax.ShapeDtypeStruct((seqs, length, LANES), f32),
            jax.ShapeDtypeStruct((seqs, length, cols), bf16),
            jax.ShapeDtypeStruct((8, model), f32),
            jax.ShapeDtypeStruct((seqs, length, model // 2), bf16),
            jax.ShapeDtypeStruct((seqs, length, model // 2), bf16),
            jax.ShapeDtypeStruct((seqs, length, model // 2), bf16),
            jax.ShapeDtypeStruct((seqs, length, width), bf16),
            jax.ShapeDtypeStruct((seqs, length, width), bf16),
            jax.ShapeDtypeStruct((tokens, width), f32),
            jax.ShapeDtypeStruct((tokens, width // 2), bf16),
            jax.ShapeDtypeStruct((tokens, width // 2), bf16),
        ],
        scratch_shapes=[
            pltpu.VMEM((8 * group, gain.shape[0]), f32),
            pltpu.VMEM(w_in.shape, bf16),
            pltpu.VMEM(out_proj.shape, bf16),
            pltpu.VMEM((seqs, length, model), bf16),
            pltpu.VMEM((tokens // 2, model), bf16),
            pltpu.VMEM((2, 2, seqs, 2 * rows, width), bf16),
            pltpu.VMEM((2, tokens, width), bf16),
            pltpu.VMEM((2, tokens, width), bf16),
            pltpu.SemaphoreType.DMA((11,)), pltpu.SemaphoreType.DMA((11,)), pltpu.SemaphoreType.DMA((5,)),
            pltpu.SemaphoreType.DMA((4,)), pltpu.SemaphoreType.DMA((4,)), pltpu.SemaphoreType.DMA((2,)),
            far_sems, far_sems, far_sems,
        ],
        compiler_params=group_params(1, 48 << 20),
        name="front",
    )(x, cot, lifted, w_in, out_proj)


def quad(hop):
    home = lax.axis_index("replica")
    if hop & 1:
        home = home + 1 - 2 * lax.rem(home, 2)
    if hop & 2:
        home = home + 2 - 4 * lax.rem(home // 2, 2)
    return home


def across(src, dst, sends, recvs, at, other):
    return pltpu.make_async_remote_copy(
        src_ref=src, dst_ref=dst, send_sem=sends.at[at], recv_sem=recvs.at[at],
        device_id={"replica": other}, device_id_type=MESH,
    )


def meet(replicas):
    barrier = pltpu.get_barrier_semaphore()
    for hop in (1, 2, 3):
        pl.semaphore_signal(barrier, inc=1, device_id={"shard": peer(hop)}, device_id_type=MESH)
    for other in replicas:
        pl.semaphore_signal(barrier, inc=1, device_id={"replica": other}, device_id_type=MESH)
    pl.semaphore_wait(barrier, 3 + len(replicas))


def ahead(step):
    count = lax.axis_size("replica")
    return lax.rem(lax.axis_index("replica") + step, count)


def collect_kernel(
    keep_ref, give_ref, gz_ref, own_half_ref, y_half_ref, z_half_ref, last_ref,
    keeps_ref, gives_ref, zb_ref, norm_out_ref, got_ref,
    gz_ref4, norm_ref, turned, sends, recvs, local,
):
    me = lax.axis_index("shard")
    half = keep_ref.shape[1]
    core = lax.rem(me, 2)
    member = lax.rem(lax.axis_index("replica"), 4)
    tokens, part = gz_ref4.shape[1:]
    tile = 256

    def norm_rows(which):
        return norm_ref.at[core, which * tokens : (which + 1) * tokens]

    meet([quad(hop) for hop in (1, 2, 3)])

    def quarter(which):
        return gz_ref.at[:, pl.ds(pl.multiple_of(which * part, LANES), part)]

    def spot(ref, owner):
        return ref.at[:, pl.ds(pl.multiple_of(owner * half, 128), half)]

    k_chip = remote(keep_ref, spot(keeps_ref, me), sends, recvs, 0, 2)
    v_chip = remote(give_ref, spot(gives_ref, me), sends, recvs, 1, 2)
    k_core = remote(keep_ref, spot(keeps_ref, me), sends, recvs, 2, 1)
    v_core = remote(give_ref, spot(gives_ref, me), sends, recvs, 3, 1)
    quads = [
        across(quarter(lax.rem(quad(hop), 4)), gz_ref4.at[hop], sends, recvs, 6 + hop, quad(hop)) for hop in (3, 1, 2)
    ]
    give_pair = across(give_ref, got_ref, sends, recvs, 11, quad(1))
    norms = [
        remote(own_half_ref, norm_rows(0), sends, recvs, 12, 1),
        remote(y_half_ref, norm_rows(1), sends, recvs, 10, 1),
        remote(z_half_ref, norm_rows(2), sends, recvs, 13, 1),
        remote(last_ref, norm_rows(3), sends, recvs, 4, 1),
    ]
    own = [
        pltpu.make_async_copy(keep_ref, spot(keeps_ref, me), local.at[0]),
        pltpu.make_async_copy(give_ref, spot(gives_ref, me), local.at[1]),
        pltpu.make_async_copy(quarter(member), gz_ref4.at[0], local.at[2]),
        pltpu.make_async_copy(own_half_ref, norm_rows(0), local.at[5]),
        pltpu.make_async_copy(y_half_ref, norm_rows(1), local.at[3]),
        pltpu.make_async_copy(z_half_ref, norm_rows(2), local.at[6]),
        pltpu.make_async_copy(last_ref, norm_rows(3), local.at[4]),
    ]
    for copy in [k_chip, v_chip] + quads + [give_pair, k_core, v_core] + norms + own:
        copy.start()
    for copy in own + quads + norms:
        copy.wait()
    out_copy = pltpu.make_async_copy(norm_ref, norm_out_ref, local.at[7])
    out_copy.start()
    for hop in range(4):
        for at in range(0, tokens, tile):
            turned[:, hop * tokens + at : hop * tokens + at + tile] = gz_ref4[hop, at : at + tile, :].T
    wide = norm_ref.shape[2] // tile

    def rows_of(t, carry):
        feature = pl.ds(pl.multiple_of(lax.rem(t, wide) * tile, tile), tile)
        value = rows_dot(turned[...], norm_ref[t // wide, :, feature])
        zb_ref[pl.ds(pl.multiple_of(t * tile, tile), tile), :] = value.astype(bf16).T
        return carry

    lax.fori_loop(0, zb_ref.shape[0] // tile, rows_of, 0)
    k_chip.wait_recv()
    k_on = remote(spot(keeps_ref, peer(2)), spot(keeps_ref, peer(2)), sends, recvs, 5, 1)
    k_on.start()
    v_chip.wait_recv()
    v_on = remote(spot(gives_ref, peer(2)), spot(gives_ref, peer(2)), sends, recvs, 6, 1)
    v_on.start()
    for copy in [give_pair, k_core, v_core, k_on, v_on, out_copy]:
        copy.wait()
    k_chip.wait_send()
    v_chip.wait_send()


def cost(microseconds):
    return pl.CostEstimate(flops=int(microseconds * 1e9), bytes_accessed=1 << 20, transcendentals=0)


def collect(keep, give, grad_z, own_half, y_half, z_half, last_norm):
    tokens, half = keep.shape
    group = lax.axis_size("shard")
    wide = jax.ShapeDtypeStruct((tokens, half * group), bf16)
    features, quarter = last_norm.shape[1], grad_z.shape[1] // 4
    return pl.pallas_call(
        collect_kernel,
        in_specs=[VMEM_SPEC] * 7,
        out_specs=[VMEM_SPEC] * 3 + [ANY_SPEC, VMEM_SPEC],
        out_shape=[
            wide, wide, jax.ShapeDtypeStruct((2 * features, quarter), bf16),
            pltpu.HBM((2, 4 * tokens, features), bf16),
            jax.ShapeDtypeStruct(give.shape, bf16),
        ],
        scratch_shapes=[
            pltpu.VMEM((4, tokens, quarter), bf16),
            pltpu.VMEM((2, 4 * tokens, features), bf16),
            pltpu.VMEM((quarter, 4 * tokens), bf16),
            pltpu.SemaphoreType.DMA((14,)), pltpu.SemaphoreType.DMA((14,)), pltpu.SemaphoreType.DMA((8,)),
        ],
        compiler_params=group_params(6, 34 << 20),
        cost_estimate=cost(25),
        name="collect",
    )(keep, give, grad_z, own_half, y_half, z_half, last_norm)


def middle_kernel(
    keeps_ref, gives_ref, got_ref, z_ref, x_hbm, o_hbm,
    both_ref, out_ref, wz_ref,
    z_got_ref, o_ref, xcol, outs, sends, recvs, far_sends, far_recvs, local, o_local,
):
    me = lax.axis_index("shard")
    side = lax.rem(lax.axis_index("replica"), 2)
    tokens, half = got_ref.shape
    gots_ref = both_ref.at[1]
    seqs, rows, _ = out_ref.shape
    cols = xcol.shape[1]
    piece = o_hbm.shape[0] // lax.axis_size("replica")
    per = half // piece
    loads = []
    for d in range(4):
        for q in range(2):
            for j in range(per):
                at = d * 2 * half + (2 * j) * piece + (side if q == 0 else 1 - side) * piece
                loads.append(
                    pltpu.make_async_copy(
                        o_hbm.at[pl.ds(pl.multiple_of(at, piece), piece), :],
                        o_ref.at[q, pl.ds(d * half + j * piece, piece), :],
                        o_local.at[len(loads)],
                    )
                )
    for copy in loads:
        copy.start()
    fetch = pltpu.make_async_copy(
        x_hbm.at[:, pl.ds(pl.multiple_of(me * cols, 128), cols)], xcol, local.at[0]
    )
    fetch.start()
    home = lax.axis_index("replica")
    count = lax.axis_size("replica")
    meet([ahead(step) for step in range(1, count)])

    def spot(owner):
        return gots_ref.at[:, pl.ds(pl.multiple_of(owner * half, 128), half)]

    g_own = pltpu.make_async_copy(got_ref, spot(me), local.at[2])
    g_chip = remote(got_ref, spot(me), sends, recvs, 0, 2)
    g_core = remote(got_ref, spot(me), sends, recvs, 1, 1)
    own = [
        pltpu.make_async_copy(keeps_ref, both_ref.at[0], local.at[1]),
    ]
    own.append(pltpu.make_async_copy(z_ref.at[home], z_got_ref.at[home], local.at[3 + seqs]))
    z_sends = [
        across(z_ref.at[ahead(step)], z_got_ref.at[home], far_sends, far_recvs, step, ahead(step))
        for step in range(1, count)
    ]
    own.append(g_own)
    for copy in [g_chip] + z_sends + [g_core] + own:
        copy.start()
    for copy in loads + [fetch]:
        copy.wait()
    tile = 256

    def product(t, carry):
        rows_at = pl.ds(pl.multiple_of(t * tile, tile), tile)
        value = (
            xcol[rows_at, :].astype(f32)
            + rows_dot(keeps_ref[rows_at, :], o_ref[0])
            + rows_dot(gives_ref[rows_at, :], o_ref[1])
        )
        outs[rows_at, :] = value.astype(bf16)
        return carry

    lax.fori_loop(0, tokens // tile, product, 0)
    length = tokens // seqs
    out_sends = []
    for seq in range(seqs):
        for n_hop, hop in enumerate((2, 3, 1)):
            src = outs.at[pl.ds(pl.multiple_of(seq * length + peer(hop) * rows, 16), rows), :]
            dst = out_ref.at[seq, :, pl.ds(pl.multiple_of(me * cols, 128), cols)]
            out_sends.append(remote(src, dst, sends, recvs, 2 + seq * 3 + n_hop, hop))
        own.append(
            pltpu.make_async_copy(
                outs.at[pl.ds(pl.multiple_of(seq * length + me * rows, 16), rows), :],
                out_ref.at[seq, :, pl.ds(pl.multiple_of(me * cols, 128), cols)],
                local.at[3 + seq],
            )
        )
        own[-1].start()
    for copy in out_sends:
        copy.start()
    base = 2 + seqs * 3
    g_chip.wait_recv()
    g_on = remote(spot(peer(2)), spot(peer(2)), sends, recvs, base + 2, 1)
    g_on.start()
    for copy in out_sends + [g_on, g_core] + own + z_sends:
        copy.wait()
    g_chip.wait_send()
    quarter = z_got_ref.shape[2]
    for q in range(4):
        total = z_got_ref[q].astype(f32)
        for group in range(1, count // 4):
            total = total + z_got_ref[4 * group + q].astype(f32)
        wz_ref[:, q * quarter : (q + 1) * quarter] = total.astype(bf16)


def middle(keeps, gives, got, z_blocks, x_all, out_proj, seqs):
    tokens, half = got.shape
    group = lax.axis_size("shard")
    model = x_all.shape[1]
    cols = model // group
    far_sems = pltpu.SemaphoreType.DMA((lax.axis_size("replica"),))
    pieces = 8 * max(1, half * lax.axis_size("replica") // out_proj.shape[0])
    return pl.pallas_call(
        middle_kernel,
        in_specs=[VMEM_SPEC] * 4 + [ANY_SPEC] * 2,
        out_specs=[VMEM_SPEC] * 3,
        out_shape=[
            jax.ShapeDtypeStruct((2, tokens, half * group), bf16),
            jax.ShapeDtypeStruct((seqs, tokens // seqs // group, model), bf16),
            jax.ShapeDtypeStruct((z_blocks.shape[1], 4 * z_blocks.shape[2]), bf16),
        ],
        scratch_shapes=[
            pltpu.VMEM(z_blocks.shape, bf16),
            pltpu.VMEM((2, half * group, cols), bf16),
            pltpu.VMEM((tokens, cols), bf16),
            pltpu.VMEM((tokens, cols), bf16),
            pltpu.SemaphoreType.DMA((5 + 3 * seqs,)), pltpu.SemaphoreType.DMA((5 + 3 * seqs,)),
            far_sems, far_sems, pltpu.SemaphoreType.DMA((4 + seqs,)), pltpu.SemaphoreType.DMA((pieces,)),
        ],
        compiler_params=group_params(7, 22 << 20),
        cost_estimate=cost(25),
        name="middle",
    )(keeps, gives, got, z_blocks, x_all, out_proj)


PARTS = 2


def finish_kernel(
    gx_ref, gz_ref, xp_ref, dp_ref, cw_ref, cb_ref, db_ref, sk_ref, wz_ref, norm_hbm, w_hbm, x_ref, cot_ref, gain_ref, xs_ref, inv_ref,
    gw_ref, gxp_ref, gdp_ref, gcw_ref, gcb_ref, gdb_ref, gsk_ref, dx_ref, ggain_ref,
    small_keep_ref, small_give_ref, small_ref, norm_ref, w_ref, gx4, cols_ref, turned, xb_ref, sb_ref, small_got, x_in, s_in, lhs, pairs, near, g_hold, g_own, g_send, g_far,
    h_send, h_cols, z_cols, s_own, gains, gain_near, gain_sum, gain_in, unit_x,
    sends, recvs, far_sends, far_recvs, home_sends, home_recvs, local,
):
    me = lax.axis_index("shard")
    home = lax.axis_index("replica")
    count = lax.axis_size("replica")
    height = count // 2
    mine = home // 2
    side = lax.rem(home, 2)
    seqs, rows, model = x_ref.shape
    tokens, width = gx_ref.shape
    length = tokens // seqs
    deep = wz_ref.shape[0]
    member = lax.rem(home, 4)
    quarter = width // 4
    part = quarter // PARTS
    tile = 256
    other = quad(1)
    load = pltpu.make_async_copy(w_hbm, w_ref, local.at[0])
    load_norm = pltpu.make_async_copy(norm_hbm, norm_ref, local.at[1])
    load_norm.start()
    load.start()
    meet([ahead(step) for step in range(1, count)])

    def far(step):
        return ahead(2 * step)

    def cut(p):
        return slice(p * part, (p + 1) * part)

    def piece_of(which, p):
        return gx_ref.at[:, pl.ds(pl.multiple_of(which * quarter + p * part, LANES), part)]

    def spot_of(hop, p):
        return gx4.at[hop * tokens : (hop + 1) * tokens, cut(p)]

    def quad_sends(p):
        return [
            across(piece_of(lax.rem(quad(hop), 4), p), spot_of(hop, p), sends, recvs, 3 * p + hop - 1, quad(hop))
            for hop in (3, 1, 2)
        ]

    small_send = across(small_give_ref, small_got, sends, recvs, 3 * PARTS, other)
    quad_own = [
        pltpu.make_async_copy(piece_of(member, p), spot_of(0, p), local.at[PARTS + 3 + 2 * seqs + p]) for p in range(PARTS)
    ]
    for copy in quad_sends(0):
        copy.start()
    lined = small_keep_ref.shape[1]

    def fill(at, put):
        low, high, begin = at * lined, (at + 1) * lined, 0
        for ref in (xp_ref, dp_ref, cw_ref, cb_ref, db_ref, sk_ref):
            stop = begin + ref.shape[0]
            a, b = max(low, begin), min(high, stop)
            if a < b:
                put(at // 2, slice(a - low, b - low), ref[a - begin : b - begin, :])
            begin = stop
        if high > begin:
            a = max(low, begin)
            put(at // 2, slice(a - low, lined), jnp.zeros((high - a, width), f32))

    def keep_rows(at, rows_at, value):
        small_keep_ref[at, rows_at, :] = value

    for at in range(count):
        pl.when(side == at % 2)(lambda at=at: fill(at, keep_rows))

        @pl.when(side != at % 2)
        def _(at=at):
            values = []
            fill(at, lambda where, rows_at, value: values.append(value))
            small_give_ref[at // 2] = jnp.concatenate(values, axis=0).astype(bf16)

    for copy in [small_send] + quad_sends(1) + quad_own:
        copy.start()

    def goal(slot):
        return (4 * slot + me) // 2

    spot = pl.ds(pl.multiple_of(lax.rem(me, 2) * width, LANES), width)

    def home_pieces(at):
        if at == PARTS:
            return 1, wz_ref, z_cols.at[:, spot]
        if at > PARTS:
            slot, seq = (at - PARTS - 1) % 2, (at - PARTS - 1) // 2
            some = slice(seq * length, (seq + 1) * length)
            return slot, (gx_ref, gz_ref)[slot].at[some], cols_ref.at[some, spot]
        some = 4 * part
        return 0, h_send.at[at], h_cols.at[at, :, pl.ds(pl.multiple_of(lax.rem(me, 2) * some, LANES), some)]

    def home_send(at):
        slot, src, dst = home_pieces(at)
        return part_copy(src, dst, home_sends.at[at], home_recvs.at[at * 2 + lax.rem(me, 2)], goal(slot))

    def home_keep(at):
        _, src, dst = home_pieces(at)
        return pltpu.make_async_copy(src, dst, local.at[2 + at])

    def home_start(at):
        slot = home_pieces(at)[0]
        pl.when(goal(slot) != me)(lambda: home_send(at).start())
        pl.when(goal(slot) == me)(lambda: home_keep(at).start())

    def home_wait(at):
        slot = home_pieces(at)[0]
        pl.when(goal(slot) != me)(lambda: home_send(at).wait_send())
        pl.when(goal(slot) == me)(lambda: home_keep(at).wait())
        for place in range(2):
            source = lax.rem(2 * me + place, 4)

            @pl.when((me // 2 == slot) & (source != me))
            def _(place=place):
                src = home_pieces(at)[1]
                part_copy(src, src, home_sends.at[at], home_recvs.at[at * 2 + place], peer(1)).wait_recv()

    for at in (*range(PARTS + 1, PARTS + 1 + 2 * seqs), PARTS):
        home_start(at)

    def far_copy(src, dst, kind, step):
        return across(src, dst, far_sends, far_recvs, kind * count + step, far(step))

    def block(step):
        return lax.rem(mine + step, height)

    order = range(1, height)

    def lines(at):
        return pl.ds(pl.multiple_of(at * deep, 16), deep)

    def x_sends(p):
        return [
            across(
                xb_ref.at[lines(ahead(step)), cut(p)], x_in.at[home, :, cut(p)], far_sends, far_recvs,
                p * count + step, ahead(step),
            )
            for step in range(1, count)
        ]

    def x_part(p):
        for copy in quad_sends(p):
            copy.wait_recv()
        quad_own[p].wait()

        for at in range(0, 4 * tokens, tile):
            turned[:, at : at + tile] = gx4[at : at + tile, cut(p)].T
        wide = norm_ref.shape[2] // tile

        def rows_of(t, carry):
            feature = pl.ds(pl.multiple_of(lax.rem(t, wide) * tile, tile), tile)
            value = rows_dot(turned[...], norm_ref[t // wide, :, feature])
            xb_ref[pl.ds(pl.multiple_of(t * tile, tile), tile), cut(p)] = value.astype(bf16).T
            return carry

        lax.fori_loop(0, xb_ref.shape[0] // tile, rows_of, 0)
        x_in[home, :, cut(p)] = xb_ref[lines(home), cut(p)]
        for copy in x_sends(p):
            copy.start()

    def lanes(t):
        return pl.ds(pl.multiple_of(t * tile, tile), tile)

    def near_send(seq):
        return remote(pairs.at[seq], near.at[seq], sends, recvs, 3 * PARTS + 8 + 2 * seq, 1)

    def chip_send(seq):
        return remote(g_send.at[seq], g_far.at[seq], sends, recvs, 3 * PARTS + 9 + 2 * seq, 2)

    def grads_of(seq):
        home_wait(PARTS + 1 + 2 * seq)
        home_wait(PARTS + 2 + 2 * seq)
        for i, owner in enumerate((peer(3), peer(1), peer(2), me)):
            at = pl.ds(pl.multiple_of(seq * length + owner * rows, 16), rows)
            lhs[i * rows : (i + 1) * rows, :] = cols_ref[at, :]
            here = pl.ds(pl.multiple_of(owner * rows, 16), rows)
            inv = inv_ref[seq, here, :]
            for low in range(0, model, LANES):
                unit_x[i * rows : (i + 1) * rows, low : low + LANES] = xs_ref[seq, here, low : low + LANES].astype(f32) * inv

        def product(t, carry):
            value = outer_dot(lhs[...], w_ref[lanes(t), :])
            pairs[seq, :, lanes(t)] = value[: 2 * rows].astype(bf16)
            g_hold[:, lanes(t)] = value[2 * rows : 3 * rows]
            g_own[seq, :, lanes(t)] = value[3 * rows :]
            terms = value * unit_x[:, lanes(t)]
            gains[:, lanes(t)] += jnp.sum(terms.reshape(rows // 2, 8, tile), axis=0)
            return carry

        lax.fori_loop(0, model // tile, product, 0)
        near_send(seq).start()

    def grads_on(seq):
        near_send(seq).wait()
        for low in range(0, model, tile):
            at = slice(low, low + tile)
            g_send[seq, :, at] = (g_hold[:, at] + near[seq, :rows, at].astype(f32)).astype(bf16)
            g_own[seq, :, at] += near[seq, rows:, at].astype(f32)
        chip_send(seq).start()

    def home_sum(p):
        for copy in x_sends(p):
            copy.wait_recv()
        for q in range(4):
            total = x_in[q, :, cut(p)].astype(f32)
            for group in range(1, count // 4):
                total = total + x_in[4 * group + q, :, cut(p)].astype(f32)
            h_send[p, :, q * part : (q + 1) * part] = total.astype(bf16)
        home_start(p)

    gains[...] = jnp.zeros_like(gains)
    load_norm.wait()
    x_part(0)
    small_send.wait_recv()
    for at in range(height):
        sb_ref[at] = (small_keep_ref[at] + small_got[at].astype(f32)).astype(bf16)
    s_sends = [far_copy(sb_ref.at[block(step)], s_in.at[step - 1], PARTS, step) for step in order]
    for copy in s_sends:
        copy.start()
    load.wait()
    grads_of(0)
    x_part(1)
    grads_on(0)
    grads_of(1)
    wide = model // 4

    def gain_part(owner):
        return gains.at[:, pl.ds(pl.multiple_of(owner * wide, LANES), wide)]

    gain_sends = [
        remote(gain_part(peer(hop)), gain_near.at[hop - 1], sends, recvs, 3 * PARTS + 2 + hop, hop) for hop in (1, 2, 3)
    ]
    for copy in gain_sends:
        copy.start()
    for copy in s_sends:
        copy.wait_recv()
    total = sb_ref[mine].astype(f32)
    for step in order:
        total = total + s_in[step - 1].astype(f32)
    s_own[...] = total.astype(bf16)
    small_ref[side, mine] = s_own[...]
    spread = [far_copy(s_own, small_ref.at[side, mine], PARTS + 1, step) for step in order]
    for copy in spread:
        copy.start()

    def pass_on(step):
        at = lax.rem(mine + height - step, height)
        return across(
            small_ref.at[side, at], small_ref.at[side, at], far_sends, far_recvs, (PARTS + 3) * count + step, other
        )

    pass_on(0).start()
    home_sum(0)
    grads_on(1)
    for copy in gain_sends:
        copy.wait()
    gain_sum[...] = gains[:, pl.ds(pl.multiple_of(me * wide, LANES), wide)] + gain_near[0] + gain_near[1] + gain_near[2]
    gain_far = [
        across(gain_sum, gain_in.at[step - 1], far_sends, far_recvs, (PARTS + 2) * count + step, ahead(step))
        for step in range(1, count)
    ]
    for copy in gain_far:
        copy.start()


    def finish_rows(seq):
        chip_send(seq).wait()

        def last(r, carry):
            at = pl.ds(pl.multiple_of(r * 16, 16), 16)
            grad = g_own[seq, at, :] + g_far[seq, at, :].astype(f32)
            vals = x_ref[seq, at, :].astype(f32)
            inv = lax.rsqrt(jnp.mean(vals * vals, axis=1, keepdims=True) + EPS)
            scaled = grad * gain_ref[0:1, :]
            mean = jnp.mean(scaled * vals, axis=1, keepdims=True)
            out = inv * (scaled - vals * (inv * inv * mean))
            dx_ref[seq, at, :] = (cot_ref[seq, at, :].astype(f32) + out).astype(bf16)
            return carry

        lax.fori_loop(0, rows // 16, last, 0)

    finish_rows(0)
    home_sum(1)
    for step in order:
        spread[step - 1].wait_recv()
        pass_on(step).start()
    finish_rows(1)
    for at in range(PARTS + 1):
        home_wait(at)

    @pl.when(me // 2 == 0)
    def _():
        for place in range(2):
            for q in range(4):
                for p in range(PARTS):
                    to = place * width + q * quarter + p * part
                    low = (place * 4 + q) * part
                    gw_ref[:, to : to + part] = h_cols[p, :, low : low + part].astype(f32)

    @pl.when(me // 2 == 1)
    def _():
        for low in range(0, 2 * width, quarter):
            gw_ref[:, low : low + quarter] = z_cols[:, low : low + quarter].astype(f32)

    for copy in gain_far:
        copy.wait()
    total = gain_sum[...]
    for step in range(1, count):
        total = total + gain_in[step - 1]
    ggain_ref[...] = jnp.sum(total, axis=0, keepdims=True)
    for step in range(height):
        pass_on(step).wait()
    goals, start = [], 0
    for ref in (gxp_ref, gdp_ref, gcw_ref, gcb_ref, gdb_ref, gsk_ref):
        goals.append((ref, start, start + ref.shape[0]))
        start += ref.shape[0]
    for at in range(count):
        low, high = at * lined, (at + 1) * lined
        if low < start:
            value = small_ref[at % 2, at // 2].astype(f32)
        for ref, begin, stop in goals:
            a, b = max(low, begin), min(high, stop)
            if a < b:
                ref[a - begin : b - begin, :] = value[a - low : b - low]
    small_send.wait_send()
    for p in range(PARTS):
        for copy in quad_sends(p) + x_sends(p):
            copy.wait_send()
    for copy in s_sends + spread:
        copy.wait_send()


def finish(gx, gz, smalls, wz, norm, w_in, x, cot, gain, xs, inv):
    tokens, width = gx.shape
    height = lax.axis_size("replica") // 2
    lines = -(-sum(value.shape[0] for value in smalls) // (16 * height)) * 8
    deep = wz.shape[0]
    seqs, rows, model = x.shape
    wide = model // 4
    gain_tile = pltpu.VMEM((8, wide), f32)
    other = max(height - 1, 1)
    count = 2 * height
    quarter = width // 4
    kinds = (PARTS + 4) * count
    homes = PARTS + 1 + 2 * seqs
    line = jax.ShapeDtypeStruct((1, width), f32)
    return pl.pallas_call(
        finish_kernel,
        in_specs=[VMEM_SPEC] * 9 + [ANY_SPEC] * 2 + [VMEM_SPEC] * 5,
        out_specs=[VMEM_SPEC] * 9,
        out_shape=[
            jax.ShapeDtypeStruct((deep, 2 * width), f32),
            jax.ShapeDtypeStruct(smalls[0].shape, f32),
            jax.ShapeDtypeStruct(smalls[1].shape, f32),
            jax.ShapeDtypeStruct((KW, width), f32),
            line, line, line,
            jax.ShapeDtypeStruct(x.shape, bf16),
            jax.ShapeDtypeStruct((1, wide), f32),
        ],
        scratch_shapes=[
            pltpu.VMEM((height, lines, width), f32),
            pltpu.VMEM((height, lines, width), bf16),
            pltpu.VMEM((2, height, lines, width), bf16),
            pltpu.VMEM(norm.shape, bf16),
            pltpu.VMEM(w_in.shape, bf16),
            pltpu.VMEM((4 * tokens, quarter), bf16),
            pltpu.VMEM((tokens, 2 * width), bf16),
            pltpu.VMEM((quarter // PARTS, 4 * tokens), bf16),
            pltpu.VMEM((count * deep, quarter), bf16),
            pltpu.VMEM((height, lines, width), bf16),
            pltpu.VMEM((height, lines, width), bf16),
            pltpu.VMEM((count, deep, quarter), bf16),
            pltpu.VMEM((other, lines, width), bf16),
            pltpu.VMEM((4 * rows, 2 * width), bf16),
            pltpu.VMEM((seqs, 2 * rows, model), bf16),
            pltpu.VMEM((seqs, 2 * rows, model), bf16),
            pltpu.VMEM((rows, model), f32),
            pltpu.VMEM((seqs, rows, model), f32),
            pltpu.VMEM((seqs, rows, model), bf16),
            pltpu.VMEM((seqs, rows, model), bf16),
            pltpu.VMEM((PARTS, deep, width // PARTS), bf16),
            pltpu.VMEM((PARTS, deep, 2 * width // PARTS), bf16),
            pltpu.VMEM((deep, 2 * width), bf16),
            pltpu.VMEM((lines, width), bf16),
            pltpu.VMEM((8, model), f32),
            pltpu.VMEM((3, 8, wide), f32),
            gain_tile,
            pltpu.VMEM((count - 1, 8, wide), f32),
            pltpu.VMEM((4 * rows, model), f32),
            pltpu.SemaphoreType.DMA((3 * PARTS + 8 + 2 * seqs,)), pltpu.SemaphoreType.DMA((3 * PARTS + 8 + 2 * seqs,)),
            pltpu.SemaphoreType.DMA((kinds,)), pltpu.SemaphoreType.DMA((kinds,)),
            pltpu.SemaphoreType.DMA((homes,)), pltpu.SemaphoreType.DMA((2 * homes,)),
            pltpu.SemaphoreType.DMA((homes + 2 + PARTS,)),
        ],
        compiler_params=group_params(8, 58 << 20),
        cost_estimate=cost(80),
        name="finish",
    )(gx, gz, *smalls, wz, norm, w_in, x, cot, gain, xs, inv)


def total_kernel(part_ref, out_ref, near, chip_sum, far, sends, recvs):
    me = lax.axis_index("shard")
    half = part_ref.shape[1] // 2
    mine = pl.ds(pl.multiple_of(lax.rem(me, 2) * half, 128), half)
    other = pl.ds(pl.multiple_of((1 - lax.rem(me, 2)) * half, 128), half)
    meet_group()
    first = remote(part_ref.at[:, other], near, sends, recvs, 0, 1)
    first.start()
    first.wait()
    chip_sum[...] = part_ref[:, mine] + near[...]
    second = remote(chip_sum, far, sends, recvs, 1, 2)
    second.start()
    second.wait()
    out_ref[:, mine] = chip_sum[...] + far[...]
    third = remote(out_ref.at[:, mine], out_ref.at[:, mine], sends, recvs, 2, 1)
    third.start()
    third.wait()


def group_total(part, collective_id):
    rows, cols = part.shape
    half = pltpu.VMEM((rows, cols // 2), f32)
    return pl.pallas_call(
        total_kernel,
        in_specs=[VMEM_SPEC],
        out_specs=VMEM_SPEC,
        out_shape=jax.ShapeDtypeStruct((rows, cols), f32),
        scratch_shapes=[half, half, half, pltpu.SemaphoreType.DMA((3,)), pltpu.SemaphoreType.DMA((3,))],
        compiler_params=group_params(collective_id, 16 << 20),
        name="group_total",
    )(part)


def by_hop(value, hop):
    return lax.ppermute(value, "shard", [(i, i ^ hop) for i in range(4)])


def far_send(blocks):
    count = lax.axis_size("replica")
    height = count // 2
    mine = lax.axis_index("replica") // 2

    def pick(at):
        return lax.dynamic_index_in_dim(blocks, at, 0, False)

    sent = []
    for step in range(1, height):
        out = pick(lax.rem(mine + step, height)).astype(bf16)
        sent.append(lax.ppermute(out, "replica", [(i, (i + 2 * step) % count) for i in range(count)]))
    return pick(mine), tuple(sent)


def far_total(own, sent):
    total = own
    for value in sent:
        total = total + value.astype(f32)
    return total


def after(value, *others):
    return lax.optimization_barrier((value,) + others)[0]


def body(
    block_input, segment_ids, norm_gain, w_in, conv_weight, conv_bias, x_proj, dt_proj, dt_bias,
    d_skip, out_proj, out_grad,
):
    seqs, local, model = block_input.shape
    length = segment_ids.shape[1]
    tokens = seqs * length
    width = d_skip.shape[0]
    rank = dt_proj.shape[0]
    n = (x_proj.shape[0] - rank) // 2
    me = lax.axis_index("shard")
    count = lax.axis_size("replica")
    height = count // 2
    side = lax.rem(lax.axis_index("replica"), 2)

    def split(values):
        return values.reshape(seqs, length, -1)

    def halves(values, blocks):
        piece = values.shape[1] // blocks // 2
        cuts = [values[:, b * piece : (b + 1) * piece] for b in range(2 * blocks)]
        even = jnp.concatenate(cuts[0::2], axis=1)
        odd = jnp.concatenate(cuts[1::2], axis=1)
        return jnp.where(side == 0, even, odd), jnp.where(side == 0, odd, even)

    xs, inv, cots, gain, own_half, y_half, z_half, x_part, z_part, gated_own, gated_send, gated_more = front(
        block_input, out_grad, norm_gain, w_in, out_proj
    )
    x_all = xs.reshape(tokens, model)
    cot = cots.reshape(tokens, -1)

    seg_padded = jnp.pad(segment_ids, ((0, 0), (KW - 1, 0)), constant_values=-1)
    taps = [
        (seg_padded[:, KW - 1 - d : KW - 1 - d + length] == segment_ids).astype(f32) for d in range(KW)
    ]
    conv_w = conv_weight.astype(f32)
    xv = x_part.astype(f32)
    x_padded = jnp.pad(xv, ((0, 0), (KW - 1, 0), (0, 0)))
    conv_pre = conv_bias.astype(f32) + conv_w[KW - 1] * xv
    for j in range(KW - 1):
        d = KW - 1 - j
        conv_pre = conv_pre + conv_w[j] * x_padded[:, j : j + length] * taps[d][:, :, None]
    conv_out = jax.nn.silu(conv_pre).astype(bf16)
    conv_flat = conv_out.reshape(tokens, width)
    own_half, y_half, z_half = (value.reshape(tokens, -1) for value in (own_half, y_half, z_half))
    last_norm = lax.ppermute(y_half, "replica", [(i, i ^ 2) for i in range(count)])
    cot_got = lax.ppermute(cot, "replica", [(i, i ^ 1) for i in range(count)])
    proj = group_total(outer_dot(x_proj, conv_flat), 3)
    gated_far = by_hop(gated_send, 2)
    proj, gated_far = lax.optimization_barrier((proj, gated_far))
    gated_rest = by_hop(after(gated_more, proj), 2)
    keep_lanes = jnp.broadcast_to(taps[1][:, :, None], (seqs, length, LANES))
    skip = d_skip.astype(f32)
    y_total, gated, rate, beta, states = recurrence_forward(
        conv_out, z_part, proj, keep_lanes, dt_proj, dt_bias.astype(f32)[None], skip[None]
    )
    y_total, gated, gated_rest, last_norm, cot_got = lax.optimization_barrier(
        (y_total, gated, gated_rest, last_norm, cot_got)
    )
    cot_both = jnp.concatenate([cot, cot_got], axis=0)
    grad_gated = split(gated_own + jnp.concatenate([gated_far, gated_rest], axis=1).astype(f32))
    z_vals = z_part.astype(f32)
    dy = grad_gated * jax.nn.silu(z_vals)
    grad_z = (grad_gated * y_total * silu_slope(z_vals)).astype(bf16).reshape(tokens, width)

    gated_keep, gated_give = halves(gated.reshape(tokens, width), height // 4)
    cols = model // 4
    keeps, gives, z_blocks, norms, gated_got = collect(
        gated_keep, gated_give, grad_z, own_half, y_half, z_half, last_norm
    )
    z_blocks = z_blocks.reshape(count, -1, width // 4)
    gated_both, block_output, grad_w_z = middle(keeps, gives, gated_got, z_blocks, x_all, out_proj, seqs)
    out_blocks = inner_dot(gated_both.reshape(2 * tokens, -1), cot_both)
    out_own, out_sent = far_send(out_blocks.astype(bf16).reshape(height, -1, cols))
    rate, out_own = lax.optimization_barrier((rate, out_own))

    grad_conv_rec, grad_dt_low, grad_proj, grad_dt_proj, grad_dt_bias, grad_d_skip = recurrence_backward(
        rate, beta, conv_out, dy, proj, keep_lanes, dt_proj, states
    )
    grad_proj, out_sent = lax.optimization_barrier((group_total(grad_proj, 4), out_sent))
    grad_proj = grad_proj.astype(bf16)
    grad_out_proj = far_total(out_own.astype(f32), out_sent)
    grad_x_proj = rows_dot(grad_proj, conv_flat)
    grad_conv = dy * skip + grad_conv_rec + split(inner_dot(grad_proj, x_proj))
    grad_pre = grad_conv * silu_slope(conv_pre)
    grad_conv_bias = jnp.sum(grad_pre, axis=(0, 1))
    grad_conv_weight = jnp.stack(
        [
            jnp.sum(grad_pre * x_padded[:, j : j + length] * taps[KW - 1 - j][:, :, None], axis=(0, 1))
            for j in range(KW)
        ]
    )
    grad_x = conv_w[KW - 1] * grad_pre
    for j in range(KW - 1):
        d = KW - 1 - j
        ahead = jnp.pad(grad_pre * taps[d][:, :, None], ((0, 0), (0, d), (0, 0)))[:, d:]
        grad_x = grad_x + conv_w[j] * ahead
    grad_x = grad_x.astype(bf16).reshape(tokens, width)

    smalls = (grad_x_proj, grad_dt_proj, grad_conv_weight, grad_conv_bias[None], grad_dt_bias, grad_d_skip)
    grad_w_in, grad_x_proj, grad_dt_proj, grad_conv_weight, conv_line, bias_line, skip_line, input_grad, grad_gain = finish(
        grad_x, grad_z, smalls, grad_w_z, norms, w_in, block_input, out_grad, gain, xs, inv
    )
    return (
        block_output, input_grad, grad_gain[0], grad_w_in, grad_conv_weight, conv_line[0], grad_x_proj, grad_dt_proj,
        bias_line[0], skip_line[0], grad_out_proj,
    )


def solution(mesh):
    return jax.shard_map(
        body,
        mesh=mesh,
        in_specs=(
            P("replica", "shard", None), P("replica", None), P("shard"), P(None, "shard"), P(None, "shard"),
            P("shard"), P(None, "shard"), P(None, "shard"), P("shard"), P("shard"), P(None, "shard"),
            P("replica", "shard", None),
        ),
        out_specs=(
            P("replica", "shard", None), P("replica", "shard", None), P("shard"), P("replica", "shard"),
            P(None, "shard"), P("shard"), P(None, "shard"), P(None, "shard"), P("shard"), P("shard"),
            P("replica", "shard"),
        ),
        check_vma=False,
    )
```

```python
import functools

import jax
import jax.numpy as jnp
from jax import lax
from jax.experimental import pallas as pl
from jax.experimental.pallas import tpu as pltpu
from jax.sharding import PartitionSpec as P

KW = 4
EPS = 1e-05
CHUNK = 16
LANES = 128
f32 = jnp.float32
bf16 = jnp.bfloat16


def rows_dot(a, b):
    return jnp.dot(a, b, preferred_element_type=f32)


def inner_dot(a, b):
    return lax.dot_general(a, b, (((0,), (0,)), ((), ())), preferred_element_type=f32)


def outer_dot(a, b):
    return lax.dot_general(a, b, (((1,), (1,)), ((), ())), preferred_element_type=f32)


def silu_slope(values):
    sig_val = jax.nn.sigmoid(values)
    return sig_val + values * sig_val * (1.0 - sig_val)

MESH = pl.DeviceIdType.MESH
BLOCK = 128
UNROLL = 4
BACK_UNROLL = 4


def lane(g):
    return slice(g * LANES, (g + 1) * LANES)


def column(block, t):
    return jnp.broadcast_to(block[:, t : t + 1], (block.shape[0], LANES))


def row(ref, t, g, n):
    return jnp.broadcast_to(ref[t : t + 1, lane(g)], (n, LANES))


def prepare(base, rate_ref, conv_ref, keep_ref, rk, u, kept):
    rows = pl.ds(base, CHUNK)
    rate = rate_ref[0, rows, :]
    keep = keep_ref[0, rows, :]
    conv = conv_ref[0, rows, :].astype(f32)
    for g in range(rate.shape[1] // LANES):
        rk[:, lane(g)] = rate[:, lane(g)] * keep
    u[...] = rate * conv
    kept[...] = keep
    return rate, conv, keep


def shifted(cols, j):
    size = cols.shape[1]
    return pltpu.roll(cols, lax.rem(size - j * CHUNK, size), 1)


def spread_mask(n, size=CHUNK):
    shape = (size, size * n)
    return lax.broadcasted_iota(jnp.int32, shape, 1) // n == lax.broadcasted_iota(jnp.int32, shape, 0)


def picker(n, size=CHUNK):
    shape = (n, size * n)
    return (lax.broadcasted_iota(jnp.int32, shape, 1) % n == lax.broadcasted_iota(jnp.int32, shape, 0)).astype(bf16)


def diagonal(rows, mask, pick):
    return jnp.where(mask, rows_dot(rows.astype(bf16), pick), 0.0).astype(bf16)


def forward_kernel(
    conv_ref, z_ref, proj_ref, keep_ref, dt_proj_ref, dt_bias_ref, skip_ref,
    y_ref, gated_ref, rate_ref, beta_ref, state_ref,
    held_ref, rk, u, kept, query_rows, fresh,
):
    width = conv_ref.shape[2]
    rank = dt_proj_ref.shape[0]
    n = (proj_ref.shape[0] - rank) // 2
    groups = width // LANES
    span = CHUNK * n

    @pl.when(pl.program_id(1) == 0)
    def _():
        held_ref[...] = jnp.zeros_like(held_ref)

    dt_low = proj_ref[0:rank, :].astype(bf16)
    keys = proj_ref[rank : rank + n, :]
    query_rows[...] = proj_ref[rank + n :, :].T
    key_square = jnp.sum(keys.T * keys.T, axis=1, keepdims=True)
    beta = jax.nn.sigmoid(inner_dot(dt_low, dt_proj_ref[...]) + dt_bias_ref[...])
    beta_ref[0] = beta
    rate_ref[0] = beta / (1.0 + beta * key_square)
    mask, pick = spread_mask(n), picker(n)

    def states_of(j, held, rk, u, kept, fresh):
        base = pl.multiple_of(j * CHUNK, CHUNK)
        prepare(base, rate_ref, conv_ref, keep_ref, rk, u, kept)
        near_keys = shifted(keys, j)
        for t in range(CHUNK):
            key = column(near_keys, t)
            key2 = key * key
            keep = jnp.broadcast_to(kept[t : t + 1, :], (n, LANES))
            at = slice(t * n, (t + 1) * n)
            for g in range(groups):
                decay = keep - row(rk, t, g, n) * key2
                held[g] = decay * held[g] + row(u, t, g, n) * key
                fresh[at, lane(g)] = held[g].astype(fresh.dtype)

    def outputs_of(j, fresh):
        base = pl.multiple_of(j * CHUNK, CHUNK)
        rows = pl.ds(base, CHUNK)
        block = fresh[...].astype(bf16)
        state_ref[0, pl.ds(pl.multiple_of(base * n, span), span), :] = block
        conv = conv_ref[0, rows, :].astype(f32)
        total = rows_dot(diagonal(query_rows[rows, :], mask, pick), block) + skip_ref[...] * conv
        y_ref[0, rows, :] = total
        z = z_ref[0, rows, :].astype(f32)
        gated_ref[0, rows, :] = (total * (z * jax.nn.sigmoid(z))).astype(bf16)

    def step(i, held):
        held = list(held)
        for k in range(UNROLL):
            states_of(i * UNROLL + k, held, rk[k], u[k], kept[k], fresh[k])
            if k > 0:
                outputs_of(i * UNROLL + k - 1, fresh[k - 1])
        outputs_of(i * UNROLL + UNROLL - 1, fresh[UNROLL - 1])
        return tuple(held)

    start = tuple(held_ref[:, lane(g)] for g in range(groups))
    end = lax.fori_loop(0, conv_ref.shape[1] // CHUNK // UNROLL, step, start)
    for g in range(groups):
        held_ref[:, lane(g)] = end[g]


def backward_kernel(
    rate_ref, beta_ref, conv_ref, dy_ref, proj_ref, keep_ref, dt_proj_ref, state_ref, last_ref,
    gconv_ref, gdt_ref, gproj_ref, gdt_proj_ref, gdt_bias_ref, gskip_ref,
    held_ref, grate, rk, u, dys, kept, key_rows, adj, adj_state, totals, lined,
):
    block_rows, width = rate_ref.shape[1:]
    rank = dt_proj_ref.shape[0]
    n = (proj_ref.shape[0] - rank) // 2
    groups = width // LANES
    chunks = block_rows // CHUNK

    @pl.when(pl.program_id(1) == 0)
    def _():
        held_ref[...] = jnp.zeros_like(held_ref)

    @pl.when((pl.program_id(0) == 0) & (pl.program_id(1) == 0))
    def _():
        gdt_proj_ref[...] = jnp.zeros_like(gdt_proj_ref)
        gdt_bias_ref[...] = jnp.zeros_like(gdt_bias_ref)
        gskip_ref[...] = jnp.zeros_like(gskip_ref)

    keys = proj_ref[rank : rank + n, :]
    queries = proj_ref[rank + n :, :]
    key_rows[...] = keys.T
    mask, pick = spread_mask(n), picker(n)

    ones = jnp.ones((CHUNK, LANES), bf16)

    def walk(j, held, rk, u, dys, kept, adj, adj_state, totals):
        base = pl.multiple_of(j * CHUNK, CHUNK)
        rows = pl.ds(base, CHUNK)
        prepare(base, rate_ref, conv_ref, keep_ref, rk, u, kept)
        dys[...] = dy_ref[0, rows, :]
        near_keys = shifted(keys, j)
        near_queries = shifted(queries, j)
        late = pl.ds(pl.multiple_of((base + CHUNK - 1) * n, n), n)
        after = [state_ref[0, late, lane(g)] for g in range(groups)]
        for t in reversed(range(CHUNK)):
            own = slice(t * n, (t + 1) * n)
            key = column(near_keys, t)
            key2 = key * key
            query = column(near_queries, t)
            keep = jnp.broadcast_to(kept[t : t + 1, :], (n, LANES))
            prior = jnp.maximum(base + t - 1, 0)
            at = pl.ds(pl.multiple_of(prior * n, n), n)
            parts = [None] * 3
            for g in range(groups):
                slope = row(dys, t, g, n)
                pace = row(rk, t, g, n)
                grad = held[g] + slope * query
                decay = keep - pace * key2
                held[g] = decay * grad
                before = state_ref[0, at, lane(g)]
                if t == 0:
                    before = jnp.where(j == 0, last_ref[0, :, lane(g)], before)
                cross = grad * before.astype(f32)
                adj[own, lane(g)] = grad
                adj_state[own, lane(g)] = cross
                terms = (grad * row(u, t, g, n), cross * pace, after[g].astype(f32) * slope)
                parts = [v if p is None else p + v for p, v in zip(parts, terms)]
                after[g] = before
            for i in range(3):
                totals[i, own, :] = parts[i]

    def settle(j, adj, adj_state, totals):
        base = pl.multiple_of(j * CHUNK, CHUNK)
        rows = pl.ds(base, CHUNK)
        key_block = key_rows[rows, :]
        w1 = rows_dot(diagonal(key_block, mask, pick), adj[...].astype(bf16))
        w2 = rows_dot(diagonal(key_block * key_block, mask, pick), adj_state[...].astype(bf16))
        for i in range(3):
            lined[i, rows, :] = jnp.where(mask, outer_dot(ones, totals[i].astype(bf16)), 0.0)
        keeps = keep_ref[0, rows, :]
        for g in range(groups):
            conv = conv_ref[0, rows, lane(g)].astype(f32)
            grate[rows, lane(g)] = conv * w1[:, lane(g)] - keeps * w2[:, lane(g)]
        gconv_ref[0, rows, :] = rate_ref[0, rows, :] * w1

    def step(i, held):
        held = list(held)
        first = chunks - 1 - i * BACK_UNROLL
        for k in range(BACK_UNROLL):
            walk(first - k, held, rk[k], u[k], dys[k], kept[k], adj[k], adj_state[k], totals[k])
            if k > 0:
                settle(first - k + 1, adj[k - 1], adj_state[k - 1], totals[k - 1])
        last = BACK_UNROLL - 1
        settle(first - last, adj[last], adj_state[last], totals[last])
        return tuple(held)

    start = tuple(held_ref[:, lane(g)] for g in range(groups))
    end = lax.fori_loop(0, chunks // BACK_UNROLL, step, start)
    for g in range(groups):
        held_ref[:, lane(g)] = end[g]

    def picked(left, value):
        high = value.astype(bf16)
        low = (value - high.astype(f32)).astype(bf16)
        return outer_dot(left, high) + outer_dot(left, low)

    rate = rate_ref[0]
    beta = beta_ref[0]
    grad_rate = grate[...]
    self_term = picked(jnp.ones((n, width), bf16), grad_rate * rate * rate)
    key_square = jnp.sum(key_rows[...] * key_rows[...], axis=1, keepdims=True)
    denom_inv = 1.0 / (1.0 + beta * key_square)
    grad_dt = grad_rate * denom_inv * denom_inv * beta * (1.0 - beta)
    low = grad_dt.astype(bf16)
    gdt_ref[0] = low
    gdt_bias_ref[...] += jnp.sum(grad_dt, axis=0, keepdims=True)
    gskip_ref[...] += jnp.sum(dy_ref[0] * conv_ref[0].astype(f32), axis=0, keepdims=True)
    gdt_proj_ref[...] += rows_dot(proj_ref[0:rank, :].astype(bf16), low)
    gproj_ref[0:rank, :] = outer_dot(dt_proj_ref[...], low)
    gproj_ref[rank : rank + n, :] = picked(pick, lined[0]) - 2.0 * keys * (picked(pick, lined[1]) + self_term)
    gproj_ref[rank + n :, :] = picked(pick, lined[2])


def specs_for(length, reverse):
    blocks = length // BLOCK

    def place(b):
        return blocks - 1 - b if reverse else b

    def spec(*shape):
        return pl.BlockSpec((1,) + shape, lambda s, b: (s, place(b)) + (0,) * (len(shape) - 1))

    def across_spec(rows):
        return pl.BlockSpec((rows, BLOCK), lambda s, b: (0, s * blocks + place(b)))

    def whole(*shape):
        return pl.BlockSpec(shape, lambda s, b: (0,) * len(shape))

    return blocks, spec, across_spec, whole


def recurrence_forward(conv, z, proj, keep_lanes, dt_proj, dt_bias, skip):
    seqs, length, width = conv.shape
    rank = dt_proj.shape[0]
    n = (proj.shape[0] - rank) // 2
    blocks, spec, across_spec, whole = specs_for(length, False)
    span = CHUNK * n
    wide = spec(BLOCK, width)
    full = jax.ShapeDtypeStruct((seqs, length, width), f32)
    return pl.pallas_call(
        forward_kernel,
        grid=(seqs, blocks),
        in_specs=[
            wide, wide, across_spec(proj.shape[0]), spec(BLOCK, LANES), whole(rank, width), whole(1, width),
            whole(1, width),
        ],
        out_specs=[wide, wide, wide, wide, spec(BLOCK * n, width)],
        out_shape=[
            full, jax.ShapeDtypeStruct((seqs, length, width), bf16),
            pltpu.HBM((seqs, length, width), f32), pltpu.HBM((seqs, length, width), f32),
            pltpu.HBM((seqs, length * n, width), bf16),
        ],
        scratch_shapes=[
            pltpu.VMEM((n, width), f32),
            [pltpu.VMEM((CHUNK, width), f32)] * UNROLL,
            [pltpu.VMEM((CHUNK, width), f32)] * UNROLL,
            [pltpu.VMEM((CHUNK, LANES), f32)] * UNROLL,
            pltpu.VMEM((BLOCK, n), f32),
            [pltpu.VMEM((span, width), f32)] * UNROLL,
        ],
        compiler_params=pltpu.CompilerParams(vmem_limit_bytes=24 << 20),
        cost_estimate=pl.CostEstimate(flops=16_000_000_000, bytes_accessed=24 << 20, transcendentals=0),
        name="recurrence_forward",
    )(conv, z, proj, keep_lanes, dt_proj, dt_bias, skip)


def recurrence_backward(rate, beta, conv, dy, proj, keep_lanes, dt_proj, states):
    seqs, length, width = rate.shape
    rank = dt_proj.shape[0]
    n = (proj.shape[0] - rank) // 2
    span = CHUNK * n
    blocks, spec, across_spec, whole = specs_for(length, True)
    wide = spec(BLOCK, width)
    before = pl.BlockSpec((1, n, width), lambda s, b: (s, jnp.maximum((blocks - 1 - b) * BLOCK - 1, 0), 0))
    return pl.pallas_call(
        backward_kernel,
        grid=(seqs, blocks),
        in_specs=[
            wide, wide, wide, wide, across_spec(proj.shape[0]), spec(BLOCK, LANES), whole(rank, width),
            spec(BLOCK * n, width), before,
        ],
        out_specs=[wide, wide, across_spec(proj.shape[0]), whole(rank, width), whole(1, width), whole(1, width)],
        out_shape=[
            jax.ShapeDtypeStruct((seqs, length, width), f32),
            jax.ShapeDtypeStruct((seqs, length, width), bf16),
            jax.ShapeDtypeStruct(proj.shape, f32),
            jax.ShapeDtypeStruct((rank, width), f32),
            jax.ShapeDtypeStruct((1, width), f32),
            jax.ShapeDtypeStruct((1, width), f32),
        ],
        scratch_shapes=[
            pltpu.VMEM((n, width), f32),
            pltpu.VMEM((BLOCK, width), f32),
            [pltpu.VMEM((CHUNK, width), f32)] * BACK_UNROLL,
            [pltpu.VMEM((CHUNK, width), f32)] * BACK_UNROLL,
            [pltpu.VMEM((CHUNK, width), f32)] * BACK_UNROLL,
            [pltpu.VMEM((CHUNK, LANES), f32)] * BACK_UNROLL,
            pltpu.VMEM((BLOCK, n), f32),
            [pltpu.VMEM((span, width), f32)] * BACK_UNROLL,
            [pltpu.VMEM((span, width), f32)] * BACK_UNROLL,
            [pltpu.VMEM((3, span, LANES), f32)] * BACK_UNROLL,
            pltpu.VMEM((3, BLOCK, span), f32),
        ],
        compiler_params=pltpu.CompilerParams(vmem_limit_bytes=36 << 20),
        cost_estimate=pl.CostEstimate(flops=30_000_000_000, bytes_accessed=28 << 20, transcendentals=0),
        name="recurrence_backward",
    )(rate, beta, conv, dy, proj, keep_lanes, dt_proj, states, states)


def peer(hop):
    me = lax.axis_index("shard")
    core = lax.rem(me, 2)
    chip = me // 2
    if hop & 1:
        core = 1 - core
    if hop & 2:
        chip = 1 - chip
    return chip * 2 + core


def meet_group():
    barrier = pltpu.get_barrier_semaphore()
    for hop in (1, 2, 3):
        pl.semaphore_signal(barrier, inc=1, device_id={"shard": peer(hop)}, device_id_type=MESH)
    pl.semaphore_wait(barrier, 3)


def remote(src, dst, sends, recvs, at, hop):
    return pltpu.make_async_remote_copy(
        src_ref=src, dst_ref=dst, send_sem=sends.at[at], recv_sem=recvs.at[at],
        device_id={"shard": peer(hop)}, device_id_type=MESH,
    )


def group_params(collective_id, limit):
    return pltpu.CompilerParams(collective_id=collective_id, has_side_effects=True, vmem_limit_bytes=limit)


VMEM_SPEC = pl.BlockSpec(memory_space=pltpu.VMEM)


ANY_SPEC = pl.BlockSpec(memory_space=pl.ANY)


def part_copy(src, dst, send, recv, shard):
    return pltpu.make_async_remote_copy(
        src_ref=src, dst_ref=dst, send_sem=send, recv_sem=recv, device_id={"shard": shard}, device_id_type=MESH
    )


def front_kernel(
    x_ref, cot_ref, gain_ref, w_hbm, o_hbm,
    xs_ref, inv_ref, cots_ref, gain_row_ref, own_half_ref, y_half_ref, z_half_ref, x_part_ref, z_part_ref, own_ref, send_ref, send_more_ref,
    gains_ref, w_ref, o_ref, normed_ref, lhs, mixed, pairs, near, sends, recvs, local, part_sends, part_recvs, part_local,
    pair_sends, pair_recvs, pair_local,
):
    me = lax.axis_index("shard")
    chip = me // 2
    slot = me // 2
    seqs, rows, model = x_ref.shape
    cols = cots_ref.shape[2]
    core = lax.rem(me, 2)
    width = x_part_ref.shape[2]
    lift = gain_ref.shape[0]
    span = 2 * rows
    tile = 256
    loads = [
        pltpu.make_async_copy(w_hbm, w_ref, local.at[3]),
        pltpu.make_async_copy(o_hbm, o_ref, local.at[4]),
    ]
    for copy in loads:
        copy.start()
    meet([quad(1), quad(2)])

    def mine(ref, owner):
        return ref.at[:, pl.ds(pl.multiple_of(owner * rows, 16), rows), :]

    def part(owner):
        return cot_ref.at[:, :, pl.ds(pl.multiple_of(owner * cols, 128), cols)]

    def gain_rows(owner):
        return gains_ref.at[pl.ds(pl.multiple_of(owner * lift, 8), lift), :]

    gain_sends = [remote(gain_ref, gain_rows(me), sends, recvs, 5 + hop, hop) for hop in (1, 2, 3)]
    x_core = remote(x_ref, mine(xs_ref, me), sends, recvs, 0, 1)
    x_chip = remote(x_ref, mine(xs_ref, me), sends, recvs, 1, 2)
    cot_sends = [remote(part(peer(hop)), mine(cots_ref, me), sends, recvs, 2 + hop, hop) for hop in (1, 2, 3)]
    for copy in gain_sends + [x_core, x_chip] + cot_sends:
        copy.start()
    own = [
        pltpu.make_async_copy(x_ref, mine(xs_ref, me), local.at[0]),
        pltpu.make_async_copy(part(me), mine(cots_ref, me), local.at[1]),
        pltpu.make_async_copy(gain_ref, gain_rows(me), local.at[2]),
    ]
    for copy in own:
        copy.start()
    for copy in own:
        copy.wait()
    for copy in gain_sends:
        copy.wait()
    x_core.wait()
    gain = jnp.concatenate([gains_ref[lift * d : lift * d + 1, :] for d in range(4)], axis=1)
    gain_row_ref[...] = jnp.broadcast_to(gain, gain_row_ref.shape)
    loads[0].wait()

    def piece(half, kind):
        where = jnp.bitwise_xor(chip, half)
        return (x_part_ref, z_part_ref)[kind].at[:, pl.ds(pl.multiple_of(where * span, 16), span), :]

    def away(i):
        return lax.rem(2 * me + i, 4) != me

    def send(half, i, kind):
        return part_copy(
            mixed.at[half, i], piece(half, kind), part_sends.at[2 * half + i], part_recvs.at[2 * kind + half],
            lax.rem(2 * me + i, 4),
        )

    def keep(half, i, kind):
        return pltpu.make_async_copy(mixed.at[half, i], piece(half, kind), part_local.at[half])

    def either(half, i, send_does, keep_does):
        for kind in range(2):
            pl.when(away(i) & (slot == kind))(lambda kind=kind: send_does(send(half, i, kind)))
            pl.when(jnp.logical_not(away(i)) & (slot == kind))(lambda kind=kind: keep_does(keep(half, i, kind)))

    def run_half(half):
        where = jnp.bitwise_xor(chip, half) * span

        for seq in range(seqs):

            def norm(r, carry, seq=seq):
                at = pl.ds(pl.multiple_of(where + r * 16, 16), 16)
                vals = xs_ref[seq, at, :].astype(f32)
                inv = lax.rsqrt(jnp.mean(vals * vals, axis=1, keepdims=True) + EPS)
                inv_ref[seq, at, :] = jnp.broadcast_to(inv, (16, LANES))
                out = (vals * inv * gain).astype(bf16)
                normed_ref[seq, at, :] = out
                lhs[pl.ds(pl.multiple_of(seq * span + r * 16, 16), 16), :] = out
                return carry

            lax.fori_loop(0, span // 16, norm, 0)
        for copy in normed_copies(half):
            copy.start()
        for i in range(2):

            def product(t, carry, i=i):
                value = rows_dot(lhs[...], w_ref[:, pl.ds(pl.multiple_of(i * width + t * tile, tile), tile)])
                for seq in range(seqs):
                    mixed[half, i, seq, :, pl.ds(pl.multiple_of(t * tile, tile), tile)] = value[
                        seq * span : (seq + 1) * span
                    ].astype(bf16)
                return carry

            lax.fori_loop(0, width // tile, product, 0)
            either(half, i, lambda copy: copy.start(), lambda copy: copy.start())

    def normed_copies(half):
        where = pl.ds(pl.multiple_of(jnp.bitwise_xor(chip, half) * span, 16), span)
        src = normed_ref.at[:, where, pl.ds(pl.multiple_of(core * (model // 2), LANES), model // 2)]
        copies = [pltpu.make_async_copy(src, own_half_ref.at[:, where, :], pair_local.at[half])]
        for hop in (1, 2):
            at = 2 * half + hop - 1
            half_ref = (y_half_ref, z_half_ref)[hop - 1]
            copies.append(across(src, half_ref.at[:, where, :], pair_sends, pair_recvs, at, quad(hop)))
        return copies

    run_half(0)
    x_chip.wait_recv()
    onward = remote(mine(xs_ref, peer(2)), mine(xs_ref, peer(2)), sends, recvs, 2, 1)
    onward.start()
    onward.wait()
    run_half(1)

    for copy in cot_sends:
        copy.wait()
    loads[1].wait()

    def partial(block, t):
        return outer_dot(
            cots_ref[...].reshape(seqs * 4 * rows, cols),
            o_ref[pl.ds(pl.multiple_of(block * width + t * tile, tile), tile), :],
        )

    def lanes(t):
        return pl.ds(pl.multiple_of(t * tile, tile), tile)

    near_sends = []
    for at, hop in enumerate((3, 1)):

        def fill(t, carry, at=at, hop=hop):
            pairs[at, :, lanes(t)] = partial(peer(hop), t).astype(bf16)
            return carry

        lax.fori_loop(0, width // tile, fill, 0)
        copy = remote(pairs.at[at], near.at[at], sends, recvs, 9 + at, 1)
        copy.start()
        near_sends.append(copy)
    near_sends[0].wait()

    pieces = width // tile // 2
    for first, ref in ((0, send_ref), (pieces, send_more_ref)):

        def to_send(t, carry, first=first, ref=ref):
            ref[:, lanes(t)] = (
                partial(peer(2), first + t) + near[0, :, lanes(first + t)].astype(f32)
            ).astype(bf16)
            return carry

        lax.fori_loop(0, pieces, to_send, 0)
    near_sends[1].wait()

    def to_own(t, carry):
        own_ref[:, lanes(t)] = partial(me, t) + near[1, :, lanes(t)].astype(f32)
        return carry

    lax.fori_loop(0, width // tile, to_own, 0)

    x_chip.wait_send()
    for copy in normed_copies(0) + normed_copies(1):
        copy.wait()
    for half in range(2):
        for i in range(2):
            either(half, i, lambda copy: copy.wait_send(), lambda copy: copy.wait())
        for at in range(2):

            @pl.when(2 * at + me // 2 != me)
            def _(at=at, half=half):
                part_copy(
                    mixed.at[0, 0], mixed.at[0, 0], part_sends.at[0], part_recvs.at[2 * at + half], peer(1)
                ).wait_recv()


def front(x, cot, gain, w_in, out_proj):
    seqs, rows, model = x.shape
    group = lax.axis_size("shard")
    length = rows * group
    cols = model // group
    width = w_in.shape[1] // 2
    tokens = seqs * length
    lifted = jnp.broadcast_to(gain.astype(f32)[None], (8, gain.shape[0]))
    far_sems = pltpu.SemaphoreType.DMA((4,))
    return pl.pallas_call(
        front_kernel,
        in_specs=[VMEM_SPEC] * 3 + [ANY_SPEC] * 2,
        out_specs=[VMEM_SPEC] * 12,
        out_shape=[
            jax.ShapeDtypeStruct((seqs, length, model), bf16),
            jax.ShapeDtypeStruct((seqs, length, LANES), f32),
            jax.ShapeDtypeStruct((seqs, length, cols), bf16),
            jax.ShapeDtypeStruct((8, model), f32),
            jax.ShapeDtypeStruct((seqs, length, model // 2), bf16),
            jax.ShapeDtypeStruct((seqs, length, model // 2), bf16),
            jax.ShapeDtypeStruct((seqs, length, model // 2), bf16),
            jax.ShapeDtypeStruct((seqs, length, width), bf16),
            jax.ShapeDtypeStruct((seqs, length, width), bf16),
            jax.ShapeDtypeStruct((tokens, width), f32),
            jax.ShapeDtypeStruct((tokens, width // 2), bf16),
            jax.ShapeDtypeStruct((tokens, width // 2), bf16),
        ],
        scratch_shapes=[
            pltpu.VMEM((8 * group, gain.shape[0]), f32),
            pltpu.VMEM(w_in.shape, bf16),
            pltpu.VMEM(out_proj.shape, bf16),
            pltpu.VMEM((seqs, length, model), bf16),
            pltpu.VMEM((tokens // 2, model), bf16),
            pltpu.VMEM((2, 2, seqs, 2 * rows, width), bf16),
            pltpu.VMEM((2, tokens, width), bf16),
            pltpu.VMEM((2, tokens, width), bf16),
            pltpu.SemaphoreType.DMA((11,)), pltpu.SemaphoreType.DMA((11,)), pltpu.SemaphoreType.DMA((5,)),
            pltpu.SemaphoreType.DMA((4,)), pltpu.SemaphoreType.DMA((4,)), pltpu.SemaphoreType.DMA((2,)),
            far_sems, far_sems, far_sems,
        ],
        compiler_params=group_params(1, 48 << 20),
        name="front",
    )(x, cot, lifted, w_in, out_proj)


def quad(hop):
    home = lax.axis_index("replica")
    if hop & 1:
        home = home + 1 - 2 * lax.rem(home, 2)
    if hop & 2:
        home = home + 2 - 4 * lax.rem(home // 2, 2)
    return home


def across(src, dst, sends, recvs, at, other):
    return pltpu.make_async_remote_copy(
        src_ref=src, dst_ref=dst, send_sem=sends.at[at], recv_sem=recvs.at[at],
        device_id={"replica": other}, device_id_type=MESH,
    )


def meet(replicas):
    barrier = pltpu.get_barrier_semaphore()
    for hop in (1, 2, 3):
        pl.semaphore_signal(barrier, inc=1, device_id={"shard": peer(hop)}, device_id_type=MESH)
    for other in replicas:
        pl.semaphore_signal(barrier, inc=1, device_id={"replica": other}, device_id_type=MESH)
    pl.semaphore_wait(barrier, 3 + len(replicas))


def ahead(step):
    count = lax.axis_size("replica")
    return lax.rem(lax.axis_index("replica") + step, count)


def collect_kernel(
    keep_ref, give_ref, gz_ref, own_half_ref, y_half_ref, z_half_ref, last_ref,
    keeps_ref, gives_ref, zb_ref, norm_out_ref, got_ref,
    gz_ref4, norm_ref, turned, sends, recvs, local,
):
    me = lax.axis_index("shard")
    half = keep_ref.shape[1]
    core = lax.rem(me, 2)
    member = lax.rem(lax.axis_index("replica"), 4)
    tokens, part = gz_ref4.shape[1:]
    tile = 256

    def norm_rows(which):
        return norm_ref.at[core, which * tokens : (which + 1) * tokens]

    meet([quad(hop) for hop in (1, 2, 3)])

    def quarter(which):
        return gz_ref.at[:, pl.ds(pl.multiple_of(which * part, LANES), part)]

    def spot(ref, owner):
        return ref.at[:, pl.ds(pl.multiple_of(owner * half, 128), half)]

    k_chip = remote(keep_ref, spot(keeps_ref, me), sends, recvs, 0, 2)
    v_chip = remote(give_ref, spot(gives_ref, me), sends, recvs, 1, 2)
    k_core = remote(keep_ref, spot(keeps_ref, me), sends, recvs, 2, 1)
    v_core = remote(give_ref, spot(gives_ref, me), sends, recvs, 3, 1)
    quads = [
        across(quarter(lax.rem(quad(hop), 4)), gz_ref4.at[hop], sends, recvs, 6 + hop, quad(hop)) for hop in (3, 1, 2)
    ]
    give_pair = across(give_ref, got_ref, sends, recvs, 11, quad(1))
    norms = [
        remote(own_half_ref, norm_rows(0), sends, recvs, 12, 1),
        remote(y_half_ref, norm_rows(1), sends, recvs, 10, 1),
        remote(z_half_ref, norm_rows(2), sends, recvs, 13, 1),
        remote(last_ref, norm_rows(3), sends, recvs, 4, 1),
    ]
    own = [
        pltpu.make_async_copy(keep_ref, spot(keeps_ref, me), local.at[0]),
        pltpu.make_async_copy(give_ref, spot(gives_ref, me), local.at[1]),
        pltpu.make_async_copy(quarter(member), gz_ref4.at[0], local.at[2]),
        pltpu.make_async_copy(own_half_ref, norm_rows(0), local.at[5]),
        pltpu.make_async_copy(y_half_ref, norm_rows(1), local.at[3]),
        pltpu.make_async_copy(z_half_ref, norm_rows(2), local.at[6]),
        pltpu.make_async_copy(last_ref, norm_rows(3), local.at[4]),
    ]
    for copy in [k_chip, v_chip] + quads + [give_pair, k_core, v_core] + norms + own:
        copy.start()
    for copy in own + quads + norms:
        copy.wait()
    out_copy = pltpu.make_async_copy(norm_ref, norm_out_ref, local.at[7])
    out_copy.start()
    for hop in range(4):
        for at in range(0, tokens, tile):
            turned[:, hop * tokens + at : hop * tokens + at + tile] = gz_ref4[hop, at : at + tile, :].T
    wide = norm_ref.shape[2] // tile

    def rows_of(t, carry):
        feature = pl.ds(pl.multiple_of(lax.rem(t, wide) * tile, tile), tile)
        value = rows_dot(turned[...], norm_ref[t // wide, :, feature])
        zb_ref[pl.ds(pl.multiple_of(t * tile, tile), tile), :] = value.astype(bf16).T
        return carry

    lax.fori_loop(0, zb_ref.shape[0] // tile, rows_of, 0)
    k_chip.wait_recv()
    k_on = remote(spot(keeps_ref, peer(2)), spot(keeps_ref, peer(2)), sends, recvs, 5, 1)
    k_on.start()
    v_chip.wait_recv()
    v_on = remote(spot(gives_ref, peer(2)), spot(gives_ref, peer(2)), sends, recvs, 6, 1)
    v_on.start()
    for copy in [give_pair, k_core, v_core, k_on, v_on, out_copy]:
        copy.wait()
    k_chip.wait_send()
    v_chip.wait_send()


def cost(microseconds):
    return pl.CostEstimate(flops=int(microseconds * 1e9), bytes_accessed=1 << 20, transcendentals=0)


def collect(keep, give, grad_z, own_half, y_half, z_half, last_norm):
    tokens, half = keep.shape
    group = lax.axis_size("shard")
    wide = jax.ShapeDtypeStruct((tokens, half * group), bf16)
    features, quarter = last_norm.shape[1], grad_z.shape[1] // 4
    return pl.pallas_call(
        collect_kernel,
        in_specs=[VMEM_SPEC] * 7,
        out_specs=[VMEM_SPEC] * 3 + [ANY_SPEC, VMEM_SPEC],
        out_shape=[
            wide, wide, jax.ShapeDtypeStruct((2 * features, quarter), bf16),
            pltpu.HBM((2, 4 * tokens, features), bf16),
            jax.ShapeDtypeStruct(give.shape, bf16),
        ],
        scratch_shapes=[
            pltpu.VMEM((4, tokens, quarter), bf16),
            pltpu.VMEM((2, 4 * tokens, features), bf16),
            pltpu.VMEM((quarter, 4 * tokens), bf16),
            pltpu.SemaphoreType.DMA((14,)), pltpu.SemaphoreType.DMA((14,)), pltpu.SemaphoreType.DMA((8,)),
        ],
        compiler_params=group_params(6, 34 << 20),
        cost_estimate=cost(25),
        name="collect",
    )(keep, give, grad_z, own_half, y_half, z_half, last_norm)


def middle_kernel(
    keeps_ref, gives_ref, got_ref, z_ref, x_hbm, o_hbm,
    both_ref, out_ref, wz_ref,
    z_got_ref, o_ref, xcol, outs, sends, recvs, far_sends, far_recvs, local, o_local,
):
    me = lax.axis_index("shard")
    side = lax.rem(lax.axis_index("replica"), 2)
    tokens, half = got_ref.shape
    gots_ref = both_ref.at[1]
    seqs, rows, _ = out_ref.shape
    cols = xcol.shape[1]
    piece = o_hbm.shape[0] // lax.axis_size("replica")
    per = half // piece
    loads = []
    for d in range(4):
        for q in range(2):
            for j in range(per):
                at = d * 2 * half + (2 * j) * piece + (side if q == 0 else 1 - side) * piece
                loads.append(
                    pltpu.make_async_copy(
                        o_hbm.at[pl.ds(pl.multiple_of(at, piece), piece), :],
                        o_ref.at[q, pl.ds(d * half + j * piece, piece), :],
                        o_local.at[len(loads)],
                    )
                )
    for copy in loads:
        copy.start()
    fetch = pltpu.make_async_copy(
        x_hbm.at[:, pl.ds(pl.multiple_of(me * cols, 128), cols)], xcol, local.at[0]
    )
    fetch.start()
    home = lax.axis_index("replica")
    count = lax.axis_size("replica")
    meet([ahead(step) for step in range(1, count)])

    def spot(owner):
        return gots_ref.at[:, pl.ds(pl.multiple_of(owner * half, 128), half)]

    g_own = pltpu.make_async_copy(got_ref, spot(me), local.at[2])
    g_chip = remote(got_ref, spot(me), sends, recvs, 0, 2)
    g_core = remote(got_ref, spot(me), sends, recvs, 1, 1)
    own = [
        pltpu.make_async_copy(keeps_ref, both_ref.at[0], local.at[1]),
    ]
    own.append(pltpu.make_async_copy(z_ref.at[home], z_got_ref.at[home], local.at[3 + seqs]))
    z_sends = [
        across(z_ref.at[ahead(step)], z_got_ref.at[home], far_sends, far_recvs, step, ahead(step))
        for step in range(1, count)
    ]
    own.append(g_own)
    for copy in [g_chip] + z_sends + [g_core] + own:
        copy.start()
    for copy in loads + [fetch]:
        copy.wait()
    tile = 256

    def product(t, carry):
        rows_at = pl.ds(pl.multiple_of(t * tile, tile), tile)
        value = (
            xcol[rows_at, :].astype(f32)
            + rows_dot(keeps_ref[rows_at, :], o_ref[0])
            + rows_dot(gives_ref[rows_at, :], o_ref[1])
        )
        outs[rows_at, :] = value.astype(bf16)
        return carry

    lax.fori_loop(0, tokens // tile, product, 0)
    length = tokens // seqs
    out_sends = []
    for seq in range(seqs):
        for n_hop, hop in enumerate((2, 3, 1)):
            src = outs.at[pl.ds(pl.multiple_of(seq * length + peer(hop) * rows, 16), rows), :]
            dst = out_ref.at[seq, :, pl.ds(pl.multiple_of(me * cols, 128), cols)]
            out_sends.append(remote(src, dst, sends, recvs, 2 + seq * 3 + n_hop, hop))
        own.append(
            pltpu.make_async_copy(
                outs.at[pl.ds(pl.multiple_of(seq * length + me * rows, 16), rows), :],
                out_ref.at[seq, :, pl.ds(pl.multiple_of(me * cols, 128), cols)],
                local.at[3 + seq],
            )
        )
        own[-1].start()
    for copy in out_sends:
        copy.start()
    base = 2 + seqs * 3
    g_chip.wait_recv()
    g_on = remote(spot(peer(2)), spot(peer(2)), sends, recvs, base + 2, 1)
    g_on.start()
    for copy in out_sends + [g_on, g_core] + own + z_sends:
        copy.wait()
    g_chip.wait_send()
    quarter = z_got_ref.shape[2]
    for q in range(4):
        total = z_got_ref[q].astype(f32)
        for group in range(1, count // 4):
            total = total + z_got_ref[4 * group + q].astype(f32)
        wz_ref[:, q * quarter : (q + 1) * quarter] = total.astype(bf16)


def middle(keeps, gives, got, z_blocks, x_all, out_proj, seqs):
    tokens, half = got.shape
    group = lax.axis_size("shard")
    model = x_all.shape[1]
    cols = model // group
    far_sems = pltpu.SemaphoreType.DMA((lax.axis_size("replica"),))
    pieces = 8 * max(1, half * lax.axis_size("replica") // out_proj.shape[0])
    return pl.pallas_call(
        middle_kernel,
        in_specs=[VMEM_SPEC] * 4 + [ANY_SPEC] * 2,
        out_specs=[VMEM_SPEC] * 3,
        out_shape=[
            jax.ShapeDtypeStruct((2, tokens, half * group), bf16),
            jax.ShapeDtypeStruct((seqs, tokens // seqs // group, model), bf16),
            jax.ShapeDtypeStruct((z_blocks.shape[1], 4 * z_blocks.shape[2]), bf16),
        ],
        scratch_shapes=[
            pltpu.VMEM(z_blocks.shape, bf16),
            pltpu.VMEM((2, half * group, cols), bf16),
            pltpu.VMEM((tokens, cols), bf16),
            pltpu.VMEM((tokens, cols), bf16),
            pltpu.SemaphoreType.DMA((5 + 3 * seqs,)), pltpu.SemaphoreType.DMA((5 + 3 * seqs,)),
            far_sems, far_sems, pltpu.SemaphoreType.DMA((4 + seqs,)), pltpu.SemaphoreType.DMA((pieces,)),
        ],
        compiler_params=group_params(7, 22 << 20),
        cost_estimate=cost(25),
        name="middle",
    )(keeps, gives, got, z_blocks, x_all, out_proj)


PARTS = 2


def finish_kernel(
    gx_ref, gz_ref, xp_ref, dp_ref, cw_ref, cb_ref, db_ref, sk_ref, wz_ref, norm_hbm, w_hbm, x_ref, cot_ref, gain_ref, xs_ref, inv_ref,
    gw_ref, gxp_ref, gdp_ref, gcw_ref, gcb_ref, gdb_ref, gsk_ref, dx_ref, ggain_ref,
    small_keep_ref, small_give_ref, small_ref, norm_ref, w_ref, gx4, cols_ref, turned, xb_ref, sb_ref, small_got, x_in, s_in, lhs, pairs, near, g_hold, g_own, g_send, g_far,
    h_send, h_cols, z_cols, s_own, gains, gain_near, gain_sum, gain_in, unit_x,
    sends, recvs, far_sends, far_recvs, home_sends, home_recvs, local,
):
    me = lax.axis_index("shard")
    home = lax.axis_index("replica")
    count = lax.axis_size("replica")
    height = count // 2
    mine = home // 2
    side = lax.rem(home, 2)
    seqs, rows, model = x_ref.shape
    tokens, width = gx_ref.shape
    length = tokens // seqs
    deep = wz_ref.shape[0]
    member = lax.rem(home, 4)
    quarter = width // 4
    part = quarter // PARTS
    tile = 256
    other = quad(1)
    load = pltpu.make_async_copy(w_hbm, w_ref, local.at[0])
    load_norm = pltpu.make_async_copy(norm_hbm, norm_ref, local.at[1])
    load_norm.start()
    load.start()
    meet([ahead(step) for step in range(1, count)])

    def far(step):
        return ahead(2 * step)

    def cut(p):
        return slice(p * part, (p + 1) * part)

    def piece_of(which, p):
        return gx_ref.at[:, pl.ds(pl.multiple_of(which * quarter + p * part, LANES), part)]

    def spot_of(hop, p):
        return gx4.at[hop * tokens : (hop + 1) * tokens, cut(p)]

    def quad_sends(p):
        return [
            across(piece_of(lax.rem(quad(hop), 4), p), spot_of(hop, p), sends, recvs, 3 * p + hop - 1, quad(hop))
            for hop in (3, 1, 2)
        ]

    small_send = across(small_give_ref, small_got, sends, recvs, 3 * PARTS, other)
    quad_own = [
        pltpu.make_async_copy(piece_of(member, p), spot_of(0, p), local.at[PARTS + 3 + 2 * seqs + p]) for p in range(PARTS)
    ]
    for copy in quad_sends(0):
        copy.start()
    lined = small_keep_ref.shape[1]

    def fill(at, put):
        low, high, begin = at * lined, (at + 1) * lined, 0
        for ref in (xp_ref, dp_ref, cw_ref, cb_ref, db_ref, sk_ref):
            stop = begin + ref.shape[0]
            a, b = max(low, begin), min(high, stop)
            if a < b:
                put(at // 2, slice(a - low, b - low), ref[a - begin : b - begin, :])
            begin = stop
        if high > begin:
            a = max(low, begin)
            put(at // 2, slice(a - low, lined), jnp.zeros((high - a, width), f32))

    def keep_rows(at, rows_at, value):
        small_keep_ref[at, rows_at, :] = value

    for at in range(count):
        pl.when(side == at % 2)(lambda at=at: fill(at, keep_rows))

        @pl.when(side != at % 2)
        def _(at=at):
            values = []
            fill(at, lambda where, rows_at, value: values.append(value))
            small_give_ref[at // 2] = jnp.concatenate(values, axis=0).astype(bf16)

    for copy in [small_send] + quad_sends(1) + quad_own:
        copy.start()

    def goal(slot):
        return (4 * slot + me) // 2

    spot = pl.ds(pl.multiple_of(lax.rem(me, 2) * width, LANES), width)

    def home_pieces(at):
        if at == PARTS:
            return 1, wz_ref, z_cols.at[:, spot]
        if at > PARTS:
            slot, seq = (at - PARTS - 1) % 2, (at - PARTS - 1) // 2
            some = slice(seq * length, (seq + 1) * length)
            return slot, (gx_ref, gz_ref)[slot].at[some], cols_ref.at[some, spot]
        some = 4 * part
        return 0, h_send.at[at], h_cols.at[at, :, pl.ds(pl.multiple_of(lax.rem(me, 2) * some, LANES), some)]

    def home_send(at):
        slot, src, dst = home_pieces(at)
        return part_copy(src, dst, home_sends.at[at], home_recvs.at[at * 2 + lax.rem(me, 2)], goal(slot))

    def home_keep(at):
        _, src, dst = home_pieces(at)
        return pltpu.make_async_copy(src, dst, local.at[2 + at])

    def home_start(at):
        slot = home_pieces(at)[0]
        pl.when(goal(slot) != me)(lambda: home_send(at).start())
        pl.when(goal(slot) == me)(lambda: home_keep(at).start())

    def home_wait(at):
        slot = home_pieces(at)[0]
        pl.when(goal(slot) != me)(lambda: home_send(at).wait_send())
        pl.when(goal(slot) == me)(lambda: home_keep(at).wait())
        for place in range(2):
            source = lax.rem(2 * me + place, 4)

            @pl.when((me // 2 == slot) & (source != me))
            def _(place=place):
                src = home_pieces(at)[1]
                part_copy(src, src, home_sends.at[at], home_recvs.at[at * 2 + place], peer(1)).wait_recv()

    for at in (*range(PARTS + 1, PARTS + 1 + 2 * seqs), PARTS):
        home_start(at)

    def far_copy(src, dst, kind, step):
        return across(src, dst, far_sends, far_recvs, kind * count + step, far(step))

    def block(step):
        return lax.rem(mine + step, height)

    order = range(1, height)

    def lines(at):
        return pl.ds(pl.multiple_of(at * deep, 16), deep)

    def x_sends(p):
        return [
            across(
                xb_ref.at[lines(ahead(step)), cut(p)], x_in.at[home, :, cut(p)], far_sends, far_recvs,
                p * count + step, ahead(step),
            )
            for step in range(1, count)
        ]

    def x_part(p):
        for copy in quad_sends(p):
            copy.wait_recv()
        quad_own[p].wait()

        for at in range(0, 4 * tokens, tile):
            turned[:, at : at + tile] = gx4[at : at + tile, cut(p)].T
        wide = norm_ref.shape[2] // tile

        def rows_of(t, carry):
            feature = pl.ds(pl.multiple_of(lax.rem(t, wide) * tile, tile), tile)
            value = rows_dot(turned[...], norm_ref[t // wide, :, feature])
            xb_ref[pl.ds(pl.multiple_of(t * tile, tile), tile), cut(p)] = value.astype(bf16).T
            return carry

        lax.fori_loop(0, xb_ref.shape[0] // tile, rows_of, 0)
        x_in[home, :, cut(p)] = xb_ref[lines(home), cut(p)]
        for copy in x_sends(p):
            copy.start()

    def lanes(t):
        return pl.ds(pl.multiple_of(t * tile, tile), tile)

    def near_send(seq):
        return remote(pairs.at[seq], near.at[seq], sends, recvs, 3 * PARTS + 8 + 2 * seq, 1)

    def chip_send(seq):
        return remote(g_send.at[seq], g_far.at[seq], sends, recvs, 3 * PARTS + 9 + 2 * seq, 2)

    def grads_of(seq):
        home_wait(PARTS + 1 + 2 * seq)
        home_wait(PARTS + 2 + 2 * seq)
        for i, owner in enumerate((peer(3), peer(1), peer(2), me)):
            at = pl.ds(pl.multiple_of(seq * length + owner * rows, 16), rows)
            lhs[i * rows : (i + 1) * rows, :] = cols_ref[at, :]
            here = pl.ds(pl.multiple_of(owner * rows, 16), rows)
            inv = inv_ref[seq, here, :]
            for low in range(0, model, LANES):
                unit_x[i * rows : (i + 1) * rows, low : low + LANES] = xs_ref[seq, here, low : low + LANES].astype(f32) * inv

        def product(t, carry):
            value = outer_dot(lhs[...], w_ref[lanes(t), :])
            pairs[seq, :, lanes(t)] = value[: 2 * rows].astype(bf16)
            g_hold[:, lanes(t)] = value[2 * rows : 3 * rows]
            g_own[seq, :, lanes(t)] = value[3 * rows :]
            terms = value * unit_x[:, lanes(t)]
            gains[:, lanes(t)] += jnp.sum(terms.reshape(rows // 2, 8, tile), axis=0)
            return carry

        lax.fori_loop(0, model // tile, product, 0)
        near_send(seq).start()

    def grads_on(seq):
        near_send(seq).wait()
        for low in range(0, model, tile):
            at = slice(low, low + tile)
            g_send[seq, :, at] = (g_hold[:, at] + near[seq, :rows, at].astype(f32)).astype(bf16)
            g_own[seq, :, at] += near[seq, rows:, at].astype(f32)
        chip_send(seq).start()

    def home_sum(p):
        for copy in x_sends(p):
            copy.wait_recv()
        for q in range(4):
            total = x_in[q, :, cut(p)].astype(f32)
            for group in range(1, count // 4):
                total = total + x_in[4 * group + q, :, cut(p)].astype(f32)
            h_send[p, :, q * part : (q + 1) * part] = total.astype(bf16)
        home_start(p)

    gains[...] = jnp.zeros_like(gains)
    load_norm.wait()
    x_part(0)
    small_send.wait_recv()
    for at in range(height):
        sb_ref[at] = (small_keep_ref[at] + small_got[at].astype(f32)).astype(bf16)
    s_sends = [far_copy(sb_ref.at[block(step)], s_in.at[step - 1], PARTS, step) for step in order]
    for copy in s_sends:
        copy.start()
    load.wait()
    grads_of(0)
    x_part(1)
    grads_on(0)
    grads_of(1)
    wide = model // 4

    def gain_part(owner):
        return gains.at[:, pl.ds(pl.multiple_of(owner * wide, LANES), wide)]

    gain_sends = [
        remote(gain_part(peer(hop)), gain_near.at[hop - 1], sends, recvs, 3 * PARTS + 2 + hop, hop) for hop in (1, 2, 3)
    ]
    for copy in gain_sends:
        copy.start()
    for copy in s_sends:
        copy.wait_recv()
    total = sb_ref[mine].astype(f32)
    for step in order:
        total = total + s_in[step - 1].astype(f32)
    s_own[...] = total.astype(bf16)
    small_ref[side, mine] = s_own[...]
    spread = [far_copy(s_own, small_ref.at[side, mine], PARTS + 1, step) for step in order]
    for copy in spread:
        copy.start()

    def pass_on(step):
        at = lax.rem(mine + height - step, height)
        return across(
            small_ref.at[side, at], small_ref.at[side, at], far_sends, far_recvs, (PARTS + 3) * count + step, other
        )

    pass_on(0).start()
    home_sum(0)
    grads_on(1)
    for copy in gain_sends:
        copy.wait()
    gain_sum[...] = gains[:, pl.ds(pl.multiple_of(me * wide, LANES), wide)] + gain_near[0] + gain_near[1] + gain_near[2]
    gain_far = [
        across(gain_sum, gain_in.at[step - 1], far_sends, far_recvs, (PARTS + 2) * count + step, ahead(step))
        for step in range(1, count)
    ]
    for copy in gain_far:
        copy.start()


    def finish_rows(seq):
        chip_send(seq).wait()

        def last(r, carry):
            at = pl.ds(pl.multiple_of(r * 16, 16), 16)
            grad = g_own[seq, at, :] + g_far[seq, at, :].astype(f32)
            vals = x_ref[seq, at, :].astype(f32)
            inv = lax.rsqrt(jnp.mean(vals * vals, axis=1, keepdims=True) + EPS)
            scaled = grad * gain_ref[0:1, :]
            mean = jnp.mean(scaled * vals, axis=1, keepdims=True)
            out = inv * (scaled - vals * (inv * inv * mean))
            dx_ref[seq, at, :] = (cot_ref[seq, at, :].astype(f32) + out).astype(bf16)
            return carry

        lax.fori_loop(0, rows // 16, last, 0)

    finish_rows(0)
    home_sum(1)
    for step in order:
        spread[step - 1].wait_recv()
        pass_on(step).start()
    finish_rows(1)
    for at in range(PARTS + 1):
        home_wait(at)

    @pl.when(me // 2 == 0)
    def _():
        for place in range(2):
            for q in range(4):
                for p in range(PARTS):
                    to = place * width + q * quarter + p * part
                    low = (place * 4 + q) * part
                    gw_ref[:, to : to + part] = h_cols[p, :, low : low + part].astype(f32)

    @pl.when(me // 2 == 1)
    def _():
        for low in range(0, 2 * width, quarter):
            gw_ref[:, low : low + quarter] = z_cols[:, low : low + quarter].astype(f32)

    for copy in gain_far:
        copy.wait()
    total = gain_sum[...]
    for step in range(1, count):
        total = total + gain_in[step - 1]
    ggain_ref[...] = jnp.sum(total, axis=0, keepdims=True)
    for step in range(height):
        pass_on(step).wait()
    goals, start = [], 0
    for ref in (gxp_ref, gdp_ref, gcw_ref, gcb_ref, gdb_ref, gsk_ref):
        goals.append((ref, start, start + ref.shape[0]))
        start += ref.shape[0]
    for at in range(count):
        low, high = at * lined, (at + 1) * lined
        if low < start:
            value = small_ref[at % 2, at // 2].astype(f32)
        for ref, begin, stop in goals:
            a, b = max(low, begin), min(high, stop)
            if a < b:
                ref[a - begin : b - begin, :] = value[a - low : b - low]
    small_send.wait_send()
    for p in range(PARTS):
        for copy in quad_sends(p) + x_sends(p):
            copy.wait_send()
    for copy in s_sends + spread:
        copy.wait_send()


def finish(gx, gz, smalls, wz, norm, w_in, x, cot, gain, xs, inv):
    tokens, width = gx.shape
    height = lax.axis_size("replica") // 2
    lines = -(-sum(value.shape[0] for value in smalls) // (16 * height)) * 8
    deep = wz.shape[0]
    seqs, rows, model = x.shape
    wide = model // 4
    gain_tile = pltpu.VMEM((8, wide), f32)
    other = max(height - 1, 1)
    count = 2 * height
    quarter = width // 4
    kinds = (PARTS + 4) * count
    homes = PARTS + 1 + 2 * seqs
    line = jax.ShapeDtypeStruct((1, width), f32)
    return pl.pallas_call(
        finish_kernel,
        in_specs=[VMEM_SPEC] * 9 + [ANY_SPEC] * 2 + [VMEM_SPEC] * 5,
        out_specs=[VMEM_SPEC] * 9,
        out_shape=[
            jax.ShapeDtypeStruct((deep, 2 * width), f32),
            jax.ShapeDtypeStruct(smalls[0].shape, f32),
            jax.ShapeDtypeStruct(smalls[1].shape, f32),
            jax.ShapeDtypeStruct((KW, width), f32),
            line, line, line,
            jax.ShapeDtypeStruct(x.shape, bf16),
            jax.ShapeDtypeStruct((1, wide), f32),
        ],
        scratch_shapes=[
            pltpu.VMEM((height, lines, width), f32),
            pltpu.VMEM((height, lines, width), bf16),
            pltpu.VMEM((2, height, lines, width), bf16),
            pltpu.VMEM(norm.shape, bf16),
            pltpu.VMEM(w_in.shape, bf16),
            pltpu.VMEM((4 * tokens, quarter), bf16),
            pltpu.VMEM((tokens, 2 * width), bf16),
            pltpu.VMEM((quarter // PARTS, 4 * tokens), bf16),
            pltpu.VMEM((count * deep, quarter), bf16),
            pltpu.VMEM((height, lines, width), bf16),
            pltpu.VMEM((height, lines, width), bf16),
            pltpu.VMEM((count, deep, quarter), bf16),
            pltpu.VMEM((other, lines, width), bf16),
            pltpu.VMEM((4 * rows, 2 * width), bf16),
            pltpu.VMEM((seqs, 2 * rows, model), bf16),
            pltpu.VMEM((seqs, 2 * rows, model), bf16),
            pltpu.VMEM((rows, model), f32),
            pltpu.VMEM((seqs, rows, model), f32),
            pltpu.VMEM((seqs, rows, model), bf16),
            pltpu.VMEM((seqs, rows, model), bf16),
            pltpu.VMEM((PARTS, deep, width // PARTS), bf16),
            pltpu.VMEM((PARTS, deep, 2 * width // PARTS), bf16),
            pltpu.VMEM((deep, 2 * width), bf16),
            pltpu.VMEM((lines, width), bf16),
            pltpu.VMEM((8, model), f32),
            pltpu.VMEM((3, 8, wide), f32),
            gain_tile,
            pltpu.VMEM((count - 1, 8, wide), f32),
            pltpu.VMEM((4 * rows, model), f32),
            pltpu.SemaphoreType.DMA((3 * PARTS + 8 + 2 * seqs,)), pltpu.SemaphoreType.DMA((3 * PARTS + 8 + 2 * seqs,)),
            pltpu.SemaphoreType.DMA((kinds,)), pltpu.SemaphoreType.DMA((kinds,)),
            pltpu.SemaphoreType.DMA((homes,)), pltpu.SemaphoreType.DMA((2 * homes,)),
            pltpu.SemaphoreType.DMA((homes + 2 + PARTS,)),
        ],
        compiler_params=group_params(8, 58 << 20),
        cost_estimate=cost(80),
        name="finish",
    )(gx, gz, *smalls, wz, norm, w_in, x, cot, gain, xs, inv)


def total_kernel(part_ref, out_ref, near, chip_sum, far, sends, recvs):
    me = lax.axis_index("shard")
    half = part_ref.shape[1] // 2
    mine = pl.ds(pl.multiple_of(lax.rem(me, 2) * half, 128), half)
    other = pl.ds(pl.multiple_of((1 - lax.rem(me, 2)) * half, 128), half)
    meet_group()
    first = remote(part_ref.at[:, other], near, sends, recvs, 0, 1)
    first.start()
    first.wait()
    chip_sum[...] = part_ref[:, mine] + near[...]
    second = remote(chip_sum, far, sends, recvs, 1, 2)
    second.start()
    second.wait()
    out_ref[:, mine] = chip_sum[...] + far[...]
    third = remote(out_ref.at[:, mine], out_ref.at[:, mine], sends, recvs, 2, 1)
    third.start()
    third.wait()


def group_total(part, collective_id):
    rows, cols = part.shape
    half = pltpu.VMEM((rows, cols // 2), f32)
    return pl.pallas_call(
        total_kernel,
        in_specs=[VMEM_SPEC],
        out_specs=VMEM_SPEC,
        out_shape=jax.ShapeDtypeStruct((rows, cols), f32),
        scratch_shapes=[half, half, half, pltpu.SemaphoreType.DMA((3,)), pltpu.SemaphoreType.DMA((3,))],
        compiler_params=group_params(collective_id, 16 << 20),
        name="group_total",
    )(part)


def by_hop(value, hop):
    return lax.ppermute(value, "shard", [(i, i ^ hop) for i in range(4)])


def far_send(blocks):
    count = lax.axis_size("replica")
    height = count // 2
    mine = lax.axis_index("replica") // 2

    def pick(at):
        return lax.dynamic_index_in_dim(blocks, at, 0, False)

    sent = []
    for step in range(1, height):
        out = pick(lax.rem(mine + step, height)).astype(bf16)
        sent.append(lax.ppermute(out, "replica", [(i, (i + 2 * step) % count) for i in range(count)]))
    return pick(mine), tuple(sent)


def far_total(own, sent):
    total = own
    for value in sent:
        total = total + value.astype(f32)
    return total


def after(value, *others):
    return lax.optimization_barrier((value,) + others)[0]


def body(
    block_input, segment_ids, norm_gain, w_in, conv_weight, conv_bias, x_proj, dt_proj, dt_bias,
    d_skip, out_proj, out_grad,
):
    seqs, local, model = block_input.shape
    length = segment_ids.shape[1]
    tokens = seqs * length
    width = d_skip.shape[0]
    rank = dt_proj.shape[0]
    n = (x_proj.shape[0] - rank) // 2
    me = lax.axis_index("shard")
    count = lax.axis_size("replica")
    height = count // 2
    side = lax.rem(lax.axis_index("replica"), 2)

    def split(values):
        return values.reshape(seqs, length, -1)

    def halves(values, blocks):
        piece = values.shape[1] // blocks // 2
        cuts = [values[:, b * piece : (b + 1) * piece] for b in range(2 * blocks)]
        even = jnp.concatenate(cuts[0::2], axis=1)
        odd = jnp.concatenate(cuts[1::2], axis=1)
        return jnp.where(side == 0, even, odd), jnp.where(side == 0, odd, even)

    xs, inv, cots, gain, own_half, y_half, z_half, x_part, z_part, gated_own, gated_send, gated_more = front(
        block_input, out_grad, norm_gain, w_in, out_proj
    )
    x_all = xs.reshape(tokens, model)
    cot = cots.reshape(tokens, -1)

    seg_padded = jnp.pad(segment_ids, ((0, 0), (KW - 1, 0)), constant_values=-1)
    taps = [
        (seg_padded[:, KW - 1 - d : KW - 1 - d + length] == segment_ids).astype(f32) for d in range(KW)
    ]
    conv_w = conv_weight.astype(f32)
    xv = x_part.astype(f32)
    x_padded = jnp.pad(x_part, ((0, 0), (KW - 1, 0), (0, 0)))
    conv_pre = conv_bias.astype(f32) + conv_w[KW - 1] * xv
    for j in range(KW - 1):
        d = KW - 1 - j
        conv_pre = conv_pre + conv_w[j] * x_padded[:, j : j + length].astype(f32) * taps[d][:, :, None]
    conv_out = jax.nn.silu(conv_pre).astype(bf16)
    conv_flat = conv_out.reshape(tokens, width)
    own_half, y_half, z_half = (value.reshape(tokens, -1) for value in (own_half, y_half, z_half))
    last_norm = lax.ppermute(y_half, "replica", [(i, i ^ 2) for i in range(count)])
    cot_got = lax.ppermute(cot, "replica", [(i, i ^ 1) for i in range(count)])
    proj = group_total(outer_dot(x_proj, conv_flat), 3)
    gated_far = by_hop(gated_send, 2)
    proj, gated_far = lax.optimization_barrier((proj, gated_far))
    gated_rest = by_hop(after(gated_more, proj), 2)
    keep_lanes = jnp.broadcast_to(taps[1][:, :, None], (seqs, length, LANES))
    skip = d_skip.astype(f32)
    y_total, gated, rate, beta, states = recurrence_forward(
        conv_out, z_part, proj, keep_lanes, dt_proj, dt_bias.astype(f32)[None], skip[None]
    )
    y_total, gated, gated_rest, last_norm, cot_got = lax.optimization_barrier(
        (y_total, gated, gated_rest, last_norm, cot_got)
    )
    cot_both = jnp.concatenate([cot, cot_got], axis=0)
    grad_gated = split(gated_own + jnp.concatenate([gated_far, gated_rest], axis=1).astype(f32))
    z_vals = z_part.astype(f32)
    dy = grad_gated * jax.nn.silu(z_vals)
    grad_z = (grad_gated * y_total * silu_slope(z_vals)).astype(bf16).reshape(tokens, width)

    gated_keep, gated_give = halves(gated.reshape(tokens, width), height // 4)
    cols = model // 4
    keeps, gives, z_blocks, norms, gated_got = collect(
        gated_keep, gated_give, grad_z, own_half, y_half, z_half, last_norm
    )
    z_blocks = z_blocks.reshape(count, -1, width // 4)
    gated_both, block_output, grad_w_z = middle(keeps, gives, gated_got, z_blocks, x_all, out_proj, seqs)
    out_blocks = inner_dot(gated_both.reshape(2 * tokens, -1), cot_both)
    out_own, out_sent = far_send(out_blocks.astype(bf16).reshape(height, -1, cols))
    rate, out_own = lax.optimization_barrier((rate, out_own))

    grad_conv_rec, grad_dt_low, grad_proj, grad_dt_proj, grad_dt_bias, grad_d_skip = recurrence_backward(
        rate, beta, conv_out, dy, proj, keep_lanes, dt_proj, states
    )
    grad_proj, out_sent = lax.optimization_barrier((group_total(grad_proj, 4), out_sent))
    grad_proj = grad_proj.astype(bf16)
    grad_out_proj = far_total(out_own.astype(f32), out_sent)
    grad_x_proj = rows_dot(grad_proj, conv_flat)
    grad_conv = dy * skip + grad_conv_rec + split(inner_dot(grad_proj, x_proj))
    grad_pre = grad_conv * silu_slope(conv_pre)
    grad_conv_bias = jnp.sum(grad_pre, axis=(0, 1))
    grad_conv_weight = jnp.stack(
        [
            jnp.sum(grad_pre * x_padded[:, j : j + length].astype(f32) * taps[KW - 1 - j][:, :, None], axis=(0, 1))
            for j in range(KW)
        ]
    )
    grad_x = conv_w[KW - 1] * grad_pre
    for j in range(KW - 1):
        d = KW - 1 - j
        ahead = jnp.pad(grad_pre * taps[d][:, :, None], ((0, 0), (0, d), (0, 0)))[:, d:]
        grad_x = grad_x + conv_w[j] * ahead
    grad_x = grad_x.astype(bf16).reshape(tokens, width)

    smalls = (grad_x_proj, grad_dt_proj, grad_conv_weight, grad_conv_bias[None], grad_dt_bias, grad_d_skip)
    grad_w_in, grad_x_proj, grad_dt_proj, grad_conv_weight, conv_line, bias_line, skip_line, input_grad, grad_gain = finish(
        grad_x, grad_z, smalls, grad_w_z, norms, w_in, block_input, out_grad, gain, xs, inv
    )
    return (
        block_output, input_grad, grad_gain[0], grad_w_in, grad_conv_weight, conv_line[0], grad_x_proj, grad_dt_proj,
        bias_line[0], skip_line[0], grad_out_proj,
    )


def solution(mesh):
    return jax.shard_map(
        body,
        mesh=mesh,
        in_specs=(
            P("replica", "shard", None), P("replica", None), P("shard"), P(None, "shard"), P(None, "shard"),
            P("shard"), P(None, "shard"), P(None, "shard"), P("shard"), P("shard"), P(None, "shard"),
            P("replica", "shard", None),
        ),
        out_specs=(
            P("replica", "shard", None), P("replica", "shard", None), P("shard"), P("replica", "shard"),
            P(None, "shard"), P("shard"), P(None, "shard"), P(None, "shard"), P("shard"), P("shard"),
            P("replica", "shard"),
        ),
        check_vma=False,
    )
```

```python
import functools

import jax
import jax.numpy as jnp
from jax import lax
from jax.experimental import pallas as pl
from jax.experimental.pallas import tpu as pltpu
from jax.sharding import PartitionSpec as P

KW = 4
EPS = 1e-05
CHUNK = 16
LANES = 128
f32 = jnp.float32
bf16 = jnp.bfloat16


def rows_dot(a, b):
    return jnp.dot(a, b, preferred_element_type=f32)


def inner_dot(a, b):
    return lax.dot_general(a, b, (((0,), (0,)), ((), ())), preferred_element_type=f32)


def outer_dot(a, b):
    return lax.dot_general(a, b, (((1,), (1,)), ((), ())), preferred_element_type=f32)


def silu_slope(values):
    sig_val = jax.nn.sigmoid(values)
    return sig_val + values * sig_val * (1.0 - sig_val)

MESH = pl.DeviceIdType.MESH
BLOCK = 128
UNROLL = 4
BACK_UNROLL = 4


def lane(g):
    return slice(g * LANES, (g + 1) * LANES)


def column(block, t):
    return jnp.broadcast_to(block[:, t : t + 1], (block.shape[0], LANES))


def row(ref, t, g, n):
    return jnp.broadcast_to(ref[t : t + 1, lane(g)], (n, LANES))


def prepare(base, rate_ref, conv_ref, keep_ref, rk, u, kept):
    rows = pl.ds(base, CHUNK)
    rate = rate_ref[0, rows, :]
    keep = keep_ref[0, rows, :]
    conv = conv_ref[0, rows, :].astype(f32)
    for g in range(rate.shape[1] // LANES):
        rk[:, lane(g)] = rate[:, lane(g)] * keep
    u[...] = rate * conv
    kept[...] = keep
    return rate, conv, keep


def shifted(cols, j):
    size = cols.shape[1]
    return pltpu.roll(cols, lax.rem(size - j * CHUNK, size), 1)


def spread_mask(n, size=CHUNK):
    shape = (size, size * n)
    return lax.broadcasted_iota(jnp.int32, shape, 1) // n == lax.broadcasted_iota(jnp.int32, shape, 0)


def picker(n, size=CHUNK):
    shape = (n, size * n)
    return (lax.broadcasted_iota(jnp.int32, shape, 1) % n == lax.broadcasted_iota(jnp.int32, shape, 0)).astype(bf16)


def diagonal(rows, mask, pick):
    return jnp.where(mask, rows_dot(rows.astype(bf16), pick), 0.0).astype(bf16)


def forward_kernel(
    conv_ref, z_ref, proj_ref, keep_ref, dt_proj_ref, dt_bias_ref, skip_ref,
    y_ref, gated_ref, rate_ref, beta_ref, state_ref,
    held_ref, rk, u, kept, query_rows, fresh,
):
    width = conv_ref.shape[2]
    rank = dt_proj_ref.shape[0]
    n = (proj_ref.shape[0] - rank) // 2
    groups = width // LANES
    span = CHUNK * n

    @pl.when(pl.program_id(1) == 0)
    def _():
        held_ref[...] = jnp.zeros_like(held_ref)

    dt_low = proj_ref[0:rank, :].astype(bf16)
    keys = proj_ref[rank : rank + n, :]
    query_rows[...] = proj_ref[rank + n :, :].T
    key_square = jnp.sum(keys.T * keys.T, axis=1, keepdims=True)
    beta = jax.nn.sigmoid(inner_dot(dt_low, dt_proj_ref[...]) + dt_bias_ref[...])
    beta_ref[0] = beta
    rate_ref[0] = beta / (1.0 + beta * key_square)
    mask, pick = spread_mask(n), picker(n)

    def states_of(j, held, rk, u, kept, fresh):
        base = pl.multiple_of(j * CHUNK, CHUNK)
        prepare(base, rate_ref, conv_ref, keep_ref, rk, u, kept)
        near_keys = shifted(keys, j)
        for t in range(CHUNK):
            key = column(near_keys, t)
            key2 = key * key
            keep = jnp.broadcast_to(kept[t : t + 1, :], (n, LANES))
            at = slice(t * n, (t + 1) * n)
            for g in range(groups):
                decay = keep - row(rk, t, g, n) * key2
                held[g] = decay * held[g] + row(u, t, g, n) * key
                fresh[at, lane(g)] = held[g].astype(fresh.dtype)

    def outputs_of(j, fresh):
        base = pl.multiple_of(j * CHUNK, CHUNK)
        rows = pl.ds(base, CHUNK)
        block = fresh[...].astype(bf16)
        state_ref[0, pl.ds(pl.multiple_of(base * n, span), span), :] = block
        conv = conv_ref[0, rows, :].astype(f32)
        total = rows_dot(diagonal(query_rows[rows, :], mask, pick), block) + skip_ref[...] * conv
        y_ref[0, rows, :] = total
        z = z_ref[0, rows, :].astype(f32)
        gated_ref[0, rows, :] = (total * (z * jax.nn.sigmoid(z))).astype(bf16)

    def step(i, held):
        held = list(held)
        for k in range(UNROLL):
            states_of(i * UNROLL + k, held, rk[k], u[k], kept[k], fresh[k])
            if k > 0:
                outputs_of(i * UNROLL + k - 1, fresh[k - 1])
        outputs_of(i * UNROLL + UNROLL - 1, fresh[UNROLL - 1])
        return tuple(held)

    start = tuple(held_ref[:, lane(g)] for g in range(groups))
    end = lax.fori_loop(0, conv_ref.shape[1] // CHUNK // UNROLL, step, start)
    for g in range(groups):
        held_ref[:, lane(g)] = end[g]


def backward_kernel(
    rate_ref, beta_ref, conv_ref, dy_ref, proj_ref, keep_ref, dt_proj_ref, state_ref, last_ref,
    gconv_ref, gdt_ref, gproj_ref, gdt_proj_ref, gdt_bias_ref, gskip_ref,
    held_ref, grate, rk, u, dys, kept, key_rows, adj, adj_state, totals, lined,
):
    block_rows, width = rate_ref.shape[1:]
    rank = dt_proj_ref.shape[0]
    n = (proj_ref.shape[0] - rank) // 2
    groups = width // LANES
    chunks = block_rows // CHUNK

    @pl.when(pl.program_id(1) == 0)
    def _():
        held_ref[...] = jnp.zeros_like(held_ref)

    @pl.when((pl.program_id(0) == 0) & (pl.program_id(1) == 0))
    def _():
        gdt_proj_ref[...] = jnp.zeros_like(gdt_proj_ref)
        gdt_bias_ref[...] = jnp.zeros_like(gdt_bias_ref)
        gskip_ref[...] = jnp.zeros_like(gskip_ref)

    keys = proj_ref[rank : rank + n, :]
    queries = proj_ref[rank + n :, :]
    key_rows[...] = keys.T
    mask, pick = spread_mask(n), picker(n)

    ones = jnp.ones((CHUNK, LANES), bf16)

    def walk(j, held, rk, u, dys, kept, adj, adj_state, totals):
        base = pl.multiple_of(j * CHUNK, CHUNK)
        rows = pl.ds(base, CHUNK)
        prepare(base, rate_ref, conv_ref, keep_ref, rk, u, kept)
        dys[...] = dy_ref[0, rows, :]
        near_keys = shifted(keys, j)
        near_queries = shifted(queries, j)
        late = pl.ds(pl.multiple_of((base + CHUNK - 1) * n, n), n)
        after = [state_ref[0, late, lane(g)] for g in range(groups)]
        for t in reversed(range(CHUNK)):
            own = slice(t * n, (t + 1) * n)
            key = column(near_keys, t)
            key2 = key * key
            query = column(near_queries, t)
            keep = jnp.broadcast_to(kept[t : t + 1, :], (n, LANES))
            prior = jnp.maximum(base + t - 1, 0)
            at = pl.ds(pl.multiple_of(prior * n, n), n)
            parts = [None] * 3
            for g in range(groups):
                slope = row(dys, t, g, n)
                pace = row(rk, t, g, n)
                grad = held[g] + slope * query
                decay = keep - pace * key2
                held[g] = decay * grad
                before = state_ref[0, at, lane(g)]
                if t == 0:
                    before = jnp.where(j == 0, last_ref[0, :, lane(g)], before)
                cross = grad * before.astype(f32)
                adj[own, lane(g)] = grad
                adj_state[own, lane(g)] = cross
                terms = (grad * row(u, t, g, n), cross * pace, after[g].astype(f32) * slope)
                parts = [v if p is None else p + v for p, v in zip(parts, terms)]
                after[g] = before
            for i in range(3):
                totals[i, own, :] = parts[i]

    def settle(j, adj, adj_state, totals):
        base = pl.multiple_of(j * CHUNK, CHUNK)
        rows = pl.ds(base, CHUNK)
        key_block = key_rows[rows, :]
        w1 = rows_dot(diagonal(key_block, mask, pick), adj[...].astype(bf16))
        w2 = rows_dot(diagonal(key_block * key_block, mask, pick), adj_state[...].astype(bf16))
        for i in range(3):
            lined[i, rows, :] = jnp.where(mask, outer_dot(ones, totals[i].astype(bf16)), 0.0)
        keeps = keep_ref[0, rows, :]
        for g in range(groups):
            conv = conv_ref[0, rows, lane(g)].astype(f32)
            grate[rows, lane(g)] = conv * w1[:, lane(g)] - keeps * w2[:, lane(g)]
        gconv_ref[0, rows, :] = rate_ref[0, rows, :] * w1

    def step(i, held):
        held = list(held)
        first = chunks - 1 - i * BACK_UNROLL
        for k in range(BACK_UNROLL):
            walk(first - k, held, rk[k], u[k], dys[k], kept[k], adj[k], adj_state[k], totals[k])
            if k > 0:
                settle(first - k + 1, adj[k - 1], adj_state[k - 1], totals[k - 1])
        last = BACK_UNROLL - 1
        settle(first - last, adj[last], adj_state[last], totals[last])
        return tuple(held)

    start = tuple(held_ref[:, lane(g)] for g in range(groups))
    end = lax.fori_loop(0, chunks // BACK_UNROLL, step, start)
    for g in range(groups):
        held_ref[:, lane(g)] = end[g]

    def picked(left, value):
        high = value.astype(bf16)
        low = (value - high.astype(f32)).astype(bf16)
        return outer_dot(left, high) + outer_dot(left, low)

    rate = rate_ref[0]
    beta = beta_ref[0]
    grad_rate = grate[...]
    self_term = picked(jnp.ones((n, width), bf16), grad_rate * rate * rate)
    key_square = jnp.sum(key_rows[...] * key_rows[...], axis=1, keepdims=True)
    denom_inv = 1.0 / (1.0 + beta * key_square)
    grad_dt = grad_rate * denom_inv * denom_inv * beta * (1.0 - beta)
    low = grad_dt.astype(bf16)
    gdt_ref[0] = low
    gdt_bias_ref[...] += jnp.sum(grad_dt, axis=0, keepdims=True)
    gskip_ref[...] += jnp.sum(dy_ref[0] * conv_ref[0].astype(f32), axis=0, keepdims=True)
    gdt_proj_ref[...] += rows_dot(proj_ref[0:rank, :].astype(bf16), low)
    gproj_ref[0:rank, :] = outer_dot(dt_proj_ref[...], low)
    gproj_ref[rank : rank + n, :] = picked(pick, lined[0]) - 2.0 * keys * (picked(pick, lined[1]) + self_term)
    gproj_ref[rank + n :, :] = picked(pick, lined[2])


def specs_for(length, reverse):
    blocks = length // BLOCK

    def place(b):
        return blocks - 1 - b if reverse else b

    def spec(*shape):
        return pl.BlockSpec((1,) + shape, lambda s, b: (s, place(b)) + (0,) * (len(shape) - 1))

    def across_spec(rows):
        return pl.BlockSpec((rows, BLOCK), lambda s, b: (0, s * blocks + place(b)))

    def whole(*shape):
        return pl.BlockSpec(shape, lambda s, b: (0,) * len(shape))

    return blocks, spec, across_spec, whole


def recurrence_forward(conv, z, proj, keep_lanes, dt_proj, dt_bias, skip):
    seqs, length, width = conv.shape
    rank = dt_proj.shape[0]
    n = (proj.shape[0] - rank) // 2
    blocks, spec, across_spec, whole = specs_for(length, False)
    span = CHUNK * n
    wide = spec(BLOCK, width)
    full = jax.ShapeDtypeStruct((seqs, length, width), f32)
    return pl.pallas_call(
        forward_kernel,
        grid=(seqs, blocks),
        in_specs=[
            wide, wide, across_spec(proj.shape[0]), spec(BLOCK, LANES), whole(rank, width), whole(1, width),
            whole(1, width),
        ],
        out_specs=[wide, wide, wide, wide, spec(BLOCK * n, width)],
        out_shape=[
            full, jax.ShapeDtypeStruct((seqs, length, width), bf16),
            pltpu.HBM((seqs, length, width), f32), pltpu.HBM((seqs, length, width), f32),
            pltpu.HBM((seqs, length * n, width), bf16),
        ],
        scratch_shapes=[
            pltpu.VMEM((n, width), f32),
            [pltpu.VMEM((CHUNK, width), f32)] * UNROLL,
            [pltpu.VMEM((CHUNK, width), f32)] * UNROLL,
            [pltpu.VMEM((CHUNK, LANES), f32)] * UNROLL,
            pltpu.VMEM((BLOCK, n), f32),
            [pltpu.VMEM((span, width), f32)] * UNROLL,
        ],
        compiler_params=pltpu.CompilerParams(vmem_limit_bytes=24 << 20),
        cost_estimate=pl.CostEstimate(flops=16_000_000_000, bytes_accessed=24 << 20, transcendentals=0),
        name="recurrence_forward",
    )(conv, z, proj, keep_lanes, dt_proj, dt_bias, skip)


def recurrence_backward(rate, beta, conv, dy, proj, keep_lanes, dt_proj, states):
    seqs, length, width = rate.shape
    rank = dt_proj.shape[0]
    n = (proj.shape[0] - rank) // 2
    span = CHUNK * n
    blocks, spec, across_spec, whole = specs_for(length, True)
    wide = spec(BLOCK, width)
    before = pl.BlockSpec((1, n, width), lambda s, b: (s, jnp.maximum((blocks - 1 - b) * BLOCK - 1, 0), 0))
    return pl.pallas_call(
        backward_kernel,
        grid=(seqs, blocks),
        in_specs=[
            wide, wide, wide, wide, across_spec(proj.shape[0]), spec(BLOCK, LANES), whole(rank, width),
            spec(BLOCK * n, width), before,
        ],
        out_specs=[wide, wide, across_spec(proj.shape[0]), whole(rank, width), whole(1, width), whole(1, width)],
        out_shape=[
            jax.ShapeDtypeStruct((seqs, length, width), f32),
            jax.ShapeDtypeStruct((seqs, length, width), bf16),
            jax.ShapeDtypeStruct(proj.shape, f32),
            jax.ShapeDtypeStruct((rank, width), f32),
            jax.ShapeDtypeStruct((1, width), f32),
            jax.ShapeDtypeStruct((1, width), f32),
        ],
        scratch_shapes=[
            pltpu.VMEM((n, width), f32),
            pltpu.VMEM((BLOCK, width), f32),
            [pltpu.VMEM((CHUNK, width), f32)] * BACK_UNROLL,
            [pltpu.VMEM((CHUNK, width), f32)] * BACK_UNROLL,
            [pltpu.VMEM((CHUNK, width), f32)] * BACK_UNROLL,
            [pltpu.VMEM((CHUNK, LANES), f32)] * BACK_UNROLL,
            pltpu.VMEM((BLOCK, n), f32),
            [pltpu.VMEM((span, width), f32)] * BACK_UNROLL,
            [pltpu.VMEM((span, width), f32)] * BACK_UNROLL,
            [pltpu.VMEM((3, span, LANES), f32)] * BACK_UNROLL,
            pltpu.VMEM((3, BLOCK, span), f32),
        ],
        compiler_params=pltpu.CompilerParams(vmem_limit_bytes=36 << 20),
        cost_estimate=pl.CostEstimate(flops=30_000_000_000, bytes_accessed=28 << 20, transcendentals=0),
        name="recurrence_backward",
    )(rate, beta, conv, dy, proj, keep_lanes, dt_proj, states, states)


def peer(hop):
    me = lax.axis_index("shard")
    core = lax.rem(me, 2)
    chip = me // 2
    if hop & 1:
        core = 1 - core
    if hop & 2:
        chip = 1 - chip
    return chip * 2 + core


def meet_group():
    barrier = pltpu.get_barrier_semaphore()
    for hop in (1, 2, 3):
        pl.semaphore_signal(barrier, inc=1, device_id={"shard": peer(hop)}, device_id_type=MESH)
    pl.semaphore_wait(barrier, 3)


def remote(src, dst, sends, recvs, at, hop):
    return pltpu.make_async_remote_copy(
        src_ref=src, dst_ref=dst, send_sem=sends.at[at], recv_sem=recvs.at[at],
        device_id={"shard": peer(hop)}, device_id_type=MESH,
    )


def group_params(collective_id, limit):
    return pltpu.CompilerParams(collective_id=collective_id, has_side_effects=True, vmem_limit_bytes=limit)


VMEM_SPEC = pl.BlockSpec(memory_space=pltpu.VMEM)


ANY_SPEC = pl.BlockSpec(memory_space=pl.ANY)


def part_copy(src, dst, send, recv, shard):
    return pltpu.make_async_remote_copy(
        src_ref=src, dst_ref=dst, send_sem=send, recv_sem=recv, device_id={"shard": shard}, device_id_type=MESH
    )


def front_kernel(
    x_ref, cot_ref, gain_ref, w_hbm, o_hbm,
    xs_ref, inv_ref, cots_ref, gain_row_ref, own_half_ref, y_half_ref, z_half_ref, x_part_ref, z_part_ref, own_ref, send_ref, send_more_ref,
    gains_ref, w_ref, o_ref, normed_ref, lhs, mixed, pairs, near, sends, recvs, local, part_sends, part_recvs, part_local,
    pair_sends, pair_recvs, pair_local,
):
    me = lax.axis_index("shard")
    chip = me // 2
    slot = me // 2
    seqs, rows, model = x_ref.shape
    cols = cots_ref.shape[2]
    core = lax.rem(me, 2)
    width = x_part_ref.shape[2]
    lift = gain_ref.shape[0]
    span = 2 * rows
    tile = 256
    loads = [
        pltpu.make_async_copy(w_hbm, w_ref, local.at[3]),
        pltpu.make_async_copy(o_hbm, o_ref, local.at[4]),
    ]
    for copy in loads:
        copy.start()
    meet([quad(1), quad(2)])

    def mine(ref, owner):
        return ref.at[:, pl.ds(pl.multiple_of(owner * rows, 16), rows), :]

    def part(owner):
        return cot_ref.at[:, :, pl.ds(pl.multiple_of(owner * cols, 128), cols)]

    def gain_rows(owner):
        return gains_ref.at[pl.ds(pl.multiple_of(owner * lift, 8), lift), :]

    gain_sends = [remote(gain_ref, gain_rows(me), sends, recvs, 5 + hop, hop) for hop in (1, 2, 3)]
    x_core = remote(x_ref, mine(xs_ref, me), sends, recvs, 0, 1)
    x_chip = remote(x_ref, mine(xs_ref, me), sends, recvs, 1, 2)
    cot_sends = [remote(part(peer(hop)), mine(cots_ref, me), sends, recvs, 2 + hop, hop) for hop in (1, 2, 3)]
    for copy in gain_sends + [x_core, x_chip] + cot_sends:
        copy.start()
    own = [
        pltpu.make_async_copy(x_ref, mine(xs_ref, me), local.at[0]),
        pltpu.make_async_copy(part(me), mine(cots_ref, me), local.at[1]),
        pltpu.make_async_copy(gain_ref, gain_rows(me), local.at[2]),
    ]
    for copy in own:
        copy.start()
    for copy in own:
        copy.wait()
    for copy in gain_sends:
        copy.wait()
    x_core.wait()
    gain = jnp.concatenate([gains_ref[lift * d : lift * d + 1, :] for d in range(4)], axis=1)
    gain_row_ref[...] = jnp.broadcast_to(gain, gain_row_ref.shape)
    loads[0].wait()

    def piece(half, kind):
        where = jnp.bitwise_xor(chip, half)
        return (x_part_ref, z_part_ref)[kind].at[:, pl.ds(pl.multiple_of(where * span, 16), span), :]

    def away(i):
        return lax.rem(2 * me + i, 4) != me

    def send(half, i, kind):
        return part_copy(
            mixed.at[half, i], piece(half, kind), part_sends.at[2 * half + i], part_recvs.at[2 * kind + half],
            lax.rem(2 * me + i, 4),
        )

    def keep(half, i, kind):
        return pltpu.make_async_copy(mixed.at[half, i], piece(half, kind), part_local.at[half])

    def either(half, i, send_does, keep_does):
        for kind in range(2):
            pl.when(away(i) & (slot == kind))(lambda kind=kind: send_does(send(half, i, kind)))
            pl.when(jnp.logical_not(away(i)) & (slot == kind))(lambda kind=kind: keep_does(keep(half, i, kind)))

    def run_half(half):
        where = jnp.bitwise_xor(chip, half) * span

        for seq in range(seqs):

            def norm(r, carry, seq=seq):
                at = pl.ds(pl.multiple_of(where + r * 16, 16), 16)
                vals = xs_ref[seq, at, :].astype(f32)
                inv = lax.rsqrt(jnp.mean(vals * vals, axis=1, keepdims=True) + EPS)
                inv_ref[seq, at, :] = jnp.broadcast_to(inv, (16, LANES))
                out = (vals * inv * gain).astype(bf16)
                normed_ref[seq, at, :] = out
                lhs[pl.ds(pl.multiple_of(seq * span + r * 16, 16), 16), :] = out
                return carry

            lax.fori_loop(0, span // 16, norm, 0)
        for copy in normed_copies(half):
            copy.start()
        for i in range(2):

            def product(t, carry, i=i):
                value = rows_dot(lhs[...], w_ref[:, pl.ds(pl.multiple_of(i * width + t * tile, tile), tile)])
                for seq in range(seqs):
                    mixed[half, i, seq, :, pl.ds(pl.multiple_of(t * tile, tile), tile)] = value[
                        seq * span : (seq + 1) * span
                    ].astype(bf16)
                return carry

            lax.fori_loop(0, width // tile, product, 0)
            either(half, i, lambda copy: copy.start(), lambda copy: copy.start())

    def normed_copies(half):
        where = pl.ds(pl.multiple_of(jnp.bitwise_xor(chip, half) * span, 16), span)
        src = normed_ref.at[:, where, pl.ds(pl.multiple_of(core * (model // 2), LANES), model // 2)]
        copies = [pltpu.make_async_copy(src, own_half_ref.at[:, where, :], pair_local.at[half])]
        for hop in (1, 2):
            at = 2 * half + hop - 1
            half_ref = (y_half_ref, z_half_ref)[hop - 1]
            copies.append(across(src, half_ref.at[:, where, :], pair_sends, pair_recvs, at, quad(hop)))
        return copies

    run_half(0)
    x_chip.wait_recv()
    onward = remote(mine(xs_ref, peer(2)), mine(xs_ref, peer(2)), sends, recvs, 2, 1)
    onward.start()
    onward.wait()
    run_half(1)

    for copy in cot_sends:
        copy.wait()
    loads[1].wait()

    def partial(block, t):
        return outer_dot(
            cots_ref[...].reshape(seqs * 4 * rows, cols),
            o_ref[pl.ds(pl.multiple_of(block * width + t * tile, tile), tile), :],
        )

    def lanes(t):
        return pl.ds(pl.multiple_of(t * tile, tile), tile)

    near_sends = []
    for at, hop in enumerate((3, 1)):

        def fill(t, carry, at=at, hop=hop):
            pairs[at, :, lanes(t)] = partial(peer(hop), t).astype(bf16)
            return carry

        lax.fori_loop(0, width // tile, fill, 0)
        copy = remote(pairs.at[at], near.at[at], sends, recvs, 9 + at, 1)
        copy.start()
        near_sends.append(copy)
    near_sends[0].wait()

    pieces = width // tile // 2
    for first, ref in ((0, send_ref), (pieces, send_more_ref)):

        def to_send(t, carry, first=first, ref=ref):
            ref[:, lanes(t)] = (
                partial(peer(2), first + t) + near[0, :, lanes(first + t)].astype(f32)
            ).astype(bf16)
            return carry

        lax.fori_loop(0, pieces, to_send, 0)
    near_sends[1].wait()

    def to_own(t, carry):
        own_ref[:, lanes(t)] = partial(me, t) + near[1, :, lanes(t)].astype(f32)
        return carry

    lax.fori_loop(0, width // tile, to_own, 0)

    x_chip.wait_send()
    for copy in normed_copies(0) + normed_copies(1):
        copy.wait()
    for half in range(2):
        for i in range(2):
            either(half, i, lambda copy: copy.wait_send(), lambda copy: copy.wait())
        for at in range(2):

            @pl.when(2 * at + me // 2 != me)
            def _(at=at, half=half):
                part_copy(
                    mixed.at[0, 0], mixed.at[0, 0], part_sends.at[0], part_recvs.at[2 * at + half], peer(1)
                ).wait_recv()


def front(x, cot, gain, w_in, out_proj):
    seqs, rows, model = x.shape
    group = lax.axis_size("shard")
    length = rows * group
    cols = model // group
    width = w_in.shape[1] // 2
    tokens = seqs * length
    lifted = jnp.broadcast_to(gain.astype(f32)[None], (8, gain.shape[0]))
    far_sems = pltpu.SemaphoreType.DMA((4,))
    return pl.pallas_call(
        front_kernel,
        in_specs=[VMEM_SPEC] * 3 + [ANY_SPEC] * 2,
        out_specs=[VMEM_SPEC] * 12,
        out_shape=[
            jax.ShapeDtypeStruct((seqs, length, model), bf16),
            jax.ShapeDtypeStruct((seqs, length, LANES), f32),
            jax.ShapeDtypeStruct((seqs, length, cols), bf16),
            jax.ShapeDtypeStruct((8, model), f32),
            jax.ShapeDtypeStruct((seqs, length, model // 2), bf16),
            jax.ShapeDtypeStruct((seqs, length, model // 2), bf16),
            jax.ShapeDtypeStruct((seqs, length, model // 2), bf16),
            jax.ShapeDtypeStruct((seqs, length, width), bf16),
            jax.ShapeDtypeStruct((seqs, length, width), bf16),
            jax.ShapeDtypeStruct((tokens, width), f32),
            jax.ShapeDtypeStruct((tokens, width // 2), bf16),
            jax.ShapeDtypeStruct((tokens, width // 2), bf16),
        ],
        scratch_shapes=[
            pltpu.VMEM((8 * group, gain.shape[0]), f32),
            pltpu.VMEM(w_in.shape, bf16),
            pltpu.VMEM(out_proj.shape, bf16),
            pltpu.VMEM((seqs, length, model), bf16),
            pltpu.VMEM((tokens // 2, model), bf16),
            pltpu.VMEM((2, 2, seqs, 2 * rows, width), bf16),
            pltpu.VMEM((2, tokens, width), bf16),
            pltpu.VMEM((2, tokens, width), bf16),
            pltpu.SemaphoreType.DMA((11,)), pltpu.SemaphoreType.DMA((11,)), pltpu.SemaphoreType.DMA((5,)),
            pltpu.SemaphoreType.DMA((4,)), pltpu.SemaphoreType.DMA((4,)), pltpu.SemaphoreType.DMA((2,)),
            far_sems, far_sems, far_sems,
        ],
        compiler_params=group_params(1, 48 << 20),
        name="front",
    )(x, cot, lifted, w_in, out_proj)


def quad(hop):
    home = lax.axis_index("replica")
    if hop & 1:
        home = home + 1 - 2 * lax.rem(home, 2)
    if hop & 2:
        home = home + 2 - 4 * lax.rem(home // 2, 2)
    return home


def across(src, dst, sends, recvs, at, other):
    return pltpu.make_async_remote_copy(
        src_ref=src, dst_ref=dst, send_sem=sends.at[at], recv_sem=recvs.at[at],
        device_id={"replica": other}, device_id_type=MESH,
    )


def meet(replicas):
    barrier = pltpu.get_barrier_semaphore()
    for hop in (1, 2, 3):
        pl.semaphore_signal(barrier, inc=1, device_id={"shard": peer(hop)}, device_id_type=MESH)
    for other in replicas:
        pl.semaphore_signal(barrier, inc=1, device_id={"replica": other}, device_id_type=MESH)
    pl.semaphore_wait(barrier, 3 + len(replicas))


def ahead(step):
    count = lax.axis_size("replica")
    return lax.rem(lax.axis_index("replica") + step, count)


def collect_kernel(
    keep_ref, give_ref, gz_ref, own_half_ref, y_half_ref, z_half_ref, last_ref,
    keeps_ref, gives_ref, zb_ref, norm_out_ref, got_ref,
    gz_ref4, norm_ref, turned, sends, recvs, local,
):
    me = lax.axis_index("shard")
    half = keep_ref.shape[1]
    core = lax.rem(me, 2)
    member = lax.rem(lax.axis_index("replica"), 4)
    tokens, part = gz_ref4.shape[1:]
    tile = 256

    def norm_rows(which):
        return norm_ref.at[core, which * tokens : (which + 1) * tokens]

    meet([quad(hop) for hop in (1, 2, 3)])

    def quarter(which):
        return gz_ref.at[:, pl.ds(pl.multiple_of(which * part, LANES), part)]

    def spot(ref, owner):
        return ref.at[:, pl.ds(pl.multiple_of(owner * half, 128), half)]

    k_chip = remote(keep_ref, spot(keeps_ref, me), sends, recvs, 0, 2)
    v_chip = remote(give_ref, spot(gives_ref, me), sends, recvs, 1, 2)
    k_core = remote(keep_ref, spot(keeps_ref, me), sends, recvs, 2, 1)
    v_core = remote(give_ref, spot(gives_ref, me), sends, recvs, 3, 1)
    quads = [
        across(quarter(lax.rem(quad(hop), 4)), gz_ref4.at[hop], sends, recvs, 6 + hop, quad(hop)) for hop in (3, 1, 2)
    ]
    give_pair = across(give_ref, got_ref, sends, recvs, 11, quad(1))
    norms = [
        remote(own_half_ref, norm_rows(0), sends, recvs, 12, 1),
        remote(y_half_ref, norm_rows(1), sends, recvs, 10, 1),
        remote(z_half_ref, norm_rows(2), sends, recvs, 13, 1),
        remote(last_ref, norm_rows(3), sends, recvs, 4, 1),
    ]
    own = [
        pltpu.make_async_copy(keep_ref, spot(keeps_ref, me), local.at[0]),
        pltpu.make_async_copy(give_ref, spot(gives_ref, me), local.at[1]),
        pltpu.make_async_copy(quarter(member), gz_ref4.at[0], local.at[2]),
        pltpu.make_async_copy(own_half_ref, norm_rows(0), local.at[5]),
        pltpu.make_async_copy(y_half_ref, norm_rows(1), local.at[3]),
        pltpu.make_async_copy(z_half_ref, norm_rows(2), local.at[6]),
        pltpu.make_async_copy(last_ref, norm_rows(3), local.at[4]),
    ]
    for copy in [k_chip, v_chip] + quads + [give_pair, k_core, v_core] + norms + own:
        copy.start()
    for copy in own + quads + norms:
        copy.wait()
    out_copy = pltpu.make_async_copy(norm_ref, norm_out_ref, local.at[7])
    out_copy.start()
    for hop in range(4):
        for at in range(0, tokens, tile):
            turned[:, hop * tokens + at : hop * tokens + at + tile] = gz_ref4[hop, at : at + tile, :].T
    wide = norm_ref.shape[2] // tile

    def rows_of(t, carry):
        feature = pl.ds(pl.multiple_of(lax.rem(t, wide) * tile, tile), tile)
        value = rows_dot(turned[...], norm_ref[t // wide, :, feature])
        zb_ref[pl.ds(pl.multiple_of(t * tile, tile), tile), :] = value.astype(bf16).T
        return carry

    lax.fori_loop(0, zb_ref.shape[0] // tile, rows_of, 0)
    k_chip.wait_recv()
    k_on = remote(spot(keeps_ref, peer(2)), spot(keeps_ref, peer(2)), sends, recvs, 5, 1)
    k_on.start()
    v_chip.wait_recv()
    v_on = remote(spot(gives_ref, peer(2)), spot(gives_ref, peer(2)), sends, recvs, 6, 1)
    v_on.start()
    for copy in [give_pair, k_core, v_core, k_on, v_on, out_copy]:
        copy.wait()
    k_chip.wait_send()
    v_chip.wait_send()


def cost(microseconds):
    return pl.CostEstimate(flops=int(microseconds * 1e9), bytes_accessed=1 << 20, transcendentals=0)


def collect(keep, give, grad_z, own_half, y_half, z_half, last_norm):
    tokens, half = keep.shape
    group = lax.axis_size("shard")
    wide = jax.ShapeDtypeStruct((tokens, half * group), bf16)
    features, quarter = last_norm.shape[1], grad_z.shape[1] // 4
    return pl.pallas_call(
        collect_kernel,
        in_specs=[VMEM_SPEC] * 7,
        out_specs=[VMEM_SPEC] * 3 + [ANY_SPEC, VMEM_SPEC],
        out_shape=[
            wide, wide, jax.ShapeDtypeStruct((2 * features, quarter), bf16),
            pltpu.HBM((2, 4 * tokens, features), bf16),
            jax.ShapeDtypeStruct(give.shape, bf16),
        ],
        scratch_shapes=[
            pltpu.VMEM((4, tokens, quarter), bf16),
            pltpu.VMEM((2, 4 * tokens, features), bf16),
            pltpu.VMEM((quarter, 4 * tokens), bf16),
            pltpu.SemaphoreType.DMA((14,)), pltpu.SemaphoreType.DMA((14,)), pltpu.SemaphoreType.DMA((8,)),
        ],
        compiler_params=group_params(6, 34 << 20),
        cost_estimate=cost(25),
        name="collect",
    )(keep, give, grad_z, own_half, y_half, z_half, last_norm)


def middle_kernel(
    keeps_ref, gives_ref, got_ref, z_ref, x_hbm, o_hbm,
    both_ref, out_ref, wz_ref,
    z_got_ref, o_ref, xcol, outs, sends, recvs, far_sends, far_recvs, local, o_local,
):
    me = lax.axis_index("shard")
    side = lax.rem(lax.axis_index("replica"), 2)
    tokens, half = got_ref.shape
    gots_ref = both_ref.at[1]
    seqs, rows, _ = out_ref.shape
    cols = xcol.shape[1]
    piece = o_hbm.shape[0] // lax.axis_size("replica")
    per = half // piece
    loads = []
    for d in range(4):
        for q in range(2):
            for j in range(per):
                at = d * 2 * half + (2 * j) * piece + (side if q == 0 else 1 - side) * piece
                loads.append(
                    pltpu.make_async_copy(
                        o_hbm.at[pl.ds(pl.multiple_of(at, piece), piece), :],
                        o_ref.at[q, pl.ds(d * half + j * piece, piece), :],
                        o_local.at[len(loads)],
                    )
                )
    for copy in loads:
        copy.start()
    fetch = pltpu.make_async_copy(
        x_hbm.at[:, pl.ds(pl.multiple_of(me * cols, 128), cols)], xcol, local.at[0]
    )
    fetch.start()
    home = lax.axis_index("replica")
    count = lax.axis_size("replica")
    meet([ahead(step) for step in range(1, count)])

    def spot(owner):
        return gots_ref.at[:, pl.ds(pl.multiple_of(owner * half, 128), half)]

    g_own = pltpu.make_async_copy(got_ref, spot(me), local.at[2])
    g_chip = remote(got_ref, spot(me), sends, recvs, 0, 2)
    g_core = remote(got_ref, spot(me), sends, recvs, 1, 1)
    own = [
        pltpu.make_async_copy(keeps_ref, both_ref.at[0], local.at[1]),
    ]
    own.append(pltpu.make_async_copy(z_ref.at[home], z_got_ref.at[home], local.at[3 + seqs]))
    z_sends = [
        across(z_ref.at[ahead(step)], z_got_ref.at[home], far_sends, far_recvs, step, ahead(step))
        for step in range(1, count)
    ]
    own.append(g_own)
    for copy in [g_chip] + z_sends + [g_core] + own:
        copy.start()
    for copy in loads + [fetch]:
        copy.wait()
    tile = 256

    def product(t, carry):
        rows_at = pl.ds(pl.multiple_of(t * tile, tile), tile)
        value = (
            xcol[rows_at, :].astype(f32)
            + rows_dot(keeps_ref[rows_at, :], o_ref[0])
            + rows_dot(gives_ref[rows_at, :], o_ref[1])
        )
        outs[rows_at, :] = value.astype(bf16)
        return carry

    lax.fori_loop(0, tokens // tile, product, 0)
    length = tokens // seqs
    out_sends = []
    for seq in range(seqs):
        for n_hop, hop in enumerate((2, 3, 1)):
            src = outs.at[pl.ds(pl.multiple_of(seq * length + peer(hop) * rows, 16), rows), :]
            dst = out_ref.at[seq, :, pl.ds(pl.multiple_of(me * cols, 128), cols)]
            out_sends.append(remote(src, dst, sends, recvs, 2 + seq * 3 + n_hop, hop))
        own.append(
            pltpu.make_async_copy(
                outs.at[pl.ds(pl.multiple_of(seq * length + me * rows, 16), rows), :],
                out_ref.at[seq, :, pl.ds(pl.multiple_of(me * cols, 128), cols)],
                local.at[3 + seq],
            )
        )
        own[-1].start()
    for copy in out_sends:
        copy.start()
    base = 2 + seqs * 3
    g_chip.wait_recv()
    g_on = remote(spot(peer(2)), spot(peer(2)), sends, recvs, base + 2, 1)
    g_on.start()
    for copy in out_sends + [g_on, g_core] + own + z_sends:
        copy.wait()
    g_chip.wait_send()
    quarter = z_got_ref.shape[2]
    for q in range(4):
        total = z_got_ref[q].astype(f32)
        for group in range(1, count // 4):
            total = total + z_got_ref[4 * group + q].astype(f32)
        wz_ref[:, q * quarter : (q + 1) * quarter] = total.astype(bf16)


def middle(keeps, gives, got, z_blocks, x_all, out_proj, seqs):
    tokens, half = got.shape
    group = lax.axis_size("shard")
    model = x_all.shape[1]
    cols = model // group
    far_sems = pltpu.SemaphoreType.DMA((lax.axis_size("replica"),))
    pieces = 8 * max(1, half * lax.axis_size("replica") // out_proj.shape[0])
    return pl.pallas_call(
        middle_kernel,
        in_specs=[VMEM_SPEC] * 4 + [ANY_SPEC] * 2,
        out_specs=[VMEM_SPEC] * 3,
        out_shape=[
            jax.ShapeDtypeStruct((2, tokens, half * group), bf16),
            jax.ShapeDtypeStruct((seqs, tokens // seqs // group, model), bf16),
            jax.ShapeDtypeStruct((z_blocks.shape[1], 4 * z_blocks.shape[2]), bf16),
        ],
        scratch_shapes=[
            pltpu.VMEM(z_blocks.shape, bf16),
            pltpu.VMEM((2, half * group, cols), bf16),
            pltpu.VMEM((tokens, cols), bf16),
            pltpu.VMEM((tokens, cols), bf16),
            pltpu.SemaphoreType.DMA((5 + 3 * seqs,)), pltpu.SemaphoreType.DMA((5 + 3 * seqs,)),
            far_sems, far_sems, pltpu.SemaphoreType.DMA((4 + seqs,)), pltpu.SemaphoreType.DMA((pieces,)),
        ],
        compiler_params=group_params(7, 22 << 20),
        cost_estimate=cost(25),
        name="middle",
    )(keeps, gives, got, z_blocks, x_all, out_proj)


PARTS = 2


def finish_kernel(
    gx_ref, gz_ref, xp_ref, dp_ref, cw_ref, cb_ref, db_ref, sk_ref, wz_ref, norm_hbm, w_hbm, x_ref, cot_ref, gain_ref, xs_ref, inv_ref,
    gw_ref, gxp_ref, gdp_ref, gcw_ref, gcb_ref, gdb_ref, gsk_ref, dx_ref, ggain_ref,
    small_keep_ref, small_give_ref, small_ref, norm_ref, w_ref, gx4, cols_ref, turned, xb_ref, sb_ref, small_got, x_in, s_in, lhs, pairs, near, g_hold, g_own, g_send, g_far,
    h_send, h_cols, z_cols, s_own, gains, gain_near, gain_sum, gain_in, unit_x,
    sends, recvs, far_sends, far_recvs, home_sends, home_recvs, local,
):
    me = lax.axis_index("shard")
    home = lax.axis_index("replica")
    count = lax.axis_size("replica")
    height = count // 2
    mine = home // 2
    side = lax.rem(home, 2)
    seqs, rows, model = x_ref.shape
    tokens, width = gx_ref.shape
    length = tokens // seqs
    deep = wz_ref.shape[0]
    member = lax.rem(home, 4)
    quarter = width // 4
    part = quarter // PARTS
    tile = 256
    other = quad(1)
    load = pltpu.make_async_copy(w_hbm, w_ref, local.at[0])
    load_norm = pltpu.make_async_copy(norm_hbm, norm_ref, local.at[1])
    load_norm.start()
    load.start()
    meet([ahead(step) for step in range(1, count)])

    def far(step):
        return ahead(2 * step)

    def cut(p):
        return slice(p * part, (p + 1) * part)

    def piece_of(which, p):
        return gx_ref.at[:, pl.ds(pl.multiple_of(which * quarter + p * part, LANES), part)]

    def spot_of(hop, p):
        return gx4.at[hop * tokens : (hop + 1) * tokens, cut(p)]

    def quad_sends(p):
        return [
            across(piece_of(lax.rem(quad(hop), 4), p), spot_of(hop, p), sends, recvs, 3 * p + hop - 1, quad(hop))
            for hop in (3, 1, 2)
        ]

    small_send = across(small_give_ref, small_got, sends, recvs, 3 * PARTS, other)
    quad_own = [
        pltpu.make_async_copy(piece_of(member, p), spot_of(0, p), local.at[PARTS + 3 + 2 * seqs + p]) for p in range(PARTS)
    ]
    for copy in quad_sends(0):
        copy.start()
    lined = small_keep_ref.shape[1]

    def fill(at, put):
        low, high, begin = at * lined, (at + 1) * lined, 0
        for ref in (xp_ref, dp_ref, cw_ref, cb_ref, db_ref, sk_ref):
            stop = begin + ref.shape[0]
            a, b = max(low, begin), min(high, stop)
            if a < b:
                put(at // 2, slice(a - low, b - low), ref[a - begin : b - begin, :])
            begin = stop
        if high > begin:
            a = max(low, begin)
            put(at // 2, slice(a - low, lined), jnp.zeros((high - a, width), f32))

    def keep_rows(at, rows_at, value):
        small_keep_ref[at, rows_at, :] = value

    for at in range(count):
        pl.when(side == at % 2)(lambda at=at: fill(at, keep_rows))

        @pl.when(side != at % 2)
        def _(at=at):
            values = []
            fill(at, lambda where, rows_at, value: values.append(value))
            small_give_ref[at // 2] = jnp.concatenate(values, axis=0).astype(bf16)

    for copy in [small_send] + quad_sends(1) + quad_own:
        copy.start()

    def goal(slot):
        return (4 * slot + me) // 2

    spot = pl.ds(pl.multiple_of(lax.rem(me, 2) * width, LANES), width)

    def home_pieces(at):
        if at == PARTS:
            return 1, wz_ref, z_cols.at[:, spot]
        if at > PARTS:
            slot, seq = (at - PARTS - 1) % 2, (at - PARTS - 1) // 2
            some = slice(seq * length, (seq + 1) * length)
            return slot, (gx_ref, gz_ref)[slot].at[some], cols_ref.at[some, spot]
        some = 4 * part
        return 0, h_send.at[at], h_cols.at[at, :, pl.ds(pl.multiple_of(lax.rem(me, 2) * some, LANES), some)]

    def home_send(at):
        slot, src, dst = home_pieces(at)
        return part_copy(src, dst, home_sends.at[at], home_recvs.at[at * 2 + lax.rem(me, 2)], goal(slot))

    def home_keep(at):
        _, src, dst = home_pieces(at)
        return pltpu.make_async_copy(src, dst, local.at[2 + at])

    def home_start(at):
        slot = home_pieces(at)[0]
        pl.when(goal(slot) != me)(lambda: home_send(at).start())
        pl.when(goal(slot) == me)(lambda: home_keep(at).start())

    def home_wait(at):
        slot = home_pieces(at)[0]
        pl.when(goal(slot) != me)(lambda: home_send(at).wait_send())
        pl.when(goal(slot) == me)(lambda: home_keep(at).wait())
        for place in range(2):
            source = lax.rem(2 * me + place, 4)

            @pl.when((me // 2 == slot) & (source != me))
            def _(place=place):
                src = home_pieces(at)[1]
                part_copy(src, src, home_sends.at[at], home_recvs.at[at * 2 + place], peer(1)).wait_recv()

    for at in (*range(PARTS + 1, PARTS + 1 + 2 * seqs), PARTS):
        home_start(at)

    def far_copy(src, dst, kind, step):
        return across(src, dst, far_sends, far_recvs, kind * count + step, far(step))

    def block(step):
        return lax.rem(mine + step, height)

    order = range(1, height)

    def lines(at):
        return pl.ds(pl.multiple_of(at * deep, 16), deep)

    def x_sends(p):
        return [
            across(
                xb_ref.at[lines(ahead(step)), cut(p)], x_in.at[home, :, cut(p)], far_sends, far_recvs,
                p * count + step, ahead(step),
            )
            for step in range(1, count)
        ]

    def x_part(p):
        for copy in quad_sends(p):
            copy.wait_recv()
        quad_own[p].wait()

        for at in range(0, 4 * tokens, tile):
            turned[:, at : at + tile] = gx4[at : at + tile, cut(p)].T
        wide = norm_ref.shape[2] // tile

        def rows_of(t, carry):
            feature = pl.ds(pl.multiple_of(lax.rem(t, wide) * tile, tile), tile)
            value = rows_dot(turned[...], norm_ref[t // wide, :, feature])
            xb_ref[pl.ds(pl.multiple_of(t * tile, tile), tile), cut(p)] = value.astype(bf16).T
            return carry

        lax.fori_loop(0, xb_ref.shape[0] // tile, rows_of, 0)
        x_in[home, :, cut(p)] = xb_ref[lines(home), cut(p)]
        for copy in x_sends(p):
            copy.start()

    def lanes(t):
        return pl.ds(pl.multiple_of(t * tile, tile), tile)

    def near_send(seq):
        return remote(pairs.at[seq], near.at[seq], sends, recvs, 3 * PARTS + 8 + 2 * seq, 1)

    def chip_send(seq):
        return remote(g_send.at[seq], g_far.at[seq], sends, recvs, 3 * PARTS + 9 + 2 * seq, 2)

    def grads_of(seq):
        home_wait(PARTS + 1 + 2 * seq)
        home_wait(PARTS + 2 + 2 * seq)
        for i, owner in enumerate((peer(3), peer(1), peer(2), me)):
            at = pl.ds(pl.multiple_of(seq * length + owner * rows, 16), rows)
            lhs[i * rows : (i + 1) * rows, :] = cols_ref[at, :]
            here = pl.ds(pl.multiple_of(owner * rows, 16), rows)
            inv = inv_ref[seq, here, :]
            for low in range(0, model, LANES):
                unit_x[i * rows : (i + 1) * rows, low : low + LANES] = xs_ref[seq, here, low : low + LANES].astype(f32) * inv

        def product(t, carry):
            value = outer_dot(lhs[...], w_ref[lanes(t), :])
            pairs[seq, :, lanes(t)] = value[: 2 * rows].astype(bf16)
            g_hold[:, lanes(t)] = value[2 * rows : 3 * rows]
            g_own[seq, :, lanes(t)] = value[3 * rows :]
            terms = value * unit_x[:, lanes(t)]
            gains[:, lanes(t)] += jnp.sum(terms.reshape(rows // 2, 8, tile), axis=0)
            return carry

        lax.fori_loop(0, model // tile, product, 0)
        near_send(seq).start()

    def grads_on(seq):
        near_send(seq).wait()
        for low in range(0, model, tile):
            at = slice(low, low + tile)
            g_send[seq, :, at] = (g_hold[:, at] + near[seq, :rows, at].astype(f32)).astype(bf16)
            g_own[seq, :, at] += near[seq, rows:, at].astype(f32)
        chip_send(seq).start()

    def home_sum(p):
        for copy in x_sends(p):
            copy.wait_recv()
        for q in range(4):
            total = x_in[q, :, cut(p)].astype(f32)
            for group in range(1, count // 4):
                total = total + x_in[4 * group + q, :, cut(p)].astype(f32)
            h_send[p, :, q * part : (q + 1) * part] = total.astype(bf16)
        home_start(p)

    gains[...] = jnp.zeros_like(gains)
    load_norm.wait()
    x_part(0)
    small_send.wait_recv()
    for at in range(height):
        sb_ref[at] = (small_keep_ref[at] + small_got[at].astype(f32)).astype(bf16)
    s_sends = [far_copy(sb_ref.at[block(step)], s_in.at[step - 1], PARTS, step) for step in order]
    for copy in s_sends:
        copy.start()
    load.wait()
    grads_of(0)
    x_part(1)
    grads_on(0)
    grads_of(1)
    wide = model // 4

    def gain_part(owner):
        return gains.at[:, pl.ds(pl.multiple_of(owner * wide, LANES), wide)]

    gain_sends = [
        remote(gain_part(peer(hop)), gain_near.at[hop - 1], sends, recvs, 3 * PARTS + 2 + hop, hop) for hop in (1, 2, 3)
    ]
    for copy in gain_sends:
        copy.start()
    for copy in s_sends:
        copy.wait_recv()
    total = sb_ref[mine].astype(f32)
    for step in order:
        total = total + s_in[step - 1].astype(f32)
    s_own[...] = total.astype(bf16)
    small_ref[side, mine] = s_own[...]
    spread = [far_copy(s_own, small_ref.at[side, mine], PARTS + 1, step) for step in order]
    for copy in spread:
        copy.start()

    def pass_on(step):
        at = lax.rem(mine + height - step, height)
        return across(
            small_ref.at[side, at], small_ref.at[side, at], far_sends, far_recvs, (PARTS + 3) * count + step, other
        )

    pass_on(0).start()
    grads_on(1)
    home_sum(0)
    for copy in gain_sends:
        copy.wait()
    gain_sum[...] = gains[:, pl.ds(pl.multiple_of(me * wide, LANES), wide)] + gain_near[0] + gain_near[1] + gain_near[2]
    gain_far = [
        across(gain_sum, gain_in.at[step - 1], far_sends, far_recvs, (PARTS + 2) * count + step, ahead(step))
        for step in range(1, count)
    ]
    for copy in gain_far:
        copy.start()


    def finish_rows(seq):
        chip_send(seq).wait()

        def last(r, carry):
            at = pl.ds(pl.multiple_of(r * 16, 16), 16)
            grad = g_own[seq, at, :] + g_far[seq, at, :].astype(f32)
            vals = x_ref[seq, at, :].astype(f32)
            inv = lax.rsqrt(jnp.mean(vals * vals, axis=1, keepdims=True) + EPS)
            scaled = grad * gain_ref[0:1, :]
            mean = jnp.mean(scaled * vals, axis=1, keepdims=True)
            out = inv * (scaled - vals * (inv * inv * mean))
            dx_ref[seq, at, :] = (cot_ref[seq, at, :].astype(f32) + out).astype(bf16)
            return carry

        lax.fori_loop(0, rows // 16, last, 0)

    finish_rows(0)
    home_sum(1)
    for step in order:
        spread[step - 1].wait_recv()
        pass_on(step).start()
    finish_rows(1)
    for at in range(PARTS + 1):
        home_wait(at)

    @pl.when(me // 2 == 0)
    def _():
        for place in range(2):
            for q in range(4):
                for p in range(PARTS):
                    to = place * width + q * quarter + p * part
                    low = (place * 4 + q) * part
                    gw_ref[:, to : to + part] = h_cols[p, :, low : low + part].astype(f32)

    @pl.when(me // 2 == 1)
    def _():
        for low in range(0, 2 * width, quarter):
            gw_ref[:, low : low + quarter] = z_cols[:, low : low + quarter].astype(f32)

    for copy in gain_far:
        copy.wait()
    total = gain_sum[...]
    for step in range(1, count):
        total = total + gain_in[step - 1]
    ggain_ref[...] = jnp.sum(total, axis=0, keepdims=True)
    for step in range(height):
        pass_on(step).wait()
    goals, start = [], 0
    for ref in (gxp_ref, gdp_ref, gcw_ref, gcb_ref, gdb_ref, gsk_ref):
        goals.append((ref, start, start + ref.shape[0]))
        start += ref.shape[0]
    for at in range(count):
        low, high = at * lined, (at + 1) * lined
        if low < start:
            value = small_ref[at % 2, at // 2].astype(f32)
        for ref, begin, stop in goals:
            a, b = max(low, begin), min(high, stop)
            if a < b:
                ref[a - begin : b - begin, :] = value[a - low : b - low]
    small_send.wait_send()
    for p in range(PARTS):
        for copy in quad_sends(p) + x_sends(p):
            copy.wait_send()
    for copy in s_sends + spread:
        copy.wait_send()


def finish(gx, gz, smalls, wz, norm, w_in, x, cot, gain, xs, inv):
    tokens, width = gx.shape
    height = lax.axis_size("replica") // 2
    lines = -(-sum(value.shape[0] for value in smalls) // (16 * height)) * 8
    deep = wz.shape[0]
    seqs, rows, model = x.shape
    wide = model // 4
    gain_tile = pltpu.VMEM((8, wide), f32)
    other = max(height - 1, 1)
    count = 2 * height
    quarter = width // 4
    kinds = (PARTS + 4) * count
    homes = PARTS + 1 + 2 * seqs
    line = jax.ShapeDtypeStruct((1, width), f32)
    return pl.pallas_call(
        finish_kernel,
        in_specs=[VMEM_SPEC] * 9 + [ANY_SPEC] * 2 + [VMEM_SPEC] * 5,
        out_specs=[VMEM_SPEC] * 9,
        out_shape=[
            jax.ShapeDtypeStruct((deep, 2 * width), f32),
            jax.ShapeDtypeStruct(smalls[0].shape, f32),
            jax.ShapeDtypeStruct(smalls[1].shape, f32),
            jax.ShapeDtypeStruct((KW, width), f32),
            line, line, line,
            jax.ShapeDtypeStruct(x.shape, bf16),
            jax.ShapeDtypeStruct((1, wide), f32),
        ],
        scratch_shapes=[
            pltpu.VMEM((height, lines, width), f32),
            pltpu.VMEM((height, lines, width), bf16),
            pltpu.VMEM((2, height, lines, width), bf16),
            pltpu.VMEM(norm.shape, bf16),
            pltpu.VMEM(w_in.shape, bf16),
            pltpu.VMEM((4 * tokens, quarter), bf16),
            pltpu.VMEM((tokens, 2 * width), bf16),
            pltpu.VMEM((quarter // PARTS, 4 * tokens), bf16),
            pltpu.VMEM((count * deep, quarter), bf16),
            pltpu.VMEM((height, lines, width), bf16),
            pltpu.VMEM((height, lines, width), bf16),
            pltpu.VMEM((count, deep, quarter), bf16),
            pltpu.VMEM((other, lines, width), bf16),
            pltpu.VMEM((4 * rows, 2 * width), bf16),
            pltpu.VMEM((seqs, 2 * rows, model), bf16),
            pltpu.VMEM((seqs, 2 * rows, model), bf16),
            pltpu.VMEM((rows, model), f32),
            pltpu.VMEM((seqs, rows, model), f32),
            pltpu.VMEM((seqs, rows, model), bf16),
            pltpu.VMEM((seqs, rows, model), bf16),
            pltpu.VMEM((PARTS, deep, width // PARTS), bf16),
            pltpu.VMEM((PARTS, deep, 2 * width // PARTS), bf16),
            pltpu.VMEM((deep, 2 * width), bf16),
            pltpu.VMEM((lines, width), bf16),
            pltpu.VMEM((8, model), f32),
            pltpu.VMEM((3, 8, wide), f32),
            gain_tile,
            pltpu.VMEM((count - 1, 8, wide), f32),
            pltpu.VMEM((4 * rows, model), f32),
            pltpu.SemaphoreType.DMA((3 * PARTS + 8 + 2 * seqs,)), pltpu.SemaphoreType.DMA((3 * PARTS + 8 + 2 * seqs,)),
            pltpu.SemaphoreType.DMA((kinds,)), pltpu.SemaphoreType.DMA((kinds,)),
            pltpu.SemaphoreType.DMA((homes,)), pltpu.SemaphoreType.DMA((2 * homes,)),
            pltpu.SemaphoreType.DMA((homes + 2 + PARTS,)),
        ],
        compiler_params=group_params(8, 58 << 20),
        cost_estimate=cost(80),
        name="finish",
    )(gx, gz, *smalls, wz, norm, w_in, x, cot, gain, xs, inv)


def total_kernel(part_ref, out_ref, near, chip_sum, far, sends, recvs):
    me = lax.axis_index("shard")
    half = part_ref.shape[1] // 2
    mine = pl.ds(pl.multiple_of(lax.rem(me, 2) * half, 128), half)
    other = pl.ds(pl.multiple_of((1 - lax.rem(me, 2)) * half, 128), half)
    meet_group()
    first = remote(part_ref.at[:, other], near, sends, recvs, 0, 1)
    first.start()
    first.wait()
    chip_sum[...] = part_ref[:, mine] + near[...]
    second = remote(chip_sum, far, sends, recvs, 1, 2)
    second.start()
    second.wait()
    out_ref[:, mine] = chip_sum[...] + far[...]
    third = remote(out_ref.at[:, mine], out_ref.at[:, mine], sends, recvs, 2, 1)
    third.start()
    third.wait()


def group_total(part, collective_id):
    rows, cols = part.shape
    half = pltpu.VMEM((rows, cols // 2), f32)
    return pl.pallas_call(
        total_kernel,
        in_specs=[VMEM_SPEC],
        out_specs=VMEM_SPEC,
        out_shape=jax.ShapeDtypeStruct((rows, cols), f32),
        scratch_shapes=[half, half, half, pltpu.SemaphoreType.DMA((3,)), pltpu.SemaphoreType.DMA((3,))],
        compiler_params=group_params(collective_id, 16 << 20),
        name="group_total",
    )(part)


def by_hop(value, hop):
    return lax.ppermute(value, "shard", [(i, i ^ hop) for i in range(4)])


def far_send(blocks):
    count = lax.axis_size("replica")
    height = count // 2
    mine = lax.axis_index("replica") // 2

    def pick(at):
        return lax.dynamic_index_in_dim(blocks, at, 0, False)

    sent = []
    for step in range(1, height):
        out = pick(lax.rem(mine + step, height)).astype(bf16)
        sent.append(lax.ppermute(out, "replica", [(i, (i + 2 * step) % count) for i in range(count)]))
    return pick(mine), tuple(sent)


def far_total(own, sent):
    total = own
    for value in sent:
        total = total + value.astype(f32)
    return total


def after(value, *others):
    return lax.optimization_barrier((value,) + others)[0]


def body(
    block_input, segment_ids, norm_gain, w_in, conv_weight, conv_bias, x_proj, dt_proj, dt_bias,
    d_skip, out_proj, out_grad,
):
    seqs, local, model = block_input.shape
    length = segment_ids.shape[1]
    tokens = seqs * length
    width = d_skip.shape[0]
    rank = dt_proj.shape[0]
    n = (x_proj.shape[0] - rank) // 2
    me = lax.axis_index("shard")
    count = lax.axis_size("replica")
    height = count // 2
    side = lax.rem(lax.axis_index("replica"), 2)

    def split(values):
        return values.reshape(seqs, length, -1)

    def halves(values, blocks):
        piece = values.shape[1] // blocks // 2
        cuts = [values[:, b * piece : (b + 1) * piece] for b in range(2 * blocks)]
        even = jnp.concatenate(cuts[0::2], axis=1)
        odd = jnp.concatenate(cuts[1::2], axis=1)
        return jnp.where(side == 0, even, odd), jnp.where(side == 0, odd, even)

    xs, inv, cots, gain, own_half, y_half, z_half, x_part, z_part, gated_own, gated_send, gated_more = front(
        block_input, out_grad, norm_gain, w_in, out_proj
    )
    x_all = xs.reshape(tokens, model)
    cot = cots.reshape(tokens, -1)

    seg_padded = jnp.pad(segment_ids, ((0, 0), (KW - 1, 0)), constant_values=-1)
    taps = [
        (seg_padded[:, KW - 1 - d : KW - 1 - d + length] == segment_ids).astype(f32) for d in range(KW)
    ]
    conv_w = conv_weight.astype(f32)
    xv = x_part.astype(f32)
    x_padded = jnp.pad(xv, ((0, 0), (KW - 1, 0), (0, 0)))
    conv_pre = conv_bias.astype(f32) + conv_w[KW - 1] * xv
    for j in range(KW - 1):
        d = KW - 1 - j
        conv_pre = conv_pre + conv_w[j] * x_padded[:, j : j + length] * taps[d][:, :, None]
    conv_out = jax.nn.silu(conv_pre).astype(bf16)
    conv_flat = conv_out.reshape(tokens, width)
    own_half, y_half, z_half = (value.reshape(tokens, -1) for value in (own_half, y_half, z_half))
    last_norm = lax.ppermute(y_half, "replica", [(i, i ^ 2) for i in range(count)])
    cot_got = lax.ppermute(cot, "replica", [(i, i ^ 1) for i in range(count)])
    proj = group_total(outer_dot(x_proj, conv_flat), 3)
    gated_far = by_hop(gated_send, 2)
    proj, gated_far = lax.optimization_barrier((proj, gated_far))
    gated_rest = by_hop(after(gated_more, proj), 2)
    keep_lanes = jnp.broadcast_to(taps[1][:, :, None], (seqs, length, LANES))
    skip = d_skip.astype(f32)
    y_total, gated, rate, beta, states = recurrence_forward(
        conv_out, z_part, proj, keep_lanes, dt_proj, dt_bias.astype(f32)[None], skip[None]
    )
    y_total, gated, gated_rest, last_norm, cot_got = lax.optimization_barrier(
        (y_total, gated, gated_rest, last_norm, cot_got)
    )
    cot_both = jnp.concatenate([cot, cot_got], axis=0)
    grad_gated = split(gated_own + jnp.concatenate([gated_far, gated_rest], axis=1).astype(f32))
    z_vals = z_part.astype(f32)
    dy = grad_gated * jax.nn.silu(z_vals)
    grad_z = (grad_gated * y_total * silu_slope(z_vals)).astype(bf16).reshape(tokens, width)

    gated_keep, gated_give = halves(gated.reshape(tokens, width), height // 4)
    cols = model // 4
    keeps, gives, z_blocks, norms, gated_got = collect(
        gated_keep, gated_give, grad_z, own_half, y_half, z_half, last_norm
    )
    z_blocks = z_blocks.reshape(count, -1, width // 4)
    gated_both, block_output, grad_w_z = middle(keeps, gives, gated_got, z_blocks, x_all, out_proj, seqs)
    out_blocks = inner_dot(gated_both.reshape(2 * tokens, -1), cot_both)
    out_own, out_sent = far_send(out_blocks.astype(bf16).reshape(height, -1, cols))
    rate, out_own = lax.optimization_barrier((rate, out_own))

    grad_conv_rec, grad_dt_low, grad_proj, grad_dt_proj, grad_dt_bias, grad_d_skip = recurrence_backward(
        rate, beta, conv_out, dy, proj, keep_lanes, dt_proj, states
    )
    grad_proj, out_sent = lax.optimization_barrier((group_total(grad_proj, 4), out_sent))
    grad_proj = grad_proj.astype(bf16)
    grad_out_proj = far_total(out_own.astype(f32), out_sent)
    grad_x_proj = rows_dot(grad_proj, conv_flat)
    grad_conv = dy * skip + grad_conv_rec + split(inner_dot(grad_proj, x_proj))
    grad_pre = grad_conv * silu_slope(conv_pre)
    grad_conv_bias = jnp.sum(grad_pre, axis=(0, 1))
    grad_conv_weight = jnp.stack(
        [
            jnp.sum(grad_pre * x_padded[:, j : j + length] * taps[KW - 1 - j][:, :, None], axis=(0, 1))
            for j in range(KW)
        ]
    )
    grad_x = conv_w[KW - 1] * grad_pre
    for j in range(KW - 1):
        d = KW - 1 - j
        ahead = jnp.pad(grad_pre * taps[d][:, :, None], ((0, 0), (0, d), (0, 0)))[:, d:]
        grad_x = grad_x + conv_w[j] * ahead
    grad_x = grad_x.astype(bf16).reshape(tokens, width)

    smalls = (grad_x_proj, grad_dt_proj, grad_conv_weight, grad_conv_bias[None], grad_dt_bias, grad_d_skip)
    grad_w_in, grad_x_proj, grad_dt_proj, grad_conv_weight, conv_line, bias_line, skip_line, input_grad, grad_gain = finish(
        grad_x, grad_z, smalls, grad_w_z, norms, w_in, block_input, out_grad, gain, xs, inv
    )
    return (
        block_output, input_grad, grad_gain[0], grad_w_in, grad_conv_weight, conv_line[0], grad_x_proj, grad_dt_proj,
        bias_line[0], skip_line[0], grad_out_proj,
    )


def solution(mesh):
    return jax.shard_map(
        body,
        mesh=mesh,
        in_specs=(
            P("replica", "shard", None), P("replica", None), P("shard"), P(None, "shard"), P(None, "shard"),
            P("shard"), P(None, "shard"), P(None, "shard"), P("shard"), P("shard"), P(None, "shard"),
            P("replica", "shard", None),
        ),
        out_specs=(
            P("replica", "shard", None), P("replica", "shard", None), P("shard"), P("replica", "shard"),
            P(None, "shard"), P("shard"), P(None, "shard"), P(None, "shard"), P("shard"), P("shard"),
            P("replica", "shard"),
        ),
        check_vma=False,
    )
```
